32 devices in a mesh: fsdp: 16 (over z, y, x), rep: 2 (over core).
Axes of the slice: x: 2, y: 2, z: 4, core: 2. Of those that a mesh axis runs over, the one named last changes fastest.
Arguments:
- tokens: bfloat16 [32768, 768], P(('fsdp', 'rep')), may hold values from -6 to 6
- cotangent: bfloat16 [32768, 768], P(('fsdp', 'rep')), may hold values from -6 to 6
- segments: int32 [32768], P(('fsdp', 'rep')), may hold values from -1 to 511, as said below
- box_coords: int32 [4, 32768], P(None, ('fsdp', 'rep')), may hold values from 0 to 1023
- w_qkv: float32 [768, 2304], P('fsdp'), may hold values from -0.21875 to 0.21875
- b_qkv: float32 [2304], P('fsdp'), may hold values from -1 to 1
- w_box: float32 [128, 64], P('fsdp'), may hold values from -0.75 to 0.75
- w_out: float32 [768, 768], P('fsdp'), may hold values from -1.25 to 1.25
- b_out: float32 [768], P('fsdp'), may hold values from -1 to 1
- gain_one: float32 [768], P('fsdp'), may hold values from 0.5 to 1.5
- shift_one: float32 [768], P('fsdp'), may hold values from -1 to 1
- w_up: float32 [768, 3072], P('fsdp'), may hold values from -0.21875 to 0.21875
- b_up: float32 [3072], P('fsdp'), may hold values from -1 to 1
- w_down: float32 [3072, 768], P('fsdp'), may hold values from -0.109375 to 0.109375
- b_down: float32 [768], P('fsdp'), may hold values from -1 to 1
- gain_two: float32 [768], P('fsdp'), may hold values from 0.5 to 1.5
- shift_two: float32 [768], P('fsdp'), may hold values from -1 to 1
Outputs:
- layer_out: bfloat16 [32768, 768], P(('fsdp', 'rep'))
- grad_tokens: float32 [32768, 768], P(('fsdp', 'rep'))
- grad_w_qkv: float32 [768, 2304], P('fsdp')
- grad_b_qkv: float32 [2304], P('fsdp')
- grad_w_box: float32 [128, 64], P('fsdp')
- grad_w_out: float32 [768, 768], P('fsdp')
- grad_b_out: float32 [768], P('fsdp')
- grad_gain_one: float32 [768], P('fsdp')
- grad_shift_one: float32 [768], P('fsdp')
- grad_w_up: float32 [768, 3072], P('fsdp')
- grad_b_up: float32 [3072], P('fsdp')
- grad_w_down: float32 [3072, 768], P('fsdp')
- grad_b_down: float32 [768], P('fsdp')
- grad_gain_two: float32 [768], P('fsdp')
- grad_shift_two: float32 [768], P('fsdp')
The draws below stay inside these ranges and needn't reach their ends.
Inputs may be any that keep to these rules, and one draw needn't show every extreme that they name: `segments`: each slot of 512 consecutive tokens holds whole pages, each page a run of consecutive tokens with the position in the slot of its first token as value, followed by padding at the slot's end valued -1; pages hold up to 512 tokens, heavy-tailed; every fourth slot (slot index divisible by 4) has no padding and ends with a page of one token, the others have 1 to 256 padding tokens.
All inputs are finite; a program needn't handle non-finite values.
Results may differ from the reference program's by a relative error of at most 0.022.
Values may be sent and summed in bfloat16 or wider, within the bound.
A program may use at most 256 MiB of HBM per device.

```python
import math
import jax
import jax.numpy as jnp
from jax import lax

D = 768
HEADS = 12
HD = 64
FF = 3072
FREQ = 16
SLOT = 512
TOKENS = 32768


def draw_segments(key, part):
    slot_count = TOKENS // SLOT
    key_exp, key_len, key_pad = jax.random.split(key, 3)
    power = jax.random.randint(key_exp, (slot_count, SLOT), 0, 8)
    ceiling = jnp.minimum(4 * jnp.left_shift(jnp.ones_like(power), power), SLOT)
    lengths = 1 + jax.random.randint(key_len, (slot_count, SLOT), 0, SLOT) % ceiling
    page_ends = jnp.cumsum(lengths, axis=1)
    page_starts = page_ends - lengths
    padding = 1 + jax.random.randint(key_pad, (slot_count,), 0, SLOT // 2)
    full_slot = jnp.arange(slot_count) % 4 == 0
    padding = jnp.where(full_slot, 0, padding)
    used = SLOT - padding
    position = jnp.arange(SLOT, dtype=jnp.int32)
    page_index = jnp.sum((page_ends[:, None, :] <= position[None, :, None]).astype(jnp.int32), axis=2)
    start = jnp.take_along_axis(page_starts, page_index, axis=1)
    segment_rows = jnp.where(position[None, :] < used[:, None], start, -1)
    last_page = full_slot[:, None] & (position[None, :] == SLOT - 1)
    segment_rows = jnp.where(last_page, SLOT - 1, segment_rows)
    return segment_rows.reshape(-1).astype(jnp.int32)


def place_ends(values, stream_key, least, top_value):
    longest = values.shape.index(max(values.shape))
    spots = []
    for shift in (0, 1):
        where = [jax.random.randint(jax.random.fold_in(stream_key, axis), (), 0, length) for axis, length in enumerate(values.shape)]
        where[longest] = (where[longest] + shift) % values.shape[longest]
        spots.append(tuple(where))
    return values.at[spots[0]].set(least).at[spots[1]].set(top_value)


def raised(values, key, source, target, parts, factor):
    def block_of(dim):
        return (jnp.arange(values.shape[dim]) // (values.shape[dim] // parts)).reshape((-1,) + (1,) * (values.ndim - 1 - dim))

    one_side = jax.random.permutation(key, parts)[block_of(target)]
    second = (block_of(target) + parts // 2) % parts
    return jnp.where((block_of(source) == one_side) | (block_of(source) == second), factor * values, values)


def level_of(key, dims, pieces, low, top_value):
    loudness, own = 1.0, jax.random.fold_in(key, 6)
    for axis_at, blocks in pieces:
        heights = jnp.exp(jax.random.uniform(jax.random.fold_in(own, axis_at), (blocks,), jnp.float32, low / len(pieces), top_value / len(pieces)))
        loudness = loudness * jnp.repeat(heights, dims[axis_at] // blocks).reshape([-1 if axis == axis_at else 1 for axis in range(len(dims))])
    return loudness


def normal_values(rng, extent, deviation, reach, cuts=(), held_as=jnp.bfloat16):
    loudness = level_of(rng, extent, cuts, -0.22, 0.18) if cuts else 1.0
    drawn = jax.random.normal(rng, extent, jnp.float32) * deviation * loudness
    return jnp.minimum(jnp.maximum(drawn, -reach), reach).astype(held_as)


def noise_with(rng, shape, scale, reach, pieces, heavy, kind=jnp.bfloat16):
    values = scale * jax.random.normal(rng, shape, jnp.float32)
    if pieces:
        values = values * level_of(rng, shape, pieces, -0.22, 0.18)
    return jnp.clip(raised(values, jax.random.fold_in(rng, 3), *heavy), -reach, reach).astype(kind)


def setup_inputs(seed: int = 0) -> dict:
    seeds = jax.random.split(jax.random.key(seed), 18)
    tokens = noise_with(seeds[0], (TOKENS, D), 1.0, 6.0, ((0, 32),), (0, 1, 32, 2.75))
    cotangent = noise_with(seeds[1], (TOKENS, D), 1.0, 6.0, ((0, 32),), (0, 1, 32, 2.75))
    segments = draw_segments(jax.random.fold_in(seeds[17], 71), 0)
    box_coords = place_ends(jax.random.randint(seeds[3], (4, TOKENS), 0, 1024), jax.random.fold_in(seeds[3], 1), 0, 1023).astype(jnp.int32)
    w_qkv = normal_values(seeds[4], (D, 3 * D), D ** -0.5, 0.21875, ((0, 16),), jnp.float32)
    b_qkv = normal_values(seeds[5], (3 * D,), 0.2, 1.0, ((0, 16),), jnp.float32)
    w_box = normal_values(seeds[6], (8 * FREQ, HD), HD ** -0.5, 0.75, ((0, 16),), jnp.float32)
    w_out = normal_values(seeds[7], (D, D), (D // 32) ** -0.5, 1.25, ((0, 16),), jnp.float32)
    b_out = normal_values(seeds[8], (D,), 0.2, 1.0, ((0, 16),), jnp.float32)
    gain_one = jnp.clip(1.0 + 0.1 * jax.random.normal(seeds[9], (D,), jnp.float32), 0.5, 1.5)
    shift_one = normal_values(seeds[10], (D,), 0.2, 1.0, ((0, 16),), jnp.float32)
    w_up = normal_values(seeds[11], (D, FF), D ** -0.5, 0.21875, ((0, 16),), jnp.float32)
    b_up = normal_values(seeds[12], (FF,), 0.2, 1.0, ((0, 16),), jnp.float32)
    w_down = normal_values(seeds[13], (FF, D), FF ** -0.5, 0.109375, ((0, 16),), jnp.float32)
    b_down = normal_values(seeds[14], (D,), 0.2, 1.0, ((0, 16),), jnp.float32)
    gain_two = jnp.clip(1.0 + 0.1 * jax.random.normal(seeds[15], (D,), jnp.float32), 0.5, 1.5)
    shift_two = normal_values(seeds[16], (D,), 0.2, 1.0, ((0, 16),), jnp.float32)
    return {"tokens": tokens, "cotangent": cotangent, "segments": segments, "box_coords": box_coords, "w_qkv": w_qkv, "b_qkv": b_qkv, "w_box": w_box, "w_out": w_out, "b_out": b_out, "gain_one": gain_one, "shift_one": shift_one, "w_up": w_up, "b_up": b_up, "w_down": w_down, "b_down": b_down, "gain_two": gain_two, "shift_two": shift_two}


@jax.custom_vjp
def low(v):
    return lax.optimization_barrier(v.astype(jnp.bfloat16)).astype(jnp.float32)

@jax.custom_vjp
def low_back(v):
    return v

def low_keep(v):
    return (low(v), None)

def low_pass(kept, grad):
    return (grad,)

def back_keep(v):
    return (v, None)

def back_low(kept, grad):
    return (low(grad),)
low.defvjp(low_keep, low_pass)
low_back.defvjp(back_keep, back_low)
highest = lax.Precision.HIGHEST
neg_large = -1e+30
eps_norm = 1e-12

def both_ways(value):
    return low(low_back(value))

def wave_tables(box_coords):
    scaled = box_coords.astype(jnp.float32) * (100.0 / 1024.0)
    frequency = jnp.exp(-math.log(10000.0) * jnp.arange(FREQ, dtype=jnp.float32) / FREQ)
    angles = scaled[:, :, None] * frequency[None, None, :]
    angles = jnp.transpose(angles, (1, 0, 2)).reshape(box_coords.shape[1], 4 * FREQ)
    return (low(jnp.sin(angles)), low(jnp.cos(angles)))

def normalize(pre_rows, gain, shift):
    center = pre_rows - lax.optimization_barrier(jnp.mean(pre_rows, axis=-1, keepdims=True))
    invdev = lax.rsqrt(lax.optimization_barrier(jnp.mean(center * center, axis=-1, keepdims=True)) + eps_norm)
    return center * invdev * gain + shift

def attend_slot(attn_params, slot_block):
    w_qkv, b_qkv, w_box, w_out, b_out = attn_params
    slot_rows, segment_rows, sine_table, cosine_table = slot_block
    row_count = slot_rows.shape[0]
    model_width = slot_rows.shape[1]
    wave_half = sine_table.shape[1]
    mixed_rows = both_ways(jnp.dot(slot_rows, w_qkv, precision=highest) + b_qkv)
    queries = mixed_rows[:, :model_width].reshape(row_count, HEADS, HD)
    keys_in = mixed_rows[:, model_width:2 * model_width].reshape(row_count, HEADS, HD)
    values_in = mixed_rows[:, 2 * model_width:].reshape(row_count, HEADS, HD)
    sine_heads = jnp.broadcast_to(sine_table[:, None, :], (row_count, HEADS, wave_half))
    cosine_heads = jnp.broadcast_to(cosine_table[:, None, :], (row_count, HEADS, wave_half))
    q_box = low_back(jnp.einsum('thd,fd->thf', queries, w_box, precision=highest))
    k_box = low_back(jnp.einsum('thd,fd->thf', keys_in, w_box, precision=highest))
    q_sin, q_cos = (q_box[..., :wave_half], q_box[..., wave_half:])
    k_sin, k_cos = (k_box[..., :wave_half], k_box[..., wave_half:])
    q_side = low(jnp.concatenate([q_sin * sine_heads + q_cos * cosine_heads, q_cos * sine_heads - q_sin * cosine_heads], axis=-1))
    k_side = low(jnp.concatenate([k_sin * cosine_heads + k_cos * sine_heads, k_cos * cosine_heads - k_sin * sine_heads], axis=-1))
    q_full = jnp.concatenate([queries, q_side, sine_heads, cosine_heads], axis=-1)
    k_full = jnp.concatenate([keys_in, cosine_heads, sine_heads, k_side], axis=-1)
    scores = low_back(jnp.einsum('qhd,khd->hqk', q_full, k_full, precision=highest) * (1.0 / math.sqrt(HD)))
    allowed = segment_rows[:, None] == segment_rows[None, :]
    scores = jnp.where(allowed[None], scores, neg_large)
    row_max = lax.optimization_barrier(jnp.max(scores, axis=-1, keepdims=True))
    exp_scores = jnp.exp(scores - row_max)
    soft_probs = low(exp_scores / lax.optimization_barrier(jnp.sum(exp_scores, axis=-1, keepdims=True)))
    context = jnp.einsum('hqk,khd->qhd', soft_probs, values_in, precision=highest).reshape(row_count, model_width)
    context = both_ways(context)
    return low_back(jnp.dot(context, w_out, precision=highest) + b_out)

def reference(tokens, cotangent, segments, box_coords, w_qkv, b_qkv, w_box, w_out, b_out, gain_one, shift_one, w_up, b_up, w_down, b_down, gain_two, shift_two):
    sine_table, cosine_table = wave_tables(box_coords)
    slot_count = tokens.shape[0] // SLOT
    checked_slot = jax.checkpoint(attend_slot)

    def forward(tokens_in, m_qkv, m_bqkv, m_box, m_out, m_bout, m_gone, m_sone, m_up, m_bup, m_down, m_bdown, m_gtwo, m_stwo):
        attn_params = (low(m_qkv), low(m_bqkv), low(m_box), low(m_out), low(m_bout))
        blocks = (tokens_in.reshape(slot_count, SLOT, -1), segments.reshape(slot_count, SLOT), sine_table.reshape(slot_count, SLOT, -1), cosine_table.reshape(slot_count, SLOT, -1))
        branch = lax.map(lambda slot_block: checked_slot(attn_params, slot_block), blocks)
        branch = branch.reshape(tokens_in.shape)
        hidden = normalize(tokens_in + branch, low(m_gone), low(m_sone))
        up_proj = low_back(jnp.dot(low(hidden), low(m_up), precision=highest) + low(m_bup))
        act_low = low(jax.nn.gelu(up_proj, approximate=False))
        down_proj = low_back(jnp.dot(act_low, low(m_down), precision=highest) + low(m_bdown))
        return normalize(hidden + down_proj, low(m_gtwo), low(m_stwo))
    result, pullback = jax.vjp(forward, tokens.astype(jnp.float32), w_qkv, b_qkv, w_box, w_out, b_out, gain_one, shift_one, w_up, b_up, w_down, b_down, gain_two, shift_two)
    gradients = pullback(cotangent.astype(jnp.float32))
    return (result.astype(jnp.bfloat16), gradients[0], gradients[1], gradients[2], gradients[3], gradients[4], gradients[5], gradients[6], gradients[7], gradients[8], gradients[9], gradients[10], gradients[11], gradients[12], gradients[13])
```

```python
import functools
import math

import jax
import jax.numpy as jnp
from jax import lax
from jax.experimental import pallas as pl
from jax.experimental.pallas import tpu as pltpu
from jax.sharding import PartitionSpec as P

HEADS = 12
HD = 64
FREQ = 16
SLOT = 512
WAVE = 4 * FREQ
PAIR = 2 * HD
QUAD = 4 * HD

f32 = jnp.float32
bf16 = jnp.bfloat16
neg_large = -1e30
eps_norm = 1e-12
scale_factor = 1.0 / math.sqrt(HD)
vmem_limit = 64_000_000


def dot_nn(left, right):
    return lax.dot_general(left, right, (((1,), (0,)), ((), ())), preferred_element_type=f32)


def dot_nt(left, right):
    return lax.dot_general(left, right, (((1,), (1,)), ((), ())), preferred_element_type=f32)


def dot_tn(left, right):
    return lax.dot_general(left, right, (((0,), (0,)), ((), ())), preferred_element_type=f32)


def aligned(index, size):
    return pl.ds(pl.multiple_of(index * size, size), size)


def wave_rows(coord_bits):
    row = lax.broadcasted_iota(jnp.int32, (2 * WAVE, 16), 0)
    col = lax.broadcasted_iota(jnp.int32, (2 * WAVE, 16), 1)
    coord_of = (row % WAVE) // FREQ
    pick = jnp.where(col == coord_of, 32.0, jnp.where(col == coord_of + 4, 1.0, 0.0)).astype(bf16)
    coords = dot_nn(pick, coord_bits)
    rows = lax.broadcasted_iota(jnp.int32, coords.shape, 0)
    freq_index = (rows % FREQ).astype(f32)
    frequency = jnp.exp(-math.log(10000.0) * freq_index / FREQ)
    angle = coords * (100.0 / 1024.0) * frequency
    turns = jnp.floor(angle * (2.0 / math.pi) + 0.5)
    rest = ((angle - turns * 1.5703125) - turns * 4.837512969970703125e-4) - turns * 7.549789954891e-8
    square = rest * rest
    sine = rest + rest * square * (
        -1.6666654611e-1 + square * (8.3321608736e-3 + square * -1.9515295891e-4)
    )
    cosine = 1.0 - 0.5 * square + square * square * (
        4.166664568298827e-2 + square * (-1.388731625493765e-3 + square * 2.443315711809948e-5)
    )
    quadrant = turns.astype(jnp.int32) + jnp.where(rows >= WAVE, 1, 0)
    value = jnp.where((quadrant & 1) == 1, cosine, sine)
    value = jnp.where((quadrant & 2) == 2, -value, value)
    return value.astype(bf16).astype(f32)


def swap_lanes(value):
    return pltpu.roll(value, WAVE, 1)


def attend_forward(
    tok, coord_bits, segs, w_qkv, b_qkv, w_box,
    q8t, k8t, v_row, e_hbm, inv_total, ctx, ctx_t, wave_t,
    k_row, v_t, bias, wave_r, e_buf, e_sem,
):
    slot_count = tok.shape[0] // SLOT
    width = tok.shape[1]
    pairs = HEADS // 2
    wave_t[...] = wave_rows(coord_bits[...])
    wave_r[...] = jnp.transpose(wave_t[...])
    for slot in range(slot_count):
        seg = segs[slot : slot + 1, :].astype(f32)
        seg_i = jnp.broadcast_to(seg, (SLOT, SLOT))
        seg_j = jnp.transpose(seg_i)
        bias[slot] = jnp.where(seg_i == seg_j, 0.0, neg_large)

    def project(step, carry):
        quad, slot = step // slot_count, step % slot_count
        rows = tok[aligned(slot, SLOT), :]

        def columns(part):
            at = pl.ds(pl.multiple_of(part * width + quad * QUAD, QUAD), QUAD)
            return (dot_nn(rows, w_qkv[:, at]) + b_qkv[:, at]).astype(bf16)

        q, k, v = columns(0), columns(1), columns(2)
        qt = jnp.transpose(q.astype(f32) * scale_factor).astype(bf16)
        kt = jnp.transpose(k.astype(f32) * scale_factor).astype(bf16)
        vt = jnp.transpose(v.astype(f32)).astype(bf16)
        for part in range(2):
            pair = quad * 2 + part
            here = slice(part * PAIR, (part + 1) * PAIR)
            q8t[slot, pair] = qt[here]
            k8t[slot, pair] = kt[here]
            v_t[slot, pair] = vt[here]
            k_row[slot, pair] = k[:, here]
            v_row[slot, pair] = v[:, here]
        return carry

    lax.fori_loop(0, slot_count * (pairs // 2), project, 0)

    lane = lax.broadcasted_iota(jnp.int32, (SLOT, PAIR), 1)

    def attend(step, carry):
        pair, slot = step // slot_count, step % slot_count
        cols = aligned(slot, SLOT)
        place = step % 2

        @pl.when(step >= 2)
        def _():
            for head in range(2):
                pltpu.make_async_copy(e_buf.at[place, head], e_hbm.at[0], e_sem.at[place, head]).wait()

        sine_t, cosine_t = wave_t[:WAVE, cols], wave_t[WAVE:, cols]
        sc_t = (wave_t[:, cols] * scale_factor).astype(bf16)
        sc_r = wave_r[cols, :]
        cs_r = swap_lanes(sc_r)
        cc_r = jnp.where(lane < WAVE, cs_r, sc_r)
        ss_r = jnp.where(lane < WAVE, sc_r, -cs_r)
        cs_low = cs_r.astype(bf16)
        keys = k_row[slot, pair]
        heads_t = []
        for head in range(2):
            span = slice(head * HD, (head + 1) * HD)
            key_box = dot_nt(keys[:, span], w_box[...])
            k_side = (key_box * cc_r + swap_lanes(key_box) * ss_r).astype(bf16)
            q_t = q8t[slot, pair, span, :]
            query_box = dot_nn(w_box[...], q_t)
            first, second = query_box[:WAVE], query_box[WAVE:]
            q_side = jnp.concatenate(
                [first * sine_t + second * cosine_t, second * sine_t - first * cosine_t], axis=0
            ).astype(bf16)
            zero = jnp.zeros_like(q_t)
            q_pair = [q_t, zero] if head == 0 else [zero, q_t]
            k_full = jnp.concatenate([keys, cs_low, k_side], axis=1)
            q_full = jnp.concatenate(q_pair + [q_side, sc_t], axis=0)
            scores = dot_nn(k_full, q_full) + bias[slot]
            top = jnp.max(scores, axis=0, keepdims=True)
            exps = jnp.exp(scores - top)
            inverse = 1.0 / jnp.sum(exps, axis=0, keepdims=True)
            low_exps = exps.astype(bf16)
            e_buf[place, head] = low_exps
            pltpu.make_async_copy(
                e_buf.at[place, head], e_hbm.at[step * 2 + head], e_sem.at[place, head]
            ).start()
            inv_total[step * 2 + head] = inverse
            heads_t.append(dot_nn(v_t[slot, pair, span, :], low_exps) * inverse)
        both = jnp.concatenate(heads_t, axis=0)
        ctx_t[aligned(pair, PAIR), cols] = both.astype(bf16)
        ctx[cols, aligned(pair, PAIR)] = jnp.transpose(both).astype(bf16)
        return carry

    steps = slot_count * pairs
    lax.fori_loop(0, steps, attend, 0)
    for place in range(2):
        for head in range(2):
            pltpu.make_async_copy(e_buf.at[place, head], e_hbm.at[0], e_sem.at[place, head]).wait()


def attend_backward(
    tok_t, q8t, k8t, v_row, e_hbm, inv_total, ctx_t, g_ctx_t, wave_t, w_qkv, w_box, w_box_t, g_pre_one,
    g_tok, g_w_qkv, g_b_qkv, g_w_box,
    g_mix, e_buf, e_sem,
):
    slot_count = tok_t.shape[1] // SLOT
    width = tok_t.shape[0]
    pairs = HEADS // 2
    steps = slot_count * pairs
    g_w_box[...] = jnp.zeros_like(g_w_box)

    def fetch(step, place):
        for head in range(2):
            pltpu.make_async_copy(
                e_hbm.at[step * 2 + head], e_buf.at[place, head], e_sem.at[place, head]
            ).start()

    fetch(0, 0)

    def attend(step, carry):
        pair, slot = step // slot_count, step % slot_count
        cols = aligned(slot, SLOT)
        place = step % 2

        @pl.when(step + 1 < steps)
        def _():
            fetch(step + 1, 1 - place)

        for head in range(2):
            pltpu.make_async_copy(e_hbm.at[0], e_buf.at[place, head], e_sem.at[place, head]).wait()
        sine_t, cosine_t = wave_t[:WAVE, cols], wave_t[WAVE:, cols]
        sc_t = (wave_t[:, cols] * scale_factor).astype(bf16)
        cs_t = (jnp.concatenate([cosine_t, sine_t], axis=0) * scale_factor).astype(bf16)
        values = v_row[slot, pair]
        g_parts = [[], [], []]
        for head in range(2):
            span = slice(head * HD, (head + 1) * HD)
            at = pl.ds(pl.multiple_of(pair * PAIR + head * HD, HD), HD)
            g_rows = g_ctx_t[at, cols].astype(f32) * inv_total[step * 2 + head]
            row_dot = jnp.sum(g_rows * ctx_t[at, cols].astype(f32), axis=0, keepdims=True)
            g_low = g_rows.astype(bf16)
            zero = jnp.zeros_like(g_low)
            g_pair = jnp.concatenate([g_low, zero] if head == 0 else [zero, g_low], axis=0)
            low_exps = e_buf[place, head]
            g_probs = dot_nn(values, g_pair)
            g_scores = (low_exps.astype(f32) * (g_probs - row_dot)).astype(bf16)
            g_parts[2].append(dot_nt(g_low, low_exps))
            k_t, q_t = k8t[slot, pair, span, :], q8t[slot, pair, span, :]
            g_q = dot_nn(jnp.concatenate([k_t, cs_t], axis=0), g_scores)
            g_k = dot_nt(jnp.concatenate([q_t, sc_t], axis=0), g_scores)
            first, second = g_q[HD : HD + WAVE], g_q[HD + WAVE :]
            g_qbox = jnp.concatenate(
                [first * sine_t - second * cosine_t, first * cosine_t + second * sine_t], axis=0
            ).astype(bf16)
            first, second = g_k[HD : HD + WAVE], g_k[HD + WAVE :]
            g_kbox = jnp.concatenate(
                [first * cosine_t - second * sine_t, first * sine_t + second * cosine_t], axis=0
            ).astype(bf16)
            g_parts[0].append(g_q[:HD] + dot_nn(w_box_t[...], g_qbox))
            g_parts[1].append(g_k[:HD] + dot_nn(w_box_t[...], g_kbox))
            g_w_box[...] += dot_nt(g_qbox, q_t) + dot_nt(g_kbox, k_t)
        for part in range(3):
            g_mix[part, aligned(pair, PAIR), cols] = jnp.concatenate(g_parts[part], axis=0).astype(bf16)
        return carry

    lax.fori_loop(0, steps, attend, 0)
    g_w_box[...] = g_w_box[...] * (1.0 / scale_factor)

    ones = jnp.ones((16, tok_t.shape[1]), bf16)

    def weight_grad(step, carry):
        part, quad = step // (pairs // 2), step % (pairs // 2)
        grad = g_mix[part, aligned(quad, QUAD), :]
        at = pl.ds(pl.multiple_of(part * width + quad * QUAD, QUAD), QUAD)
        g_w_qkv[:, at] = dot_nt(tok_t[...], grad).astype(bf16)
        g_b_qkv[:, at] = dot_nt(ones, grad)[:1]
        return carry

    lax.fori_loop(0, 3 * (pairs // 2), weight_grad, 0)

    def token_grad(step, carry):
        cols = aligned(step, QUAD)
        total = dot_nn(w_qkv[:, :width], g_mix[0, :, cols])
        total += dot_nn(w_qkv[:, width : 2 * width], g_mix[1, :, cols])
        total += dot_nn(w_qkv[:, 2 * width :], g_mix[2, :, cols])
        g_tok[cols, :] = jnp.transpose(total) + g_pre_one[cols, :]
        return carry

    lax.fori_loop(0, tok_t.shape[1] // QUAD, token_grad, 0)


def gelu_parts(value):
    size = jnp.abs(value) * math.sqrt(0.5)
    t = 1.0 / (1.0 + 0.3275911 * size)
    bell = jnp.exp(-0.5 * value * value)
    tail = t * (
        0.254829592 + t * (-0.284496736 + t * (1.421413741 + t * (-1.453152027 + t * 1.061405429)))
    )
    half_tail = 0.5 * tail * bell
    return jnp.where(value >= 0, 1.0 - half_tail, half_tail), bell * (1.0 / math.sqrt(2.0 * math.pi))


def row_mean(value):
    return jnp.mean(value, axis=-1, keepdims=True)


ROWS = 256
FCOLS = 512


def feed_forward(
    tok, cot, ctx, ctx_t, w_out, b_out, gain_one, shift_one, w_up, b_up, w_down, b_down, gain_two, shift_two,
    layer_out, g_pre_one, g_ctx_t, tok_t, g_w_out, g_w_up, g_w_down, g_b_up, g_small,
    act, slope, normed, total, low_hidden, low_hidden_t, g_down, inv_one,
):
    width = tok.shape[1]
    row_blocks = tok.shape[0] // ROWS
    col_blocks = w_up.shape[1] // FCOLS
    g_small[...] = jnp.zeros_like(g_small)
    g_b_up[...] = jnp.zeros_like(g_b_up)

    def column_sum(value):
        return jnp.sum(value, axis=0, keepdims=True)

    def first_norm(block, carry):
        rows = aligned(block, ROWS)
        token_rows = tok[rows, :].astype(f32)
        tok_t[:, rows] = jnp.transpose(token_rows).astype(bf16)
        pre = token_rows + dot_nn(ctx[rows, :], w_out[...]) + b_out[...]
        center = pre - row_mean(pre)
        invdev = lax.rsqrt(row_mean(center * center) + eps_norm)
        unit = center * invdev
        inv_one[rows, :] = jnp.broadcast_to(invdev, (ROWS, 128))
        normed[rows, :] = unit
        hidden = unit * gain_one[...] + shift_one[...]
        low_hidden[rows, :] = hidden.astype(bf16)
        low_hidden_t[:, rows] = jnp.transpose(hidden).astype(bf16)
        return carry

    lax.fori_loop(0, row_blocks, first_norm, 0)

    def up_down(step, carry):
        col, block = step // row_blocks, step % row_blocks
        rows, cols = aligned(block, ROWS), aligned(col, FCOLS)
        up = dot_nn(low_hidden[rows, :], w_up[:, cols]) + b_up[:, cols]
        cdf, pdf = gelu_parts(up)
        low_act = (up * cdf).astype(bf16)
        act[col, rows, :] = low_act
        slope[col, rows, :] = (cdf + up * pdf).astype(bf16)
        down = dot_nn(low_act, w_down[cols, :])

        @pl.when(col == 0)
        def _():
            total[rows, :] = down

        @pl.when(col > 0)
        def _():
            total[rows, :] += down

        return carry

    lax.fori_loop(0, col_blocks * row_blocks, up_down, 0)

    def second_norm(block, carry):
        rows = aligned(block, ROWS)
        pre = normed[rows, :] * gain_one[...] + shift_one[...] + total[rows, :] + b_down[...]
        center = pre - row_mean(pre)
        invdev = lax.rsqrt(row_mean(center * center) + eps_norm)
        unit = center * invdev
        layer_out[rows, :] = (unit * gain_two[...] + shift_two[...]).astype(bf16)
        grad = cot[rows, :].astype(f32)
        scaled = grad * gain_two[...]
        g_pre = invdev * (scaled - row_mean(scaled) - unit * row_mean(scaled * unit))
        total[rows, :] = g_pre
        low_pre = g_pre.astype(bf16)
        g_down[rows, :] = low_pre
        g_small[0:1, :] += column_sum(grad * unit)
        g_small[1:2, :] += column_sum(grad)
        g_small[2:3, :] += column_sum(low_pre.astype(f32))
        return carry

    lax.fori_loop(0, row_blocks, second_norm, 0)

    def back_columns(col, carry):
        cols = aligned(col, FCOLS)

        def back_rows(block, inner):
            rows = aligned(block, ROWS)
            g_act = dot_nt(g_down[rows, :], w_down[cols, :])
            g_up = (g_act * slope[col, rows, :].astype(f32)).astype(bf16)
            slope[col, rows, :] = g_up
            g_b_up[:, cols] += column_sum(g_up.astype(f32))
            total[rows, :] += dot_nt(g_up, w_up[:, cols])
            return inner

        lax.fori_loop(0, row_blocks, back_rows, 0)
        g_w_down[cols, :] = dot_tn(act[col], g_down[...]).astype(bf16)
        g_w_up[:, cols] = dot_nn(low_hidden_t[...], slope[col]).astype(bf16)
        return carry

    lax.fori_loop(0, col_blocks, back_columns, 0)

    def first_back(block, carry):
        rows = aligned(block, ROWS)
        grad, unit = total[rows, :], normed[rows, :]
        scaled = grad * gain_one[...]
        g_pre = inv_one[rows, :1] * (scaled - row_mean(scaled) - unit * row_mean(scaled * unit))
        g_pre_one[rows, :] = g_pre
        low_pre = g_pre.astype(bf16)
        g_down[rows, :] = low_pre
        g_small[3:4, :] += column_sum(grad * unit)
        g_small[4:5, :] += column_sum(grad)
        g_small[5:6, :] += column_sum(low_pre.astype(f32))
        g_ctx_t[:, rows] = dot_nt(w_out[...], low_pre).astype(bf16)
        return carry

    lax.fori_loop(0, row_blocks, first_back, 0)

    def out_grad(block, carry):
        rows = aligned(block, ROWS)
        g_w_out[rows, :] = dot_nn(ctx_t[rows, :], g_down[...]).astype(bf16)
        return carry

    lax.fori_loop(0, width // ROWS, out_grad, 0)


def shaped(shape, dtype):
    return jax.ShapeDtypeStruct(shape, dtype)


def in_vmem(count):
    return [pl.BlockSpec(memory_space=pltpu.VMEM)] * count


def params():
    return pltpu.CompilerParams(vmem_limit_bytes=vmem_limit)


def run_forward(tokens, coord_bits, segs, w_qkv, b_qkv, w_box):
    count, width = tokens.shape
    slots, pairs = count // SLOT, HEADS // 2
    out_shape = [
        shaped((slots, pairs, PAIR, SLOT), bf16),
        shaped((slots, pairs, PAIR, SLOT), bf16),
        shaped((slots, pairs, SLOT, PAIR), bf16),
        shaped((slots * HEADS, SLOT, SLOT), bf16),
        shaped((slots * HEADS, 1, SLOT), f32),
        shaped((count, width), bf16),
        shaped((width, count), bf16),
        shaped((2 * WAVE, count), f32),
    ]
    out_specs = in_vmem(3) + [pl.BlockSpec(memory_space=pl.ANY)] + in_vmem(4)
    return pl.pallas_call(
        attend_forward,
        out_shape=out_shape,
        in_specs=in_vmem(6),
        out_specs=out_specs,
        scratch_shapes=[
            pltpu.VMEM((slots, pairs, SLOT, PAIR), bf16),
            pltpu.VMEM((slots, pairs, PAIR, SLOT), bf16),
            pltpu.VMEM((slots, SLOT, SLOT), f32),
            pltpu.VMEM((count, 2 * WAVE), f32),
            pltpu.VMEM((2, 2, SLOT, SLOT), bf16),
            pltpu.SemaphoreType.DMA((2, 2)),
        ],
        compiler_params=params(),
        name="attend_forward",
    )(tokens, coord_bits, segs, w_qkv, b_qkv, w_box)


def run_feed_forward(tok, cot, ctx, ctx_t, w_out, b_out, g1, s1, w_up, b_up, w_down, b_down, g2, s2):
    count, width = tok.shape
    ff = w_up.shape[1]
    out_shape = [
        shaped((count, width), bf16),
        shaped((count, width), f32),
        shaped((width, count), bf16),
        shaped((width, count), bf16),
        shaped(w_out.shape, bf16),
        shaped(w_up.shape, bf16),
        shaped(w_down.shape, bf16),
        shaped((1, ff), f32),
        shaped((8, width), f32),
    ]
    return pl.pallas_call(
        feed_forward,
        out_shape=out_shape,
        in_specs=in_vmem(14),
        out_specs=in_vmem(9),
        scratch_shapes=[
            pltpu.VMEM((ff // FCOLS, count, FCOLS), bf16),
            pltpu.VMEM((ff // FCOLS, count, FCOLS), bf16),
            pltpu.VMEM((count, width), f32),
            pltpu.VMEM((count, width), f32),
            pltpu.VMEM((count, width), bf16),
            pltpu.VMEM((width, count), bf16),
            pltpu.VMEM((count, width), bf16),
            pltpu.VMEM((count, 128), f32),
        ],
        compiler_params=params(),
        name="feed_forward",
    )(tok, cot, ctx, ctx_t, w_out, b_out, g1, s1, w_up, b_up, w_down, b_down, g2, s2)


def run_backward(tok_t, q8t, k8t, v_row, e_hbm, inv_total, ctx_t, g_ctx_t, wave_t, w_qkv, w_box, w_box_t, g_pre_one):
    width, count = tok_t.shape
    out_shape = [
        shaped((count, width), f32),
        shaped(w_qkv.shape, bf16),
        shaped((1, w_qkv.shape[1]), f32),
        shaped(w_box.shape, f32),
    ]
    return pl.pallas_call(
        attend_backward,
        out_shape=out_shape,
        in_specs=in_vmem(4) + [pl.BlockSpec(memory_space=pl.ANY)] + in_vmem(8),
        out_specs=in_vmem(4),
        scratch_shapes=[
            pltpu.VMEM((3, width, count), bf16),
            pltpu.VMEM((2, 2, SLOT, SLOT), bf16),
            pltpu.SemaphoreType.DMA((2, 2)),
        ],
        compiler_params=params(),
        name="attend_backward",
    )(tok_t, q8t, k8t, v_row, e_hbm, inv_total, ctx_t, g_ctx_t, wave_t, w_qkv, w_box, w_box_t, g_pre_one)


def per_device(
    fsdp, tokens, cotangent, segments, box_coords, w_qkv, b_qkv, w_box, w_out, b_out, gain_one, shift_one,
    w_up, b_up, w_down, b_down, gain_two, shift_two,
):
    count, width = tokens.shape
    low = lambda value: value.astype(bf16)
    gather = lambda value: lax.all_gather(low(value), "fsdp", axis=0, tiled=True)
    wq, wo, wu, wd = gather(w_qkv), gather(w_out), gather(w_up), gather(w_down)
    vectors = [b_qkv, b_out, gain_one, shift_one, b_up, b_down, gain_two, shift_two, w_box.reshape(-1)]
    sizes = [v.shape[0] for v in vectors]
    total = sum(sizes)
    padded = -(-total // 128) * 128
    packed = jnp.concatenate([low(v) for v in vectors] + [jnp.zeros((padded - total,), bf16)]).reshape(1, padded)
    table = lax.all_gather(packed, "fsdp", axis=0, tiled=True)
    full, at = [], 0
    for size in sizes:
        full.append(table[:, at : at + size].reshape(1, -1).astype(f32))
        at += size
    bq, bo, g1, s1, bu, bd, g2, s2 = full[:8]
    wb = full[8].reshape(-1, HD).astype(bf16)

    bits = jnp.concatenate([box_coords >> 5, box_coords & 31, jnp.zeros((8, count), jnp.int32)], axis=0).astype(bf16)
    segs = segments.reshape(-1, SLOT)
    q8t, k8t, v_row, e_hbm, inv_total, ctx, ctx_t, wave_t = run_forward(tokens, bits, segs, wq, bq, wb)
    layer_out, g_pre_one, g_ctx_t, tok_t, g_wo, g_wu, g_wd, g_bu, g_small = run_feed_forward(
        tokens, cotangent, ctx, ctx_t, wo, bo, g1, s1, wu, bu, wd, bd, g2, s2
    )
    g_tok, g_wq, g_bq, g_wb = run_backward(
        tok_t, q8t, k8t, v_row, e_hbm, inv_total, ctx_t, g_ctx_t, wave_t, wq, wb, wb.T, g_pre_one
    )

    def scatter(grad):
        part = lax.psum_scatter(grad, "fsdp", scatter_dimension=0, tiled=True)
        return lax.psum(part, "rep").astype(f32)

    p_wq, p_wo, p_wu, p_wd = scatter(g_wq), scatter(g_wo), scatter(g_wu), scatter(g_wd)
    small = [g_bq, g_small[5], g_small[3], g_small[4], g_bu, g_small[2], g_small[0], g_small[1], g_wb]
    rows = jnp.concatenate([s.reshape(fsdp, -1) for s in small], axis=1)
    mine = lax.psum(lax.psum_scatter(rows, "fsdp", scatter_dimension=0, tiled=True), "rep").reshape(-1)
    parts, at = [], 0
    for size in sizes:
        parts.append(mine[at : at + size])
        at += size
    p_bq, p_bo, p_g1, p_s1, p_bu, p_bd, p_g2, p_s2, p_wb = parts
    return (
        layer_out, g_tok, p_wq, p_bq, p_wb.reshape(w_box.shape), p_wo, p_bo, p_g1, p_s1,
        p_wu, p_bu, p_wd, p_bd, p_g2, p_s2,
    )


def solution(mesh):
    tokens = P(("fsdp", "rep"), None)
    matrix, vector = P("fsdp", None), P("fsdp")
    kinds = [matrix, vector, matrix, matrix, vector, vector, vector, matrix, vector, matrix, vector, vector, vector]
    return jax.shard_map(
        functools.partial(per_device, mesh.shape["fsdp"]),
        mesh=mesh,
        in_specs=(tokens, tokens, P(("fsdp", "rep")), P(None, ("fsdp", "rep")), *kinds),
        out_specs=(tokens, tokens, *kinds),
        check_vma=False,
    )
```

```python
import functools
import math

import jax
import jax.numpy as jnp
from jax import lax
from jax.experimental import pallas as pl
from jax.experimental.pallas import tpu as pltpu
from jax.sharding import PartitionSpec as P

HEADS = 12
HD = 64
FREQ = 16
SLOT = 512
WAVE = 4 * FREQ
PAIR = 2 * HD
QUAD = 4 * HD

f32 = jnp.float32
bf16 = jnp.bfloat16
neg_large = -1e30
eps_norm = 1e-12
scale_factor = 1.0 / math.sqrt(HD)
vmem_limit = 67_000_000


def dot_nn(left, right):
    return lax.dot_general(left, right, (((1,), (0,)), ((), ())), preferred_element_type=f32)


def dot_nt(left, right):
    return lax.dot_general(left, right, (((1,), (1,)), ((), ())), preferred_element_type=f32)


def dot_tn(left, right):
    return lax.dot_general(left, right, (((0,), (0,)), ((), ())), preferred_element_type=f32)


def aligned(index, size):
    return pl.ds(pl.multiple_of(index * size, size), size)


def wave_rows(coord_bits):
    row = lax.broadcasted_iota(jnp.int32, (2 * WAVE, 16), 0)
    col = lax.broadcasted_iota(jnp.int32, (2 * WAVE, 16), 1)
    coord_of = (row % WAVE) // FREQ
    pick = jnp.where(col == coord_of, 32.0, jnp.where(col == coord_of + 4, 1.0, 0.0)).astype(bf16)
    coords = dot_nn(pick, coord_bits)
    rows = lax.broadcasted_iota(jnp.int32, coords.shape, 0)
    freq_index = (rows % FREQ).astype(f32)
    frequency = jnp.exp(-math.log(10000.0) * freq_index / FREQ)
    angle = coords * (100.0 / 1024.0) * frequency
    turns = jnp.floor(angle * (2.0 / math.pi) + 0.5)
    rest = ((angle - turns * 1.5703125) - turns * 4.837512969970703125e-4) - turns * 7.549789954891e-8
    square = rest * rest
    sine = rest + rest * square * (
        -1.6666654611e-1 + square * (8.3321608736e-3 + square * -1.9515295891e-4)
    )
    cosine = 1.0 - 0.5 * square + square * square * (
        4.166664568298827e-2 + square * (-1.388731625493765e-3 + square * 2.443315711809948e-5)
    )
    quadrant = turns.astype(jnp.int32) + jnp.where(rows >= WAVE, 1, 0)
    value = jnp.where((quadrant & 1) == 1, cosine, sine)
    value = jnp.where((quadrant & 2) == 2, -value, value)
    return value.astype(bf16).astype(f32)


def swap_lanes(value):
    return pltpu.roll(value, WAVE, 1)


def gelu_parts(value):
    size = jnp.abs(value) * math.sqrt(0.5)
    t = 1.0 / (1.0 + 0.3275911 * size)
    bell = jnp.exp(-0.5 * value * value)
    tail = t * (
        0.254829592 + t * (-0.284496736 + t * (1.421413741 + t * (-1.453152027 + t * 1.061405429)))
    )
    half_tail = 0.5 * tail * bell
    return jnp.where(value >= 0, 1.0 - half_tail, half_tail), bell * (1.0 / math.sqrt(2.0 * math.pi))


def row_mean(value):
    return jnp.mean(value, axis=-1, keepdims=True)


ROWS = 256
BLOCK = 768
PIECE = 48
HALF = BLOCK // 2
SMALL = 512
STREAMS = 12
VECTORS = 6


def widths(width, ff):
    return 3 * width // 16, ff // 16, width // 16


class Route:
    def __init__(self):
        self.me = lax.axis_index("fsdp")
        self.core = lax.axis_index("rep")
        near_step, far_step = 1 + self.core, 2 - self.core
        near_move = near_step * (1 - 2 * ((self.me // near_step) % 2))
        far_move = far_step * (1 - 2 * ((self.me // far_step) % 2))
        self.near = self.me + near_move
        self.far = self.me + far_move
        self.across = self.me + near_move + far_move

    def column(self, base):
        return [(base + 4 * k) % 16 for k in range(4)]

    def peers(self):
        chips = self.column(self.me)[1:] + [self.near, self.far]
        return [(chip, self.core) for chip in chips] + [(self.me, 1 - self.core)]


def remote(source, target, send, recv, chip, core):
    return pltpu.make_async_remote_copy(
        src_ref=source, dst_ref=target, send_sem=send, recv_sem=recv,
        device_id=(chip, core), device_id_type=pl.DeviceIdType.MESH,
    )


class Streams:
    count = STREAMS

    def __init__(self, held, stage, final, sems):
        self.held, self.stage, self.final = held, stage, final
        self.gather_recv, self.gather_send, self.sum_recv, self.sum_send, self.final_sem = sems

    def window(self, stream, shard, half):
        lower = stream // 8
        row = (1 - lower) * (stream * BLOCK + PIECE * shard) + lower * (
            8 * BLOCK + PIECE * (stream - 8) + 4 * PIECE * shard
        )
        return self.held.at[pl.ds(pl.multiple_of(row, 16), PIECE), pl.ds(pl.multiple_of(half * HALF, HALF), HALF)]

    def several(self, pieces):
        return self.held.at[: PIECE * pieces, :HALF]

    def landing(self, stream, kind, index):
        row = stream * BLOCK + PIECE * (index + (0, 0, 8, 12)[kind])
        column = 0 if kind == 0 else HALF
        return self.stage.at[pl.ds(pl.multiple_of(row, 16), PIECE), column : column + HALF]

    def result(self, stream, half):
        return self.final.at[
            pl.ds(pl.multiple_of(stream * PIECE, 16), PIECE), pl.ds(pl.multiple_of(half * HALF, HALF), HALF)
        ]

    def results(self):
        return self.final.at[:, :HALF]


class Vectors:
    def __init__(self, held, stage, final, sems):
        self.held, self.stage, self.final = held, stage, final
        self.gather_recv, self.gather_send, self.sum_recv, self.sum_send, self.final_sem = sems

    def window(self, stream, shard, half):
        wide = SMALL // 2
        return self.held.at[pl.ds(pl.multiple_of(shard * 8, 8), 8), pl.ds(pl.multiple_of(half * wide, wide), wide)]

    def several(self, pieces):
        if pieces <= 16:
            return self.held.at[: 8 * pieces, : SMALL // 2]
        return self.stage.at[: 8 * pieces, :]

    def landing(self, stream, kind, index):
        row = 8 * (index + (0, 16, 24, 28)[kind])
        return self.stage.at[pl.ds(pl.multiple_of(row, 8), 8), :]

    def result(self, stream, half):
        wide = SMALL // 2
        return self.final.at[:, pl.ds(pl.multiple_of(half * wide, wide), wide)]

    def results(self):
        return self.final.at[:, : SMALL // 2]


def drain(view, sem):
    pltpu.make_async_copy(view, view, sem).wait()


class Exchange:
    def __init__(self, route, parts):
        self.route, self.parts = route, parts


    def share(self, stream, shard, chip, kind):
        p, r = self.parts, self.route
        view = p.window(stream, shard, r.core)
        remote(view, view, p.gather_send.at[stream, 0], p.gather_recv.at[stream, kind], chip, r.core).start()

    def hand_over(self, stream, shard):
        p, r = self.parts, self.route
        view = p.window(stream, shard, r.core)
        remote(view, view, p.gather_send.at[stream, 1], p.gather_recv.at[stream, 3], r.me, 1 - r.core).start()

    def gather_own(self, stream):
        r = self.route
        for peer in r.column(r.me)[1:]:
            self.share(stream, r.me, peer, 0)
        self.share(stream, r.me, r.near, 1)
        self.share(stream, r.me, r.far, 2)

    def gather_column(self, stream):
        p, r = self.parts, self.route
        drain(p.several(3), p.gather_recv.at[stream, 0])
        for shard in r.column(r.me)[1:]:
            self.share(stream, shard, r.near, 1)
            self.share(stream, shard, r.far, 2)
        for shard in r.column(r.me)[1:]:
            self.hand_over(stream, shard)

    def gather_near(self, stream):
        p, r = self.parts, self.route
        drain(p.several(4), p.gather_recv.at[stream, 1])
        for shard in r.column(r.near):
            self.share(stream, shard, r.far, 2)
        for shard in r.column(r.near):
            self.hand_over(stream, shard)

    def gather_far(self, stream):
        p, r = self.parts, self.route
        drain(p.several(8), p.gather_recv.at[stream, 2])
        for shard in r.column(r.far) + r.column(r.across):
            self.hand_over(stream, shard)

    def gathered(self, stream):
        p = self.parts
        drain(p.several(15), p.gather_recv.at[stream, 3])

    def gather_sent(self, stream):
        p = self.parts
        drain(p.several(15), p.gather_send.at[stream, 0])
        drain(p.several(15), p.gather_send.at[stream, 1])


    def add(self, stream, shard, kind, index):
        p, r = self.parts, self.route
        view = p.window(stream, shard, r.core)
        landed = p.landing(stream, kind, index)
        view[...] = (view[...].astype(f32) + landed[...].astype(f32)).astype(view.dtype)

    def pass_on(self, stream, shard, kind, index, chip):
        p, r = self.parts, self.route
        remote(
            p.window(stream, shard, r.core), p.landing(stream, kind, index),
            p.sum_send.at[stream], p.sum_recv.at[stream, kind], chip, r.core,
        ).start()

    def sum_cores(self, stream):
        p, r = self.parts, self.route
        for shard in range(16):
            remote(
                p.window(stream, shard, 1 - r.core), p.landing(stream, 0, shard),
                p.sum_send.at[stream], p.sum_recv.at[stream, 0], r.me, 1 - r.core,
            ).start()

    def sum_far(self, stream):
        p, r = self.parts, self.route
        drain(p.several(16), p.sum_recv.at[stream, 0])
        leaving = r.column(r.far) + r.column(r.across)
        for index, shard in enumerate(leaving):
            self.add(stream, shard, 0, shard)
        for index, shard in enumerate(leaving):
            self.pass_on(stream, shard, 1, index, r.far)
        for shard in r.column(r.me) + r.column(r.near):
            self.add(stream, shard, 0, shard)

    def sum_near(self, stream):
        p, r = self.parts, self.route
        drain(p.several(8), p.sum_recv.at[stream, 1])
        for index, shard in enumerate(r.column(r.near)):
            self.add(stream, shard, 1, 4 + index)
        for index, shard in enumerate(r.column(r.near)):
            self.pass_on(stream, shard, 2, index, r.near)
        for index, shard in enumerate(r.column(r.me)):
            self.add(stream, shard, 1, index)

    def sum_column(self, stream):
        p, r = self.parts, self.route
        drain(p.several(4), p.sum_recv.at[stream, 2])
        shards = r.column(r.me)
        for index in range(1, 4):
            self.add(stream, shards[index], 2, index)
        for index in range(1, 4):
            self.pass_on(stream, shards[index], 3, index - 1, shards[index])
        self.add(stream, shards[0], 2, 0)

    def sum_end(self, stream):
        p, r = self.parts, self.route
        drain(p.several(3), p.sum_recv.at[stream, 3])
        total = p.window(stream, r.me, r.core)[...].astype(f32)
        for index in range(3):
            total += p.landing(stream, 3, index)[...].astype(f32)
        view = p.result(stream, r.core)
        view[...] = total
        remote(view, view, p.final_sem.at[0], p.final_sem.at[1], r.me, 1 - r.core).start()

    def summed(self, stream):
        p = self.parts
        drain(p.several(31), p.sum_send.at[stream])

    def results_in(self):
        p = self.parts
        drain(p.results(), p.final_sem.at[0])
        drain(p.results(), p.final_sem.at[1])


def owner_tables(start, share, depth, order=None):
    col = lax.broadcasted_iota(jnp.int32, (depth, BLOCK), 1) + start
    source = col if order is None else order(col)
    pick = (source % share == lax.broadcasted_iota(jnp.int32, (depth, BLOCK), 0)).astype(bf16)
    col = lax.broadcasted_iota(jnp.int32, (128, BLOCK), 1) + start
    row = lax.broadcasted_iota(jnp.int32, (128, BLOCK), 0)
    source = col if order is None else order(col)
    return pick, source // share == row // 8, row % 8


def quad_order(col):
    return (col % BLOCK) // QUAD * BLOCK + col // BLOCK * QUAD + col % QUAD


def layer_kernel(comm, *refs):
    refs = list(refs)

    def take(count):
        taken, refs[:] = refs[:count], refs[count:]
        return taken

    tok_in, cot_in, bits, segs = take(4)
    if comm:
        w_qkv_in, w_out_in, w_up_in, w_down_in = take(4)
        small_in = take(9)
    else:
        held_in, w_box_in, b_qkv_in, b_up_in, vectors_in = take(5)
    layer_out, g_tok_out, e_hbm = take(3)
    if comm:
        p_qkv, p_out, p_up, p_down, p_small = take(5)
    else:
        g_held, g_w_box_out, g_b_qkv_out, g_b_up_out, g_vectors_out = take(5)
    (held, stage, slope, q8t, k8t, v_row, ctx_t, wave_t, wave_r, e_buf, normed, total, flip, g_down, tok_t, g_ctx_t,
     inv_one, inv_total, w_box, w_box_t, b_qkv, b_up, vectors, g_w_box, g_b_qkv, g_b_up, g_vectors, e_sem, io_sem) = take(29)
    if comm:
        final, small, small_stage, g_small, mid_sem = take(5)
        block_sems, small_sems, small_final_sems = take(5), take(4), take(1)

    count, width = tok_t.shape[1], tok_t.shape[0]
    ff = slope.shape[0] // count * BLOCK
    slots, pairs = count // SLOT, HEADS // 2
    row_blocks = count // ROWS
    up_blocks = ff // BLOCK
    quads = pairs // 2
    act = stage.at[: up_blocks * count]
    ctx = stage.at[up_blocks * count : (up_blocks + 1) * count]
    low = stage.at[(up_blocks + 1) * count : (up_blocks + 2) * count]
    cot = stage.at[(up_blocks + 2) * count : (up_blocks + 3) * count]
    tok = stage.at[(up_blocks + 3) * count : (up_blocks + 4) * count]
    up_at, down_at = 4 * BLOCK, 8 * BLOCK

    def copy_in(source, target, index=0):
        return pltpu.make_async_copy(source, target, io_sem.at[index])

    tok_copy = copy_in(tok_in, tok, 0)
    cot_copy = copy_in(cot_in, cot, 1)
    tok_copy.start()
    cot_copy.start()

    if comm:
        route = Route()
        blocks = Exchange(route, Streams(held, stage, final, block_sems))
        extras = Exchange(route, Vectors(small, small_stage, p_small, [*small_sems, *small_final_sems]))
        sums = Exchange(route, Vectors(g_small, small_stage, p_small, [*small_sems, *small_final_sems]))
        barrier = pltpu.get_barrier_semaphore()
        for chip, core in route.peers():
            pl.semaphore_signal(barrier, inc=1, device_id=(chip, core), device_id_type=pl.DeviceIdType.MESH)
        moves = []
        for quad in range(quads):
            for part in range(3):
                moves.append((
                    w_qkv_in.at[:, part * width + quad * QUAD : part * width + (quad + 1) * QUAD],
                    total.at[quad * PIECE : (quad + 1) * PIECE, part * QUAD : (part + 1) * QUAD],
                ))
        moves.append((w_out_in, total.at[3 * PIECE : 4 * PIECE]))
        for block in range(up_blocks):
            moves.append((
                w_up_in.at[:, block * BLOCK : (block + 1) * BLOCK],
                total.at[(4 + block) * PIECE : (5 + block) * PIECE],
            ))
        moves.append((w_down_in, total.at[8 * PIECE : 12 * PIECE]))
        for index, (source, target) in enumerate(moves):
            copy_in(source, target, 2 + index).start()
        small_in = [ref[...].astype(bf16).astype(f32) for ref in small_in]
        g_small[:8, :] = jnp.zeros((8, SMALL), f32)
        g_small[:8, :HD] = small_in[8]
        for row in range(8):
            value = small_in[row]
            g_small[row : row + 1, 128 : 128 + value.shape[1]] = value
        small[pl.ds(pl.multiple_of(route.me * 8, 8), 8), :] = g_small[:8, :]
        for index, (source, target) in enumerate(moves):
            copy_in(source, target, 2 + index).wait()
        for block in range(STREAMS - up_blocks):
            at = pl.ds(pl.multiple_of(block * BLOCK + PIECE * route.me, 16), PIECE)
            held[at, :] = total[block * PIECE : (block + 1) * PIECE, :].astype(bf16)
        at = pl.ds(pl.multiple_of(down_at + 4 * PIECE * route.me, 16), 4 * PIECE)
        held[at, :] = total[8 * PIECE : 12 * PIECE, :].astype(bf16)
        pl.semaphore_wait(barrier, 6)
        extras.gather_own(0)
        for stream in range(4):
            blocks.gather_own(stream)
    else:
        copy_in(held_in, held, 2).start()
        w_box[...] = w_box_in[...]
        b_qkv[...] = b_qkv_in[...]
        b_up[...] = b_up_in[...]
        vectors[...] = vectors_in[...]

    wave_t[...] = wave_rows(bits[...])
    wave_r[...] = jnp.transpose(wave_t[...])
    for slot in range(slots):
        seg_i = jnp.broadcast_to(segs[slot : slot + 1, :].astype(f32), (SLOT, SLOT))
        seg_j = jnp.transpose(seg_i)
        normed[slot * SLOT : (slot + 1) * SLOT, :SLOT] = jnp.where(seg_i == seg_j, 0.0, neg_large)
    g_w_box[...] = jnp.zeros_like(g_w_box)
    g_b_up[...] = jnp.zeros_like(g_b_up)
    g_vectors[...] = jnp.zeros_like(g_vectors)
    tok_copy.wait()

    if comm:
        extras.gather_column(0)
        blocks.gather_column(0)
        extras.gather_near(0)
        blocks.gather_near(0)
        blocks.gather_column(1)
        extras.gather_far(0)
        blocks.gather_far(0)
        blocks.gather_near(1)
        blocks.gather_column(2)
        extras.gathered(0)
        table = small[...].astype(bf16)
        w_box[...] = table[:, :HD]
        share_qkv, share_up, share = widths(width, ff)
        for row, columns, share_of, depth, order, target in (
            (0, 3 * width, share_qkv, 256, quad_order, b_qkv),
            (1, ff, share_up, 256, None, b_up),
            (None, width, share, 128, None, vectors),
        ):
            @pl.loop(0, columns // BLOCK)
            def _(block):
                pick, owned, row_of = owner_tables(block * BLOCK, share_of, depth, order)
                spread = dot_nn(table[:, 128 : 128 + depth], pick)
                keep = owned if row is None else owned & (row_of == row)
                rows = jnp.sum(jnp.where(keep, spread, 0.0).reshape(16, 8, BLOCK), axis=0)
                target[:, aligned(block, BLOCK)] = rows if row is None else jnp.sum(rows, axis=0, keepdims=True)

    else:
        copy_in(held_in, held, 2).wait()
    w_box_t[...] = jnp.transpose(w_box[...].astype(f32)).astype(bf16)

    def gather_tick(step):
        if not comm:
            return
        for ahead, act_on in enumerate((blocks.gather_far, blocks.gather_near, blocks.gather_column, blocks.gather_own)):
            pl.when(step + ahead < STREAMS)(functools.partial(act_on, step + ahead))

    def need(stream):
        if comm:
            blocks.gathered(stream)

    b_out, gain_one, shift_one, b_down, gain_two, shift_two = [vectors[2 + i : 3 + i, :] for i in range(VECTORS)]
    lane = lax.broadcasted_iota(jnp.int32, (SLOT, PAIR), 1)

    def project(quad, slot):
        rows = tok[aligned(slot, SLOT), :]

        def columns(part):
            weight = held[aligned(quad, BLOCK), part * QUAD : (part + 1) * QUAD]
            shift = b_qkv[:, pl.ds(pl.multiple_of(quad * BLOCK + part * QUAD, QUAD), QUAD)]
            return (dot_nn(rows, weight) + shift).astype(bf16)

        q, k, v = columns(0), columns(1), columns(2)
        low[aligned(slot, SLOT), aligned(quad, QUAD)] = k
        flip[aligned(quad, QUAD), aligned(slot, SLOT)] = jnp.transpose(v.astype(f32)).astype(bf16)
        qt = jnp.transpose(q.astype(f32) * scale_factor).astype(bf16)
        kt = jnp.transpose(k.astype(f32) * scale_factor).astype(bf16)
        for part in range(2):
            here = slice(part * PAIR, (part + 1) * PAIR)
            q8t[slot, quad * 2 + part] = qt[here]
            k8t[slot, quad * 2 + part] = kt[here]
            v_row[slot, quad * 2 + part] = v[:, here]

    def e_copy(place, head, index, out):
        pair = (e_buf.at[place, head], e_hbm.at[index])
        return pltpu.make_async_copy(*(pair if out else pair[::-1]), e_sem.at[place, head])

    def attend(step):
        pair, slot = step // slots, step % slots
        cols = aligned(slot, SLOT)
        place = step % 2

        @pl.when(step >= 2)
        def _():
            for head in range(2):
                e_copy(place, head, 0, True).wait()

        sine_t, cosine_t = wave_t[:WAVE, cols], wave_t[WAVE:, cols]
        sc_t = (wave_t[:, cols] * scale_factor).astype(bf16)
        sc_r = wave_r[cols, :]
        cs_r = swap_lanes(sc_r)
        cc_r = jnp.where(lane < WAVE, cs_r, sc_r)
        ss_r = jnp.where(lane < WAVE, sc_r, -cs_r)
        cs_low = cs_r.astype(bf16)
        keys = low[cols, aligned(pair, PAIR)]
        heads_t = []
        for head in range(2):
            span = slice(head * HD, (head + 1) * HD)
            key_box = dot_nt(keys[:, span], w_box[...])
            k_side = (key_box * cc_r + swap_lanes(key_box) * ss_r).astype(bf16)
            q_t = q8t[slot, pair, span, :]
            query_box = dot_nn(w_box[...], q_t)
            first, second = query_box[:WAVE], query_box[WAVE:]
            q_side = jnp.concatenate(
                [first * sine_t + second * cosine_t, second * sine_t - first * cosine_t], axis=0
            ).astype(bf16)
            zero = jnp.zeros_like(q_t)
            q_pair = [q_t, zero] if head == 0 else [zero, q_t]
            k_full = jnp.concatenate([keys, cs_low, k_side], axis=1)
            q_full = jnp.concatenate(q_pair + [q_side, sc_t], axis=0)
            scores = dot_nn(k_full, q_full) + normed[cols, :SLOT]
            top = jnp.max(scores, axis=0, keepdims=True)
            exps = jnp.exp(scores - top)
            inverse = 1.0 / jnp.sum(exps, axis=0, keepdims=True)
            low_exps = exps.astype(bf16)
            e_buf[place, head] = low_exps
            e_copy(place, head, step * 2 + head, True).start()
            inv_total[step * 2 + head] = inverse
            at = pl.ds(pl.multiple_of(pair * PAIR + head * HD, HD), HD)
            heads_t.append(dot_nn(flip[at, cols], low_exps) * inverse)
        both = jnp.concatenate(heads_t, axis=0)
        ctx_t[aligned(pair, PAIR), cols] = both.astype(bf16)
        ctx[cols, aligned(pair, PAIR)] = jnp.transpose(both).astype(bf16)

    steps = slots * pairs
    quad_steps = 2 * slots

    @pl.loop(0, quads)
    def _(quad):
        need(quad)

        @pl.loop(0, slots)
        def _(slot):
            project(quad, slot)

        @pl.loop(0, quad_steps)
        def _(inner):
            step = quad * quad_steps + inner
            if comm:
                pl.when(step % 2 == 1)(functools.partial(gather_tick, (step + 1) // 2))
            attend(step)

    for place in range(2):
        for head in range(2):
            e_copy(place, head, 0, True).wait()

    def column_sum(value):
        return jnp.sum(value, axis=0, keepdims=True)

    need(3)
    gather_tick(7)

    @pl.loop(0, row_blocks)
    def _(block):
        rows = aligned(block, ROWS)
        token_rows = tok[rows, :].astype(f32)
        tok_t[:, rows] = jnp.transpose(token_rows).astype(bf16)
        pre = token_rows + dot_nn(ctx[rows, :], held[3 * BLOCK : 4 * BLOCK, :]) + b_out
        center = pre - row_mean(pre)
        invdev = lax.rsqrt(row_mean(center * center) + eps_norm)
        unit = center * invdev
        inv_one[rows, :] = jnp.broadcast_to(invdev, (ROWS, 128))
        normed[rows, :] = unit
        hidden = unit * gain_one + shift_one
        low[rows, :] = hidden.astype(bf16)
        flip[:, rows] = jnp.transpose(hidden).astype(bf16)

    @pl.loop(0, up_blocks)
    def _(block):
        gather_tick(8 + block)
        need(4 + block)

        @pl.loop(0, row_blocks)
        def _(row):
            rows = aligned(row, ROWS)
            at = pl.ds(pl.multiple_of(block * count + row * ROWS, ROWS), ROWS)
            weight = held[pl.ds(pl.multiple_of(up_at + block * BLOCK, BLOCK), BLOCK), :]
            up = dot_nn(low[rows, :], weight) + b_up[:, aligned(block, BLOCK)]
            cdf, pdf = gelu_parts(up)
            act[at, :] = (up * cdf).astype(bf16)
            slope[at, :] = (cdf + up * pdf).astype(bf16)

    for block in range(up_blocks):
        need(8 + block)
    cot_copy.wait()

    @pl.loop(0, row_blocks)
    def _(block):
        rows = aligned(block, ROWS)
        pre = normed[rows, :] * gain_one + shift_one + b_down
        for part in range(up_blocks):
            at = pl.ds(pl.multiple_of(part * count + block * ROWS, ROWS), ROWS)
            pre += dot_nn(act[at, :], held[down_at + part * BLOCK : down_at + (part + 1) * BLOCK, :])
        center = pre - row_mean(pre)
        invdev = lax.rsqrt(row_mean(center * center) + eps_norm)
        unit = center * invdev
        grad = cot[rows, :].astype(f32)
        cot[rows, :] = (unit * gain_two + shift_two).astype(bf16)
        scaled = grad * gain_two
        g_pre = invdev * (scaled - row_mean(scaled) - unit * row_mean(scaled * unit))
        total[rows, :] = g_pre
        low_pre = g_pre.astype(bf16)
        g_down[rows, :] = low_pre
        g_vectors[5:6, :] += column_sum(low_pre.astype(f32))
        g_vectors[6:7, :] += column_sum(grad * unit)
        g_vectors[7:8, :] += column_sum(grad)

    out_copy = pltpu.make_async_copy(cot, layer_out, io_sem.at[0])
    out_copy.start()
    if comm:
        for stream in range(STREAMS):
            blocks.gather_sent(stream)
        extras.gather_sent(0)

    @pl.loop(0, up_blocks)
    def _(block):
        down_rows = pl.ds(pl.multiple_of(down_at + block * BLOCK, BLOCK), BLOCK)

        @pl.loop(0, row_blocks)
        def _(row):
            rows = aligned(row, ROWS)
            at = pl.ds(pl.multiple_of(block * count + row * ROWS, ROWS), ROWS)
            g_act = dot_nt(g_down[rows, :], held[down_rows, :])
            g_up = (g_act * slope[at, :].astype(f32)).astype(bf16)
            slope[at, :] = g_up
            g_b_up[:, aligned(block, BLOCK)] += column_sum(g_up.astype(f32))

        @pl.loop(0, BLOCK // ROWS)
        def _(part):
            at = pl.ds(pl.multiple_of(down_at + block * BLOCK + part * ROWS, ROWS), ROWS)
            held[at, :] = dot_tn(act[aligned(block, count), aligned(part, ROWS)], g_down[...]).astype(bf16)

    out_copy.wait()

    def last(step):
        return STREAMS - 1 - step

    def sum_start(step):
        if comm:
            blocks.sum_cores(last(step))

    def sum_tick(step):
        if not comm:
            return
        for behind, act_on in enumerate((blocks.sum_far, blocks.sum_near, blocks.sum_column, blocks.sum_end)):
            at = step - behind
            if isinstance(at, int):
                if 0 <= at < STREAMS:
                    act_on(last(at))
            else:
                pl.when((at >= 0) & (at < STREAMS))(functools.partial(act_on, last(at)))

    if comm:
        for chip, core in route.peers():
            pl.semaphore_signal(mid_sem, inc=1, device_id=(chip, core), device_id_type=pl.DeviceIdType.MESH)
        pl.semaphore_wait(mid_sem, 6)

    for step in range(up_blocks):
        sum_start(step)

    @pl.loop(0, up_blocks)
    def _(index):
        block = up_blocks - 1 - index
        up_rows = pl.ds(pl.multiple_of(up_at + block * BLOCK, BLOCK), BLOCK)

        @pl.loop(0, row_blocks)
        def _(row):
            rows = aligned(row, ROWS)
            at = pl.ds(pl.multiple_of(block * count + row * ROWS, ROWS), ROWS)
            total[rows, :] += dot_nt(slope[at, :], held[up_rows, :])

        @pl.loop(0, BLOCK // ROWS)
        def _(part):
            at = pl.ds(pl.multiple_of(up_at + block * BLOCK + part * ROWS, ROWS), ROWS)
            held[at, :] = dot_nn(flip[aligned(part, ROWS), :], slope[aligned(block, count), :]).astype(bf16)

        sum_start(up_blocks + index)
        sum_tick(index)

    @pl.loop(0, row_blocks)
    def _(block):
        rows = aligned(block, ROWS)
        grad, unit = total[rows, :], normed[rows, :]
        scaled = grad * gain_one
        g_pre = inv_one[rows, :1] * (scaled - row_mean(scaled) - unit * row_mean(scaled * unit))
        total[rows, :] = g_pre
        low_pre = g_pre.astype(bf16)
        g_down[rows, :] = low_pre
        g_vectors[2:3, :] += column_sum(low_pre.astype(f32))
        g_vectors[3:4, :] += column_sum(grad * unit)
        g_vectors[4:5, :] += column_sum(grad)
        g_ctx_t[:, rows] = dot_nt(held[3 * BLOCK : 4 * BLOCK, :], low_pre).astype(bf16)

    @pl.loop(0, BLOCK // ROWS)
    def _(part):
        at = pl.ds(pl.multiple_of(3 * BLOCK + part * ROWS, ROWS), ROWS)
        held[at, :] = dot_nn(ctx_t[aligned(part, ROWS), :], g_down[...]).astype(bf16)

    sum_start(8)
    sum_tick(4)

    def e_step(order):
        quad = quads - 1 - order // quad_steps
        return quad * quad_steps + order % quad_steps

    def fetch(order):
        for head in range(2):
            e_copy(order % 2, head, e_step(order) * 2 + head, False).start()

    fetch(0)
    ones = jnp.ones((16, count), bf16)

    def attend_back(order):
        step = e_step(order)
        pair, slot = step // slots, step % slots
        cols = aligned(slot, SLOT)
        place = order % 2

        @pl.when(order + 1 < steps)
        def _():
            fetch(order + 1)

        for head in range(2):
            e_copy(place, head, 0, False).wait()
        sine_t, cosine_t = wave_t[:WAVE, cols], wave_t[WAVE:, cols]
        sc_t = (wave_t[:, cols] * scale_factor).astype(bf16)
        cs_t = (jnp.concatenate([cosine_t, sine_t], axis=0) * scale_factor).astype(bf16)
        values = v_row[slot, pair]
        g_parts = [[], [], []]
        for head in range(2):
            span = slice(head * HD, (head + 1) * HD)
            at = pl.ds(pl.multiple_of(pair * PAIR + head * HD, HD), HD)
            g_rows = g_ctx_t[at, cols].astype(f32) * inv_total[step * 2 + head]
            row_dot = jnp.sum(g_rows * ctx_t[at, cols].astype(f32), axis=0, keepdims=True)
            g_low = g_rows.astype(bf16)
            zero = jnp.zeros_like(g_low)
            g_pair = jnp.concatenate([g_low, zero] if head == 0 else [zero, g_low], axis=0)
            low_exps = e_buf[place, head]
            g_probs = dot_nn(values, g_pair)
            g_scores = (low_exps.astype(f32) * (g_probs - row_dot)).astype(bf16)
            g_parts[2].append(dot_nt(g_low, low_exps))
            k_t, q_t = k8t[slot, pair, span, :], q8t[slot, pair, span, :]
            g_q = dot_nn(jnp.concatenate([k_t, cs_t], axis=0), g_scores)
            g_k = dot_nt(jnp.concatenate([q_t, sc_t], axis=0), g_scores)
            first, second = g_q[HD : HD + WAVE], g_q[HD + WAVE :]
            g_qbox = jnp.concatenate(
                [first * sine_t - second * cosine_t, first * cosine_t + second * sine_t], axis=0
            ).astype(bf16)
            first, second = g_k[HD : HD + WAVE], g_k[HD + WAVE :]
            g_kbox = jnp.concatenate(
                [first * cosine_t - second * sine_t, first * sine_t + second * cosine_t], axis=0
            ).astype(bf16)
            g_parts[0].append(g_q[:HD] + dot_nn(w_box_t[...], g_qbox))
            g_parts[1].append(g_k[:HD] + dot_nn(w_box_t[...], g_kbox))
            g_w_box[...] += dot_nt(g_qbox, q_t) + dot_nt(g_kbox, k_t)
        for part in range(3):
            at = pl.ds(pl.multiple_of(part * QUAD + pair % 2 * PAIR, PAIR), PAIR)
            flip[at, cols] = jnp.concatenate(g_parts[part], axis=0).astype(bf16)

    def token_grad(quad):
        @pl.loop(0, row_blocks)
        def _(block):
            rows = aligned(block, ROWS)
            part = dot_nn(held[aligned(quad, BLOCK), :], flip[:, rows])
            total[rows, :] += jnp.transpose(part)

    @pl.loop(0, quads)
    def _(turn):
        quad = quads - 1 - turn

        @pl.loop(0, quad_steps)
        def _(inner):
            order = turn * quad_steps + inner
            if comm:
                pl.when(order % 2 == 1)(functools.partial(sum_tick, 5 + order // 2))
            attend_back(order)

        token_grad(quad)

        @pl.loop(0, BLOCK // ROWS)
        def _(part):
            at = pl.ds(pl.multiple_of(quad * BLOCK + part * ROWS, ROWS), ROWS)
            held[at, :] = dot_nt(tok_t[aligned(part, ROWS), :], flip[...]).astype(bf16)

        g_b_qkv[:, aligned(quad, BLOCK)] = dot_nt(ones, flip[...])[:1]
        sum_start(9 + turn)

    g_w_box[...] = g_w_box[...] * (1.0 / scale_factor)
    tok_out = pltpu.make_async_copy(total, g_tok_out, io_sem.at[0])
    tok_out.start()

    if comm:
        g_small[...] = jnp.zeros_like(g_small)
        g_small[:, :HD] = g_w_box[...]
        share_qkv, share_up, share = widths(width, ff)
        for row, columns, share_of, order, source in (
            (0, 3 * width, share_qkv, quad_order, g_b_qkv),
            (1, ff, share_up, None, g_b_up),
            (None, width, share, None, g_vectors),
        ):
            @pl.loop(0, columns // BLOCK)
            def _(block):
                pick, owned, row_of = owner_tables(block * BLOCK, share_of, 256, order)
                keep = owned if row is None else owned & (row_of == row)
                wide = 1 if row is not None else 8
                full = source[:, aligned(block, BLOCK)].reshape(1, wide, BLOCK)
                spread = jnp.broadcast_to(full, (16, 8, BLOCK)).reshape(128, BLOCK)
                spread = jnp.where(keep, spread, 0.0)
                upper = spread.astype(bf16)
                g_small[:, 128:384] += dot_nt(upper, pick) + dot_nt((spread - upper.astype(f32)).astype(bf16), pick)

        sums.sum_cores(0)
        sum_tick(11)
        sums.sum_far(0)
        sum_tick(12)
        sums.sum_near(0)
        sum_tick(13)
        sums.sum_column(0)
        sum_tick(14)
        sums.sum_end(0)
        for stream in range(STREAMS):
            blocks.summed(stream)
        sums.summed(0)
        blocks.results_in()
        sums.results_in()
        moves = []
        for quad in range(quads):
            for part in range(3):
                moves.append((
                    final.at[quad * PIECE : (quad + 1) * PIECE, part * QUAD : (part + 1) * QUAD],
                    p_qkv.at[:, part * width + quad * QUAD : part * width + (quad + 1) * QUAD],
                ))
        moves.append((final.at[3 * PIECE : 4 * PIECE], p_out))
        for block in range(up_blocks):
            moves.append((
                final.at[(4 + block) * PIECE : (5 + block) * PIECE],
                p_up.at[:, block * BLOCK : (block + 1) * BLOCK],
            ))
        moves.append((final.at[8 * PIECE : 12 * PIECE], p_down))
        for index, (source, target) in enumerate(moves):
            copy_in(source, target, 2 + index).start()
        for index, (source, target) in enumerate(moves):
            copy_in(source, target, 2 + index).wait()
    else:
        g_w_box_out[...] = g_w_box[...]
        g_b_qkv_out[...] = g_b_qkv[...]
        g_b_up_out[...] = g_b_up[...]
        g_vectors_out[...] = g_vectors[...]
        out = copy_in(held, g_held, 2)
        out.start()
        out.wait()
    tok_out.wait()


def shaped(shape, dtype):
    return jax.ShapeDtypeStruct(shape, dtype)


def in_vmem(count):
    return [pl.BlockSpec(memory_space=pltpu.VMEM)] * count


def in_hbm(count):
    return [pl.BlockSpec(memory_space=pl.ANY)] * count


def run_layer(comm, tokens, cotangent, bits, segs, big, little, shard_shapes):
    count, width = tokens.shape
    ff = 4 * BLOCK
    slots, pairs = count // SLOT, HEADS // 2
    held_shape = (STREAMS * BLOCK, BLOCK)
    out_shape = [
        shaped((count, width), bf16),
        shaped((count, width), f32),
        shaped((slots * HEADS, SLOT, SLOT), bf16),
    ]
    out_specs = in_hbm(3)
    if comm:
        out_shape += [shaped(shape, f32) for shape in shard_shapes] + [shaped((8, SMALL), f32)]
        out_specs += in_hbm(4) + in_vmem(1)
    else:
        out_shape += [shaped(held_shape, bf16), shaped((2 * WAVE, HD), f32), shaped((1, 3 * width), f32)]
        out_shape += [shaped((1, ff), f32), shaped((8, width), f32)]
        out_specs += in_hbm(1) + in_vmem(4)
    vmem = pltpu.VMEM
    dma = pltpu.SemaphoreType.DMA
    scratch = [
        vmem(held_shape, bf16),
        vmem(held_shape, bf16),
        vmem((ff // BLOCK * count, BLOCK), bf16),
        vmem((slots, pairs, PAIR, SLOT), bf16),
        vmem((slots, pairs, PAIR, SLOT), bf16),
        vmem((slots, pairs, SLOT, PAIR), bf16),
        vmem((width, count), bf16),
        vmem((2 * WAVE, count), f32),
        vmem((count, 2 * WAVE), f32),
        vmem((2, 2, SLOT, SLOT), bf16),
        vmem((count, width), f32),
        vmem((count, width), f32),
        vmem((width, count), bf16),
        vmem((count, width), bf16),
        vmem((width, count), bf16),
        vmem((width, count), bf16),
        vmem((count, 128), f32),
        vmem((slots * HEADS, 1, SLOT), f32),
        vmem((2 * WAVE, HD), bf16),
        vmem((HD, 2 * WAVE), bf16),
        vmem((1, 3 * width), f32),
        vmem((1, ff), f32),
        vmem((8, width), f32),
        vmem((2 * WAVE, HD), f32),
        vmem((1, 3 * width), f32),
        vmem((1, ff), f32),
        vmem((8, width), f32),
        dma((2, 2)),
        dma((20,)),
    ]
    if comm:
        scratch += [
            vmem((STREAMS * PIECE, BLOCK), f32),
            vmem((128, SMALL), f32),
            vmem((256, SMALL // 2), f32),
            vmem((128, SMALL), f32),
            pltpu.SemaphoreType.REGULAR,
            dma((STREAMS, 4)), dma((STREAMS, 2)), dma((STREAMS, 4)), dma((STREAMS,)), dma((2,)),
            dma((1, 4)), dma((1, 2)), dma((1, 4)), dma((1,)),
            dma((2,)),
        ]
        extra = dict(collective_id=0, has_side_effects=True)
    else:
        extra = {}
    return pl.pallas_call(
        functools.partial(layer_kernel, comm),
        out_shape=out_shape,
        in_specs=in_hbm(2) + in_vmem(2) + in_hbm(len(big)) + in_vmem(len(little)),
        out_specs=out_specs,
        scratch_shapes=scratch,
        compiler_params=pltpu.CompilerParams(vmem_limit_bytes=vmem_limit, **extra),
        name="layer",
    )(tokens, cotangent, bits, segs, *big, *little)


def to_blocks(w_qkv, w_out, w_up, w_down):
    width = w_out.shape[1]
    qkv = w_qkv.reshape(width, 3, width // QUAD, QUAD).transpose(2, 0, 1, 3).reshape(-1, BLOCK)
    up = w_up.reshape(width, -1, BLOCK).transpose(1, 0, 2).reshape(-1, BLOCK)
    return jnp.concatenate([qkv, w_out, up, w_down], axis=0)


def from_blocks(held, width):
    qkv = held[: 3 * BLOCK].reshape(width // QUAD, width, 3, QUAD).transpose(1, 2, 0, 3).reshape(width, -1)
    up = held[4 * BLOCK : 8 * BLOCK].reshape(-1, width, BLOCK).transpose(1, 0, 2).reshape(width, -1)
    return qkv, held[3 * BLOCK : 4 * BLOCK], up, held[8 * BLOCK :]


def per_device(
    mesh_shape, tokens, cotangent, segments, box_coords, w_qkv, b_qkv, w_box, w_out, b_out, gain_one, shift_one,
    w_up, b_up, w_down, b_down, gain_two, shift_two,
):
    count, width = tokens.shape
    bits = jnp.concatenate([box_coords >> 5, box_coords & 31, jnp.zeros((8, count), jnp.int32)], axis=0).astype(bf16)
    segs = segments.reshape(-1, SLOT)
    vectors = [b_qkv, b_up, b_out, gain_one, shift_one, b_down, gain_two, shift_two]
    if mesh_shape == (16, 2):
        little = [v.reshape(1, -1) for v in vectors] + [w_box]
        big = [w_qkv, w_out, w_up, w_down]
        layer_out, g_tok, _, p_wq, p_wo, p_wu, p_wd, small = run_layer(
            True, tokens, cotangent, bits, segs, big, little, [w.shape for w in big]
        )
        p_wb = small[:, :HD]
        p_bq, p_bu, p_bo, p_g1, p_s1, p_bd, p_g2, p_s2 = [
            small[row, 128 : 128 + v.shape[0]] for row, v in enumerate(vectors)
        ]
    else:
        low = lambda value: value.astype(bf16)
        gather = lambda value: lax.all_gather(low(value), "fsdp", axis=0, tiled=True)
        held = to_blocks(gather(w_qkv), gather(w_out), gather(w_up), gather(w_down))
        wb, bq, bu, *six = [gather(v) for v in [w_box] + vectors]
        order = quad_order(jnp.arange(3 * width))
        rows = jnp.stack([jnp.zeros((width,), bf16)] * 2 + six).astype(f32)
        layer_out, g_tok, _, g_held, g_wb, g_bq, g_bu, g_six = run_layer(
            False, tokens, cotangent, bits, segs, [held],
            [wb, bq[order].astype(f32).reshape(1, -1), bu.astype(f32).reshape(1, -1), rows], None,
        )

        def scatter(grad):
            part = lax.psum_scatter(grad, "fsdp", scatter_dimension=0, tiled=True)
            return lax.psum(part, "rep").astype(f32)

        p_wq, p_wo, p_wu, p_wd = [scatter(g) for g in from_blocks(g_held, width)]
        g_bq = jnp.zeros((3 * width,), f32).at[order].set(g_bq[0])
        p_wb, p_bq, p_bu = scatter(g_wb), scatter(g_bq), scatter(g_bu[0])
        p_bo, p_g1, p_s1, p_bd, p_g2, p_s2 = [scatter(g_six[2 + i]) for i in range(VECTORS)]
    return (
        layer_out, g_tok, p_wq, p_bq, p_wb, p_wo, p_bo, p_g1, p_s1,
        p_wu, p_bu, p_wd, p_bd, p_g2, p_s2,
    )


def solution(mesh):
    tokens = P(("fsdp", "rep"), None)
    matrix, vector = P("fsdp", None), P("fsdp")
    kinds = [matrix, vector, matrix, matrix, vector, vector, vector, matrix, vector, matrix, vector, vector, vector]
    return jax.shard_map(
        functools.partial(per_device, (mesh.shape["fsdp"], mesh.shape["rep"])),
        mesh=mesh,
        in_specs=(tokens, tokens, P(("fsdp", "rep")), P(None, ("fsdp", "rep")), *kinds),
        out_specs=(tokens, tokens, *kinds),
        check_vma=False,
    )
```

```python
import functools
import math

import jax
import jax.numpy as jnp
from jax import lax
from jax.experimental import pallas as pl
from jax.experimental.pallas import tpu as pltpu
from jax.sharding import PartitionSpec as P

HEADS = 12
HD = 64
FREQ = 16
SLOT = 512
WAVE = 4 * FREQ
PAIR = 2 * HD
QUAD = 4 * HD

f32 = jnp.float32
bf16 = jnp.bfloat16
neg_large = -1e30
eps_norm = 1e-12
scale_factor = 1.0 / math.sqrt(HD)
vmem_limit = 67_000_000


def dot_nn(left, right):
    return lax.dot_general(left, right, (((1,), (0,)), ((), ())), preferred_element_type=f32)


def dot_nt(left, right):
    return lax.dot_general(left, right, (((1,), (1,)), ((), ())), preferred_element_type=f32)


def dot_tn(left, right):
    return lax.dot_general(left, right, (((0,), (0,)), ((), ())), preferred_element_type=f32)


def aligned(index, size):
    return pl.ds(pl.multiple_of(index * size, size), size)


def wave_rows(coords):
    count = coords.shape[1]
    spread = [jnp.broadcast_to(coords[c : c + 1, :].astype(f32), (FREQ, count)) for c in range(4)]
    scaled = jnp.concatenate(spread + spread, axis=0) * (100.0 / 1024.0)
    rows = lax.broadcasted_iota(jnp.int32, scaled.shape, 0)
    frequency = jnp.exp(-math.log(10000.0) * (rows & (FREQ - 1)).astype(f32) / FREQ)
    angle = scaled * frequency
    turns = jnp.floor(angle * (2.0 / math.pi) + 0.5)
    rest = ((angle - turns * 1.5703125) - turns * 4.837512969970703125e-4) - turns * 7.549789954891e-8
    square = rest * rest
    sine = rest + rest * square * (
        -1.6666654611e-1 + square * (8.3321608736e-3 + square * -1.9515295891e-4)
    )
    cosine = 1.0 - 0.5 * square + square * square * (
        4.166664568298827e-2 + square * (-1.388731625493765e-3 + square * 2.443315711809948e-5)
    )
    quadrant = turns.astype(jnp.int32) + jnp.where(rows >= WAVE, 1, 0)
    value = jnp.where((quadrant & 1) == 1, cosine, sine)
    value = jnp.where((quadrant & 2) == 2, -value, value)
    return value.astype(bf16).astype(f32)


def swap_lanes(value):
    return pltpu.roll(value, WAVE, 1)


def gelu_parts(value):
    size = jnp.abs(value) * math.sqrt(0.5)
    t = 1.0 / (1.0 + 0.3275911 * size)
    bell = jnp.exp(-0.5 * value * value)
    tail = t * (
        0.254829592 + t * (-0.284496736 + t * (1.421413741 + t * (-1.453152027 + t * 1.061405429)))
    )
    half_tail = 0.5 * tail * bell
    return jnp.where(value >= 0, 1.0 - half_tail, half_tail), bell * (1.0 / math.sqrt(2.0 * math.pi))


def row_mean(value):
    return jnp.mean(value, axis=-1, keepdims=True)


ROWS = 256
BLOCK = 768
PIECE = 48
HALF = BLOCK // 2
SMALL = 512
STREAMS = 12
VECTORS = 6


def widths(width, ff):
    return 3 * width // 16, ff // 16, width // 16


class Route:
    def __init__(self):
        self.me = lax.axis_index("fsdp")
        self.core = lax.axis_index("rep")
        near_step, far_step = 1 + self.core, 2 - self.core
        near_move = near_step * (1 - 2 * ((self.me // near_step) % 2))
        far_move = far_step * (1 - 2 * ((self.me // far_step) % 2))
        self.near = self.me + near_move
        self.far = self.me + far_move
        self.across = self.me + near_move + far_move

    def column(self, base):
        return [(base + 4 * k) % 16 for k in range(4)]

    def peers(self):
        chips = self.column(self.me)[1:] + [self.near, self.far]
        return [(chip, self.core) for chip in chips] + [(self.me, 1 - self.core)]


def remote(source, target, send, recv, chip, core):
    return pltpu.make_async_remote_copy(
        src_ref=source, dst_ref=target, send_sem=send, recv_sem=recv,
        device_id=(chip, core), device_id_type=pl.DeviceIdType.MESH,
    )


class Streams:
    count = STREAMS

    def __init__(self, held, stage, final, sems):
        self.held, self.stage, self.final = held, stage, final
        self.gather_recv, self.gather_send, self.sum_recv, self.sum_send, self.final_sem = sems

    def window(self, stream, shard, half):
        lower = stream // 8
        row = (1 - lower) * (stream * BLOCK + PIECE * shard) + lower * (
            8 * BLOCK + PIECE * (stream - 8) + 4 * PIECE * shard
        )
        return self.held.at[pl.ds(pl.multiple_of(row, 16), PIECE), pl.ds(pl.multiple_of(half * HALF, HALF), HALF)]

    def several(self, pieces):
        return self.held.at[: PIECE * pieces, :HALF]

    def landing(self, stream, kind, index):
        row = (stream + 8) % STREAMS * BLOCK + PIECE * (index + (0, 0, 8, 12)[kind])
        column = 0 if kind == 0 else HALF
        return self.stage.at[pl.ds(pl.multiple_of(row, 16), PIECE), column : column + HALF]

    def result(self, stream, half):
        return self.final.at[
            pl.ds(pl.multiple_of(stream * PIECE, 16), PIECE), pl.ds(pl.multiple_of(half * HALF, HALF), HALF)
        ]

    def results(self):
        return self.final.at[:, :HALF]


class Vectors:
    def __init__(self, held, stage, final, sems):
        self.held, self.stage, self.final = held, stage, final
        self.gather_recv, self.gather_send, self.sum_recv, self.sum_send, self.final_sem = sems

    def window(self, stream, shard, half):
        wide = SMALL // 2
        return self.held.at[pl.ds(pl.multiple_of(shard * 8, 8), 8), pl.ds(pl.multiple_of(half * wide, wide), wide)]

    def several(self, pieces):
        if pieces <= 16:
            return self.held.at[: 8 * pieces, : SMALL // 2]
        return self.stage.at[: 8 * pieces, :]

    def landing(self, stream, kind, index):
        row = 8 * (index + (0, 16, 24, 28)[kind])
        return self.stage.at[pl.ds(pl.multiple_of(row, 8), 8), :]

    def result(self, stream, half):
        wide = SMALL // 2
        return self.final.at[:, pl.ds(pl.multiple_of(half * wide, wide), wide)]

    def results(self):
        return self.final.at[:, : SMALL // 2]


def drain(view, sem):
    pltpu.make_async_copy(view, view, sem).wait()


class Exchange:
    def __init__(self, route, parts):
        self.route, self.parts = route, parts


    def share(self, stream, shard, chip, kind):
        p, r = self.parts, self.route
        view = p.window(stream, shard, r.core)
        remote(view, view, p.gather_send.at[stream, 0], p.gather_recv.at[stream, kind], chip, r.core).start()

    def hand_over(self, stream, shard):
        p, r = self.parts, self.route
        view = p.window(stream, shard, r.core)
        remote(view, view, p.gather_send.at[stream, 1], p.gather_recv.at[stream, 3], r.me, 1 - r.core).start()

    def gather_own(self, stream):
        r = self.route
        for peer in r.column(r.me)[1:]:
            self.share(stream, r.me, peer, 0)
        self.share(stream, r.me, r.near, 1)
        self.share(stream, r.me, r.far, 2)

    def gather_column(self, stream):
        p, r = self.parts, self.route
        drain(p.several(3), p.gather_recv.at[stream, 0])
        for shard in r.column(r.me)[1:]:
            self.share(stream, shard, r.near, 1)
            self.share(stream, shard, r.far, 2)
        for shard in r.column(r.me)[1:]:
            self.hand_over(stream, shard)

    def gather_near(self, stream):
        p, r = self.parts, self.route
        drain(p.several(4), p.gather_recv.at[stream, 1])
        for shard in r.column(r.near):
            self.share(stream, shard, r.far, 2)
        for shard in r.column(r.near):
            self.hand_over(stream, shard)

    def gather_far(self, stream):
        p, r = self.parts, self.route
        drain(p.several(8), p.gather_recv.at[stream, 2])
        for shard in r.column(r.far) + r.column(r.across):
            self.hand_over(stream, shard)

    def gathered(self, stream):
        p = self.parts
        drain(p.several(15), p.gather_recv.at[stream, 3])

    def gather_sent(self, stream):
        p = self.parts
        drain(p.several(15), p.gather_send.at[stream, 0])
        drain(p.several(15), p.gather_send.at[stream, 1])


    def add(self, stream, shard, kind, index):
        p, r = self.parts, self.route
        view = p.window(stream, shard, r.core)
        landed = p.landing(stream, kind, index)
        view[...] = (view[...].astype(f32) + landed[...].astype(f32)).astype(view.dtype)

    def pass_on(self, stream, shard, kind, index, chip):
        p, r = self.parts, self.route
        remote(
            p.window(stream, shard, r.core), p.landing(stream, kind, index),
            p.sum_send.at[stream], p.sum_recv.at[stream, kind], chip, r.core,
        ).start()

    def sum_cores(self, stream):
        p, r = self.parts, self.route
        for shard in range(16):
            remote(
                p.window(stream, shard, 1 - r.core), p.landing(stream, 0, shard),
                p.sum_send.at[stream], p.sum_recv.at[stream, 0], r.me, 1 - r.core,
            ).start()

    def sum_far(self, stream):
        p, r = self.parts, self.route
        drain(p.several(16), p.sum_recv.at[stream, 0])
        leaving = r.column(r.far) + r.column(r.across)
        for index, shard in enumerate(leaving):
            self.add(stream, shard, 0, shard)
        for index, shard in enumerate(leaving):
            self.pass_on(stream, shard, 1, index, r.far)
        for shard in r.column(r.me) + r.column(r.near):
            self.add(stream, shard, 0, shard)

    def sum_near(self, stream):
        p, r = self.parts, self.route
        drain(p.several(8), p.sum_recv.at[stream, 1])
        for index, shard in enumerate(r.column(r.near)):
            self.add(stream, shard, 1, 4 + index)
        for index, shard in enumerate(r.column(r.near)):
            self.pass_on(stream, shard, 2, index, r.near)
        for index, shard in enumerate(r.column(r.me)):
            self.add(stream, shard, 1, index)

    def sum_column(self, stream):
        p, r = self.parts, self.route
        drain(p.several(4), p.sum_recv.at[stream, 2])
        shards = r.column(r.me)
        for index in range(1, 4):
            self.add(stream, shards[index], 2, index)
        for index in range(1, 4):
            self.pass_on(stream, shards[index], 3, index - 1, shards[index])
        self.add(stream, shards[0], 2, 0)

    def sum_end(self, stream):
        p, r = self.parts, self.route
        drain(p.several(3), p.sum_recv.at[stream, 3])
        total = p.window(stream, r.me, r.core)[...].astype(f32)
        for index in range(3):
            total += p.landing(stream, 3, index)[...].astype(f32)
        view = p.result(stream, r.core)
        view[...] = total
        remote(view, view, p.final_sem.at[0], p.final_sem.at[1], r.me, 1 - r.core).start()

    def summed(self, stream):
        p = self.parts
        drain(p.several(31), p.sum_send.at[stream])

    def results_in(self):
        p = self.parts
        drain(p.results(), p.final_sem.at[0])
        drain(p.results(), p.final_sem.at[1])


def owner_tables(start, share, depth, order=None):
    col = lax.broadcasted_iota(jnp.int32, (1, BLOCK), 1) + start
    source = col if order is None else order(col)
    owner, entry = source // share, source % share
    pick = (entry == lax.broadcasted_iota(jnp.int32, (depth, BLOCK), 0)).astype(bf16)
    row = lax.broadcasted_iota(jnp.int32, (128, BLOCK), 0)
    return pick, owner == (row >> 3), row & 7


def quad_order(col):
    return (col % BLOCK) // QUAD * BLOCK + col // BLOCK * QUAD + col % QUAD


def layer_kernel(comm, *refs):
    refs = list(refs)

    def take(count):
        taken, refs[:] = refs[:count], refs[count:]
        return taken

    tok_in, cot_in, coords_in, segs_in = take(4)
    if comm:
        w_qkv_in, w_out_in, w_up_in, w_down_in = take(4)
        small_in = take(9)
    else:
        held_in, w_box_in, b_qkv_in, b_up_in, vectors_in = take(5)
    layer_out, g_tok_out, e_hbm = take(3)
    if comm:
        final_out, small_out = take(2)
    else:
        g_held, g_w_box_out, g_b_qkv_out, g_b_up_out, g_vectors_out = take(5)
    (held, stage, slope, q8t, k8t, v_row, ctx_t, wave_t, wave_r, e_buf, normed, total, flip, g_down, tok_t, g_ctx_t,
     inv_one, inv_total, w_box, w_box_t, b_qkv, b_up, vectors, g_w_box, g_b_qkv, g_b_up, g_vectors, e_sem, io_sem, coords, segs) = take(31)
    if comm:
        final, small, small_stage, g_small, small_final, mid_sem = take(6)
        small_held = take(9)
        block_sems, small_sems, small_final_sems = take(5), take(4), take(1)

    count, width = tok_t.shape[1], tok_t.shape[0]
    ff = slope.shape[0] // count * BLOCK
    slots, pairs = count // SLOT, HEADS // 2
    row_blocks = count // ROWS
    up_blocks = ff // BLOCK
    quads = pairs // 2
    ctx, low, cot, tok = [stage.at[part * count : (part + 1) * count] for part in range(4)]
    act = stage.at[STREAMS * BLOCK - up_blocks * count :]
    up_at, down_at = 4 * BLOCK, 8 * BLOCK

    def copy_in(source, target, index=0):
        return pltpu.make_async_copy(source, target, io_sem.at[index])

    tok_copy = copy_in(tok_in, tok, 0)
    cot_copy = copy_in(cot_in, cot, 1)
    coord_copy = copy_in(coords_in, coords, 2)
    seg_copy = copy_in(segs_in, segs, 3)

    if comm:
        route = Route()
        blocks = Exchange(route, Streams(held, stage, final, block_sems))
        extras = Exchange(route, Vectors(small, small_stage, small_final, [*small_sems, *small_final_sems]))
        sums = Exchange(route, Vectors(g_small, small_stage, small_final, [*small_sems, *small_final_sems]))
        barrier = pltpu.get_barrier_semaphore()
        for chip, core in route.peers():
            pl.semaphore_signal(barrier, inc=1, device_id=(chip, core), device_id_type=pl.DeviceIdType.MESH)
        moves = []
        for quad in range(quads):
            for part in range(3):
                moves.append((
                    w_qkv_in.at[:, part * width + quad * QUAD : part * width + (quad + 1) * QUAD],
                    total.at[quad * PIECE : (quad + 1) * PIECE, part * QUAD : (part + 1) * QUAD],
                ))
        moves.append((w_out_in, total.at[3 * PIECE : 4 * PIECE]))
        for block in range(up_blocks):
            moves.append((
                w_up_in.at[:, block * BLOCK : (block + 1) * BLOCK],
                total.at[(4 + block) * PIECE : (5 + block) * PIECE],
            ))
        moves.append((w_down_in, total.at[8 * PIECE : 12 * PIECE]))
        moves += list(zip(small_in, small_held))
        moves = [copy_in(source, target, 4 + index) for index, (source, target) in enumerate(moves)]
        first = 3 * quads
        for copy in moves[:first] + moves[first + 1 + up_blocks + 1 :] + moves[first : first + 1 + up_blocks + 1]:
            copy.start()
        for copy in (coord_copy, seg_copy, tok_copy, cot_copy):
            copy.start()

        def round_block(block):
            at = pl.ds(pl.multiple_of(block * BLOCK + PIECE * route.me, 16), PIECE)
            held[at, :] = total[block * PIECE : (block + 1) * PIECE, :].astype(bf16)

        g_small[:8, :] = jnp.zeros((8, SMALL), f32)
        for copy in moves[:first]:
            copy.wait()
        for block in range(quads):
            round_block(block)
        for copy in moves[first + 1 + up_blocks + 1 :]:
            copy.wait()
        g_small[:8, :HD] = small_held[8][...].astype(bf16).astype(f32)
        for row in range(8):
            value = small_held[row][...].astype(bf16).astype(f32)
            g_small[row : row + 1, 128 : 128 + value.shape[1]] = value
        small[pl.ds(pl.multiple_of(route.me * 8, 8), 8), :] = g_small[:8, :]
        pl.semaphore_wait(barrier, 6)
        extras.gather_own(0)
        for stream in range(quads):
            blocks.gather_own(stream)
        for copy in moves[first : first + 1 + up_blocks + 1]:
            copy.wait()
        for block in range(quads, STREAMS - up_blocks):
            round_block(block)
        at = pl.ds(pl.multiple_of(down_at + 4 * PIECE * route.me, 16), 4 * PIECE)
        held[at, :] = total[8 * PIECE : 12 * PIECE, :].astype(bf16)
        blocks.gather_own(quads)
    else:
        for copy in (coord_copy, seg_copy, tok_copy, cot_copy):
            copy.start()
        copy_in(held_in, held, 4).start()
        w_box[...] = w_box_in[...]
        b_qkv[...] = b_qkv_in[...]
        b_up[...] = b_up_in[...]
        vectors[...] = vectors_in[...]

    coord_copy.wait()
    seg_copy.wait()
    wave_t[...] = wave_rows(coords[...])
    wave_r[...] = jnp.transpose(wave_t[...])
    for slot in range(slots):
        seg_i = jnp.broadcast_to(segs[:, slot * SLOT : (slot + 1) * SLOT].astype(f32), (SLOT, SLOT))
        seg_j = jnp.transpose(seg_i)
        normed[slot * SLOT : (slot + 1) * SLOT, :SLOT] = jnp.where(seg_i == seg_j, 0.0, neg_large)
    g_w_box[...] = jnp.zeros_like(g_w_box)
    g_b_up[...] = jnp.zeros_like(g_b_up)
    g_vectors[...] = jnp.zeros_like(g_vectors)
    tok_copy.wait()

    if comm:
        extras.gather_column(0)
        blocks.gather_column(0)
        extras.gather_near(0)
        blocks.gather_near(0)
        blocks.gather_column(1)
        extras.gather_far(0)
        blocks.gather_far(0)
        blocks.gather_near(1)
        blocks.gather_column(2)
        extras.gathered(0)
        table = small[...].astype(bf16)
        w_box[...] = table[:, :HD]
        share_qkv, share_up, share = widths(width, ff)
        for row, columns, share_of, depth, order, target in (
            (0, 3 * width, share_qkv, 256, quad_order, b_qkv),
            (1, ff, share_up, 256, None, b_up),
            (None, width, share, 128, None, vectors),
        ):
            @pl.loop(0, columns // BLOCK)
            def _(block):
                pick, owned, row_of = owner_tables(block * BLOCK, share_of, depth, order)
                spread = dot_nn(table[:, 128 : 128 + depth], pick)
                keep = owned if row is None else owned & (row_of == row)
                rows = jnp.sum(jnp.where(keep, spread, 0.0).reshape(16, 8, BLOCK), axis=0)
                target[:, aligned(block, BLOCK)] = rows if row is None else jnp.sum(rows, axis=0, keepdims=True)

    else:
        copy_in(held_in, held, 4).wait()
    w_box_t[...] = jnp.transpose(w_box[...].astype(f32)).astype(bf16)

    def gather_tick(step):
        if not comm:
            return
        for ahead, act_on in enumerate((blocks.gather_far, blocks.gather_near, blocks.gather_column, blocks.gather_own)):
            pl.when(step + ahead < STREAMS)(functools.partial(act_on, step + ahead))

    def need(stream):
        if comm:
            blocks.gathered(stream)

    b_out, gain_one, shift_one, b_down, gain_two, shift_two = [vectors[2 + i : 3 + i, :] for i in range(VECTORS)]
    lane = lax.broadcasted_iota(jnp.int32, (SLOT, PAIR), 1)

    def project(quad, slot):
        rows = tok[aligned(slot, SLOT), :]

        def columns(part):
            weight = held[aligned(quad, BLOCK), part * QUAD : (part + 1) * QUAD]
            shift = b_qkv[:, pl.ds(pl.multiple_of(quad * BLOCK + part * QUAD, QUAD), QUAD)]
            return (dot_nn(rows, weight) + shift).astype(bf16)

        q, k, v = columns(0), columns(1), columns(2)
        low[aligned(slot, SLOT), aligned(quad, QUAD)] = k
        flip[aligned(quad, QUAD), aligned(slot, SLOT)] = jnp.transpose(v.astype(f32)).astype(bf16)
        qt = jnp.transpose(q.astype(f32) * scale_factor).astype(bf16)
        kt = jnp.transpose(k.astype(f32) * scale_factor).astype(bf16)
        for part in range(2):
            here = slice(part * PAIR, (part + 1) * PAIR)
            q8t[slot, quad * 2 + part] = qt[here]
            k8t[slot, quad * 2 + part] = kt[here]
            v_row[slot, quad * 2 + part] = v[:, here]

    def e_copy(place, head, index, out):
        pair = (e_buf.at[place, head], e_hbm.at[index])
        return pltpu.make_async_copy(*(pair if out else pair[::-1]), e_sem.at[place, head])

    def attend(step):
        pair, slot = step // slots, step % slots
        cols = aligned(slot, SLOT)
        place = step % 2

        @pl.when(step >= 2)
        def _():
            for head in range(2):
                e_copy(place, head, 0, True).wait()

        sine_t, cosine_t = wave_t[:WAVE, cols], wave_t[WAVE:, cols]
        sc_t = (wave_t[:, cols] * scale_factor).astype(bf16)
        sc_r = wave_r[cols, :]
        cs_r = swap_lanes(sc_r)
        cc_r = jnp.where(lane < WAVE, cs_r, sc_r)
        ss_r = jnp.where(lane < WAVE, sc_r, -cs_r)
        cs_low = cs_r.astype(bf16)
        keys = low[cols, aligned(pair, PAIR)]
        heads_t = []
        for head in range(2):
            span = slice(head * HD, (head + 1) * HD)
            key_box = dot_nt(keys[:, span], w_box[...])
            k_side = (key_box * cc_r + swap_lanes(key_box) * ss_r).astype(bf16)
            q_t = q8t[slot, pair, span, :]
            query_box = dot_nn(w_box[...], q_t)
            first, second = query_box[:WAVE], query_box[WAVE:]
            q_side = jnp.concatenate(
                [first * sine_t + second * cosine_t, second * sine_t - first * cosine_t], axis=0
            ).astype(bf16)
            zero = jnp.zeros_like(q_t)
            q_pair = [q_t, zero] if head == 0 else [zero, q_t]
            k_full = jnp.concatenate([keys, cs_low, k_side], axis=1)
            q_full = jnp.concatenate(q_pair + [q_side, sc_t], axis=0)
            scores = dot_nn(k_full, q_full) + normed[cols, :SLOT]
            top = jnp.max(scores, axis=0, keepdims=True)
            exps = jnp.exp(scores - top)
            inverse = 1.0 / jnp.sum(exps, axis=0, keepdims=True)
            low_exps = exps.astype(bf16)
            e_buf[place, head] = low_exps
            e_copy(place, head, step * 2 + head, True).start()
            inv_total[step * 2 + head] = inverse
            at = pl.ds(pl.multiple_of(pair * PAIR + head * HD, HD), HD)
            heads_t.append(dot_nn(flip[at, cols], low_exps) * inverse)
        both = jnp.concatenate(heads_t, axis=0)
        ctx_t[aligned(pair, PAIR), cols] = both.astype(bf16)
        ctx[cols, aligned(pair, PAIR)] = jnp.transpose(both).astype(bf16)

    steps = slots * pairs
    quad_steps = 2 * slots

    @pl.loop(0, quads)
    def _(quad):
        need(quad)

        @pl.loop(0, slots)
        def _(slot):
            project(quad, slot)

        @pl.loop(0, quad_steps)
        def _(inner):
            step = quad * quad_steps + inner
            if comm:
                pl.when(step % 2 == 1)(functools.partial(gather_tick, (step + 1) // 2))
            attend(step)

    for place in range(2):
        for head in range(2):
            e_copy(place, head, 0, True).wait()

    def column_sum(value):
        return jnp.sum(value, axis=0, keepdims=True)

    need(3)
    gather_tick(7)

    @pl.loop(0, row_blocks)
    def _(block):
        rows = aligned(block, ROWS)
        token_rows = tok[rows, :].astype(f32)
        tok_t[:, rows] = jnp.transpose(token_rows).astype(bf16)
        pre = token_rows + dot_nn(ctx[rows, :], held[3 * BLOCK : 4 * BLOCK, :]) + b_out
        center = pre - row_mean(pre)
        invdev = lax.rsqrt(row_mean(center * center) + eps_norm)
        unit = center * invdev
        inv_one[rows, :] = jnp.broadcast_to(invdev, (ROWS, 128))
        normed[rows, :] = unit
        hidden = unit * gain_one + shift_one
        low[rows, :] = hidden.astype(bf16)
        flip[:, rows] = jnp.transpose(hidden).astype(bf16)

    @pl.loop(0, up_blocks)
    def _(block):
        gather_tick(8 + block)
        need(4 + block)

        @pl.loop(0, row_blocks)
        def _(row):
            rows = aligned(row, ROWS)
            at = pl.ds(pl.multiple_of(block * count + row * ROWS, ROWS), ROWS)
            weight = held[pl.ds(pl.multiple_of(up_at + block * BLOCK, BLOCK), BLOCK), :]
            up = dot_nn(low[rows, :], weight) + b_up[:, aligned(block, BLOCK)]
            cdf, pdf = gelu_parts(up)
            act[at, :] = (up * cdf).astype(bf16)
            slope[at, :] = (cdf + up * pdf).astype(bf16)

    for block in range(up_blocks):
        need(8 + block)
    cot_copy.wait()

    @pl.loop(0, row_blocks)
    def _(block):
        rows = aligned(block, ROWS)
        pre = normed[rows, :] * gain_one + shift_one + b_down
        for part in range(up_blocks):
            at = pl.ds(pl.multiple_of(part * count + block * ROWS, ROWS), ROWS)
            pre += dot_nn(act[at, :], held[down_at + part * BLOCK : down_at + (part + 1) * BLOCK, :])
        center = pre - row_mean(pre)
        invdev = lax.rsqrt(row_mean(center * center) + eps_norm)
        unit = center * invdev
        grad = cot[rows, :].astype(f32)
        cot[rows, :] = (unit * gain_two + shift_two).astype(bf16)
        scaled = grad * gain_two
        g_pre = invdev * (scaled - row_mean(scaled) - unit * row_mean(scaled * unit))
        total[rows, :] = g_pre
        low_pre = g_pre.astype(bf16)
        g_down[rows, :] = low_pre
        g_vectors[5:6, :] += column_sum(low_pre.astype(f32))
        g_vectors[6:7, :] += column_sum(grad * unit)
        g_vectors[7:8, :] += column_sum(grad)

    out_copy = pltpu.make_async_copy(cot, layer_out, io_sem.at[0])
    out_copy.start()
    if comm:
        for stream in range(STREAMS):
            blocks.gather_sent(stream)
        extras.gather_sent(0)

    def last(step):
        turn = step // 4
        return STREAMS - 1 - step + (14 - 6 * turn) * turn - 4

    def sum_start(step):
        if comm:
            blocks.sum_cores(last(step))

    def sum_tick(step, stages=(0, 1, 2, 3)):
        if not comm:
            return
        acts = (blocks.sum_far, blocks.sum_near, blocks.sum_column, blocks.sum_end)
        for behind in stages:
            at = step - behind
            if isinstance(at, int):
                if 0 <= at < STREAMS:
                    acts[behind](last(at))
            else:
                pl.when((at >= 0) & (at < STREAMS))(functools.partial(acts[behind], last(at)))

    def meet(sem):
        if comm:
            for chip, core in route.peers():
                pl.semaphore_signal(sem, inc=1, device_id=(chip, core), device_id_type=pl.DeviceIdType.MESH)
            pl.semaphore_wait(sem, 6)

    out_copy.wait()
    if comm:
        meet(mid_sem.at[0])

    @pl.loop(0, up_blocks)
    def _(index):
        block = up_blocks - 1 - index
        down_rows = pl.ds(pl.multiple_of(down_at + block * BLOCK, BLOCK), BLOCK)
        up_rows = pl.ds(pl.multiple_of(up_at + block * BLOCK, BLOCK), BLOCK)
        for row in range(2):
            rows = slice(row * (count // 2), (row + 1) * (count // 2))
            at = pl.ds(pl.multiple_of(block * count + row * (count // 2), count // 2), count // 2)
            g_act = dot_nt(g_down[rows, :], held[down_rows, :])
            g_up = (g_act * slope[at, :].astype(f32)).astype(bf16)
            slope[at, :] = g_up
            g_b_up[:, aligned(block, BLOCK)] += column_sum(g_up.astype(f32))
            total[rows, :] += dot_nt(g_up, held[up_rows, :])
        g_up = slope[aligned(block, count), :]
        for part in range(2):
            at = pl.ds(pl.multiple_of(up_at + block * BLOCK + part * HALF, HALF), HALF)
            held[at, :] = dot_nn(flip[part * HALF : (part + 1) * HALF, :], g_up).astype(bf16)
        sum_start(index)
        for part in range(2):
            at = pl.ds(pl.multiple_of(down_at + block * BLOCK + part * HALF, HALF), HALF)
            grads = dot_tn(act[aligned(block, count), part * HALF : (part + 1) * HALF], g_down[...])
            held[at, :] = grads.astype(bf16)
        sum_tick(index)

    if comm:
        meet(mid_sem.at[1])
    for step in range(up_blocks):
        sum_start(up_blocks + step)

    @pl.loop(0, row_blocks)
    def _(block):
        rows = aligned(block, ROWS)
        grad, unit = total[rows, :], normed[rows, :]
        scaled = grad * gain_one
        g_pre = inv_one[rows, :1] * (scaled - row_mean(scaled) - unit * row_mean(scaled * unit))
        total[rows, :] = g_pre
        low_pre = g_pre.astype(bf16)
        g_down[rows, :] = low_pre
        g_vectors[2:3, :] += column_sum(low_pre.astype(f32))
        g_vectors[3:4, :] += column_sum(grad * unit)
        g_vectors[4:5, :] += column_sum(grad)
        g_ctx_t[:, rows] = dot_nt(held[3 * BLOCK : 4 * BLOCK, :], low_pre).astype(bf16)

    @pl.loop(0, BLOCK // ROWS)
    def _(part):
        at = pl.ds(pl.multiple_of(3 * BLOCK + part * ROWS, ROWS), ROWS)
        held[at, :] = dot_nn(ctx_t[aligned(part, ROWS), :], g_down[...]).astype(bf16)

    sum_start(8)
    sum_tick(4)

    def e_step(order):
        quad = quads - 1 - order // quad_steps
        return quad * quad_steps + order % quad_steps

    def fetch(order):
        for head in range(2):
            e_copy(order % 2, head, e_step(order) * 2 + head, False).start()

    fetch(0)
    ones = jnp.ones((16, count), bf16)

    def attend_back(order):
        step = e_step(order)
        pair, slot = step // slots, step % slots
        cols = aligned(slot, SLOT)
        place = order % 2

        @pl.when(order + 1 < steps)
        def _():
            fetch(order + 1)

        for head in range(2):
            e_copy(place, head, 0, False).wait()
        sine_t, cosine_t = wave_t[:WAVE, cols], wave_t[WAVE:, cols]
        sc_t = (wave_t[:, cols] * scale_factor).astype(bf16)
        cs_t = (jnp.concatenate([cosine_t, sine_t], axis=0) * scale_factor).astype(bf16)
        values = v_row[slot, pair]
        g_parts = [[], [], []]
        for head in range(2):
            span = slice(head * HD, (head + 1) * HD)
            at = pl.ds(pl.multiple_of(pair * PAIR + head * HD, HD), HD)
            g_rows = g_ctx_t[at, cols].astype(f32) * inv_total[step * 2 + head]
            row_dot = jnp.sum(g_rows * ctx_t[at, cols].astype(f32), axis=0, keepdims=True)
            g_low = g_rows.astype(bf16)
            zero = jnp.zeros_like(g_low)
            g_pair = jnp.concatenate([g_low, zero] if head == 0 else [zero, g_low], axis=0)
            low_exps = e_buf[place, head]
            g_probs = dot_nn(values, g_pair)
            g_scores = (low_exps.astype(f32) * (g_probs - row_dot)).astype(bf16)
            g_parts[2].append(dot_nt(g_low, low_exps))
            k_t, q_t = k8t[slot, pair, span, :], q8t[slot, pair, span, :]
            g_q = dot_nn(jnp.concatenate([k_t, cs_t], axis=0), g_scores)
            g_k = dot_nt(jnp.concatenate([q_t, sc_t], axis=0), g_scores)
            first, second = g_q[HD : HD + WAVE], g_q[HD + WAVE :]
            g_qbox = jnp.concatenate(
                [first * sine_t - second * cosine_t, first * cosine_t + second * sine_t], axis=0
            ).astype(bf16)
            first, second = g_k[HD : HD + WAVE], g_k[HD + WAVE :]
            g_kbox = jnp.concatenate(
                [first * cosine_t - second * sine_t, first * sine_t + second * cosine_t], axis=0
            ).astype(bf16)
            g_parts[0].append(g_q[:HD] + dot_nn(w_box_t[...], g_qbox))
            g_parts[1].append(g_k[:HD] + dot_nn(w_box_t[...], g_kbox))
            g_w_box[...] += dot_nt(g_qbox, q_t) + dot_nt(g_kbox, k_t)
        for part in range(3):
            at = pl.ds(pl.multiple_of(part * QUAD + pair % 2 * PAIR, PAIR), PAIR)
            flip[at, cols] = jnp.concatenate(g_parts[part], axis=0).astype(bf16)

    def token_grad():
        @pl.loop(0, row_blocks)
        def _(block):
            rows = aligned(block, ROWS)
            part = dot_nn(slope[:BLOCK, :], flip[:, rows])
            total[rows, :] += jnp.transpose(part)

    @pl.loop(0, quads)
    def _(turn):
        quad = quads - 1 - turn

        @pl.loop(0, quad_steps)
        def _(inner):
            order = turn * quad_steps + inner
            if comm:
                pl.when(order % 2 == 0)(functools.partial(sum_tick, 5 + order // 2, (0,)))
                pl.when(order % 2 == 1)(functools.partial(sum_tick, 5 + order // 2, (1, 2, 3)))
            attend_back(order)

        slope[:BLOCK, :] = held[aligned(quad, BLOCK), :]
        for part in range(2):
            at = pl.ds(pl.multiple_of(quad * BLOCK + part * HALF, HALF), HALF)
            held[at, :] = dot_nt(tok_t[part * HALF : (part + 1) * HALF, :], flip[...]).astype(bf16)
        sum_start(9 + turn)
        g_b_qkv[:, aligned(quad, BLOCK)] = dot_nt(ones, flip[...])[:1]
        token_grad()

    g_w_box[...] = g_w_box[...] * (1.0 / scale_factor)
    tok_out = pltpu.make_async_copy(total, g_tok_out, io_sem.at[0])
    tok_out.start()

    if comm:
        g_small[...] = jnp.zeros_like(g_small)
        g_small[:, :HD] = g_w_box[...]
        share_qkv, share_up, share = widths(width, ff)
        for row, columns, share_of, order, source in (
            (0, 3 * width, share_qkv, quad_order, g_b_qkv),
            (1, ff, share_up, None, g_b_up),
            (None, width, share, None, g_vectors),
        ):
            @pl.loop(0, columns // BLOCK)
            def _(block):
                pick, owned, row_of = owner_tables(block * BLOCK, share_of, 256, order)
                keep = owned if row is None else owned & (row_of == row)
                wide = 1 if row is not None else 8
                full = source[:, aligned(block, BLOCK)].reshape(1, wide, BLOCK)
                spread = jnp.broadcast_to(full, (16, 8, BLOCK)).reshape(128, BLOCK)
                spread = jnp.where(keep, spread, 0.0)
                upper = spread.astype(bf16)
                g_small[:, 128:384] += dot_nt(upper, pick) + dot_nt((spread - upper.astype(f32)).astype(bf16), pick)

        sums.sum_cores(0)
        sum_tick(11, (1, 2, 3))
        sum_tick(11, (0,))
        sums.sum_far(0)
        sum_tick(12, (2, 3))
        sum_tick(12, (1,))
        sums.sum_near(0)
        sum_tick(13, (3,))
        sum_tick(13, (2,))
        sums.sum_column(0)
        sum_tick(14, (3,))
        sums.sum_end(0)
        for stream in range(STREAMS):
            blocks.summed(stream)
        sums.summed(0)
        blocks.results_in()
        sums.results_in()
        moves = [copy_in(final, final_out, 2), copy_in(small_final, small_out, 3)]
        for copy in moves:
            copy.start()
        for copy in moves:
            copy.wait()
    else:
        g_w_box_out[...] = g_w_box[...]
        g_b_qkv_out[...] = g_b_qkv[...]
        g_b_up_out[...] = g_b_up[...]
        g_vectors_out[...] = g_vectors[...]
        out = copy_in(held, g_held, 2)
        out.start()
        out.wait()
    tok_out.wait()


def shaped(shape, dtype):
    return jax.ShapeDtypeStruct(shape, dtype)


def in_vmem(count):
    return [pl.BlockSpec(memory_space=pltpu.VMEM)] * count


def in_hbm(count):
    return [pl.BlockSpec(memory_space=pl.ANY)] * count


def run_layer(comm, tokens, cotangent, coords, segs, big, little):
    count, width = tokens.shape
    ff = 4 * BLOCK
    slots, pairs = count // SLOT, HEADS // 2
    held_shape = (STREAMS * BLOCK, BLOCK)
    out_shape = [
        shaped((count, width), bf16),
        shaped((count, width), f32),
        shaped((slots * HEADS, SLOT, SLOT), bf16),
    ]
    out_specs = in_hbm(3)
    if comm:
        out_shape += [shaped((STREAMS * PIECE, BLOCK), f32), shaped((8, SMALL), f32)]
        out_specs += in_hbm(2)
    else:
        out_shape += [shaped(held_shape, bf16), shaped((2 * WAVE, HD), f32), shaped((1, 3 * width), f32)]
        out_shape += [shaped((1, ff), f32), shaped((8, width), f32)]
        out_specs += in_hbm(1) + in_vmem(4)
    vmem = pltpu.VMEM
    dma = pltpu.SemaphoreType.DMA
    scratch = [
        vmem(held_shape, bf16),
        vmem(held_shape, bf16),
        vmem((ff // BLOCK * count, BLOCK), bf16),
        vmem((slots, pairs, PAIR, SLOT), bf16),
        vmem((slots, pairs, PAIR, SLOT), bf16),
        vmem((slots, pairs, SLOT, PAIR), bf16),
        vmem((width, count), bf16),
        vmem((2 * WAVE, count), f32),
        vmem((count, 2 * WAVE), f32),
        vmem((2, 2, SLOT, SLOT), bf16),
        vmem((count, width), f32),
        vmem((count, width), f32),
        vmem((width, count), bf16),
        vmem((count, width), bf16),
        vmem((width, count), bf16),
        vmem((width, count), bf16),
        vmem((count, 128), f32),
        vmem((slots * HEADS, 1, SLOT), f32),
        vmem((2 * WAVE, HD), bf16),
        vmem((HD, 2 * WAVE), bf16),
        vmem((1, 3 * width), f32),
        vmem((1, ff), f32),
        vmem((8, width), f32),
        vmem((2 * WAVE, HD), f32),
        vmem((1, 3 * width), f32),
        vmem((1, ff), f32),
        vmem((8, width), f32),
        dma((2, 2)),
        dma((32,)),
        vmem(coords.shape, jnp.int32),
        vmem(segs.shape, jnp.int32),
    ]
    if comm:
        scratch += [
            vmem((STREAMS * PIECE, BLOCK), f32),
            vmem((128, SMALL), f32),
            vmem((256, SMALL // 2), f32),
            vmem((128, SMALL), f32),
            vmem((8, SMALL), f32),
            pltpu.SemaphoreType.REGULAR((2,)),
            *[vmem(value.shape, f32) for value in little],
            dma((STREAMS, 4)), dma((STREAMS, 2)), dma((STREAMS, 4)), dma((STREAMS,)), dma((2,)),
            dma((1, 4)), dma((1, 2)), dma((1, 4)), dma((1,)),
            dma((2,)),
        ]
        extra = dict(collective_id=0, has_side_effects=True)
    else:
        extra = {}
    return pl.pallas_call(
        functools.partial(layer_kernel, comm),
        out_shape=out_shape,
        in_specs=in_hbm(4 + len(big)) + (in_hbm if comm else in_vmem)(len(little)),
        out_specs=out_specs,
        scratch_shapes=scratch,
        compiler_params=pltpu.CompilerParams(vmem_limit_bytes=vmem_limit, **extra),
        name="layer",
    )(tokens, cotangent, coords, segs, *big, *little)


def finish_kernel(*refs):
    layer_in, tok_in, blocks_in, small_in = refs[:4]
    layer_out, tok_out, p_qkv, p_out, p_up, p_down = refs[4:10]
    small_out = refs[10:19]
    layer, tok, blocks, small = refs[19:23]
    small_rows = refs[23:32]
    load_sem, store_sem = refs[32:]
    width = layer_in.shape[1]
    loads, stores = [], []
    parts = 4
    rows = layer_in.shape[0] // parts
    small_load = pltpu.make_async_copy(small_in, small, load_sem.at[0])
    loads.append((pltpu.make_async_copy(blocks_in, blocks, load_sem.at[1]), []))
    for quad in range(width // QUAD):
        for part in range(3):
            loads[0][1].append((
                blocks.at[quad * PIECE : (quad + 1) * PIECE, part * QUAD : (part + 1) * QUAD],
                p_qkv.at[:, part * width + quad * QUAD : part * width + (quad + 1) * QUAD],
            ))
    loads[0][1].append((blocks.at[3 * PIECE : 4 * PIECE], p_out))
    for block in range(4):
        loads[0][1].append((
            blocks.at[(4 + block) * PIECE : (5 + block) * PIECE], p_up.at[:, block * BLOCK : (block + 1) * BLOCK]
        ))
    loads[0][1].append((blocks.at[8 * PIECE : 12 * PIECE], p_down))
    for source, held, target in ((tok_in, tok, tok_out), (layer_in, layer, layer_out)):
        for part in range(parts):
            at = slice(part * rows, (part + 1) * rows)
            copy = pltpu.make_async_copy(source.at[at], held.at[at], load_sem.at[1 + len(loads)])
            loads.append((copy, [(held.at[at], target.at[at])]))
    small_load.start()
    for copy, _ in loads:
        copy.start()

    def store(source, target):
        stores.append(pltpu.make_async_copy(source, target, store_sem.at[len(stores)]))
        stores[-1].start()

    small_load.wait()
    for row in range(8):
        small_rows[row][...] = small[row : row + 1, 128 : 128 + small_rows[row].shape[1]]
    small_rows[8][...] = small[:, :HD]
    for source, target in zip(small_rows, small_out):
        store(source, target)
    for copy, moves in loads:
        copy.wait()
        for source, target in moves:
            store(source, target)
    for copy in stores:
        copy.wait()


def run_finish(layer_out, g_tok, blocks, small, big, little):
    shapes = [shaped(layer_out.shape, bf16), shaped(g_tok.shape, f32)]
    shapes += [shaped(w.shape, f32) for w in big + little]
    dma = pltpu.SemaphoreType.DMA
    return pl.pallas_call(
        finish_kernel,
        out_shape=shapes,
        in_specs=in_hbm(4),
        out_specs=in_hbm(len(shapes)),
        scratch_shapes=[
            pltpu.VMEM(layer_out.shape, bf16), pltpu.VMEM(g_tok.shape, f32), pltpu.VMEM(blocks.shape, f32),
            pltpu.VMEM(small.shape, f32), *[pltpu.VMEM(v.shape, f32) for v in little], dma((16,)), dma((40,)),
        ],
        compiler_params=pltpu.CompilerParams(vmem_limit_bytes=16_000_000),
        name="finish",
    )(layer_out, g_tok, blocks, small)


def to_blocks(w_qkv, w_out, w_up, w_down):
    width = w_out.shape[1]
    qkv = w_qkv.reshape(width, 3, width // QUAD, QUAD).transpose(2, 0, 1, 3).reshape(-1, BLOCK)
    up = w_up.reshape(width, -1, BLOCK).transpose(1, 0, 2).reshape(-1, BLOCK)
    return jnp.concatenate([qkv, w_out, up, w_down], axis=0)


def from_blocks(held, width):
    qkv = held[: 3 * BLOCK].reshape(width // QUAD, width, 3, QUAD).transpose(1, 2, 0, 3).reshape(width, -1)
    up = held[4 * BLOCK : 8 * BLOCK].reshape(-1, width, BLOCK).transpose(1, 0, 2).reshape(width, -1)
    return qkv, held[3 * BLOCK : 4 * BLOCK], up, held[8 * BLOCK :]


def per_device(
    mesh_shape, tokens, cotangent, segments, box_coords, w_qkv, b_qkv, w_box, w_out, b_out, gain_one, shift_one,
    w_up, b_up, w_down, b_down, gain_two, shift_two,
):
    count, width = tokens.shape
    segs = segments.reshape(1, -1)
    vectors = [b_qkv, b_up, b_out, gain_one, shift_one, b_down, gain_two, shift_two]
    if mesh_shape == (16, 2):
        little = [v.reshape(1, -1) for v in vectors] + [w_box]
        big = [w_qkv, w_out, w_up, w_down]
        layer_out, g_tok, _, blocks, small = run_layer(True, tokens, cotangent, box_coords, segs, big, little)
        layer_out, g_tok, p_wq, p_wo, p_wu, p_wd, *rest = run_finish(layer_out, g_tok, blocks, small, big, little)
        p_bq, p_bu, p_bo, p_g1, p_s1, p_bd, p_g2, p_s2 = [v.reshape(-1) for v in rest[:8]]
        p_wb = rest[8]
    else:
        low = lambda value: value.astype(bf16)
        gather = lambda value: lax.all_gather(low(value), "fsdp", axis=0, tiled=True)
        held = to_blocks(gather(w_qkv), gather(w_out), gather(w_up), gather(w_down))
        wb, bq, bu, *six = [gather(v) for v in [w_box] + vectors]
        order = quad_order(jnp.arange(3 * width))
        rows = jnp.stack([jnp.zeros((width,), bf16)] * 2 + six).astype(f32)
        layer_out, g_tok, _, g_held, g_wb, g_bq, g_bu, g_six = run_layer(
            False, tokens, cotangent, box_coords, segs, [held],
            [wb, bq[order].astype(f32).reshape(1, -1), bu.astype(f32).reshape(1, -1), rows],
        )

        def scatter(grad):
            part = lax.psum_scatter(grad, "fsdp", scatter_dimension=0, tiled=True)
            return lax.psum(part, "rep").astype(f32)

        p_wq, p_wo, p_wu, p_wd = [scatter(g) for g in from_blocks(g_held, width)]
        g_bq = jnp.zeros((3 * width,), f32).at[order].set(g_bq[0])
        p_wb, p_bq, p_bu = scatter(g_wb), scatter(g_bq), scatter(g_bu[0])
        p_bo, p_g1, p_s1, p_bd, p_g2, p_s2 = [scatter(g_six[2 + i]) for i in range(VECTORS)]
    return (
        layer_out, g_tok, p_wq, p_bq, p_wb, p_wo, p_bo, p_g1, p_s1,
        p_wu, p_bu, p_wd, p_bd, p_g2, p_s2,
    )


def solution(mesh):
    tokens = P(("fsdp", "rep"), None)
    matrix, vector = P("fsdp", None), P("fsdp")
    kinds = [matrix, vector, matrix, matrix, vector, vector, vector, matrix, vector, matrix, vector, vector, vector]
    return jax.shard_map(
        functools.partial(per_device, (mesh.shape["fsdp"], mesh.shape["rep"])),
        mesh=mesh,
        in_specs=(tokens, tokens, P(("fsdp", "rep")), P(None, ("fsdp", "rep")), *kinds),
        out_specs=(tokens, tokens, *kinds),
        check_vma=False,
    )
```

```python
import functools
import math

import jax
import jax.numpy as jnp
from jax import lax
from jax.experimental import pallas as pl
from jax.experimental.pallas import tpu as pltpu
from jax.sharding import PartitionSpec as P

HEADS = 12
HD = 64
FREQ = 16
SLOT = 512
WAVE = 4 * FREQ
PAIR = 2 * HD
QUAD = 4 * HD

f32 = jnp.float32
bf16 = jnp.bfloat16
neg_large = -1e30
eps_norm = 1e-12
scale_factor = 1.0 / math.sqrt(HD)
vmem_limit = 67_000_000


def dot_nn(left, right):
    return lax.dot_general(left, right, (((1,), (0,)), ((), ())), preferred_element_type=f32)


def dot_nt(left, right):
    return lax.dot_general(left, right, (((1,), (1,)), ((), ())), preferred_element_type=f32)


def dot_tn(left, right):
    return lax.dot_general(left, right, (((0,), (0,)), ((), ())), preferred_element_type=f32)


def aligned(index, size):
    return pl.ds(pl.multiple_of(index * size, size), size)


def wave_rows(coords):
    count = coords.shape[1]
    spread = [jnp.broadcast_to(coords[c : c + 1, :].astype(f32), (FREQ, count)) for c in range(4)]
    scaled = jnp.concatenate(spread + spread, axis=0) * (100.0 / 1024.0)
    rows = lax.broadcasted_iota(jnp.int32, scaled.shape, 0)
    frequency = jnp.exp(-math.log(10000.0) * (rows & (FREQ - 1)).astype(f32) / FREQ)
    angle = scaled * frequency
    turns = jnp.floor(angle * (2.0 / math.pi) + 0.5)
    rest = ((angle - turns * 1.5703125) - turns * 4.837512969970703125e-4) - turns * 7.549789954891e-8
    square = rest * rest
    sine = rest + rest * square * (
        -1.6666654611e-1 + square * (8.3321608736e-3 + square * -1.9515295891e-4)
    )
    cosine = 1.0 - 0.5 * square + square * square * (
        4.166664568298827e-2 + square * (-1.388731625493765e-3 + square * 2.443315711809948e-5)
    )
    quadrant = turns.astype(jnp.int32) + jnp.where(rows >= WAVE, 1, 0)
    value = jnp.where((quadrant & 1) == 1, cosine, sine)
    value = jnp.where((quadrant & 2) == 2, -value, value)
    return value.astype(bf16).astype(f32)


def swap_lanes(value):
    return pltpu.roll(value, WAVE, 1)


def gelu_parts(value):
    size = jnp.abs(value) * math.sqrt(0.5)
    t = 1.0 / (1.0 + 0.3275911 * size)
    bell = jnp.exp(-0.5 * value * value)
    tail = t * (
        0.254829592 + t * (-0.284496736 + t * (1.421413741 + t * (-1.453152027 + t * 1.061405429)))
    )
    half_tail = 0.5 * tail * bell
    return jnp.where(value >= 0, 1.0 - half_tail, half_tail), bell * (1.0 / math.sqrt(2.0 * math.pi))


def row_mean(value):
    return jnp.mean(value, axis=-1, keepdims=True)


ROWS = 256
BLOCK = 768
PIECE = 48
HALF = BLOCK // 2
SMALL = 512
STREAMS = 12
VECTORS = 6


def widths(width, ff):
    return 3 * width // 16, ff // 16, width // 16


class Route:
    def __init__(self):
        chip = lax.axis_index("fsdp")
        self.core = lax.axis_index("rep")
        self.level, self.me = chip // 4, chip % 4
        near_step, far_step = 1 + self.core, 2 - self.core
        near_move = near_step * (1 - 2 * ((self.me // near_step) % 2))
        far_move = far_step * (1 - 2 * ((self.me // far_step) % 2))
        self.near = self.me + near_move
        self.far = self.me + far_move
        self.across = self.me + near_move + far_move

    def chip(self, level, place):
        return level * 4 + place

    def levels(self):
        return [(self.level + k) % 4 for k in range(1, 4)]

    def peers(self):
        chips = [self.chip(level, self.me) for level in self.levels()]
        chips += [self.chip(self.level, self.near), self.chip(self.level, self.far)]
        return [(chip, self.core) for chip in chips] + [(self.chip(self.level, self.me), 1 - self.core)]


def remote(source, target, send, recv, chip, core):
    return pltpu.make_async_remote_copy(
        src_ref=source, dst_ref=target, send_sem=send, recv_sem=recv,
        device_id=(chip, core), device_id_type=pl.DeviceIdType.MESH,
    )


def half_columns(half, size):
    return pl.ds(pl.multiple_of(half * size, size), size)


class Streams:
    def __init__(self, held, stage, final, sems):
        self.held = held
        self.upper = held.at[: 8 * BLOCK].reshape(8, 4, 4, PIECE, BLOCK)
        self.lower = held.at[8 * BLOCK :].reshape(4, 4, 4, PIECE, BLOCK)
        self.stage = stage.reshape(STREAMS, 4, 4, PIECE, BLOCK)
        self.final = final
        self.gather_recv, self.gather_send, self.sum_recv, self.sum_send, self.final_sem = sems

    def on(self, stream, act):
        if isinstance(stream, int):
            act(self.upper.at[stream] if stream < 8 else self.lower.at[:, :, stream - 8])
        else:
            pl.when(stream < 8)(lambda: act(self.upper.at[stream]))
            pl.when(stream >= 8)(lambda: act(self.lower.at[:, :, stream - 8]))

    def half(self, half):
        return half_columns(half, HALF)

    def several(self, pieces):
        return self.held.at[: PIECE * pieces, :HALF]

    def landing(self, stream, kind):
        block = self.stage.at[(stream + 8) % STREAMS]
        if kind == 0:
            return block.at[:, :, :, :HALF]
        return block.at[(0, 0, 2, 3)[kind] : (0, 2, 3, 4)[kind], :, :, HALF:]

    def result(self, stream, half):
        return self.final.at[pl.ds(pl.multiple_of(stream * PIECE, 16), PIECE), self.half(half)]

    def results(self):
        return self.final.at[:, :HALF]


class Vectors:
    def __init__(self, held, stage, final, sems):
        self.held, self.flat, self.final = held, stage, final
        self.shards = held.reshape(4, 4, 8, SMALL)
        self.stage = stage.reshape(8, 4, 8, SMALL // 2)
        self.gather_recv, self.gather_send, self.sum_recv, self.sum_send, self.final_sem = sems

    def on(self, stream, act):
        act(self.shards)

    def half(self, half):
        return half_columns(half, SMALL // 2)

    def several(self, pieces):
        if pieces <= 16:
            return self.held.at[: 8 * pieces, : SMALL // 2]
        return self.flat.at[: 8 * pieces, :]

    def landing(self, stream, kind):
        return self.stage.at[(0, 4, 6, 7)[kind] : (4, 6, 7, 8)[kind]]

    def result(self, stream, half):
        return self.final.at[:, self.half(half)]

    def results(self):
        return self.final.at[:, : SMALL // 2]


def drain(view, sem):
    pltpu.make_async_copy(view, view, sem).wait()


class Exchange:
    def __init__(self, route, parts):
        self.route, self.parts = route, parts

    def send(self, source, target, send, recv, level, place, core):
        remote(source, target, send, recv, self.route.chip(level, place), core).start()


    def share(self, stream, view, place, kind):
        p, r = self.parts, self.route
        self.send(
            view, view, p.gather_send.at[stream, 0], p.gather_recv.at[stream, kind], r.level, place, r.core
        )

    def hand_over(self, stream, view):
        p, r = self.parts, self.route
        self.send(
            view, view, p.gather_send.at[stream, 1], p.gather_recv.at[stream, 3], r.level, r.me, 1 - r.core
        )

    def gather_own(self, stream):
        p, r = self.parts, self.route

        def act(shards):
            view = shards.at[r.level, r.me, :, p.half(r.core)]
            for level in r.levels():
                self.send(
                    view, view, p.gather_send.at[stream, 0], p.gather_recv.at[stream, 0], level, r.me, r.core
                )

        p.on(stream, act)

    def gather_column(self, stream):
        p, r = self.parts, self.route
        drain(p.several(3), p.gather_recv.at[stream, 0])

        def act(shards):
            view = shards.at[:, r.me, :, p.half(r.core)]
            self.share(stream, view, r.near, 1)
            self.share(stream, view, r.far, 2)
            for level in r.levels():
                self.hand_over(stream, shards.at[level, r.me, :, p.half(r.core)])

        p.on(stream, act)

    def gather_near(self, stream):
        p, r = self.parts, self.route
        drain(p.several(4), p.gather_recv.at[stream, 1])

        def act(shards):
            view = shards.at[:, r.near, :, p.half(r.core)]
            self.share(stream, view, r.far, 2)
            self.hand_over(stream, view)

        p.on(stream, act)

    def gather_far(self, stream):
        p, r = self.parts, self.route
        drain(p.several(8), p.gather_recv.at[stream, 2])

        def act(shards):
            for place in (r.far, r.across):
                self.hand_over(stream, shards.at[:, place, :, p.half(r.core)])

        p.on(stream, act)

    def gathered(self, stream):
        p = self.parts
        drain(p.several(15), p.gather_recv.at[stream, 3])

    def gather_sent(self, stream):
        p = self.parts
        drain(p.several(15), p.gather_send.at[stream, 0])
        drain(p.several(15), p.gather_send.at[stream, 1])


    def pass_on(self, stream, view, landing, kind, level, place):
        p, r = self.parts, self.route
        self.send(view, landing, p.sum_send.at[stream], p.sum_recv.at[stream, kind], level, place, r.core)

    def sum_cores(self, stream):
        p, r = self.parts, self.route

        def act(shards):
            self.send(
                shards.at[:, :, :, p.half(1 - r.core)], p.landing(stream, 0),
                p.sum_send.at[stream], p.sum_recv.at[stream, 0], r.level, r.me, 1 - r.core,
            )

        p.on(stream, act)

    def sum_far(self, stream):
        p, r = self.parts, self.route
        drain(p.several(16), p.sum_recv.at[stream, 0])
        landed, target = p.landing(stream, 0), p.landing(stream, 1)

        def act(shards):
            def add(place):
                view = shards.at[:, place, :, p.half(r.core)]
                view[...] += landed[:, place]
                return view

            for index, place in enumerate((r.far, r.across)):
                self.pass_on(stream, add(place), target.at[index], 1, r.level, r.far)
            for place in (r.me, r.near):
                add(place)

        p.on(stream, act)

    def sum_near(self, stream):
        p, r = self.parts, self.route
        drain(p.several(8), p.sum_recv.at[stream, 1])
        landed, target = p.landing(stream, 1), p.landing(stream, 2)

        def act(shards):
            view = shards.at[:, r.near, :, p.half(r.core)]
            view[...] += landed[1]
            self.pass_on(stream, view, target.at[0], 2, r.level, r.near)
            view = shards.at[:, r.me, :, p.half(r.core)]
            view[...] += landed[0]

        p.on(stream, act)

    def sum_column(self, stream):
        p, r = self.parts, self.route
        drain(p.several(4), p.sum_recv.at[stream, 2])
        landed, target = p.landing(stream, 2), p.landing(stream, 3)

        def act(shards):
            view = shards.at[:, r.me, :, p.half(r.core)]
            view[...] += landed[0]
            for index, level in enumerate(r.levels()):
                self.pass_on(
                    stream, shards.at[level, r.me, :, p.half(r.core)], target.at[0, index], 3, level, r.me
                )

        p.on(stream, act)

    def sum_end(self, stream):
        p, r = self.parts, self.route
        drain(p.several(3), p.sum_recv.at[stream, 3])
        landed = p.landing(stream, 3)
        view = p.result(stream, r.core)

        def act(shards):
            total = shards[r.level, r.me, :, p.half(r.core)].astype(f32)
            for index in range(3):
                total += landed[0, index].astype(f32)
            view[...] = total

        p.on(stream, act)
        self.send(view, view, p.final_sem.at[0], p.final_sem.at[1], r.level, r.me, 1 - r.core)

    def summed(self, stream):
        p = self.parts
        drain(p.several(31), p.sum_send.at[stream])

    def results_in(self):
        p = self.parts
        drain(p.results(), p.final_sem.at[0])
        drain(p.results(), p.final_sem.at[1])


def owner_tables(start, share, depth, order=None):
    col = lax.broadcasted_iota(jnp.int32, (1, BLOCK), 1) + start
    source = col if order is None else order(col)
    owner, entry = source // share, source % share
    pick = (entry == lax.broadcasted_iota(jnp.int32, (depth, BLOCK), 0)).astype(bf16)
    row = lax.broadcasted_iota(jnp.int32, (128, BLOCK), 0)
    return pick, owner == (row >> 3), row & 7


def quad_order(col):
    return (col % BLOCK) // QUAD * BLOCK + col // BLOCK * QUAD + col % QUAD


def layer_kernel(comm, *refs):
    refs = list(refs)

    def take(count):
        taken, refs[:] = refs[:count], refs[count:]
        return taken

    tok_in, cot_in, coords_in, segs_in = take(4)
    if comm:
        w_qkv_in, w_out_in, w_up_in, w_down_in = take(4)
        small_in = take(9)
    else:
        held_in, w_box_in, b_qkv_in, b_up_in, vectors_in = take(5)
    layer_out, g_tok_out, e_hbm = take(3)
    if comm:
        final_out, small_out = take(2)
    else:
        g_held, g_w_box_out, g_b_qkv_out, g_b_up_out, g_vectors_out = take(5)
    (held, stage, slope, q8t, k8t, v_row, ctx_t, wave_t, wave_r, e_buf, normed, total, flip, g_down, tok_t, g_ctx_t,
     inv_one, inv_total, w_box, w_box_t, b_qkv, b_up, vectors, g_w_box, g_b_qkv, g_b_up, g_vectors, e_sem, io_sem, coords, segs) = take(31)
    if comm:
        final, small, small_stage, g_small, small_final, mid_sem = take(6)
        small_held = take(9)
        block_sems, small_sems, small_final_sems = take(5), take(4), take(1)

    count, width = tok_t.shape[1], tok_t.shape[0]
    ff = slope.shape[0] // count * BLOCK
    slots, pairs = count // SLOT, HEADS // 2
    row_blocks = count // ROWS
    up_blocks = ff // BLOCK
    quads = pairs // 2
    ctx, low, cot, tok = [stage.at[part * count : (part + 1) * count] for part in range(4)]
    act = stage.at[STREAMS * BLOCK - up_blocks * count :]
    up_at, down_at = 4 * BLOCK, 8 * BLOCK

    def copy_in(source, target, index=0):
        return pltpu.make_async_copy(source, target, io_sem.at[index])

    tok_copy = copy_in(tok_in, tok, 0)
    cot_copy = copy_in(cot_in, cot, 1)
    coord_copy = copy_in(coords_in, coords, 2)
    seg_copy = copy_in(segs_in, segs, 3)

    if comm:
        route = Route()
        chip = route.chip(route.level, route.me)
        blocks = Exchange(route, Streams(held, stage, final, block_sems))
        extras = Exchange(route, Vectors(small, small_stage, small_final, [*small_sems, *small_final_sems]))
        sums = Exchange(route, Vectors(g_small, small_stage, small_final, [*small_sems, *small_final_sems]))
        barrier = pltpu.get_barrier_semaphore()
        for peer, core in route.peers():
            pl.semaphore_signal(barrier, inc=1, device_id=(peer, core), device_id_type=pl.DeviceIdType.MESH)
        moves = []
        for quad in range(quads):
            for part in range(3):
                moves.append((
                    w_qkv_in.at[:, part * width + quad * QUAD : part * width + (quad + 1) * QUAD],
                    total.at[quad * PIECE : (quad + 1) * PIECE, part * QUAD : (part + 1) * QUAD],
                ))
        moves.append((w_out_in, total.at[3 * PIECE : 4 * PIECE]))
        for block in range(up_blocks):
            moves.append((
                w_up_in.at[:, block * BLOCK : (block + 1) * BLOCK],
                total.at[(4 + block) * PIECE : (5 + block) * PIECE],
            ))
        moves.append((w_down_in, total.at[8 * PIECE : 12 * PIECE]))
        moves += list(zip(small_in, small_held))
        moves = [copy_in(source, target, 4 + index) for index, (source, target) in enumerate(moves)]
        first = 3 * quads
        for copy in moves[:first] + moves[first + 1 + up_blocks + 1 :] + moves[first : first + 1 + up_blocks + 1]:
            copy.start()
        for copy in (coord_copy, seg_copy, tok_copy, cot_copy):
            copy.start()

        def round_block(block):
            at = pl.ds(pl.multiple_of(block * BLOCK + PIECE * chip, 16), PIECE)
            held[at, :] = total[block * PIECE : (block + 1) * PIECE, :].astype(bf16)

        g_small[:8, :] = jnp.zeros((8, SMALL), f32)
        for copy in moves[:first]:
            copy.wait()
        for block in range(quads):
            round_block(block)
        for copy in moves[first + 1 + up_blocks + 1 :]:
            copy.wait()
        g_small[:8, :HD] = small_held[8][...].astype(bf16).astype(f32)
        for row in range(8):
            value = small_held[row][...].astype(bf16).astype(f32)
            g_small[row : row + 1, 128 : 128 + value.shape[1]] = value
        small[pl.ds(pl.multiple_of(chip * 8, 8), 8), :] = g_small[:8, :]
        pl.semaphore_wait(barrier, 6)
        extras.gather_own(0)
        for stream in range(quads):
            blocks.gather_own(stream)
        for copy in moves[first : first + 1 + up_blocks + 1]:
            copy.wait()
        for block in range(quads, STREAMS - up_blocks):
            round_block(block)
        at = pl.ds(pl.multiple_of(down_at + 4 * PIECE * chip, 16), 4 * PIECE)
        held[at, :] = total[8 * PIECE : 12 * PIECE, :].astype(bf16)
        for stream in range(quads, STREAMS):
            blocks.gather_own(stream)
    else:
        for copy in (coord_copy, seg_copy, tok_copy, cot_copy):
            copy.start()
        copy_in(held_in, held, 4).start()
        w_box[...] = w_box_in[...]
        b_qkv[...] = b_qkv_in[...]
        b_up[...] = b_up_in[...]
        vectors[...] = vectors_in[...]

    coord_copy.wait()
    seg_copy.wait()
    wave_t[...] = wave_rows(coords[...])
    wave_r[...] = jnp.transpose(wave_t[...])
    for slot in range(slots):
        seg_i = jnp.broadcast_to(segs[:, slot * SLOT : (slot + 1) * SLOT].astype(f32), (SLOT, SLOT))
        seg_j = jnp.transpose(seg_i)
        normed[slot * SLOT : (slot + 1) * SLOT, :SLOT] = jnp.where(seg_i == seg_j, 0.0, neg_large)
    g_w_box[...] = jnp.zeros_like(g_w_box)
    g_b_up[...] = jnp.zeros_like(g_b_up)
    g_vectors[...] = jnp.zeros_like(g_vectors)
    tok_copy.wait()

    if comm:
        extras.gather_column(0)
        blocks.gather_column(0)
        extras.gather_near(0)
        blocks.gather_near(0)
        blocks.gather_column(1)
        extras.gather_far(0)
        blocks.gather_far(0)
        blocks.gather_near(1)
        blocks.gather_column(2)
        blocks.gather_column(3)
        extras.gathered(0)
        table = small[...].astype(bf16)
        w_box[...] = table[:, :HD]
        share_qkv, share_up, share = widths(width, ff)
        for row, columns, share_of, depth, order, target in (
            (0, 3 * width, share_qkv, 256, quad_order, b_qkv),
            (1, ff, share_up, 256, None, b_up),
            (None, width, share, 128, None, vectors),
        ):
            @pl.loop(0, columns // BLOCK)
            def _(block):
                pick, owned, row_of = owner_tables(block * BLOCK, share_of, depth, order)
                spread = dot_nn(table[:, 128 : 128 + depth], pick)
                keep = owned if row is None else owned & (row_of == row)
                rows = jnp.sum(jnp.where(keep, spread, 0.0).reshape(16, 8, BLOCK), axis=0)
                target[:, aligned(block, BLOCK)] = rows if row is None else jnp.sum(rows, axis=0, keepdims=True)

    else:
        copy_in(held_in, held, 4).wait()
    w_box_t[...] = jnp.transpose(w_box[...].astype(f32)).astype(bf16)

    def gather_tick(step):
        if not comm:
            return
        for ahead, act_on in ((1, blocks.gather_near), (3, blocks.gather_column), (0, blocks.gather_far)):
            if isinstance(step, int):
                if step + ahead < STREAMS:
                    act_on(step + ahead)
            else:
                pl.when(step + ahead < STREAMS)(functools.partial(act_on, step + ahead))

    def need(stream):
        if comm:
            blocks.gathered(stream)

    b_out, gain_one, shift_one, b_down, gain_two, shift_two = [vectors[2 + i : 3 + i, :] for i in range(VECTORS)]
    lane = lax.broadcasted_iota(jnp.int32, (SLOT, PAIR), 1)

    def project(quad, slot):
        rows = tok[aligned(slot, SLOT), :]

        def columns(part):
            weight = held[aligned(quad, BLOCK), part * QUAD : (part + 1) * QUAD]
            shift = b_qkv[:, pl.ds(pl.multiple_of(quad * BLOCK + part * QUAD, QUAD), QUAD)]
            return (dot_nn(rows, weight) + shift).astype(bf16)

        q, k, v = columns(0), columns(1), columns(2)
        low[aligned(slot, SLOT), aligned(quad, QUAD)] = k
        flip[aligned(quad, QUAD), aligned(slot, SLOT)] = jnp.transpose(v.astype(f32)).astype(bf16)
        qt = jnp.transpose(q.astype(f32) * scale_factor).astype(bf16)
        kt = jnp.transpose(k.astype(f32) * scale_factor).astype(bf16)
        for part in range(2):
            here = slice(part * PAIR, (part + 1) * PAIR)
            q8t[slot, quad * 2 + part] = qt[here]
            k8t[slot, quad * 2 + part] = kt[here]
            v_row[slot, quad * 2 + part] = v[:, here]

    def e_copy(place, head, index, out):
        pair = (e_buf.at[place, head], e_hbm.at[index])
        return pltpu.make_async_copy(*(pair if out else pair[::-1]), e_sem.at[place, head])

    def attend(step):
        pair, slot = step // slots, step % slots
        cols = aligned(slot, SLOT)
        place = step % 2

        @pl.when(step >= 2)
        def _():
            for head in range(2):
                e_copy(place, head, 0, True).wait()

        sine_t, cosine_t = wave_t[:WAVE, cols], wave_t[WAVE:, cols]
        sc_t = (wave_t[:, cols] * scale_factor).astype(bf16)
        sc_r = wave_r[cols, :]
        cs_r = swap_lanes(sc_r)
        cc_r = jnp.where(lane < WAVE, cs_r, sc_r)
        ss_r = jnp.where(lane < WAVE, sc_r, -cs_r)
        cs_low = cs_r.astype(bf16)
        keys = low[cols, aligned(pair, PAIR)]
        heads_t = []
        for head in range(2):
            span = slice(head * HD, (head + 1) * HD)
            key_box = dot_nt(keys[:, span], w_box[...])
            k_side = (key_box * cc_r + swap_lanes(key_box) * ss_r).astype(bf16)
            q_t = q8t[slot, pair, span, :]
            query_box = dot_nn(w_box[...], q_t)
            first, second = query_box[:WAVE], query_box[WAVE:]
            q_side = jnp.concatenate(
                [first * sine_t + second * cosine_t, second * sine_t - first * cosine_t], axis=0
            ).astype(bf16)
            zero = jnp.zeros_like(q_t)
            q_pair = [q_t, zero] if head == 0 else [zero, q_t]
            k_full = jnp.concatenate([keys, cs_low, k_side], axis=1)
            q_full = jnp.concatenate(q_pair + [q_side, sc_t], axis=0)
            scores = dot_nn(k_full, q_full) + normed[cols, :SLOT]
            top = jnp.max(scores, axis=0, keepdims=True)
            exps = jnp.exp(scores - top)
            inverse = 1.0 / jnp.sum(exps, axis=0, keepdims=True)
            low_exps = exps.astype(bf16)
            e_buf[place, head] = low_exps
            e_copy(place, head, step * 2 + head, True).start()
            inv_total[step * 2 + head] = inverse
            at = pl.ds(pl.multiple_of(pair * PAIR + head * HD, HD), HD)
            heads_t.append(dot_nn(flip[at, cols], low_exps) * inverse)
        both = jnp.concatenate(heads_t, axis=0)
        ctx_t[aligned(pair, PAIR), cols] = both.astype(bf16)
        ctx[cols, aligned(pair, PAIR)] = jnp.transpose(both).astype(bf16)

    steps = slots * pairs
    quad_steps = 2 * slots

    @pl.loop(0, quads)
    def _(quad):
        need(quad)

        @pl.loop(0, slots)
        def _(slot):
            project(quad, slot)

        @pl.loop(0, quad_steps)
        def _(inner):
            step = quad * quad_steps + inner
            if comm:
                pl.when((step % 2 == 0) & (step > 0))(functools.partial(gather_tick, step // 2))
            attend(step)

    for place in range(2):
        for head in range(2):
            e_copy(place, head, 0, True).wait()

    def column_sum(value):
        return jnp.sum(value, axis=0, keepdims=True)

    need(3)
    gather_tick(6)

    @pl.loop(0, row_blocks)
    def _(block):
        rows = aligned(block, ROWS)
        token_rows = tok[rows, :].astype(f32)
        tok_t[:, rows] = jnp.transpose(token_rows).astype(bf16)
        pre = token_rows + dot_nn(ctx[rows, :], held[3 * BLOCK : 4 * BLOCK, :]) + b_out
        center = pre - row_mean(pre)
        invdev = lax.rsqrt(row_mean(center * center) + eps_norm)
        unit = center * invdev
        inv_one[rows, :] = jnp.broadcast_to(invdev, (ROWS, 128))
        normed[rows, :] = unit
        hidden = unit * gain_one + shift_one
        low[rows, :] = hidden.astype(bf16)
        flip[:, rows] = jnp.transpose(hidden).astype(bf16)

    @pl.loop(0, up_blocks)
    def _(block):
        gather_tick(7 + block)
        need(4 + block)

        @pl.loop(0, row_blocks)
        def _(row):
            rows = aligned(row, ROWS)
            at = pl.ds(pl.multiple_of(block * count + row * ROWS, ROWS), ROWS)
            weight = held[pl.ds(pl.multiple_of(up_at + block * BLOCK, BLOCK), BLOCK), :]
            up = dot_nn(low[rows, :], weight) + b_up[:, aligned(block, BLOCK)]
            cdf, pdf = gelu_parts(up)
            act[at, :] = (up * cdf).astype(bf16)
            slope[at, :] = (cdf + up * pdf).astype(bf16)

    gather_tick(11)
    for block in range(up_blocks):
        need(8 + block)
    cot_copy.wait()

    @pl.loop(0, row_blocks)
    def _(block):
        rows = aligned(block, ROWS)
        pre = normed[rows, :] * gain_one + shift_one + b_down
        for part in range(up_blocks):
            at = pl.ds(pl.multiple_of(part * count + block * ROWS, ROWS), ROWS)
            pre += dot_nn(act[at, :], held[down_at + part * BLOCK : down_at + (part + 1) * BLOCK, :])
        center = pre - row_mean(pre)
        invdev = lax.rsqrt(row_mean(center * center) + eps_norm)
        unit = center * invdev
        grad = cot[rows, :].astype(f32)
        cot[rows, :] = (unit * gain_two + shift_two).astype(bf16)
        scaled = grad * gain_two
        g_pre = invdev * (scaled - row_mean(scaled) - unit * row_mean(scaled * unit))
        total[rows, :] = g_pre
        low_pre = g_pre.astype(bf16)
        g_down[rows, :] = low_pre
        g_vectors[5:6, :] += column_sum(low_pre.astype(f32))
        g_vectors[6:7, :] += column_sum(grad * unit)
        g_vectors[7:8, :] += column_sum(grad)

    out_copy = pltpu.make_async_copy(cot, layer_out, io_sem.at[0])
    out_copy.start()
    if comm:
        for stream in range(STREAMS):
            blocks.gather_sent(stream)
        extras.gather_sent(0)

    def last(step):
        turn = step // 4
        return STREAMS - 1 - step + (14 - 6 * turn) * turn - 4

    def sum_start(step):
        if comm:
            blocks.sum_cores(last(step))

    def sum_tick(step, stages=(0, 1, 2, 3)):
        if not comm:
            return
        acts = (blocks.sum_far, blocks.sum_near, blocks.sum_column, blocks.sum_end)
        for behind in stages:
            at = step - behind
            if isinstance(at, int):
                if 0 <= at < STREAMS:
                    acts[behind](last(at))
            else:
                pl.when((at >= 0) & (at < STREAMS))(functools.partial(acts[behind], last(at)))

    def meet(sem):
        if comm:
            for peer, core in route.peers():
                pl.semaphore_signal(sem, inc=1, device_id=(peer, core), device_id_type=pl.DeviceIdType.MESH)
            pl.semaphore_wait(sem, 6)

    out_copy.wait()
    if comm:
        meet(mid_sem.at[0])

    @pl.loop(0, up_blocks)
    def _(index):
        block = up_blocks - 1 - index
        down_rows = pl.ds(pl.multiple_of(down_at + block * BLOCK, BLOCK), BLOCK)
        up_rows = pl.ds(pl.multiple_of(up_at + block * BLOCK, BLOCK), BLOCK)
        for row in range(2):
            rows = slice(row * (count // 2), (row + 1) * (count // 2))
            at = pl.ds(pl.multiple_of(block * count + row * (count // 2), count // 2), count // 2)
            g_act = dot_nt(g_down[rows, :], held[down_rows, :])
            g_up = (g_act * slope[at, :].astype(f32)).astype(bf16)
            slope[at, :] = g_up
            g_b_up[:, aligned(block, BLOCK)] += column_sum(g_up.astype(f32))
            total[rows, :] += dot_nt(g_up, held[up_rows, :])
        sum_tick(index - 1, (0,))
        sum_tick(index - 1, (1, 2, 3))
        g_up = slope[aligned(block, count), :]
        for part in range(2):
            at = pl.ds(pl.multiple_of(up_at + block * BLOCK + part * HALF, HALF), HALF)
            held[at, :] = dot_nn(flip[part * HALF : (part + 1) * HALF, :], g_up).astype(bf16)
        sum_start(index)
        for part in range(2):
            at = pl.ds(pl.multiple_of(down_at + block * BLOCK + part * HALF, HALF), HALF)
            grads = dot_tn(act[aligned(block, count), part * HALF : (part + 1) * HALF], g_down[...])
            held[at, :] = grads.astype(bf16)

    if comm:
        meet(mid_sem.at[1])
    sum_tick(3)
    for step in range(up_blocks):
        sum_start(up_blocks + step)

    @pl.loop(0, row_blocks)
    def _(block):
        rows = aligned(block, ROWS)
        grad, unit = total[rows, :], normed[rows, :]
        scaled = grad * gain_one
        g_pre = inv_one[rows, :1] * (scaled - row_mean(scaled) - unit * row_mean(scaled * unit))
        total[rows, :] = g_pre
        low_pre = g_pre.astype(bf16)
        g_down[rows, :] = low_pre
        g_vectors[2:3, :] += column_sum(low_pre.astype(f32))
        g_vectors[3:4, :] += column_sum(grad * unit)
        g_vectors[4:5, :] += column_sum(grad)
        g_ctx_t[:, rows] = dot_nt(held[3 * BLOCK : 4 * BLOCK, :], low_pre).astype(bf16)

    @pl.loop(0, BLOCK // ROWS)
    def _(part):
        at = pl.ds(pl.multiple_of(3 * BLOCK + part * ROWS, ROWS), ROWS)
        held[at, :] = dot_nn(ctx_t[aligned(part, ROWS), :], g_down[...]).astype(bf16)

    sum_start(8)
    sum_tick(4)

    def e_step(order):
        quad = quads - 1 - order // quad_steps
        return quad * quad_steps + order % quad_steps

    def fetch(order):
        for head in range(2):
            e_copy(order % 2, head, e_step(order) * 2 + head, False).start()

    fetch(0)
    ones = jnp.ones((16, count), bf16)

    def attend_back(order):
        step = e_step(order)
        pair, slot = step // slots, step % slots
        cols = aligned(slot, SLOT)
        place = order % 2

        @pl.when(order + 1 < steps)
        def _():
            fetch(order + 1)

        for head in range(2):
            e_copy(place, head, 0, False).wait()
        sine_t, cosine_t = wave_t[:WAVE, cols], wave_t[WAVE:, cols]
        sc_t = (wave_t[:, cols] * scale_factor).astype(bf16)
        cs_t = (jnp.concatenate([cosine_t, sine_t], axis=0) * scale_factor).astype(bf16)
        values = v_row[slot, pair]
        g_parts = [[], [], []]
        for head in range(2):
            span = slice(head * HD, (head + 1) * HD)
            at = pl.ds(pl.multiple_of(pair * PAIR + head * HD, HD), HD)
            g_rows = g_ctx_t[at, cols].astype(f32) * inv_total[step * 2 + head]
            row_dot = jnp.sum(g_rows * ctx_t[at, cols].astype(f32), axis=0, keepdims=True)
            g_low = g_rows.astype(bf16)
            zero = jnp.zeros_like(g_low)
            g_pair = jnp.concatenate([g_low, zero] if head == 0 else [zero, g_low], axis=0)
            low_exps = e_buf[place, head]
            g_probs = dot_nn(values, g_pair)
            g_scores = (low_exps.astype(f32) * (g_probs - row_dot)).astype(bf16)
            g_parts[2].append(dot_nt(g_low, low_exps))
            k_t, q_t = k8t[slot, pair, span, :], q8t[slot, pair, span, :]
            g_q = dot_nn(jnp.concatenate([k_t, cs_t], axis=0), g_scores)
            g_k = dot_nt(jnp.concatenate([q_t, sc_t], axis=0), g_scores)
            first, second = g_q[HD : HD + WAVE], g_q[HD + WAVE :]
            g_qbox = jnp.concatenate(
                [first * sine_t - second * cosine_t, first * cosine_t + second * sine_t], axis=0
            ).astype(bf16)
            first, second = g_k[HD : HD + WAVE], g_k[HD + WAVE :]
            g_kbox = jnp.concatenate(
                [first * cosine_t - second * sine_t, first * sine_t + second * cosine_t], axis=0
            ).astype(bf16)
            g_parts[0].append(g_q[:HD] + dot_nn(w_box_t[...], g_qbox))
            g_parts[1].append(g_k[:HD] + dot_nn(w_box_t[...], g_kbox))
            g_w_box[...] += dot_nt(g_qbox, q_t) + dot_nt(g_kbox, k_t)
        for part in range(3):
            at = pl.ds(pl.multiple_of(part * QUAD + pair % 2 * PAIR, PAIR), PAIR)
            flip[at, cols] = jnp.concatenate(g_parts[part], axis=0).astype(bf16)

    kept = slope.at[3 * count : 3 * count + BLOCK]
    kept_last = g_down.at[:BLOCK]

    @pl.loop(0, quads)
    def _(turn):
        quad = quads - 1 - turn

        @pl.loop(0, quad_steps)
        def _(inner):
            order = turn * quad_steps + inner
            if comm:
                pl.when(order % 2 == 1)(functools.partial(sum_tick, 5 + order // 2, (0,)))
                pl.when((order % 2 == 0) & (order > 0))(functools.partial(sum_tick, 4 + order // 2, (1, 2, 3)))
            attend_back(order)

        if comm:
            pl.when(turn == quads - 1)(functools.partial(sum_tick, 10, (1, 2, 3)))

        @pl.when(turn < quads - 1)
        def _():
            kept[...] = held[aligned(quad, BLOCK), :]

        @pl.when(turn == quads - 1)
        def _():
            kept_last[...] = held[aligned(quad, BLOCK), :]

        for part in range(2):
            at = pl.ds(pl.multiple_of(quad * BLOCK + part * HALF, HALF), HALF)
            held[at, :] = dot_nt(tok_t[part * HALF : (part + 1) * HALF, :], flip[...]).astype(bf16)
        sum_start(9 + turn)
        g_b_qkv[:, aligned(quad, BLOCK)] = dot_nt(ones, flip[...])[:1]

        @pl.when(turn == 0)
        def _():
            for block in range(row_blocks):
                rows = slice(block * ROWS, (block + 1) * ROWS)
                total[rows, :] += jnp.transpose(dot_nn(kept[...], flip[:, rows]))

        @pl.when(turn == 1)
        def _():
            for block in range(row_blocks):
                rows = slice(block * ROWS, (block + 1) * ROWS)
                slope[rows, :] = jnp.transpose(flip[:, rows].astype(f32)).astype(bf16)

    g_w_box[...] = g_w_box[...] * (1.0 / scale_factor)
    tok_out = []

    def token_grad(block):
        rows = slice(block * ROWS, (block + 1) * ROWS)
        last_part = jnp.transpose(dot_nn(kept_last[...], flip[:, rows]))
        total[rows, :] += last_part + dot_nt(slope[rows, :], kept[...])
        tok_out.append(pltpu.make_async_copy(total.at[rows], g_tok_out.at[rows], io_sem.at[4 + block]))
        tok_out[-1].start()

    if comm:
        g_small[...] = jnp.zeros_like(g_small)
        g_small[:, :HD] = g_w_box[...]
        share_qkv, share_up, share = widths(width, ff)
        for row, columns, share_of, order, source in (
            (0, 3 * width, share_qkv, quad_order, g_b_qkv),
            (1, ff, share_up, None, g_b_up),
            (None, width, share, None, g_vectors),
        ):
            @pl.loop(0, columns // BLOCK)
            def _(block):
                pick, owned, row_of = owner_tables(block * BLOCK, share_of, 256, order)
                keep = owned if row is None else owned & (row_of == row)
                wide = 1 if row is not None else 8
                full = source[:, aligned(block, BLOCK)].reshape(1, wide, BLOCK)
                spread = jnp.broadcast_to(full, (16, 8, BLOCK)).reshape(128, BLOCK)
                spread = jnp.where(keep, spread, 0.0)
                upper = spread.astype(bf16)
                g_small[:, 128:384] += dot_nt(upper, pick) + dot_nt((spread - upper.astype(f32)).astype(bf16), pick)

        sums.sum_cores(0)
        sum_tick(11, (1, 2, 3))
        sum_tick(11, (0,))
        sums.sum_far(0)
        sum_tick(12, (2, 3))
        token_grad(0)
        token_grad(1)
        sum_tick(12, (1,))
        sums.sum_near(0)
        token_grad(2)
        sum_tick(13, (3,))
        sum_tick(13, (2,))
        sums.sum_column(0)
        token_grad(3)
        sum_tick(14, (3,))
        sums.sum_end(0)
        for stream in range(STREAMS):
            blocks.summed(stream)
        sums.summed(0)
        blocks.results_in()
        sums.results_in()
        moves = [copy_in(final, final_out, 2), copy_in(small_final, small_out, 3)]
        for copy in moves:
            copy.start()
        for copy in moves:
            copy.wait()
    else:
        for block in range(row_blocks):
            token_grad(block)
        g_w_box_out[...] = g_w_box[...]
        g_b_qkv_out[...] = g_b_qkv[...]
        g_b_up_out[...] = g_b_up[...]
        g_vectors_out[...] = g_vectors[...]
        out = copy_in(held, g_held, 2)
        out.start()
        out.wait()
    for copy in tok_out:
        copy.wait()


def shaped(shape, dtype):
    return jax.ShapeDtypeStruct(shape, dtype)


def in_vmem(count):
    return [pl.BlockSpec(memory_space=pltpu.VMEM)] * count


def in_hbm(count):
    return [pl.BlockSpec(memory_space=pl.ANY)] * count


def run_layer(comm, tokens, cotangent, coords, segs, big, little):
    count, width = tokens.shape
    ff = 4 * BLOCK
    slots, pairs = count // SLOT, HEADS // 2
    held_shape = (STREAMS * BLOCK, BLOCK)
    out_shape = [
        shaped((count, width), bf16),
        shaped((count, width), f32),
        shaped((slots * HEADS, SLOT, SLOT), bf16),
    ]
    out_specs = in_hbm(3)
    if comm:
        out_shape += [shaped((STREAMS * PIECE, BLOCK), f32), shaped((8, SMALL), f32)]
        out_specs += in_hbm(2)
    else:
        out_shape += [shaped(held_shape, bf16), shaped((2 * WAVE, HD), f32), shaped((1, 3 * width), f32)]
        out_shape += [shaped((1, ff), f32), shaped((8, width), f32)]
        out_specs += in_hbm(1) + in_vmem(4)
    vmem = pltpu.VMEM
    dma = pltpu.SemaphoreType.DMA
    scratch = [
        vmem(held_shape, bf16),
        vmem(held_shape, bf16),
        vmem((ff // BLOCK * count, BLOCK), bf16),
        vmem((slots, pairs, PAIR, SLOT), bf16),
        vmem((slots, pairs, PAIR, SLOT), bf16),
        vmem((slots, pairs, SLOT, PAIR), bf16),
        vmem((width, count), bf16),
        vmem((2 * WAVE, count), f32),
        vmem((count, 2 * WAVE), f32),
        vmem((2, 2, SLOT, SLOT), bf16),
        vmem((count, width), f32),
        vmem((count, width), f32),
        vmem((width, count), bf16),
        vmem((count, width), bf16),
        vmem((width, count), bf16),
        vmem((width, count), bf16),
        vmem((count, 128), f32),
        vmem((slots * HEADS, 1, SLOT), f32),
        vmem((2 * WAVE, HD), bf16),
        vmem((HD, 2 * WAVE), bf16),
        vmem((1, 3 * width), f32),
        vmem((1, ff), f32),
        vmem((8, width), f32),
        vmem((2 * WAVE, HD), f32),
        vmem((1, 3 * width), f32),
        vmem((1, ff), f32),
        vmem((8, width), f32),
        dma((2, 2)),
        dma((32,)),
        vmem(coords.shape, jnp.int32),
        vmem(segs.shape, jnp.int32),
    ]
    if comm:
        scratch += [
            vmem((STREAMS * PIECE, BLOCK), f32),
            vmem((128, SMALL), f32),
            vmem((256, SMALL // 2), f32),
            vmem((128, SMALL), f32),
            vmem((8, SMALL), f32),
            pltpu.SemaphoreType.REGULAR((2,)),
            *[vmem(value.shape, f32) for value in little],
            dma((STREAMS, 4)), dma((STREAMS, 2)), dma((STREAMS, 4)), dma((STREAMS,)), dma((2,)),
            dma((1, 4)), dma((1, 2)), dma((1, 4)), dma((1,)),
            dma((2,)),
        ]
        extra = dict(collective_id=0, has_side_effects=True)
    else:
        extra = {}
    return pl.pallas_call(
        functools.partial(layer_kernel, comm),
        out_shape=out_shape,
        in_specs=in_hbm(4 + len(big)) + (in_hbm if comm else in_vmem)(len(little)),
        out_specs=out_specs,
        scratch_shapes=scratch,
        compiler_params=pltpu.CompilerParams(vmem_limit_bytes=vmem_limit, **extra),
        name="layer",
    )(tokens, cotangent, coords, segs, *big, *little)


def finish_kernel(*refs):
    layer_in, tok_in, blocks_in, small_in = refs[:4]
    layer_out, tok_out, p_qkv, p_out, p_up, p_down = refs[4:10]
    small_out = refs[10:19]
    layer, tok, blocks, small = refs[19:23]
    small_rows = refs[23:32]
    load_sem, store_sem = refs[32:]
    width = layer_in.shape[1]
    loads, stores = [], []
    parts = 4
    rows = layer_in.shape[0] // parts
    small_load = pltpu.make_async_copy(small_in, small, load_sem.at[0])
    loads.append((pltpu.make_async_copy(blocks_in, blocks, load_sem.at[1]), []))
    for quad in range(width // QUAD):
        for part in range(3):
            loads[0][1].append((
                blocks.at[quad * PIECE : (quad + 1) * PIECE, part * QUAD : (part + 1) * QUAD],
                p_qkv.at[:, part * width + quad * QUAD : part * width + (quad + 1) * QUAD],
            ))
    loads[0][1].append((blocks.at[3 * PIECE : 4 * PIECE], p_out))
    for block in range(4):
        loads[0][1].append((
            blocks.at[(4 + block) * PIECE : (5 + block) * PIECE], p_up.at[:, block * BLOCK : (block + 1) * BLOCK]
        ))
    loads[0][1].append((blocks.at[8 * PIECE : 12 * PIECE], p_down))
    for source, held, target in ((tok_in, tok, tok_out), (layer_in, layer, layer_out)):
        for part in range(parts):
            at = slice(part * rows, (part + 1) * rows)
            copy = pltpu.make_async_copy(source.at[at], held.at[at], load_sem.at[1 + len(loads)])
            loads.append((copy, [(held.at[at], target.at[at])]))
    small_load.start()
    for copy, _ in loads:
        copy.start()

    def store(source, target):
        stores.append(pltpu.make_async_copy(source, target, store_sem.at[len(stores)]))
        stores[-1].start()

    small_load.wait()
    for row in range(8):
        small_rows[row][...] = small[row : row + 1, 128 : 128 + small_rows[row].shape[1]]
    small_rows[8][...] = small[:, :HD]
    for source, target in zip(small_rows, small_out):
        store(source, target)
    for copy, moves in loads:
        copy.wait()
        for source, target in moves:
            store(source, target)
    for copy in stores:
        copy.wait()


def run_finish(layer_out, g_tok, blocks, small, big, little):
    shapes = [shaped(layer_out.shape, bf16), shaped(g_tok.shape, f32)]
    shapes += [shaped(w.shape, f32) for w in big + little]
    dma = pltpu.SemaphoreType.DMA
    return pl.pallas_call(
        finish_kernel,
        out_shape=shapes,
        in_specs=in_hbm(4),
        out_specs=in_hbm(len(shapes)),
        scratch_shapes=[
            pltpu.VMEM(layer_out.shape, bf16), pltpu.VMEM(g_tok.shape, f32), pltpu.VMEM(blocks.shape, f32),
            pltpu.VMEM(small.shape, f32), *[pltpu.VMEM(v.shape, f32) for v in little], dma((16,)), dma((40,)),
        ],
        compiler_params=pltpu.CompilerParams(vmem_limit_bytes=vmem_limit),
        name="finish",
    )(layer_out, g_tok, blocks, small)


def to_blocks(w_qkv, w_out, w_up, w_down):
    width = w_out.shape[1]
    qkv = w_qkv.reshape(width, 3, width // QUAD, QUAD).transpose(2, 0, 1, 3).reshape(-1, BLOCK)
    up = w_up.reshape(width, -1, BLOCK).transpose(1, 0, 2).reshape(-1, BLOCK)
    return jnp.concatenate([qkv, w_out, up, w_down], axis=0)


def from_blocks(held, width):
    qkv = held[: 3 * BLOCK].reshape(width // QUAD, width, 3, QUAD).transpose(1, 2, 0, 3).reshape(width, -1)
    up = held[4 * BLOCK : 8 * BLOCK].reshape(-1, width, BLOCK).transpose(1, 0, 2).reshape(width, -1)
    return qkv, held[3 * BLOCK : 4 * BLOCK], up, held[8 * BLOCK :]


def per_device(
    mesh_shape, tokens, cotangent, segments, box_coords, w_qkv, b_qkv, w_box, w_out, b_out, gain_one, shift_one,
    w_up, b_up, w_down, b_down, gain_two, shift_two,
):
    count, width = tokens.shape
    segs = segments.reshape(1, -1)
    vectors = [b_qkv, b_up, b_out, gain_one, shift_one, b_down, gain_two, shift_two]
    if mesh_shape == (16, 2):
        little = [v.reshape(1, -1) for v in vectors] + [w_box]
        big = [w_qkv, w_out, w_up, w_down]
        layer_out, g_tok, _, blocks, small = run_layer(True, tokens, cotangent, box_coords, segs, big, little)
        layer_out, g_tok, p_wq, p_wo, p_wu, p_wd, *rest = run_finish(layer_out, g_tok, blocks, small, big, little)
        p_bq, p_bu, p_bo, p_g1, p_s1, p_bd, p_g2, p_s2 = [v.reshape(-1) for v in rest[:8]]
        p_wb = rest[8]
    else:
        low = lambda value: value.astype(bf16)
        gather = lambda value: lax.all_gather(low(value), "fsdp", axis=0, tiled=True)
        held = to_blocks(gather(w_qkv), gather(w_out), gather(w_up), gather(w_down))
        wb, bq, bu, *six = [gather(v) for v in [w_box] + vectors]
        order = quad_order(jnp.arange(3 * width))
        rows = jnp.stack([jnp.zeros((width,), bf16)] * 2 + six).astype(f32)
        layer_out, g_tok, _, g_held, g_wb, g_bq, g_bu, g_six = run_layer(
            False, tokens, cotangent, box_coords, segs, [held],
            [wb, bq[order].astype(f32).reshape(1, -1), bu.astype(f32).reshape(1, -1), rows],
        )

        def scatter(grad):
            part = lax.psum_scatter(grad, "fsdp", scatter_dimension=0, tiled=True)
            return lax.psum(part, "rep").astype(f32)

        p_wq, p_wo, p_wu, p_wd = [scatter(g) for g in from_blocks(g_held, width)]
        g_bq = jnp.zeros((3 * width,), f32).at[order].set(g_bq[0])
        p_wb, p_bq, p_bu = scatter(g_wb), scatter(g_bq), scatter(g_bu[0])
        p_bo, p_g1, p_s1, p_bd, p_g2, p_s2 = [scatter(g_six[2 + i]) for i in range(VECTORS)]
    return (
        layer_out, g_tok, p_wq, p_bq, p_wb, p_wo, p_bo, p_g1, p_s1,
        p_wu, p_bu, p_wd, p_bd, p_g2, p_s2,
    )


def solution(mesh):
    tokens = P(("fsdp", "rep"), None)
    matrix, vector = P("fsdp", None), P("fsdp")
    kinds = [matrix, vector, matrix, matrix, vector, vector, vector, matrix, vector, matrix, vector, vector, vector]
    return jax.shard_map(
        functools.partial(per_device, (mesh.shape["fsdp"], mesh.shape["rep"])),
        mesh=mesh,
        in_specs=(tokens, tokens, P(("fsdp", "rep")), P(None, ("fsdp", "rep")), *kinds),
        out_specs=(tokens, tokens, *kinds),
        check_vma=False,
    )
```

```python
import functools
import math

import jax
import jax.numpy as jnp
from jax import lax
from jax.experimental import pallas as pl
from jax.experimental.pallas import tpu as pltpu
from jax.sharding import PartitionSpec as P

HEADS = 12
HD = 64
FREQ = 16
SLOT = 512
WAVE = 4 * FREQ
PAIR = 2 * HD
QUAD = 4 * HD

f32 = jnp.float32
bf16 = jnp.bfloat16
neg_large = -1e30
eps_norm = 1e-12
scale_factor = 1.0 / math.sqrt(HD)
vmem_limit = 67_000_000


def dot_nn(left, right):
    return lax.dot_general(left, right, (((1,), (0,)), ((), ())), preferred_element_type=f32)


def dot_nt(left, right):
    return lax.dot_general(left, right, (((1,), (1,)), ((), ())), preferred_element_type=f32)


def dot_tn(left, right):
    return lax.dot_general(left, right, (((0,), (0,)), ((), ())), preferred_element_type=f32)


def aligned(index, size):
    return pl.ds(pl.multiple_of(index * size, size), size)


def wave_rows(coords):
    count = coords.shape[1]
    spread = [jnp.broadcast_to(coords[c : c + 1, :].astype(f32), (FREQ, count)) for c in range(4)]
    scaled = jnp.concatenate(spread + spread, axis=0) * (100.0 / 1024.0)
    rows = lax.broadcasted_iota(jnp.int32, scaled.shape, 0)
    frequency = jnp.exp(-math.log(10000.0) * (rows & (FREQ - 1)).astype(f32) / FREQ)
    angle = scaled * frequency
    turns = jnp.floor(angle * (2.0 / math.pi) + 0.5)
    rest = ((angle - turns * 1.5703125) - turns * 4.837512969970703125e-4) - turns * 7.549789954891e-8
    square = rest * rest
    sine = rest + rest * square * (
        -1.6666654611e-1 + square * (8.3321608736e-3 + square * -1.9515295891e-4)
    )
    cosine = 1.0 - 0.5 * square + square * square * (
        4.166664568298827e-2 + square * (-1.388731625493765e-3 + square * 2.443315711809948e-5)
    )
    quadrant = turns.astype(jnp.int32) + jnp.where(rows >= WAVE, 1, 0)
    value = jnp.where((quadrant & 1) == 1, cosine, sine)
    value = jnp.where((quadrant & 2) == 2, -value, value)
    return value.astype(bf16).astype(f32)


def swap_lanes(value):
    return pltpu.roll(value, WAVE, 1)


def gelu_parts(value):
    t = 1.0 / (1.0 + (0.3275911 * math.sqrt(0.5)) * jnp.abs(value))
    bell = jnp.exp2(value * value * (-0.5 * math.log2(math.e)))
    half_tail = bell * t * (
        0.127414796 + t * (-0.142248368 + t * (0.7107068705 + t * (-0.7265760135 + t * 0.5307027145)))
    )
    return jnp.where(value >= 0, 1.0 - half_tail, half_tail), bell * (1.0 / math.sqrt(2.0 * math.pi))


def row_mean(value):
    return jnp.mean(value, axis=-1, keepdims=True)


ROWS = 256
BLOCK = 768
PIECE = 48
HALF = BLOCK // 2
SMALL = 512
STREAMS = 12
VECTORS = 6


def widths(width, ff):
    return 3 * width // 16, ff // 16, width // 16


class Route:
    def __init__(self):
        chip = lax.axis_index("fsdp")
        self.core = lax.axis_index("rep")
        self.level, self.me = chip // 4, chip % 4
        near_step, far_step = 1 + self.core, 2 - self.core
        near_move = near_step * (1 - 2 * ((self.me // near_step) % 2))
        far_move = far_step * (1 - 2 * ((self.me // far_step) % 2))
        self.near = self.me + near_move
        self.far = self.me + far_move
        self.across = self.me + near_move + far_move

    def chip(self, level, place):
        return level * 4 + place

    def levels(self):
        return [(self.level + k) % 4 for k in range(1, 4)]

    def peers(self):
        chips = [self.chip(level, self.me) for level in self.levels()]
        chips += [self.chip(self.level, self.near), self.chip(self.level, self.far)]
        return [(chip, self.core) for chip in chips] + [(self.chip(self.level, self.me), 1 - self.core)]


def remote(source, target, send, recv, chip, core):
    return pltpu.make_async_remote_copy(
        src_ref=source, dst_ref=target, send_sem=send, recv_sem=recv,
        device_id=(chip, core), device_id_type=pl.DeviceIdType.MESH,
    )


def half_columns(half, size):
    return pl.ds(pl.multiple_of(half * size, size), size)


class Streams:
    def __init__(self, held, stage, final, sems):
        self.held = held
        self.upper = held.at[: 8 * BLOCK].reshape(8, 4, 4, PIECE, BLOCK)
        self.lower = held.at[8 * BLOCK :].reshape(4, 4, 4, PIECE, BLOCK)
        self.stage = stage.reshape(STREAMS, 4, 4, PIECE, BLOCK)
        self.final = final
        self.gather_recv, self.gather_send, self.sum_recv, self.sum_send, self.final_sem = sems

    def on(self, stream, act):
        if isinstance(stream, int):
            act(self.upper.at[stream] if stream < 8 else self.lower.at[:, :, stream - 8])
        else:
            pl.when(stream < 8)(lambda: act(self.upper.at[stream]))
            pl.when(stream >= 8)(lambda: act(self.lower.at[:, :, stream - 8]))

    def half(self, half):
        return half_columns(half, HALF)

    def several(self, pieces):
        return self.held.at[: PIECE * pieces, :HALF]

    def landing(self, stream, kind):
        block = self.stage.at[(stream + 8) % STREAMS]
        if kind == 0:
            return block.at[:, :, :, :HALF]
        return block.at[(0, 0, 2, 3)[kind] : (0, 2, 3, 4)[kind], :, :, HALF:]

    def result(self, stream, half):
        return self.final.at[pl.ds(pl.multiple_of(stream * PIECE, 16), PIECE), self.half(half)]

    def results(self):
        return self.final.at[:, :HALF]


class Vectors:
    def __init__(self, held, stage, final, sems):
        self.held, self.flat, self.final = held, stage, final
        self.shards = held.reshape(4, 4, 8, SMALL)
        self.stage = stage.reshape(8, 4, 8, SMALL // 2)
        self.gather_recv, self.gather_send, self.sum_recv, self.sum_send, self.final_sem = sems

    def on(self, stream, act):
        act(self.shards)

    def half(self, half):
        return half_columns(half, SMALL // 2)

    def several(self, pieces):
        if pieces <= 16:
            return self.held.at[: 8 * pieces, : SMALL // 2]
        return self.flat.at[: 8 * pieces, :]

    def landing(self, stream, kind):
        return self.stage.at[(0, 4, 6, 7)[kind] : (4, 6, 7, 8)[kind]]

    def result(self, stream, half):
        return self.final.at[:, self.half(half)]

    def results(self):
        return self.final.at[:, : SMALL // 2]


def drain(view, sem):
    pltpu.make_async_copy(view, view, sem).wait()


class Exchange:
    def __init__(self, route, parts):
        self.route, self.parts = route, parts

    def send(self, source, target, send, recv, level, place, core):
        remote(source, target, send, recv, self.route.chip(level, place), core).start()


    def share(self, stream, view, place, kind):
        p, r = self.parts, self.route
        self.send(
            view, view, p.gather_send.at[stream, 0], p.gather_recv.at[stream, kind], r.level, place, r.core
        )

    def hand_over(self, stream, view):
        p, r = self.parts, self.route
        self.send(
            view, view, p.gather_send.at[stream, 1], p.gather_recv.at[stream, 3], r.level, r.me, 1 - r.core
        )

    def gather_own(self, stream):
        p, r = self.parts, self.route

        def act(shards):
            view = shards.at[r.level, r.me, :, p.half(r.core)]
            for level in r.levels():
                self.send(
                    view, view, p.gather_send.at[stream, 0], p.gather_recv.at[stream, 0], level, r.me, r.core
                )

        p.on(stream, act)

    def gather_column(self, stream):
        p, r = self.parts, self.route
        drain(p.several(3), p.gather_recv.at[stream, 0])

        def act(shards):
            view = shards.at[:, r.me, :, p.half(r.core)]
            self.share(stream, view, r.near, 1)
            self.share(stream, view, r.far, 2)
            for level in r.levels():
                self.hand_over(stream, shards.at[level, r.me, :, p.half(r.core)])

        p.on(stream, act)

    def gather_near(self, stream):
        p, r = self.parts, self.route
        drain(p.several(4), p.gather_recv.at[stream, 1])

        def act(shards):
            view = shards.at[:, r.near, :, p.half(r.core)]
            self.share(stream, view, r.far, 2)
            self.hand_over(stream, view)

        p.on(stream, act)

    def gather_far(self, stream):
        p, r = self.parts, self.route
        drain(p.several(8), p.gather_recv.at[stream, 2])

        def act(shards):
            for place in (r.far, r.across):
                self.hand_over(stream, shards.at[:, place, :, p.half(r.core)])

        p.on(stream, act)

    def gathered(self, stream):
        p = self.parts
        drain(p.several(15), p.gather_recv.at[stream, 3])

    def gather_sent(self, stream):
        p = self.parts
        drain(p.several(15), p.gather_send.at[stream, 0])
        drain(p.several(15), p.gather_send.at[stream, 1])


    def pass_on(self, stream, view, landing, kind, level, place):
        p, r = self.parts, self.route
        self.send(view, landing, p.sum_send.at[stream], p.sum_recv.at[stream, kind], level, place, r.core)

    def sum_cores(self, stream):
        p, r = self.parts, self.route

        def act(shards):
            self.send(
                shards.at[:, :, :, p.half(1 - r.core)], p.landing(stream, 0),
                p.sum_send.at[stream], p.sum_recv.at[stream, 0], r.level, r.me, 1 - r.core,
            )

        p.on(stream, act)

    def sum_far(self, stream):
        p, r = self.parts, self.route
        drain(p.several(16), p.sum_recv.at[stream, 0])
        landed, target = p.landing(stream, 0), p.landing(stream, 1)

        def act(shards):
            def add(place):
                view = shards.at[:, place, :, p.half(r.core)]
                view[...] += landed[:, place]
                return view

            for index, place in enumerate((r.far, r.across)):
                self.pass_on(stream, add(place), target.at[index], 1, r.level, r.far)
            for place in (r.me, r.near):
                add(place)

        p.on(stream, act)

    def sum_near(self, stream):
        p, r = self.parts, self.route
        drain(p.several(8), p.sum_recv.at[stream, 1])
        landed, target = p.landing(stream, 1), p.landing(stream, 2)

        def act(shards):
            view = shards.at[:, r.near, :, p.half(r.core)]
            view[...] += landed[1]
            self.pass_on(stream, view, target.at[0], 2, r.level, r.near)
            view = shards.at[:, r.me, :, p.half(r.core)]
            view[...] += landed[0]

        p.on(stream, act)

    def sum_column(self, stream):
        p, r = self.parts, self.route
        drain(p.several(4), p.sum_recv.at[stream, 2])
        landed, target = p.landing(stream, 2), p.landing(stream, 3)

        def act(shards):
            view = shards.at[:, r.me, :, p.half(r.core)]
            view[...] += landed[0]
            for index, level in enumerate(r.levels()):
                self.pass_on(
                    stream, shards.at[level, r.me, :, p.half(r.core)], target.at[0, index], 3, level, r.me
                )

        p.on(stream, act)

    def sum_end(self, stream):
        p, r = self.parts, self.route
        drain(p.several(3), p.sum_recv.at[stream, 3])
        landed = p.landing(stream, 3)
        view = p.result(stream, r.core)

        def act(shards):
            total = shards[r.level, r.me, :, p.half(r.core)].astype(f32)
            for index in range(3):
                total += landed[0, index].astype(f32)
            view[...] = total

        p.on(stream, act)
        self.send(view, view, p.final_sem.at[0], p.final_sem.at[1], r.level, r.me, 1 - r.core)

    def summed(self, stream):
        p = self.parts
        drain(p.several(31), p.sum_send.at[stream])

    def results_in(self):
        p = self.parts
        drain(p.results(), p.final_sem.at[0])
        drain(p.results(), p.final_sem.at[1])


def owner_tables(start, share, depth, order=None):
    col = lax.broadcasted_iota(jnp.int32, (1, BLOCK), 1) + start
    source = col if order is None else order(col)
    owner, entry = source // share, source % share
    pick = (entry == lax.broadcasted_iota(jnp.int32, (depth, BLOCK), 0)).astype(bf16)
    row = lax.broadcasted_iota(jnp.int32, (128, BLOCK), 0)
    return pick, owner == (row >> 3), row & 7


def quad_order(col):
    return (col % BLOCK) // QUAD * BLOCK + col // BLOCK * QUAD + col % QUAD


def layer_kernel(comm, *refs):
    refs = list(refs)

    def take(count):
        taken, refs[:] = refs[:count], refs[count:]
        return taken

    tok_in, cot_in, coords_in, segs_in = take(4)
    if comm:
        w_qkv_in, w_out_in, w_up_in, w_down_in = take(4)
        small_in = take(9)
    else:
        held_in, w_box_in, b_qkv_in, b_up_in, vectors_in = take(5)
    layer_out, g_tok_out, e_hbm = take(3)
    if comm:
        final_out, small_out = take(2)
    else:
        g_held, g_w_box_out, g_b_qkv_out, g_b_up_out, g_vectors_out = take(5)
    (held, stage, slope, q8t, k8t, v_row, ctx_t, wave_t, wave_r, e_buf, normed, total, flip, g_down, tok_t, g_ctx_t,
     inv_one, inv_total, w_box, w_box_t, b_qkv, b_up, vectors, g_w_box, g_b_qkv, g_b_up, g_vectors, e_sem, io_sem, coords, segs, w_pair, w_pair_t) = take(33)
    if comm:
        final, small, small_stage, g_small, small_final, mid_sem = take(6)
        small_held = take(9)
        block_sems, small_sems, small_final_sems = take(5), take(4), take(1)

    count, width = tok_t.shape[1], tok_t.shape[0]
    ff = slope.shape[0] // count * BLOCK
    slots, pairs = count // SLOT, HEADS // 2
    row_blocks = count // ROWS
    up_blocks = ff // BLOCK
    quads = pairs // 2
    ctx, low, cot, tok = [stage.at[part * count : (part + 1) * count] for part in range(4)]
    act = stage.at[STREAMS * BLOCK - up_blocks * count :]
    up_at, down_at = 4 * BLOCK, 8 * BLOCK

    def copy_in(source, target, index=0):
        return pltpu.make_async_copy(source, target, io_sem.at[index])

    tok_copy = copy_in(tok_in, tok, 0)
    cot_copy = copy_in(cot_in, cot, 1)
    coord_copy = copy_in(coords_in, coords, 2)
    seg_copy = copy_in(segs_in, segs, 3)

    if comm:
        route = Route()
        chip = route.chip(route.level, route.me)
        blocks = Exchange(route, Streams(held, stage, final, block_sems))
        extras = Exchange(route, Vectors(small, small_stage, small_final, [*small_sems, *small_final_sems]))
        sums = Exchange(route, Vectors(g_small, small_stage, small_final, [*small_sems, *small_final_sems]))
        barrier = pltpu.get_barrier_semaphore()
        for peer, core in route.peers():
            pl.semaphore_signal(barrier, inc=1, device_id=(peer, core), device_id_type=pl.DeviceIdType.MESH)
        moves = []
        for quad in range(quads):
            for part in range(3):
                moves.append((
                    w_qkv_in.at[:, part * width + quad * QUAD : part * width + (quad + 1) * QUAD],
                    total.at[quad * PIECE : (quad + 1) * PIECE, part * QUAD : (part + 1) * QUAD],
                ))
        moves.append((w_out_in, total.at[3 * PIECE : 4 * PIECE]))
        for block in range(up_blocks):
            moves.append((
                w_up_in.at[:, block * BLOCK : (block + 1) * BLOCK],
                total.at[(4 + block) * PIECE : (5 + block) * PIECE],
            ))
        moves.append((w_down_in, total.at[8 * PIECE : 12 * PIECE]))
        moves += list(zip(small_in, small_held))
        moves = [copy_in(source, target, 4 + index) for index, (source, target) in enumerate(moves)]
        first = 3 * quads
        for copy in moves[:first] + moves[first + 1 + up_blocks + 1 :] + moves[first : first + 1 + up_blocks + 1]:
            copy.start()
        for copy in (coord_copy, seg_copy, tok_copy, cot_copy):
            copy.start()

        def round_block(block):
            at = pl.ds(pl.multiple_of(block * BLOCK + PIECE * chip, 16), PIECE)
            held[at, :] = total[block * PIECE : (block + 1) * PIECE, :].astype(bf16)

        g_small[:8, :] = jnp.zeros((8, SMALL), f32)
        for copy in moves[:first]:
            copy.wait()
        for block in range(quads):
            round_block(block)
        for copy in moves[first + 1 + up_blocks + 1 :]:
            copy.wait()
        g_small[:8, :HD] = small_held[8][...].astype(bf16).astype(f32)
        for row in range(8):
            value = small_held[row][...].astype(bf16).astype(f32)
            g_small[row : row + 1, 128 : 128 + value.shape[1]] = value
        small[pl.ds(pl.multiple_of(chip * 8, 8), 8), :] = g_small[:8, :]
        pl.semaphore_wait(barrier, 6)
        extras.gather_own(0)
        for stream in range(quads):
            blocks.gather_own(stream)
        for copy in moves[first : first + 1 + up_blocks + 1]:
            copy.wait()
        for block in range(quads, STREAMS - up_blocks):
            round_block(block)
        at = pl.ds(pl.multiple_of(down_at + 4 * PIECE * chip, 16), 4 * PIECE)
        held[at, :] = total[8 * PIECE : 12 * PIECE, :].astype(bf16)
        for stream in range(quads, STREAMS):
            blocks.gather_own(stream)
    else:
        for copy in (coord_copy, seg_copy, tok_copy, cot_copy):
            copy.start()
        copy_in(held_in, held, 4).start()
        w_box[...] = w_box_in[...]
        b_qkv[...] = b_qkv_in[...]
        b_up[...] = b_up_in[...]
        vectors[...] = vectors_in[...]

    coord_copy.wait()
    seg_copy.wait()
    wave_t[...] = wave_rows(coords[...])
    wave_r[...] = jnp.transpose(wave_t[...])
    for slot in range(slots):
        seg_i = jnp.broadcast_to(segs[:, slot * SLOT : (slot + 1) * SLOT].astype(f32), (SLOT, SLOT))
        seg_j = jnp.transpose(seg_i)
        normed[slot * SLOT : (slot + 1) * SLOT, :SLOT] = jnp.where(seg_i == seg_j, 0.0, neg_large)
    g_w_box[...] = jnp.zeros_like(g_w_box)
    g_b_up[...] = jnp.zeros_like(g_b_up)
    g_vectors[...] = jnp.zeros_like(g_vectors)
    tok_copy.wait()

    if comm:
        extras.gather_column(0)
        blocks.gather_column(0)
        extras.gather_near(0)
        blocks.gather_near(0)
        blocks.gather_column(1)
        extras.gather_far(0)
        blocks.gather_far(0)
        blocks.gather_near(1)
        blocks.gather_column(2)
        blocks.gather_column(3)
        extras.gathered(0)
        table = small[...].astype(bf16)
        w_box[...] = table[:, :HD]
        share_qkv, share_up, share = widths(width, ff)
        for row, columns, share_of, depth, order, target in (
            (0, 3 * width, share_qkv, 256, quad_order, b_qkv),
            (1, ff, share_up, 256, None, b_up),
            (None, width, share, 128, None, vectors),
        ):
            @pl.loop(0, columns // BLOCK)
            def _(block):
                pick, owned, row_of = owner_tables(block * BLOCK, share_of, depth, order)
                spread = dot_nn(table[:, 128 : 128 + depth], pick)
                keep = owned if row is None else owned & (row_of == row)
                rows = jnp.sum(jnp.where(keep, spread, 0.0).reshape(16, 8, BLOCK), axis=0)
                target[:, aligned(block, BLOCK)] = rows if row is None else jnp.sum(rows, axis=0, keepdims=True)

    else:
        copy_in(held_in, held, 4).wait()
    w_box_t[...] = jnp.transpose(w_box[...].astype(f32)).astype(bf16)
    blank = jnp.zeros((2 * WAVE, HD), bf16)
    w_pair_t[: 2 * WAVE, :] = jnp.concatenate([w_box[...], blank], axis=1)
    w_pair_t[2 * WAVE :, :] = jnp.concatenate([blank, w_box[...]], axis=1)
    w_pair[...] = jnp.transpose(w_pair_t[...].astype(f32)).astype(bf16)

    def gather_tick(step):
        if not comm:
            return
        for ahead, act_on in ((1, blocks.gather_near), (3, blocks.gather_column), (0, blocks.gather_far)):
            if isinstance(step, int):
                if step + ahead < STREAMS:
                    act_on(step + ahead)
            else:
                pl.when(step + ahead < STREAMS)(functools.partial(act_on, step + ahead))

    def need(stream):
        if comm:
            blocks.gathered(stream)

    b_out, gain_one, shift_one, b_down, gain_two, shift_two = [vectors[2 + i : 3 + i, :] for i in range(VECTORS)]
    lane = lax.broadcasted_iota(jnp.int32, (SLOT, PAIR), 1)
    scores = total.reshape(2, SLOT, width)

    def project(quad, slot):
        rows = tok[aligned(slot, SLOT), :]

        def columns(part):
            weight = held[aligned(quad, BLOCK), part * QUAD : (part + 1) * QUAD]
            shift = b_qkv[:, pl.ds(pl.multiple_of(quad * BLOCK + part * QUAD, QUAD), QUAD)]
            return (dot_nn(rows, weight) + shift).astype(bf16)

        q, k, v = columns(0), columns(1), columns(2)
        low[aligned(slot, SLOT), aligned(quad, QUAD)] = k
        flip[aligned(quad, QUAD), aligned(slot, SLOT)] = jnp.transpose(v.astype(f32)).astype(bf16)
        qt = jnp.transpose(q.astype(f32) * scale_factor).astype(bf16)
        kt = jnp.transpose(k.astype(f32) * scale_factor).astype(bf16)
        for part in range(2):
            here = slice(part * PAIR, (part + 1) * PAIR)
            q8t[slot, quad * 2 + part] = qt[here]
            k8t[slot, quad * 2 + part] = kt[here]
            v_row[slot, quad * 2 + part] = v[:, here]

    def e_copy(place, head, index, out):
        pair = (e_buf.at[place, head], e_hbm.at[index])
        return pltpu.make_async_copy(*(pair if out else pair[::-1]), e_sem.at[place, head])

    def attend(step):
        pair, slot = step // slots, step % slots
        cols = aligned(slot, SLOT)
        place = step % 2

        @pl.when(step >= 2)
        def _():
            for head in range(2):
                e_copy(place, head, 0, True).wait()

        sine_t, cosine_t = wave_t[:WAVE, cols], wave_t[WAVE:, cols]
        sc_t = (wave_t[:, cols] * scale_factor).astype(bf16)
        sc_r = wave_r[cols, :]
        cs_r = swap_lanes(sc_r)
        cc_r = jnp.where(lane < WAVE, cs_r, sc_r)
        ss_r = jnp.where(lane < WAVE, sc_r, -cs_r)
        cs_low = cs_r.astype(bf16)
        keys = low[cols, aligned(pair, PAIR)]
        queries = q8t[slot, pair]
        key_box = dot_nn(keys, w_pair[...])
        query_box = dot_nn(w_pair_t[...], queries)
        low_exps, inverse, heads_t = [], [], []
        for head in range(2):
            here = slice(head * 2 * WAVE, (head + 1) * 2 * WAVE)
            side = key_box[:, here]
            k_side = (side * cc_r + swap_lanes(side) * ss_r).astype(bf16)
            first, second = query_box[here][:WAVE], query_box[here][WAVE:]
            q_side = jnp.concatenate(
                [first * sine_t + second * cosine_t, second * sine_t - first * cosine_t], axis=0
            ).astype(bf16)
            q_t = queries[head * HD : (head + 1) * HD]
            zero = jnp.zeros_like(q_t)
            q_pair = [q_t, zero] if head == 0 else [zero, q_t]
            k_full = jnp.concatenate([keys, cs_low, k_side], axis=1)
            q_full = jnp.concatenate(q_pair + [q_side, sc_t], axis=0)
            scores[head, :, :SLOT] = dot_nn(k_full, q_full) + normed[cols, :SLOT]
        for head in range(2):
            masked = scores[head, :, :SLOT]
            exps = jnp.exp(masked - jnp.max(masked, axis=0, keepdims=True))
            inverse.append(1.0 / jnp.sum(exps, axis=0, keepdims=True))
            low_exps.append(exps.astype(bf16))
            e_buf[place, head] = low_exps[head]
            e_copy(place, head, step * 2 + head, True).start()
            inv_total[step * 2 + head] = inverse[head]
        for head in range(2):
            at = pl.ds(pl.multiple_of(pair * PAIR + head * HD, HD), HD)
            heads_t.append(dot_nn(flip[at, cols], low_exps[head]) * inverse[head])
        both = jnp.concatenate(heads_t, axis=0)
        ctx_t[aligned(pair, PAIR), cols] = both.astype(bf16)
        ctx[cols, aligned(pair, PAIR)] = jnp.transpose(both).astype(bf16)

    steps = slots * pairs
    quad_steps = 2 * slots

    @pl.loop(0, quads)
    def _(quad):
        need(quad)

        @pl.loop(0, slots)
        def _(slot):
            project(quad, slot)

        @pl.loop(0, quad_steps)
        def _(inner):
            step = quad * quad_steps + inner
            if comm:
                pl.when((step % 2 == 0) & (step > 0))(functools.partial(gather_tick, step // 2))
            attend(step)

    for place in range(2):
        for head in range(2):
            e_copy(place, head, 0, True).wait()

    def column_sum(value):
        return jnp.sum(value, axis=0, keepdims=True)

    need(3)
    gather_tick(6)

    @pl.loop(0, row_blocks)
    def _(block):
        rows = aligned(block, ROWS)
        token_rows = tok[rows, :].astype(f32)
        tok_t[:, rows] = jnp.transpose(token_rows).astype(bf16)
        pre = token_rows + dot_nn(ctx[rows, :], held[3 * BLOCK : 4 * BLOCK, :]) + b_out
        center = pre - row_mean(pre)
        invdev = lax.rsqrt(row_mean(center * center) + eps_norm)
        unit = center * invdev
        inv_one[rows, :] = jnp.broadcast_to(invdev, (ROWS, 128))
        normed[rows, :] = unit
        hidden = unit * gain_one + shift_one
        low[rows, :] = hidden.astype(bf16)
        flip[:, rows] = jnp.transpose(hidden).astype(bf16)

    @pl.loop(0, up_blocks)
    def _(block):
        gather_tick(7 + block)
        need(4 + block)

        weight = held[pl.ds(pl.multiple_of(up_at + block * BLOCK, BLOCK), BLOCK), :]
        for row in range(row_blocks):
            rows = slice(row * ROWS, (row + 1) * ROWS)
            total[rows, :] = dot_nn(low[rows, :], weight) + b_up[:, aligned(block, BLOCK)]
        for row in range(row_blocks):
            at = pl.ds(pl.multiple_of(block * count + row * ROWS, ROWS), ROWS)
            up = total[row * ROWS : (row + 1) * ROWS, :]
            cdf, pdf = gelu_parts(up)
            act[at, :] = (up * cdf).astype(bf16)
            slope[at, :] = (cdf + up * pdf).astype(bf16)

    gather_tick(11)
    for block in range(up_blocks):
        need(8 + block)
    cot_copy.wait()

    @pl.loop(0, row_blocks)
    def _(block):
        rows = aligned(block, ROWS)
        pre = normed[rows, :] * gain_one + shift_one + b_down
        for part in range(up_blocks):
            at = pl.ds(pl.multiple_of(part * count + block * ROWS, ROWS), ROWS)
            pre += dot_nn(act[at, :], held[down_at + part * BLOCK : down_at + (part + 1) * BLOCK, :])
        center = pre - row_mean(pre)
        invdev = lax.rsqrt(row_mean(center * center) + eps_norm)
        unit = center * invdev
        grad = cot[rows, :].astype(f32)
        cot[rows, :] = (unit * gain_two + shift_two).astype(bf16)
        scaled = grad * gain_two
        g_pre = invdev * (scaled - row_mean(scaled) - unit * row_mean(scaled * unit))
        total[rows, :] = g_pre
        low_pre = g_pre.astype(bf16)
        g_down[rows, :] = low_pre
        g_vectors[5:6, :] += column_sum(low_pre.astype(f32))
        g_vectors[6:7, :] += column_sum(grad * unit)
        g_vectors[7:8, :] += column_sum(grad)

    out_copy = pltpu.make_async_copy(cot, layer_out, io_sem.at[0])
    out_copy.start()
    if comm:
        for stream in range(STREAMS):
            blocks.gather_sent(stream)
        extras.gather_sent(0)

    def last(step):
        turn = step // 4
        return STREAMS - 1 - step + (14 - 6 * turn) * turn - 4

    def sum_start(step):
        if comm:
            blocks.sum_cores(last(step))

    def sum_tick(step, stages=(0, 1, 2, 3)):
        if not comm:
            return
        acts = (blocks.sum_far, blocks.sum_near, blocks.sum_column, blocks.sum_end)
        for behind in stages:
            at = step - behind
            if isinstance(at, int):
                if 0 <= at < STREAMS:
                    acts[behind](last(at))
            else:
                pl.when((at >= 0) & (at < STREAMS))(functools.partial(acts[behind], last(at)))

    def meet(sem):
        if comm:
            for peer, core in route.peers():
                pl.semaphore_signal(sem, inc=1, device_id=(peer, core), device_id_type=pl.DeviceIdType.MESH)
            pl.semaphore_wait(sem, 6)

    out_copy.wait()
    if comm:
        meet(mid_sem.at[0])

    @pl.loop(0, up_blocks)
    def _(index):
        block = up_blocks - 1 - index
        down_rows = pl.ds(pl.multiple_of(down_at + block * BLOCK, BLOCK), BLOCK)
        up_rows = pl.ds(pl.multiple_of(up_at + block * BLOCK, BLOCK), BLOCK)
        for row in range(2):
            rows = slice(row * (count // 2), (row + 1) * (count // 2))
            at = pl.ds(pl.multiple_of(block * count + row * (count // 2), count // 2), count // 2)
            g_act = dot_nt(g_down[rows, :], held[down_rows, :])
            g_up = (g_act * slope[at, :].astype(f32)).astype(bf16)
            slope[at, :] = g_up
            g_b_up[:, aligned(block, BLOCK)] += column_sum(g_up.astype(f32))
            total[rows, :] += dot_nt(g_up, held[up_rows, :])
        sum_tick(index - 1, (0,))
        sum_tick(index - 1, (1, 2, 3))
        g_up = slope[aligned(block, count), :]
        for part in range(2):
            at = pl.ds(pl.multiple_of(up_at + block * BLOCK + part * HALF, HALF), HALF)
            held[at, :] = dot_nn(flip[part * HALF : (part + 1) * HALF, :], g_up).astype(bf16)
        sum_start(index)
        for part in range(2):
            at = pl.ds(pl.multiple_of(down_at + block * BLOCK + part * HALF, HALF), HALF)
            grads = dot_tn(act[aligned(block, count), part * HALF : (part + 1) * HALF], g_down[...])
            held[at, :] = grads.astype(bf16)

    if comm:
        meet(mid_sem.at[1])
    sum_tick(3)
    for step in range(up_blocks):
        sum_start(up_blocks + step)

    @pl.loop(0, row_blocks)
    def _(block):
        rows = aligned(block, ROWS)
        grad, unit = total[rows, :], normed[rows, :]
        scaled = grad * gain_one
        g_pre = inv_one[rows, :1] * (scaled - row_mean(scaled) - unit * row_mean(scaled * unit))
        total[rows, :] = g_pre
        low_pre = g_pre.astype(bf16)
        g_down[rows, :] = low_pre
        g_vectors[2:3, :] += column_sum(low_pre.astype(f32))
        g_vectors[3:4, :] += column_sum(grad * unit)
        g_vectors[4:5, :] += column_sum(grad)

    for part in range(2):
        rows = slice(part * (count // 2), (part + 1) * (count // 2))
        g_ctx_t[:, rows] = dot_nt(held[3 * BLOCK : 4 * BLOCK, :], g_down[rows, :]).astype(bf16)
    for part in range(2):
        at = slice(3 * BLOCK + part * HALF, 3 * BLOCK + (part + 1) * HALF)
        held[at, :] = dot_nn(ctx_t[part * HALF : (part + 1) * HALF, :], g_down[...]).astype(bf16)

    sum_start(8)
    sum_tick(4)

    def e_step(order):
        quad = quads - 1 - order // quad_steps
        return quad * quad_steps + order % quad_steps

    def fetch(order):
        for head in range(2):
            e_copy(order % 2, head, e_step(order) * 2 + head, False).start()

    fetch(0)
    ones = jnp.ones((16, count), bf16)

    def attend_back(order):
        step = e_step(order)
        pair, slot = step // slots, step % slots
        cols = aligned(slot, SLOT)
        place = order % 2

        @pl.when(order + 1 < steps)
        def _():
            fetch(order + 1)

        for head in range(2):
            e_copy(place, head, 0, False).wait()
        sine_t, cosine_t = wave_t[:WAVE, cols], wave_t[WAVE:, cols]
        sc_t = (wave_t[:, cols] * scale_factor).astype(bf16)
        cs_t = (jnp.concatenate([cosine_t, sine_t], axis=0) * scale_factor).astype(bf16)
        values = v_row[slot, pair]
        g_lows, row_dots, g_probs, g_scores, g_qs, g_ks = [], [], [], [], [], []
        g_parts = [[], [], []]
        spans = [slice(head * HD, (head + 1) * HD) for head in range(2)]
        for head in range(2):
            at = pl.ds(pl.multiple_of(pair * PAIR + head * HD, HD), HD)
            g_rows = g_ctx_t[at, cols].astype(f32) * inv_total[step * 2 + head]
            row_dots.append(jnp.sum(g_rows * ctx_t[at, cols].astype(f32), axis=0, keepdims=True))
            g_lows.append(g_rows.astype(bf16))
            zero = jnp.zeros_like(g_lows[head])
            g_pair = jnp.concatenate([g_lows[head], zero] if head == 0 else [zero, g_lows[head]], axis=0)
            g_probs.append(dot_nn(values, g_pair))
        for head in range(2):
            g_scores.append((e_buf[place, head].astype(f32) * (g_probs[head] - row_dots[head])).astype(bf16))
        for head in range(2):
            g_qs.append(dot_nn(jnp.concatenate([k8t[slot, pair, spans[head], :], cs_t], axis=0), g_scores[head]))
        for head in range(2):
            g_ks.append(dot_nt(jnp.concatenate([q8t[slot, pair, spans[head], :], sc_t], axis=0), g_scores[head]))
        for head in range(2):
            g_parts[2].append(dot_nt(g_lows[head], e_buf[place, head]))
        for head in range(2):
            k_t, q_t = k8t[slot, pair, spans[head], :], q8t[slot, pair, spans[head], :]
            g_q, g_k = g_qs[head], g_ks[head]
            first, second = g_q[HD : HD + WAVE], g_q[HD + WAVE :]
            g_qbox = jnp.concatenate(
                [first * sine_t - second * cosine_t, first * cosine_t + second * sine_t], axis=0
            ).astype(bf16)
            first, second = g_k[HD : HD + WAVE], g_k[HD + WAVE :]
            g_kbox = jnp.concatenate(
                [first * cosine_t - second * sine_t, first * sine_t + second * cosine_t], axis=0
            ).astype(bf16)
            g_parts[0].append(g_q[:HD] + dot_nn(w_box_t[...], g_qbox))
            g_parts[1].append(g_k[:HD] + dot_nn(w_box_t[...], g_kbox))
            g_w_box[...] += dot_nt(g_qbox, q_t) + dot_nt(g_kbox, k_t)
        for part in range(3):
            at = pl.ds(pl.multiple_of(part * QUAD + pair % 2 * PAIR, PAIR), PAIR)
            flip[at, cols] = jnp.concatenate(g_parts[part], axis=0).astype(bf16)

    kept = slope.at[3 * count : 3 * count + BLOCK]
    kept_last = g_down.at[:BLOCK]

    @pl.loop(0, quads)
    def _(turn):
        quad = quads - 1 - turn

        @pl.loop(0, quad_steps)
        def _(inner):
            order = turn * quad_steps + inner
            if comm:
                pl.when(order % 2 == 1)(functools.partial(sum_tick, 5 + order // 2, (0,)))
                pl.when((order % 2 == 0) & (order > 0))(functools.partial(sum_tick, 4 + order // 2, (1, 2, 3)))
            attend_back(order)

        if comm:
            pl.when(turn == quads - 1)(functools.partial(sum_tick, 10, (1, 2, 3)))

        @pl.when(turn < quads - 1)
        def _():
            kept[...] = held[aligned(quad, BLOCK), :]

        @pl.when(turn == quads - 1)
        def _():
            kept_last[...] = held[aligned(quad, BLOCK), :]

        for part in range(2):
            at = pl.ds(pl.multiple_of(quad * BLOCK + part * HALF, HALF), HALF)
            held[at, :] = dot_nt(tok_t[part * HALF : (part + 1) * HALF, :], flip[...]).astype(bf16)
        sum_start(9 + turn)
        g_b_qkv[:, aligned(quad, BLOCK)] = dot_nt(ones, flip[...])[:1]

        @pl.when(turn == 0)
        def _():
            for block in range(row_blocks):
                rows = slice(block * ROWS, (block + 1) * ROWS)
                total[rows, :] += jnp.transpose(dot_nn(kept[...], flip[:, rows]))

        @pl.when(turn == 1)
        def _():
            for block in range(row_blocks):
                rows = slice(block * ROWS, (block + 1) * ROWS)
                slope[rows, :] = jnp.transpose(flip[:, rows].astype(f32)).astype(bf16)

    g_w_box[...] = g_w_box[...] * (1.0 / scale_factor)
    tok_out = []

    def token_grad(block):
        rows = slice(block * ROWS, (block + 1) * ROWS)
        last_part = jnp.transpose(dot_nn(kept_last[...], flip[:, rows]))
        total[rows, :] += last_part + dot_nt(slope[rows, :], kept[...])
        tok_out.append(pltpu.make_async_copy(total.at[rows], g_tok_out.at[rows], io_sem.at[4 + block]))
        tok_out[-1].start()

    if comm:
        g_small[...] = jnp.zeros_like(g_small)
        g_small[:, :HD] = g_w_box[...]
        share_qkv, share_up, share = widths(width, ff)
        for row, columns, share_of, order, source in (
            (0, 3 * width, share_qkv, quad_order, g_b_qkv),
            (1, ff, share_up, None, g_b_up),
            (None, width, share, None, g_vectors),
        ):
            @pl.loop(0, columns // BLOCK)
            def _(block):
                pick, owned, row_of = owner_tables(block * BLOCK, share_of, 256, order)
                keep = owned if row is None else owned & (row_of == row)
                wide = 1 if row is not None else 8
                full = source[:, aligned(block, BLOCK)].reshape(1, wide, BLOCK)
                spread = jnp.broadcast_to(full, (16, 8, BLOCK)).reshape(128, BLOCK)
                spread = jnp.where(keep, spread, 0.0)
                upper = spread.astype(bf16)
                g_small[:, 128:384] += dot_nt(upper, pick) + dot_nt((spread - upper.astype(f32)).astype(bf16), pick)

        sums.sum_cores(0)
        sum_tick(11, (1, 2, 3))
        sum_tick(11, (0,))
        sums.sum_far(0)
        sum_tick(12, (2, 3))
        token_grad(0)
        token_grad(1)
        sum_tick(12, (1,))
        sums.sum_near(0)
        token_grad(2)
        sum_tick(13, (3,))
        sum_tick(13, (2,))
        sums.sum_column(0)
        token_grad(3)
        sum_tick(14, (3,))
        sums.sum_end(0)
        for stream in range(STREAMS):
            blocks.summed(stream)
        sums.summed(0)
        blocks.results_in()
        sums.results_in()
        moves = [copy_in(final, final_out, 2), copy_in(small_final, small_out, 3)]
        for copy in moves:
            copy.start()
        for copy in moves:
            copy.wait()
    else:
        for block in range(row_blocks):
            token_grad(block)
        g_w_box_out[...] = g_w_box[...]
        g_b_qkv_out[...] = g_b_qkv[...]
        g_b_up_out[...] = g_b_up[...]
        g_vectors_out[...] = g_vectors[...]
        out = copy_in(held, g_held, 2)
        out.start()
        out.wait()
    for copy in tok_out:
        copy.wait()


def shaped(shape, dtype):
    return jax.ShapeDtypeStruct(shape, dtype)


def in_vmem(count):
    return [pl.BlockSpec(memory_space=pltpu.VMEM)] * count


def in_hbm(count):
    return [pl.BlockSpec(memory_space=pl.ANY)] * count


def run_layer(comm, tokens, cotangent, coords, segs, big, little):
    count, width = tokens.shape
    ff = 4 * BLOCK
    slots, pairs = count // SLOT, HEADS // 2
    held_shape = (STREAMS * BLOCK, BLOCK)
    out_shape = [
        shaped((count, width), bf16),
        shaped((count, width), f32),
        shaped((slots * HEADS, SLOT, SLOT), bf16),
    ]
    out_specs = in_hbm(3)
    if comm:
        out_shape += [shaped((STREAMS * PIECE, BLOCK), f32), shaped((8, SMALL), f32)]
        out_specs += in_hbm(2)
    else:
        out_shape += [shaped(held_shape, bf16), shaped((2 * WAVE, HD), f32), shaped((1, 3 * width), f32)]
        out_shape += [shaped((1, ff), f32), shaped((8, width), f32)]
        out_specs += in_hbm(1) + in_vmem(4)
    vmem = pltpu.VMEM
    dma = pltpu.SemaphoreType.DMA
    scratch = [
        vmem(held_shape, bf16),
        vmem(held_shape, bf16),
        vmem((ff // BLOCK * count, BLOCK), bf16),
        vmem((slots, pairs, PAIR, SLOT), bf16),
        vmem((slots, pairs, PAIR, SLOT), bf16),
        vmem((slots, pairs, SLOT, PAIR), bf16),
        vmem((width, count), bf16),
        vmem((2 * WAVE, count), f32),
        vmem((count, 2 * WAVE), f32),
        vmem((2, 2, SLOT, SLOT), bf16),
        vmem((count, width), f32),
        vmem((count, width), f32),
        vmem((width, count), bf16),
        vmem((count, width), bf16),
        vmem((width, count), bf16),
        vmem((width, count), bf16),
        vmem((count, 128), f32),
        vmem((slots * HEADS, 1, SLOT), f32),
        vmem((2 * WAVE, HD), bf16),
        vmem((HD, 2 * WAVE), bf16),
        vmem((1, 3 * width), f32),
        vmem((1, ff), f32),
        vmem((8, width), f32),
        vmem((2 * WAVE, HD), f32),
        vmem((1, 3 * width), f32),
        vmem((1, ff), f32),
        vmem((8, width), f32),
        dma((2, 2)),
        dma((32,)),
        vmem(coords.shape, jnp.int32),
        vmem(segs.shape, jnp.int32),
        vmem((PAIR, 4 * WAVE), bf16),
        vmem((4 * WAVE, PAIR), bf16),
    ]
    if comm:
        scratch += [
            vmem((STREAMS * PIECE, BLOCK), f32),
            vmem((128, SMALL), f32),
            vmem((256, SMALL // 2), f32),
            vmem((128, SMALL), f32),
            vmem((8, SMALL), f32),
            pltpu.SemaphoreType.REGULAR((2,)),
            *[vmem(value.shape, f32) for value in little],
            dma((STREAMS, 4)), dma((STREAMS, 2)), dma((STREAMS, 4)), dma((STREAMS,)), dma((2,)),
            dma((1, 4)), dma((1, 2)), dma((1, 4)), dma((1,)),
            dma((2,)),
        ]
        extra = dict(collective_id=0, has_side_effects=True)
    else:
        extra = {}
    return pl.pallas_call(
        functools.partial(layer_kernel, comm),
        out_shape=out_shape,
        in_specs=in_hbm(4 + len(big)) + (in_hbm if comm else in_vmem)(len(little)),
        out_specs=out_specs,
        scratch_shapes=scratch,
        compiler_params=pltpu.CompilerParams(vmem_limit_bytes=vmem_limit, **extra),
        name="layer",
    )(tokens, cotangent, coords, segs, *big, *little)


def finish_kernel(*refs):
    layer_in, tok_in, blocks_in, small_in = refs[:4]
    layer_out, tok_out, p_qkv, p_out, p_up, p_down = refs[4:10]
    small_out = refs[10:19]
    layer, tok, blocks, small = refs[19:23]
    small_rows = refs[23:32]
    load_sem, store_sem = refs[32:]
    width = layer_in.shape[1]
    loads, stores = [], []
    parts = 4
    rows = layer_in.shape[0] // parts
    small_load = pltpu.make_async_copy(small_in, small, load_sem.at[0])
    loads.append((pltpu.make_async_copy(blocks_in, blocks, load_sem.at[1]), []))
    for quad in range(width // QUAD):
        for part in range(3):
            loads[0][1].append((
                blocks.at[quad * PIECE : (quad + 1) * PIECE, part * QUAD : (part + 1) * QUAD],
                p_qkv.at[:, part * width + quad * QUAD : part * width + (quad + 1) * QUAD],
            ))
    loads[0][1].append((blocks.at[3 * PIECE : 4 * PIECE], p_out))
    for block in range(4):
        loads[0][1].append((
            blocks.at[(4 + block) * PIECE : (5 + block) * PIECE], p_up.at[:, block * BLOCK : (block + 1) * BLOCK]
        ))
    loads[0][1].append((blocks.at[8 * PIECE : 12 * PIECE], p_down))
    for source, held, target in ((tok_in, tok, tok_out), (layer_in, layer, layer_out)):
        for part in range(parts):
            at = slice(part * rows, (part + 1) * rows)
            copy = pltpu.make_async_copy(source.at[at], held.at[at], load_sem.at[1 + len(loads)])
            loads.append((copy, [(held.at[at], target.at[at])]))
    small_load.start()
    for copy, _ in loads:
        copy.start()

    def store(source, target):
        stores.append(pltpu.make_async_copy(source, target, store_sem.at[len(stores)]))
        stores[-1].start()

    small_load.wait()
    for row in range(8):
        small_rows[row][...] = small[row : row + 1, 128 : 128 + small_rows[row].shape[1]]
    small_rows[8][...] = small[:, :HD]
    for source, target in zip(small_rows, small_out):
        store(source, target)
    for copy, moves in loads:
        copy.wait()
        for source, target in moves:
            store(source, target)
    for copy in stores:
        copy.wait()


def run_finish(layer_out, g_tok, blocks, small, big, little):
    shapes = [shaped(layer_out.shape, bf16), shaped(g_tok.shape, f32)]
    shapes += [shaped(w.shape, f32) for w in big + little]
    dma = pltpu.SemaphoreType.DMA
    return pl.pallas_call(
        finish_kernel,
        out_shape=shapes,
        in_specs=in_hbm(4),
        out_specs=in_hbm(len(shapes)),
        scratch_shapes=[
            pltpu.VMEM(layer_out.shape, bf16), pltpu.VMEM(g_tok.shape, f32), pltpu.VMEM(blocks.shape, f32),
            pltpu.VMEM(small.shape, f32), *[pltpu.VMEM(v.shape, f32) for v in little], dma((16,)), dma((40,)),
        ],
        compiler_params=pltpu.CompilerParams(vmem_limit_bytes=vmem_limit),
        name="finish",
    )(layer_out, g_tok, blocks, small)


def to_blocks(w_qkv, w_out, w_up, w_down):
    width = w_out.shape[1]
    qkv = w_qkv.reshape(width, 3, width // QUAD, QUAD).transpose(2, 0, 1, 3).reshape(-1, BLOCK)
    up = w_up.reshape(width, -1, BLOCK).transpose(1, 0, 2).reshape(-1, BLOCK)
    return jnp.concatenate([qkv, w_out, up, w_down], axis=0)


def from_blocks(held, width):
    qkv = held[: 3 * BLOCK].reshape(width // QUAD, width, 3, QUAD).transpose(1, 2, 0, 3).reshape(width, -1)
    up = held[4 * BLOCK : 8 * BLOCK].reshape(-1, width, BLOCK).transpose(1, 0, 2).reshape(width, -1)
    return qkv, held[3 * BLOCK : 4 * BLOCK], up, held[8 * BLOCK :]


def per_device(
    mesh_shape, tokens, cotangent, segments, box_coords, w_qkv, b_qkv, w_box, w_out, b_out, gain_one, shift_one,
    w_up, b_up, w_down, b_down, gain_two, shift_two,
):
    count, width = tokens.shape
    segs = segments.reshape(1, -1)
    vectors = [b_qkv, b_up, b_out, gain_one, shift_one, b_down, gain_two, shift_two]
    if mesh_shape == (16, 2):
        little = [v.reshape(1, -1) for v in vectors] + [w_box]
        big = [w_qkv, w_out, w_up, w_down]
        layer_out, g_tok, _, blocks, small = run_layer(True, tokens, cotangent, box_coords, segs, big, little)
        layer_out, g_tok, p_wq, p_wo, p_wu, p_wd, *rest = run_finish(layer_out, g_tok, blocks, small, big, little)
        p_bq, p_bu, p_bo, p_g1, p_s1, p_bd, p_g2, p_s2 = [v.reshape(-1) for v in rest[:8]]
        p_wb = rest[8]
    else:
        low = lambda value: value.astype(bf16)
        gather = lambda value: lax.all_gather(low(value), "fsdp", axis=0, tiled=True)
        held = to_blocks(gather(w_qkv), gather(w_out), gather(w_up), gather(w_down))
        wb, bq, bu, *six = [gather(v) for v in [w_box] + vectors]
        order = quad_order(jnp.arange(3 * width))
        rows = jnp.stack([jnp.zeros((width,), bf16)] * 2 + six).astype(f32)
        layer_out, g_tok, _, g_held, g_wb, g_bq, g_bu, g_six = run_layer(
            False, tokens, cotangent, box_coords, segs, [held],
            [wb, bq[order].astype(f32).reshape(1, -1), bu.astype(f32).reshape(1, -1), rows],
        )

        def scatter(grad):
            part = lax.psum_scatter(grad, "fsdp", scatter_dimension=0, tiled=True)
            return lax.psum(part, "rep").astype(f32)

        p_wq, p_wo, p_wu, p_wd = [scatter(g) for g in from_blocks(g_held, width)]
        g_bq = jnp.zeros((3 * width,), f32).at[order].set(g_bq[0])
        p_wb, p_bq, p_bu = scatter(g_wb), scatter(g_bq), scatter(g_bu[0])
        p_bo, p_g1, p_s1, p_bd, p_g2, p_s2 = [scatter(g_six[2 + i]) for i in range(VECTORS)]
    return (
        layer_out, g_tok, p_wq, p_bq, p_wb, p_wo, p_bo, p_g1, p_s1,
        p_wu, p_bu, p_wd, p_bd, p_g2, p_s2,
    )


def solution(mesh):
    tokens = P(("fsdp", "rep"), None)
    matrix, vector = P("fsdp", None), P("fsdp")
    kinds = [matrix, vector, matrix, matrix, vector, vector, vector, matrix, vector, matrix, vector, vector, vector]
    return jax.shard_map(
        functools.partial(per_device, (mesh.shape["fsdp"], mesh.shape["rep"])),
        mesh=mesh,
        in_specs=(tokens, tokens, P(("fsdp", "rep")), P(None, ("fsdp", "rep")), *kinds),
        out_specs=(tokens, tokens, *kinds),
        check_vma=False,
    )
```

```python
import functools
import math

import jax
import jax.numpy as jnp
from jax import lax
from jax.experimental import pallas as pl
from jax.experimental.pallas import tpu as pltpu
from jax.sharding import PartitionSpec as P

HEADS = 12
HD = 64
FREQ = 16
SLOT = 512
WAVE = 4 * FREQ
PAIR = 2 * HD
QUAD = 4 * HD

f32 = jnp.float32
bf16 = jnp.bfloat16
neg_large = -1e30
eps_norm = 1e-12
scale_factor = 1.0 / math.sqrt(HD)
vmem_limit = 67_000_000


def dot_nn(left, right):
    return lax.dot_general(left, right, (((1,), (0,)), ((), ())), preferred_element_type=f32)


def dot_nt(left, right):
    return lax.dot_general(left, right, (((1,), (1,)), ((), ())), preferred_element_type=f32)


def dot_tn(left, right):
    return lax.dot_general(left, right, (((0,), (0,)), ((), ())), preferred_element_type=f32)


def aligned(index, size):
    return pl.ds(pl.multiple_of(index * size, size), size)


def wave_rows(coords):
    count = coords.shape[1]
    spread = [jnp.broadcast_to(coords[c : c + 1, :].astype(f32), (FREQ, count)) for c in range(4)]
    scaled = jnp.concatenate(spread + spread, axis=0) * (100.0 / 1024.0)
    rows = lax.broadcasted_iota(jnp.int32, scaled.shape, 0)
    frequency = jnp.exp(-math.log(10000.0) * (rows & (FREQ - 1)).astype(f32) / FREQ)
    angle = scaled * frequency
    turns = jnp.floor(angle * (2.0 / math.pi) + 0.5)
    rest = ((angle - turns * 1.5703125) - turns * 4.837512969970703125e-4) - turns * 7.549789954891e-8
    square = rest * rest
    sine = rest + rest * square * (
        -1.6666654611e-1 + square * (8.3321608736e-3 + square * -1.9515295891e-4)
    )
    cosine = 1.0 - 0.5 * square + square * square * (
        4.166664568298827e-2 + square * (-1.388731625493765e-3 + square * 2.443315711809948e-5)
    )
    quadrant = turns.astype(jnp.int32) + jnp.where(rows >= WAVE, 1, 0)
    value = jnp.where((quadrant & 1) == 1, cosine, sine)
    value = jnp.where((quadrant & 2) == 2, -value, value)
    return value.astype(bf16).astype(f32)


def swap_lanes(value):
    return pltpu.roll(value, WAVE, 1)


def gelu_parts(value):
    t = 1.0 / (1.0 + (0.3275911 * math.sqrt(0.5)) * jnp.abs(value))
    bell = jnp.exp2(value * value * (-0.5 * math.log2(math.e)))
    half_tail = bell * t * (
        0.127414796 + t * (-0.142248368 + t * (0.7107068705 + t * (-0.7265760135 + t * 0.5307027145)))
    )
    return jnp.where(value >= 0, 1.0 - half_tail, half_tail), bell * (1.0 / math.sqrt(2.0 * math.pi))


def row_mean(value):
    return jnp.mean(value, axis=-1, keepdims=True)


ROWS = 256
BLOCK = 768
PIECE = 48
HALF = BLOCK // 2
SMALL = 512
STREAMS = 12
VECTORS = 6
LEVEL_FIRST = 7


def widths(width, ff):
    return 3 * width // 16, ff // 16, width // 16


class Route:
    def __init__(self):
        chip = lax.axis_index("fsdp")
        self.core = lax.axis_index("rep")
        self.level, self.me = chip // 4, chip % 4
        near_step, far_step = 1 + self.core, 2 - self.core
        near_move = near_step * (1 - 2 * ((self.me // near_step) % 2))
        far_move = far_step * (1 - 2 * ((self.me // far_step) % 2))
        self.near = self.me + near_move
        self.far = self.me + far_move
        self.across = self.me + near_move + far_move

    def chip(self, level, place):
        return level * 4 + place

    def levels(self):
        return [(self.level + k) % 4 for k in range(1, 4)]

    def peers(self):
        chips = [self.chip(level, self.me) for level in self.levels()]
        chips += [self.chip(self.level, self.near), self.chip(self.level, self.far)]
        return [(chip, self.core) for chip in chips] + [(self.chip(self.level, self.me), 1 - self.core)]


def remote(source, target, send, recv, chip, core):
    return pltpu.make_async_remote_copy(
        src_ref=source, dst_ref=target, send_sem=send, recv_sem=recv,
        device_id=(chip, core), device_id_type=pl.DeviceIdType.MESH,
    )


def half_columns(half, size):
    return pl.ds(pl.multiple_of(half * size, size), size)


class Streams:
    def __init__(self, held, stage, final, sems):
        self.held = held
        self.upper = held.at[: 8 * BLOCK].reshape(8, 4, 4, PIECE, BLOCK)
        self.lower = held.at[8 * BLOCK :].reshape(4, 4, 4, PIECE, BLOCK)
        self.stage = stage.reshape(STREAMS, 4, 4, PIECE, BLOCK)
        self.final = final
        self.gather_recv, self.gather_send, self.sum_recv, self.sum_send, self.final_sem = sems

    def on(self, stream, act):
        if isinstance(stream, int):
            act(self.upper.at[stream] if stream < 8 else self.lower.at[:, :, stream - 8])
        else:
            pl.when(stream < 8)(lambda: act(self.upper.at[stream]))
            pl.when(stream >= 8)(lambda: act(self.lower.at[:, :, stream - 8]))

    def half(self, half):
        return half_columns(half, HALF)

    def several(self, pieces):
        return self.held.at[: PIECE * pieces, :HALF]

    def landing(self, stream, kind):
        block = self.stage.at[(stream + 8) % STREAMS]
        if kind == 0:
            return block.at[:, :, :, :HALF]
        return block.at[(0, 0, 2, 3)[kind] : (0, 2, 3, 4)[kind], :, :, HALF:]

    def result(self, stream, half):
        return self.final.at[pl.ds(pl.multiple_of(stream * PIECE, 16), PIECE), self.half(half)]

    def results(self):
        return self.final.at[:, :HALF]


class Vectors:
    def __init__(self, held, stage, final, sems):
        self.held, self.flat, self.final = held, stage, final
        self.shards = held.reshape(4, 4, 8, SMALL)
        self.stage = stage.reshape(8, 4, 8, SMALL // 2)
        self.gather_recv, self.gather_send, self.sum_recv, self.sum_send, self.final_sem = sems

    def on(self, stream, act):
        act(self.shards)

    def half(self, half):
        return half_columns(half, SMALL // 2)

    def several(self, pieces):
        if pieces <= 16:
            return self.held.at[: 8 * pieces, : SMALL // 2]
        return self.flat.at[: 8 * pieces, :]

    def landing(self, stream, kind):
        return self.stage.at[(0, 4, 6, 7)[kind] : (4, 6, 7, 8)[kind]]

    def result(self, stream, half):
        return self.final.at[:, self.half(half)]

    def results(self):
        return self.final.at[:, : SMALL // 2]


def drain(view, sem):
    pltpu.make_async_copy(view, view, sem).wait()


class Exchange:
    def __init__(self, route, parts):
        self.route, self.parts = route, parts

    def send(self, source, target, send, recv, level, place, core):
        remote(source, target, send, recv, self.route.chip(level, place), core).start()


    def share(self, stream, view, place, kind):
        p, r = self.parts, self.route
        self.send(
            view, view, p.gather_send.at[stream, 0], p.gather_recv.at[stream, kind], r.level, place, r.core
        )

    def hand_over(self, stream, view):
        p, r = self.parts, self.route
        self.send(
            view, view, p.gather_send.at[stream, 1], p.gather_recv.at[stream, 3], r.level, r.me, 1 - r.core
        )

    def gather_own(self, stream):
        p, r = self.parts, self.route

        def act(shards):
            view = shards.at[r.level, r.me, :, p.half(r.core)]
            for level in r.levels():
                self.send(
                    view, view, p.gather_send.at[stream, 0], p.gather_recv.at[stream, 0], level, r.me, r.core
                )

        p.on(stream, act)

    def gather_column(self, stream):
        p, r = self.parts, self.route
        drain(p.several(3), p.gather_recv.at[stream, 0])

        def act(shards):
            view = shards.at[:, r.me, :, p.half(r.core)]
            self.share(stream, view, r.near, 1)
            self.share(stream, view, r.far, 2)
            for level in r.levels():
                self.hand_over(stream, shards.at[level, r.me, :, p.half(r.core)])

        p.on(stream, act)

    def gather_near(self, stream):
        p, r = self.parts, self.route
        drain(p.several(4), p.gather_recv.at[stream, 1])

        def act(shards):
            view = shards.at[:, r.near, :, p.half(r.core)]
            self.share(stream, view, r.far, 2)
            self.hand_over(stream, view)

        p.on(stream, act)

    def gather_far(self, stream):
        p, r = self.parts, self.route
        drain(p.several(8), p.gather_recv.at[stream, 2])

        def act(shards):
            for place in (r.far, r.across):
                self.hand_over(stream, shards.at[:, place, :, p.half(r.core)])

        p.on(stream, act)


    def level_own(self, stream):
        p, r = self.parts, self.route

        def act(shards):
            view = shards.at[r.level, r.me, :, p.half(r.core)]
            self.share(stream, view, r.near, 1)
            self.share(stream, view, r.far, 2)

        p.on(stream, act)

    def level_near(self, stream):
        p, r = self.parts, self.route
        drain(p.several(1), p.gather_recv.at[stream, 1])

        def act(shards):
            view = shards.at[r.level, r.near, :, p.half(r.core)]
            self.share(stream, view, r.far, 2)
            self.hand_over(stream, view)

        p.on(stream, act)

    def level_far(self, stream):
        p, r = self.parts, self.route
        drain(p.several(2), p.gather_recv.at[stream, 2])

        def act(shards):
            view = shards.at[r.level, :, :, p.half(r.core)]
            for level in r.levels():
                self.send(
                    view, view, p.gather_send.at[stream, 0], p.gather_recv.at[stream, 0], level, r.me, r.core
                )
            for place in (r.far, r.across):
                self.hand_over(stream, shards.at[r.level, place, :, p.half(r.core)])

        p.on(stream, act)

    def level_column(self, stream):
        p, r = self.parts, self.route
        drain(p.several(12), p.gather_recv.at[stream, 0])

        def act(shards):
            for level in r.levels():
                self.hand_over(stream, shards.at[level, :, :, p.half(r.core)])

        p.on(stream, act)

    def gathered(self, stream):
        p = self.parts
        drain(p.several(15), p.gather_recv.at[stream, 3])

    def gather_sent(self, stream):
        p = self.parts
        drain(p.several(15), p.gather_send.at[stream, 0])
        drain(p.several(15), p.gather_send.at[stream, 1])


    def pass_on(self, stream, view, landing, kind, level, place):
        p, r = self.parts, self.route
        self.send(view, landing, p.sum_send.at[stream], p.sum_recv.at[stream, kind], level, place, r.core)

    def sum_cores(self, stream):
        p, r = self.parts, self.route

        def act(shards):
            self.send(
                shards.at[:, :, :, p.half(1 - r.core)], p.landing(stream, 0),
                p.sum_send.at[stream], p.sum_recv.at[stream, 0], r.level, r.me, 1 - r.core,
            )

        p.on(stream, act)

    def sum_far(self, stream):
        p, r = self.parts, self.route
        drain(p.several(16), p.sum_recv.at[stream, 0])
        landed, target = p.landing(stream, 0), p.landing(stream, 1)

        def act(shards):
            def add(place):
                view = shards.at[:, place, :, p.half(r.core)]
                view[...] += landed[:, place]
                return view

            for index, place in enumerate((r.far, r.across)):
                self.pass_on(stream, add(place), target.at[index], 1, r.level, r.far)
            for place in (r.me, r.near):
                add(place)

        p.on(stream, act)

    def sum_near(self, stream):
        p, r = self.parts, self.route
        drain(p.several(8), p.sum_recv.at[stream, 1])
        landed, target = p.landing(stream, 1), p.landing(stream, 2)

        def act(shards):
            view = shards.at[:, r.near, :, p.half(r.core)]
            view[...] += landed[1]
            self.pass_on(stream, view, target.at[0], 2, r.level, r.near)
            view = shards.at[:, r.me, :, p.half(r.core)]
            view[...] += landed[0]

        p.on(stream, act)

    def sum_column(self, stream):
        p, r = self.parts, self.route
        drain(p.several(4), p.sum_recv.at[stream, 2])
        landed, target = p.landing(stream, 2), p.landing(stream, 3)

        def act(shards):
            view = shards.at[:, r.me, :, p.half(r.core)]
            view[...] += landed[0]
            for index, level in enumerate(r.levels()):
                self.pass_on(
                    stream, shards.at[level, r.me, :, p.half(r.core)], target.at[0, index], 3, level, r.me
                )

        p.on(stream, act)

    def sum_end(self, stream):
        p, r = self.parts, self.route
        drain(p.several(3), p.sum_recv.at[stream, 3])
        landed = p.landing(stream, 3)
        view = p.result(stream, r.core)

        def act(shards):
            total = shards[r.level, r.me, :, p.half(r.core)].astype(f32)
            for index in range(3):
                total += landed[0, index].astype(f32)
            view[...] = total

        p.on(stream, act)
        self.send(view, view, p.final_sem.at[0], p.final_sem.at[1], r.level, r.me, 1 - r.core)

    def summed(self, stream):
        p = self.parts
        drain(p.several(31), p.sum_send.at[stream])

    def results_in(self):
        p = self.parts
        drain(p.results(), p.final_sem.at[0])
        drain(p.results(), p.final_sem.at[1])


def owner_tables(start, share, depth, order=None):
    col = lax.broadcasted_iota(jnp.int32, (1, BLOCK), 1) + start
    source = col if order is None else order(col)
    owner, entry = source // share, source % share
    pick = (entry == lax.broadcasted_iota(jnp.int32, (depth, BLOCK), 0)).astype(bf16)
    row = lax.broadcasted_iota(jnp.int32, (128, BLOCK), 0)
    return pick, owner == (row >> 3), row & 7


def quad_order(col):
    return (col % BLOCK) // QUAD * BLOCK + col // BLOCK * QUAD + col % QUAD


def layer_kernel(comm, *refs):
    refs = list(refs)

    def take(count):
        taken, refs[:] = refs[:count], refs[count:]
        return taken

    tok_in, cot_in, coords_in, segs_in = take(4)
    if comm:
        w_qkv_in, w_out_in, w_up_in, w_down_in = take(4)
        small_in = take(9)
    else:
        held_in, w_box_in, b_qkv_in, b_up_in, vectors_in = take(5)
    layer_out, g_tok_out, e_hbm = take(3)
    if comm:
        final_out, small_out = take(2)
    else:
        g_held, g_w_box_out, g_b_qkv_out, g_b_up_out, g_vectors_out = take(5)
    (held, stage, slope, q8t, k8t, v_row, ctx_t, wave_t, wave_r, e_buf, normed, total, flip, g_down, tok_t, g_ctx_t,
     inv_one, inv_total, w_box, w_box_t, b_qkv, b_up, vectors, g_w_box, g_b_qkv, g_b_up, g_vectors, e_sem, io_sem, coords, segs, w_pair, w_pair_t) = take(33)
    if comm:
        final, small, small_stage, g_small, small_final, mid_sem = take(6)
        small_held = take(9)
        block_sems, small_sems, small_final_sems = take(5), take(4), take(1)

    count, width = tok_t.shape[1], tok_t.shape[0]
    ff = slope.shape[0] // count * BLOCK
    slots, pairs = count // SLOT, HEADS // 2
    row_blocks = count // ROWS
    up_blocks = ff // BLOCK
    quads = pairs // 2
    ctx, low, cot, tok = [stage.at[part * count : (part + 1) * count] for part in range(4)]
    act = stage.at[STREAMS * BLOCK - up_blocks * count :]
    up_at, down_at = 4 * BLOCK, 8 * BLOCK

    def copy_in(source, target, index=0):
        return pltpu.make_async_copy(source, target, io_sem.at[index])

    tok_copy = copy_in(tok_in, tok, 0)
    cot_copy = copy_in(cot_in, cot, 1)
    coord_copy = copy_in(coords_in, coords, 2)
    seg_copy = copy_in(segs_in, segs, 3)

    if comm:
        route = Route()
        chip = route.chip(route.level, route.me)
        blocks = Exchange(route, Streams(held, stage, final, block_sems))
        extras = Exchange(route, Vectors(small, small_stage, small_final, [*small_sems, *small_final_sems]))
        sums = Exchange(route, Vectors(g_small, small_stage, small_final, [*small_sems, *small_final_sems]))
        barrier = pltpu.get_barrier_semaphore()
        for peer, core in route.peers():
            pl.semaphore_signal(barrier, inc=1, device_id=(peer, core), device_id_type=pl.DeviceIdType.MESH)
        moves = []
        for quad in range(quads):
            for part in range(3):
                moves.append((
                    w_qkv_in.at[:, part * width + quad * QUAD : part * width + (quad + 1) * QUAD],
                    total.at[quad * PIECE : (quad + 1) * PIECE, part * QUAD : (part + 1) * QUAD],
                ))
        moves.append((w_out_in, total.at[3 * PIECE : 4 * PIECE]))
        for block in range(up_blocks):
            moves.append((
                w_up_in.at[:, block * BLOCK : (block + 1) * BLOCK],
                total.at[(4 + block) * PIECE : (5 + block) * PIECE],
            ))
        moves.append((w_down_in, total.at[8 * PIECE : 12 * PIECE]))
        moves += list(zip(small_in, small_held))
        moves = [copy_in(source, target, 4 + index) for index, (source, target) in enumerate(moves)]
        first = 3 * quads
        for copy in moves[:first] + moves[first + 1 + up_blocks + 1 :] + moves[first : first + 1 + up_blocks + 1]:
            copy.start()
        for copy in (coord_copy, seg_copy, tok_copy, cot_copy):
            copy.start()

        def round_block(block):
            at = pl.ds(pl.multiple_of(block * BLOCK + PIECE * chip, 16), PIECE)
            held[at, :] = total[block * PIECE : (block + 1) * PIECE, :].astype(bf16)

        g_small[:8, :] = jnp.zeros((8, SMALL), f32)
        for copy in moves[:first]:
            copy.wait()
        for block in range(quads):
            round_block(block)
        for copy in moves[first + 1 + up_blocks + 1 :]:
            copy.wait()
        g_small[:8, :HD] = small_held[8][...].astype(bf16).astype(f32)
        for row in range(8):
            value = small_held[row][...].astype(bf16).astype(f32)
            g_small[row : row + 1, 128 : 128 + value.shape[1]] = value
        small[pl.ds(pl.multiple_of(chip * 8, 8), 8), :] = g_small[:8, :]
        pl.semaphore_wait(barrier, 6)
        extras.gather_own(0)
        for stream in range(quads):
            blocks.gather_own(stream)
        for copy in moves[first : first + 1 + up_blocks + 1]:
            copy.wait()
        for block in range(quads, STREAMS - up_blocks):
            round_block(block)
        at = pl.ds(pl.multiple_of(down_at + 4 * PIECE * chip, 16), 4 * PIECE)
        held[at, :] = total[8 * PIECE : 12 * PIECE, :].astype(bf16)
        blocks.level_own(LEVEL_FIRST)
        for stream in range(quads, STREAMS):
            if stream != LEVEL_FIRST:
                blocks.gather_own(stream)
    else:
        for copy in (coord_copy, seg_copy, tok_copy, cot_copy):
            copy.start()
        copy_in(held_in, held, 4).start()
        w_box[...] = w_box_in[...]
        b_qkv[...] = b_qkv_in[...]
        b_up[...] = b_up_in[...]
        vectors[...] = vectors_in[...]

    coord_copy.wait()
    seg_copy.wait()
    wave_t[...] = wave_rows(coords[...])
    wave_r[...] = jnp.transpose(wave_t[...])
    for slot in range(slots):
        seg_i = jnp.broadcast_to(segs[:, slot * SLOT : (slot + 1) * SLOT].astype(f32), (SLOT, SLOT))
        seg_j = jnp.transpose(seg_i)
        normed[slot * SLOT : (slot + 1) * SLOT, :SLOT] = jnp.where(seg_i == seg_j, 0.0, neg_large)
    g_w_box[...] = jnp.zeros_like(g_w_box)
    g_b_up[...] = jnp.zeros_like(g_b_up)
    g_vectors[...] = jnp.zeros_like(g_vectors)
    tok_copy.wait()

    if comm:
        extras.gather_column(0)
        blocks.gather_column(0)
        extras.gather_near(0)
        blocks.gather_near(0)
        blocks.gather_column(1)
        extras.gather_far(0)
        blocks.gather_far(0)
        blocks.gather_near(1)
        blocks.gather_column(2)
        blocks.level_near(LEVEL_FIRST)
        extras.gathered(0)
        table = small[...].astype(bf16)
        w_box[...] = table[:, :HD]
        share_qkv, share_up, share = widths(width, ff)
        for row, columns, share_of, depth, order, target in (
            (0, 3 * width, share_qkv, 256, quad_order, b_qkv),
            (1, ff, share_up, 256, None, b_up),
            (None, width, share, 128, None, vectors),
        ):
            @pl.loop(0, columns // BLOCK)
            def _(block):
                pick, owned, row_of = owner_tables(block * BLOCK, share_of, depth, order)
                spread = dot_nn(table[:, 128 : 128 + depth], pick)
                keep = owned if row is None else owned & (row_of == row)
                rows = jnp.sum(jnp.where(keep, spread, 0.0).reshape(16, 8, BLOCK), axis=0)
                target[:, aligned(block, BLOCK)] = rows if row is None else jnp.sum(rows, axis=0, keepdims=True)

    else:
        copy_in(held_in, held, 4).wait()
    w_box_t[...] = jnp.transpose(w_box[...].astype(f32)).astype(bf16)
    blank = jnp.zeros((2 * WAVE, HD), bf16)
    w_pair_t[: 2 * WAVE, :] = jnp.concatenate([w_box[...], blank], axis=1)
    w_pair_t[2 * WAVE :, :] = jnp.concatenate([blank, w_box[...]], axis=1)
    w_pair[...] = jnp.transpose(w_pair_t[...].astype(f32)).astype(bf16)

    def gather_tick(step):
        if not comm:
            return

        def stream_of(order):
            return order + order // LEVEL_FIRST

        for ahead, act_on in ((1, blocks.gather_near), (3, blocks.gather_column), (0, blocks.gather_far)):
            order = step + ahead
            if isinstance(order, int):
                if order < STREAMS - 1:
                    act_on(stream_of(order))
            else:
                pl.when(order < STREAMS - 1)(functools.partial(act_on, stream_of(order)))

    def need(stream):
        if comm:
            blocks.gathered(stream)

    b_out, gain_one, shift_one, b_down, gain_two, shift_two = [vectors[2 + i : 3 + i, :] for i in range(VECTORS)]
    lane = lax.broadcasted_iota(jnp.int32, (SLOT, PAIR), 1)
    scores = total.reshape(2, SLOT, width)

    def project(quad, slot):
        rows = tok[aligned(slot, SLOT), :]

        def columns(part):
            weight = held[aligned(quad, BLOCK), part * QUAD : (part + 1) * QUAD]
            shift = b_qkv[:, pl.ds(pl.multiple_of(quad * BLOCK + part * QUAD, QUAD), QUAD)]
            return (dot_nn(rows, weight) + shift).astype(bf16)

        q, k, v = columns(0), columns(1), columns(2)
        low[aligned(slot, SLOT), aligned(quad, QUAD)] = k
        flip[aligned(quad, QUAD), aligned(slot, SLOT)] = jnp.transpose(v.astype(f32)).astype(bf16)
        qt = jnp.transpose(q.astype(f32) * scale_factor).astype(bf16)
        kt = jnp.transpose(k.astype(f32) * scale_factor).astype(bf16)
        for part in range(2):
            here = slice(part * PAIR, (part + 1) * PAIR)
            q8t[slot, quad * 2 + part] = qt[here]
            k8t[slot, quad * 2 + part] = kt[here]
            v_row[slot, quad * 2 + part] = v[:, here]

    def e_copy(place, head, index, out):
        pair = (e_buf.at[place, head], e_hbm.at[index])
        return pltpu.make_async_copy(*(pair if out else pair[::-1]), e_sem.at[place, head])

    def attend(step):
        pair, slot = step // slots, step % slots
        cols = aligned(slot, SLOT)
        place = step % 2

        @pl.when(step >= 2)
        def _():
            for head in range(2):
                e_copy(place, head, 0, True).wait()

        sine_t, cosine_t = wave_t[:WAVE, cols], wave_t[WAVE:, cols]
        sc_t = (wave_t[:, cols] * scale_factor).astype(bf16)
        sc_r = wave_r[cols, :]
        cs_r = swap_lanes(sc_r)
        cc_r = jnp.where(lane < WAVE, cs_r, sc_r)
        ss_r = jnp.where(lane < WAVE, sc_r, -cs_r)
        cs_low = cs_r.astype(bf16)
        keys = low[cols, aligned(pair, PAIR)]
        queries = q8t[slot, pair]
        key_box = dot_nn(keys, w_pair[...])
        query_box = dot_nn(w_pair_t[...], queries)
        low_exps, inverse, heads_t = [], [], []
        for head in range(2):
            here = slice(head * 2 * WAVE, (head + 1) * 2 * WAVE)
            side = key_box[:, here]
            k_side = (side * cc_r + swap_lanes(side) * ss_r).astype(bf16)
            first, second = query_box[here][:WAVE], query_box[here][WAVE:]
            q_side = jnp.concatenate(
                [first * sine_t + second * cosine_t, second * sine_t - first * cosine_t], axis=0
            ).astype(bf16)
            q_t = queries[head * HD : (head + 1) * HD]
            zero = jnp.zeros_like(q_t)
            q_pair = [q_t, zero] if head == 0 else [zero, q_t]
            k_full = jnp.concatenate([keys, cs_low, k_side], axis=1)
            q_full = jnp.concatenate(q_pair + [q_side, sc_t], axis=0)
            scores[head, :, :SLOT] = dot_nn(k_full, q_full) + normed[cols, :SLOT]
        for head in range(2):
            masked = scores[head, :, :SLOT]
            exps = jnp.exp(masked - jnp.max(masked, axis=0, keepdims=True))
            inverse.append(1.0 / jnp.sum(exps, axis=0, keepdims=True))
            low_exps.append(exps.astype(bf16))
            e_buf[place, head] = low_exps[head]
            e_copy(place, head, step * 2 + head, True).start()
            inv_total[step * 2 + head] = inverse[head]
        for head in range(2):
            at = pl.ds(pl.multiple_of(pair * PAIR + head * HD, HD), HD)
            heads_t.append(dot_nn(flip[at, cols], low_exps[head]) * inverse[head])
        both = jnp.concatenate(heads_t, axis=0)
        ctx_t[aligned(pair, PAIR), cols] = both.astype(bf16)
        ctx[cols, aligned(pair, PAIR)] = jnp.transpose(both).astype(bf16)

    steps = slots * pairs
    quad_steps = 2 * slots

    @pl.loop(0, quads)
    def _(quad):
        need(quad)

        @pl.loop(0, slots)
        def _(slot):
            project(quad, slot)

        @pl.loop(0, quad_steps)
        def _(inner):
            step = quad * quad_steps + inner
            if comm:
                @pl.when(step == 1)
                def _():
                    blocks.gather_column(quads)
                    blocks.level_far(LEVEL_FIRST)

                pl.when((step % 2 == 0) & (step > 0))(functools.partial(gather_tick, step // 2))
            attend(step)

    for place in range(2):
        for head in range(2):
            e_copy(place, head, 0, True).wait()

    def column_sum(value):
        return jnp.sum(value, axis=0, keepdims=True)

    need(3)
    gather_tick(6)

    @pl.loop(0, row_blocks)
    def _(block):
        rows = aligned(block, ROWS)
        token_rows = tok[rows, :].astype(f32)
        tok_t[:, rows] = jnp.transpose(token_rows).astype(bf16)
        pre = token_rows + dot_nn(ctx[rows, :], held[3 * BLOCK : 4 * BLOCK, :]) + b_out
        center = pre - row_mean(pre)
        invdev = lax.rsqrt(row_mean(center * center) + eps_norm)
        unit = center * invdev
        inv_one[rows, :] = jnp.broadcast_to(invdev, (ROWS, 128))
        normed[rows, :] = unit
        hidden = unit * gain_one + shift_one
        low[rows, :] = hidden.astype(bf16)
        flip[:, rows] = jnp.transpose(hidden).astype(bf16)

    @pl.loop(0, up_blocks)
    def _(block):
        gather_tick(7 + block)
        if comm:
            pl.when(block == 2)(functools.partial(blocks.level_column, LEVEL_FIRST))
        need(4 + block)

        weight = held[pl.ds(pl.multiple_of(up_at + block * BLOCK, BLOCK), BLOCK), :]
        for row in range(row_blocks):
            rows = slice(row * ROWS, (row + 1) * ROWS)
            total[rows, :] = dot_nn(low[rows, :], weight) + b_up[:, aligned(block, BLOCK)]
        for row in range(row_blocks):
            at = pl.ds(pl.multiple_of(block * count + row * ROWS, ROWS), ROWS)
            up = total[row * ROWS : (row + 1) * ROWS, :]
            cdf, pdf = gelu_parts(up)
            act[at, :] = (up * cdf).astype(bf16)
            slope[at, :] = (cdf + up * pdf).astype(bf16)

    for block in range(up_blocks):
        need(8 + block)
    cot_copy.wait()

    @pl.loop(0, row_blocks)
    def _(block):
        rows = aligned(block, ROWS)
        pre = normed[rows, :] * gain_one + shift_one + b_down
        for part in range(up_blocks):
            at = pl.ds(pl.multiple_of(part * count + block * ROWS, ROWS), ROWS)
            pre += dot_nn(act[at, :], held[down_at + part * BLOCK : down_at + (part + 1) * BLOCK, :])
        center = pre - row_mean(pre)
        invdev = lax.rsqrt(row_mean(center * center) + eps_norm)
        unit = center * invdev
        grad = cot[rows, :].astype(f32)
        cot[rows, :] = (unit * gain_two + shift_two).astype(bf16)
        scaled = grad * gain_two
        g_pre = invdev * (scaled - row_mean(scaled) - unit * row_mean(scaled * unit))
        total[rows, :] = g_pre
        low_pre = g_pre.astype(bf16)
        g_down[rows, :] = low_pre
        g_vectors[5:6, :] += column_sum(low_pre.astype(f32))
        g_vectors[6:7, :] += column_sum(grad * unit)
        g_vectors[7:8, :] += column_sum(grad)

    out_copy = pltpu.make_async_copy(cot, layer_out, io_sem.at[0])
    out_copy.start()
    if comm:
        for stream in range(STREAMS):
            blocks.gather_sent(stream)
        extras.gather_sent(0)

    def last(step):
        turn = step // 4
        return STREAMS - 1 - step + (14 - 6 * turn) * turn - 4

    def sum_start(step):
        if comm:
            blocks.sum_cores(last(step))

    def sum_tick(step, stages=(0, 1, 2, 3)):
        if not comm:
            return
        acts = (blocks.sum_far, blocks.sum_near, blocks.sum_column, blocks.sum_end)
        for behind in stages:
            at = step - behind
            if isinstance(at, int):
                if 0 <= at < STREAMS:
                    acts[behind](last(at))
            else:
                pl.when((at >= 0) & (at < STREAMS))(functools.partial(acts[behind], last(at)))

    def meet(sem):
        if comm:
            for peer, core in route.peers():
                pl.semaphore_signal(sem, inc=1, device_id=(peer, core), device_id_type=pl.DeviceIdType.MESH)
            pl.semaphore_wait(sem, 6)

    out_copy.wait()
    if comm:
        meet(mid_sem.at[0])

    @pl.loop(0, up_blocks)
    def _(index):
        block = up_blocks - 1 - index
        down_rows = pl.ds(pl.multiple_of(down_at + block * BLOCK, BLOCK), BLOCK)
        up_rows = pl.ds(pl.multiple_of(up_at + block * BLOCK, BLOCK), BLOCK)
        for row in range(2):
            rows = slice(row * (count // 2), (row + 1) * (count // 2))
            at = pl.ds(pl.multiple_of(block * count + row * (count // 2), count // 2), count // 2)
            g_act = dot_nt(g_down[rows, :], held[down_rows, :])
            g_up = (g_act * slope[at, :].astype(f32)).astype(bf16)
            slope[at, :] = g_up
            g_b_up[:, aligned(block, BLOCK)] += column_sum(g_up.astype(f32))
            total[rows, :] += dot_nt(g_up, held[up_rows, :])
        sum_tick(index - 1, (0,))
        sum_tick(index - 1, (1, 2, 3))
        g_up = slope[aligned(block, count), :]
        for part in range(2):
            at = pl.ds(pl.multiple_of(up_at + block * BLOCK + part * HALF, HALF), HALF)
            held[at, :] = dot_nn(flip[part * HALF : (part + 1) * HALF, :], g_up).astype(bf16)
        sum_start(index)
        for part in range(2):
            at = pl.ds(pl.multiple_of(down_at + block * BLOCK + part * HALF, HALF), HALF)
            grads = dot_tn(act[aligned(block, count), part * HALF : (part + 1) * HALF], g_down[...])
            held[at, :] = grads.astype(bf16)

    if comm:
        meet(mid_sem.at[1])
    sum_tick(3)
    for step in range(up_blocks):
        sum_start(up_blocks + step)

    @pl.loop(0, row_blocks)
    def _(block):
        rows = aligned(block, ROWS)
        grad, unit = total[rows, :], normed[rows, :]
        scaled = grad * gain_one
        g_pre = inv_one[rows, :1] * (scaled - row_mean(scaled) - unit * row_mean(scaled * unit))
        total[rows, :] = g_pre
        low_pre = g_pre.astype(bf16)
        g_down[rows, :] = low_pre
        g_vectors[2:3, :] += column_sum(low_pre.astype(f32))
        g_vectors[3:4, :] += column_sum(grad * unit)
        g_vectors[4:5, :] += column_sum(grad)

    for part in range(2):
        rows = slice(part * (count // 2), (part + 1) * (count // 2))
        g_ctx_t[:, rows] = dot_nt(held[3 * BLOCK : 4 * BLOCK, :], g_down[rows, :]).astype(bf16)
    for part in range(2):
        at = slice(3 * BLOCK + part * HALF, 3 * BLOCK + (part + 1) * HALF)
        held[at, :] = dot_nn(ctx_t[part * HALF : (part + 1) * HALF, :], g_down[...]).astype(bf16)

    sum_start(8)
    sum_tick(4)

    def e_step(order):
        quad = quads - 1 - order // quad_steps
        return quad * quad_steps + order % quad_steps

    def fetch(order):
        for head in range(2):
            e_copy(order % 2, head, e_step(order) * 2 + head, False).start()

    fetch(0)
    ones = jnp.ones((16, count), bf16)

    def attend_back(order):
        step = e_step(order)
        pair, slot = step // slots, step % slots
        cols = aligned(slot, SLOT)
        place = order % 2

        @pl.when(order + 1 < steps)
        def _():
            fetch(order + 1)

        for head in range(2):
            e_copy(place, head, 0, False).wait()
        sine_t, cosine_t = wave_t[:WAVE, cols], wave_t[WAVE:, cols]
        sc_t = (wave_t[:, cols] * scale_factor).astype(bf16)
        cs_t = (jnp.concatenate([cosine_t, sine_t], axis=0) * scale_factor).astype(bf16)
        values = v_row[slot, pair]
        g_lows, row_dots, g_probs, g_scores, g_qs, g_ks = [], [], [], [], [], []
        g_parts = [[], [], []]
        spans = [slice(head * HD, (head + 1) * HD) for head in range(2)]
        for head in range(2):
            at = pl.ds(pl.multiple_of(pair * PAIR + head * HD, HD), HD)
            g_rows = g_ctx_t[at, cols].astype(f32) * inv_total[step * 2 + head]
            row_dots.append(jnp.sum(g_rows * ctx_t[at, cols].astype(f32), axis=0, keepdims=True))
            g_lows.append(g_rows.astype(bf16))
            zero = jnp.zeros_like(g_lows[head])
            g_pair = jnp.concatenate([g_lows[head], zero] if head == 0 else [zero, g_lows[head]], axis=0)
            g_probs.append(dot_nn(values, g_pair))
        for head in range(2):
            g_scores.append((e_buf[place, head].astype(f32) * (g_probs[head] - row_dots[head])).astype(bf16))
        for head in range(2):
            g_qs.append(dot_nn(jnp.concatenate([k8t[slot, pair, spans[head], :], cs_t], axis=0), g_scores[head]))
        for head in range(2):
            g_ks.append(dot_nt(jnp.concatenate([q8t[slot, pair, spans[head], :], sc_t], axis=0), g_scores[head]))
        for head in range(2):
            g_parts[2].append(dot_nt(g_lows[head], e_buf[place, head]))
        for head in range(2):
            k_t, q_t = k8t[slot, pair, spans[head], :], q8t[slot, pair, spans[head], :]
            g_q, g_k = g_qs[head], g_ks[head]
            first, second = g_q[HD : HD + WAVE], g_q[HD + WAVE :]
            g_qbox = jnp.concatenate(
                [first * sine_t - second * cosine_t, first * cosine_t + second * sine_t], axis=0
            ).astype(bf16)
            first, second = g_k[HD : HD + WAVE], g_k[HD + WAVE :]
            g_kbox = jnp.concatenate(
                [first * cosine_t - second * sine_t, first * sine_t + second * cosine_t], axis=0
            ).astype(bf16)
            g_parts[0].append(g_q[:HD] + dot_nn(w_box_t[...], g_qbox))
            g_parts[1].append(g_k[:HD] + dot_nn(w_box_t[...], g_kbox))
            g_w_box[...] += dot_nt(g_qbox, q_t) + dot_nt(g_kbox, k_t)
        for part in range(3):
            at = pl.ds(pl.multiple_of(part * QUAD + pair % 2 * PAIR, PAIR), PAIR)
            flip[at, cols] = jnp.concatenate(g_parts[part], axis=0).astype(bf16)

    kept = slope.at[3 * count : 3 * count + BLOCK]
    kept_last = g_down.at[:BLOCK]

    @pl.loop(0, quads)
    def _(turn):
        quad = quads - 1 - turn

        @pl.loop(0, quad_steps)
        def _(inner):
            order = turn * quad_steps + inner
            if comm:
                pl.when(order % 2 == 1)(functools.partial(sum_tick, 5 + order // 2, (0,)))
                pl.when((order % 2 == 0) & (order > 0))(functools.partial(sum_tick, 4 + order // 2, (1, 2, 3)))
            attend_back(order)

        if comm:
            pl.when(turn == quads - 1)(functools.partial(sum_tick, 10, (1, 2, 3)))

        @pl.when(turn < quads - 1)
        def _():
            kept[...] = held[aligned(quad, BLOCK), :]

        @pl.when(turn == quads - 1)
        def _():
            kept_last[...] = held[aligned(quad, BLOCK), :]

        for part in range(2):
            at = pl.ds(pl.multiple_of(quad * BLOCK + part * HALF, HALF), HALF)
            held[at, :] = dot_nt(tok_t[part * HALF : (part + 1) * HALF, :], flip[...]).astype(bf16)
        sum_start(9 + turn)
        g_b_qkv[:, aligned(quad, BLOCK)] = dot_nt(ones, flip[...])[:1]

        @pl.when(turn == 0)
        def _():
            for block in range(row_blocks):
                rows = slice(block * ROWS, (block + 1) * ROWS)
                total[rows, :] += jnp.transpose(dot_nn(kept[...], flip[:, rows]))

        @pl.when(turn == 1)
        def _():
            for block in range(row_blocks):
                rows = slice(block * ROWS, (block + 1) * ROWS)
                slope[rows, :] = jnp.transpose(flip[:, rows].astype(f32)).astype(bf16)

    g_w_box[...] = g_w_box[...] * (1.0 / scale_factor)
    tok_out = []

    def token_grad(block):
        rows = slice(block * ROWS, (block + 1) * ROWS)
        last_part = jnp.transpose(dot_nn(kept_last[...], flip[:, rows]))
        total[rows, :] += last_part + dot_nt(slope[rows, :], kept[...])
        tok_out.append(pltpu.make_async_copy(total.at[rows], g_tok_out.at[rows], io_sem.at[4 + block]))
        tok_out[-1].start()

    if comm:
        g_small[...] = jnp.zeros_like(g_small)
        g_small[:, :HD] = g_w_box[...]
        share_qkv, share_up, share = widths(width, ff)
        for row, columns, share_of, order, source in (
            (0, 3 * width, share_qkv, quad_order, g_b_qkv),
            (1, ff, share_up, None, g_b_up),
            (None, width, share, None, g_vectors),
        ):
            @pl.loop(0, columns // BLOCK)
            def _(block):
                pick, owned, row_of = owner_tables(block * BLOCK, share_of, 256, order)
                keep = owned if row is None else owned & (row_of == row)
                wide = 1 if row is not None else 8
                full = source[:, aligned(block, BLOCK)].reshape(1, wide, BLOCK)
                spread = jnp.broadcast_to(full, (16, 8, BLOCK)).reshape(128, BLOCK)
                spread = jnp.where(keep, spread, 0.0)
                upper = spread.astype(bf16)
                g_small[:, 128:384] += dot_nt(upper, pick) + dot_nt((spread - upper.astype(f32)).astype(bf16), pick)

        sums.sum_cores(0)
        sum_tick(11, (1, 2, 3))
        sum_tick(11, (0,))
        sums.sum_far(0)
        sum_tick(12, (2, 3))
        token_grad(0)
        token_grad(1)
        sum_tick(12, (1,))
        sums.sum_near(0)
        token_grad(2)
        sum_tick(13, (3,))
        sum_tick(13, (2,))
        sums.sum_column(0)
        token_grad(3)
        sum_tick(14, (3,))
        sums.sum_end(0)
        for stream in range(STREAMS):
            blocks.summed(stream)
        sums.summed(0)
        blocks.results_in()
        sums.results_in()
        moves = [copy_in(final, final_out, 2), copy_in(small_final, small_out, 3)]
        for copy in moves:
            copy.start()
        for copy in moves:
            copy.wait()
    else:
        for block in range(row_blocks):
            token_grad(block)
        g_w_box_out[...] = g_w_box[...]
        g_b_qkv_out[...] = g_b_qkv[...]
        g_b_up_out[...] = g_b_up[...]
        g_vectors_out[...] = g_vectors[...]
        out = copy_in(held, g_held, 2)
        out.start()
        out.wait()
    for copy in tok_out:
        copy.wait()


def shaped(shape, dtype):
    return jax.ShapeDtypeStruct(shape, dtype)


def in_vmem(count):
    return [pl.BlockSpec(memory_space=pltpu.VMEM)] * count


def in_hbm(count):
    return [pl.BlockSpec(memory_space=pl.ANY)] * count


def run_layer(comm, tokens, cotangent, coords, segs, big, little):
    count, width = tokens.shape
    ff = 4 * BLOCK
    slots, pairs = count // SLOT, HEADS // 2
    held_shape = (STREAMS * BLOCK, BLOCK)
    out_shape = [
        shaped((count, width), bf16),
        shaped((count, width), f32),
        shaped((slots * HEADS, SLOT, SLOT), bf16),
    ]
    out_specs = in_hbm(3)
    if comm:
        out_shape += [shaped((STREAMS * PIECE, BLOCK), f32), shaped((8, SMALL), f32)]
        out_specs += in_hbm(2)
    else:
        out_shape += [shaped(held_shape, bf16), shaped((2 * WAVE, HD), f32), shaped((1, 3 * width), f32)]
        out_shape += [shaped((1, ff), f32), shaped((8, width), f32)]
        out_specs += in_hbm(1) + in_vmem(4)
    vmem = pltpu.VMEM
    dma = pltpu.SemaphoreType.DMA
    scratch = [
        vmem(held_shape, bf16),
        vmem(held_shape, bf16),
        vmem((ff // BLOCK * count, BLOCK), bf16),
        vmem((slots, pairs, PAIR, SLOT), bf16),
        vmem((slots, pairs, PAIR, SLOT), bf16),
        vmem((slots, pairs, SLOT, PAIR), bf16),
        vmem((width, count), bf16),
        vmem((2 * WAVE, count), f32),
        vmem((count, 2 * WAVE), f32),
        vmem((2, 2, SLOT, SLOT), bf16),
        vmem((count, width), f32),
        vmem((count, width), f32),
        vmem((width, count), bf16),
        vmem((count, width), bf16),
        vmem((width, count), bf16),
        vmem((width, count), bf16),
        vmem((count, 128), f32),
        vmem((slots * HEADS, 1, SLOT), f32),
        vmem((2 * WAVE, HD), bf16),
        vmem((HD, 2 * WAVE), bf16),
        vmem((1, 3 * width), f32),
        vmem((1, ff), f32),
        vmem((8, width), f32),
        vmem((2 * WAVE, HD), f32),
        vmem((1, 3 * width), f32),
        vmem((1, ff), f32),
        vmem((8, width), f32),
        dma((2, 2)),
        dma((32,)),
        vmem(coords.shape, jnp.int32),
        vmem(segs.shape, jnp.int32),
        vmem((PAIR, 4 * WAVE), bf16),
        vmem((4 * WAVE, PAIR), bf16),
    ]
    if comm:
        scratch += [
            vmem((STREAMS * PIECE, BLOCK), f32),
            vmem((128, SMALL), f32),
            vmem((256, SMALL // 2), f32),
            vmem((128, SMALL), f32),
            vmem((8, SMALL), f32),
            pltpu.SemaphoreType.REGULAR((2,)),
            *[vmem(value.shape, f32) for value in little],
            dma((STREAMS, 4)), dma((STREAMS, 2)), dma((STREAMS, 4)), dma((STREAMS,)), dma((2,)),
            dma((1, 4)), dma((1, 2)), dma((1, 4)), dma((1,)),
            dma((2,)),
        ]
        extra = dict(collective_id=0, has_side_effects=True)
    else:
        extra = {}
    return pl.pallas_call(
        functools.partial(layer_kernel, comm),
        out_shape=out_shape,
        in_specs=in_hbm(4 + len(big)) + (in_hbm if comm else in_vmem)(len(little)),
        out_specs=out_specs,
        scratch_shapes=scratch,
        compiler_params=pltpu.CompilerParams(vmem_limit_bytes=vmem_limit, **extra),
        name="layer",
    )(tokens, cotangent, coords, segs, *big, *little)


def finish_kernel(*refs):
    layer_in, tok_in, blocks_in, small_in = refs[:4]
    layer_out, tok_out, p_qkv, p_out, p_up, p_down = refs[4:10]
    small_out = refs[10:19]
    layer, tok, blocks, small = refs[19:23]
    small_rows = refs[23:32]
    load_sem, store_sem = refs[32:]
    width = layer_in.shape[1]
    loads, stores = [], []
    parts = 4
    rows = layer_in.shape[0] // parts
    small_load = pltpu.make_async_copy(small_in, small, load_sem.at[0])
    loads.append((pltpu.make_async_copy(blocks_in, blocks, load_sem.at[1]), []))
    for quad in range(width // QUAD):
        for part in range(3):
            loads[0][1].append((
                blocks.at[quad * PIECE : (quad + 1) * PIECE, part * QUAD : (part + 1) * QUAD],
                p_qkv.at[:, part * width + quad * QUAD : part * width + (quad + 1) * QUAD],
            ))
    loads[0][1].append((blocks.at[3 * PIECE : 4 * PIECE], p_out))
    for block in range(4):
        loads[0][1].append((
            blocks.at[(4 + block) * PIECE : (5 + block) * PIECE], p_up.at[:, block * BLOCK : (block + 1) * BLOCK]
        ))
    loads[0][1].append((blocks.at[8 * PIECE : 12 * PIECE], p_down))
    for source, held, target in ((tok_in, tok, tok_out), (layer_in, layer, layer_out)):
        for part in range(parts):
            at = slice(part * rows, (part + 1) * rows)
            copy = pltpu.make_async_copy(source.at[at], held.at[at], load_sem.at[1 + len(loads)])
            loads.append((copy, [(held.at[at], target.at[at])]))
    small_load.start()
    for copy, _ in loads:
        copy.start()

    def store(source, target):
        stores.append(pltpu.make_async_copy(source, target, store_sem.at[len(stores)]))
        stores[-1].start()

    small_load.wait()
    for row in range(8):
        small_rows[row][...] = small[row : row + 1, 128 : 128 + small_rows[row].shape[1]]
    small_rows[8][...] = small[:, :HD]
    for source, target in zip(small_rows, small_out):
        store(source, target)
    for copy, moves in loads:
        copy.wait()
        for source, target in moves:
            store(source, target)
    for copy in stores:
        copy.wait()


def run_finish(layer_out, g_tok, blocks, small, big, little):
    shapes = [shaped(layer_out.shape, bf16), shaped(g_tok.shape, f32)]
    shapes += [shaped(w.shape, f32) for w in big + little]
    dma = pltpu.SemaphoreType.DMA
    return pl.pallas_call(
        finish_kernel,
        out_shape=shapes,
        in_specs=in_hbm(4),
        out_specs=in_hbm(len(shapes)),
        scratch_shapes=[
            pltpu.VMEM(layer_out.shape, bf16), pltpu.VMEM(g_tok.shape, f32), pltpu.VMEM(blocks.shape, f32),
            pltpu.VMEM(small.shape, f32), *[pltpu.VMEM(v.shape, f32) for v in little], dma((16,)), dma((40,)),
        ],
        compiler_params=pltpu.CompilerParams(vmem_limit_bytes=vmem_limit),
        name="finish",
    )(layer_out, g_tok, blocks, small)


def to_blocks(w_qkv, w_out, w_up, w_down):
    width = w_out.shape[1]
    qkv = w_qkv.reshape(width, 3, width // QUAD, QUAD).transpose(2, 0, 1, 3).reshape(-1, BLOCK)
    up = w_up.reshape(width, -1, BLOCK).transpose(1, 0, 2).reshape(-1, BLOCK)
    return jnp.concatenate([qkv, w_out, up, w_down], axis=0)


def from_blocks(held, width):
    qkv = held[: 3 * BLOCK].reshape(width // QUAD, width, 3, QUAD).transpose(1, 2, 0, 3).reshape(width, -1)
    up = held[4 * BLOCK : 8 * BLOCK].reshape(-1, width, BLOCK).transpose(1, 0, 2).reshape(width, -1)
    return qkv, held[3 * BLOCK : 4 * BLOCK], up, held[8 * BLOCK :]


def per_device(
    mesh_shape, tokens, cotangent, segments, box_coords, w_qkv, b_qkv, w_box, w_out, b_out, gain_one, shift_one,
    w_up, b_up, w_down, b_down, gain_two, shift_two,
):
    count, width = tokens.shape
    segs = segments.reshape(1, -1)
    vectors = [b_qkv, b_up, b_out, gain_one, shift_one, b_down, gain_two, shift_two]
    if mesh_shape == (16, 2):
        little = [v.reshape(1, -1) for v in vectors] + [w_box]
        big = [w_qkv, w_out, w_up, w_down]
        layer_out, g_tok, _, blocks, small = run_layer(True, tokens, cotangent, box_coords, segs, big, little)
        layer_out, g_tok, p_wq, p_wo, p_wu, p_wd, *rest = run_finish(layer_out, g_tok, blocks, small, big, little)
        p_bq, p_bu, p_bo, p_g1, p_s1, p_bd, p_g2, p_s2 = [v.reshape(-1) for v in rest[:8]]
        p_wb = rest[8]
    else:
        low = lambda value: value.astype(bf16)
        gather = lambda value: lax.all_gather(low(value), "fsdp", axis=0, tiled=True)
        held = to_blocks(gather(w_qkv), gather(w_out), gather(w_up), gather(w_down))
        wb, bq, bu, *six = [gather(v) for v in [w_box] + vectors]
        order = quad_order(jnp.arange(3 * width))
        rows = jnp.stack([jnp.zeros((width,), bf16)] * 2 + six).astype(f32)
        layer_out, g_tok, _, g_held, g_wb, g_bq, g_bu, g_six = run_layer(
            False, tokens, cotangent, box_coords, segs, [held],
            [wb, bq[order].astype(f32).reshape(1, -1), bu.astype(f32).reshape(1, -1), rows],
        )

        def scatter(grad):
            part = lax.psum_scatter(grad, "fsdp", scatter_dimension=0, tiled=True)
            return lax.psum(part, "rep").astype(f32)

        p_wq, p_wo, p_wu, p_wd = [scatter(g) for g in from_blocks(g_held, width)]
        g_bq = jnp.zeros((3 * width,), f32).at[order].set(g_bq[0])
        p_wb, p_bq, p_bu = scatter(g_wb), scatter(g_bq), scatter(g_bu[0])
        p_bo, p_g1, p_s1, p_bd, p_g2, p_s2 = [scatter(g_six[2 + i]) for i in range(VECTORS)]
    return (
        layer_out, g_tok, p_wq, p_bq, p_wb, p_wo, p_bo, p_g1, p_s1,
        p_wu, p_bu, p_wd, p_bd, p_g2, p_s2,
    )


def solution(mesh):
    tokens = P(("fsdp", "rep"), None)
    matrix, vector = P("fsdp", None), P("fsdp")
    kinds = [matrix, vector, matrix, matrix, vector, vector, vector, matrix, vector, matrix, vector, vector, vector]
    return jax.shard_map(
        functools.partial(per_device, (mesh.shape["fsdp"], mesh.shape["rep"])),
        mesh=mesh,
        in_specs=(tokens, tokens, P(("fsdp", "rep")), P(None, ("fsdp", "rep")), *kinds),
        out_specs=(tokens, tokens, *kinds),
        check_vma=False,
    )
```

```python
import functools
import math

import jax
import jax.numpy as jnp
from jax import lax
from jax.experimental import pallas as pl
from jax.experimental.pallas import tpu as pltpu
from jax.sharding import PartitionSpec as P

HEADS = 12
HD = 64
FREQ = 16
SLOT = 512
WAVE = 4 * FREQ
PAIR = 2 * HD
QUAD = 4 * HD

f32 = jnp.float32
bf16 = jnp.bfloat16
neg_large = -1e30
eps_norm = 1e-12
scale_factor = 1.0 / math.sqrt(HD)
vmem_limit = 67_000_000


def dot_nn(left, right):
    return lax.dot_general(left, right, (((1,), (0,)), ((), ())), preferred_element_type=f32)


def dot_nt(left, right):
    return lax.dot_general(left, right, (((1,), (1,)), ((), ())), preferred_element_type=f32)


def dot_tn(left, right):
    return lax.dot_general(left, right, (((0,), (0,)), ((), ())), preferred_element_type=f32)


def aligned(index, size):
    return pl.ds(pl.multiple_of(index * size, size), size)


def wave_rows(coords):
    count = coords.shape[1]
    spread = [jnp.broadcast_to(coords[c : c + 1, :].astype(f32), (FREQ, count)) for c in range(4)]
    scaled = jnp.concatenate(spread + spread, axis=0) * (100.0 / 1024.0)
    rows = lax.broadcasted_iota(jnp.int32, scaled.shape, 0)
    frequency = jnp.exp(-math.log(10000.0) * (rows & (FREQ - 1)).astype(f32) / FREQ)
    angle = scaled * frequency
    turns = jnp.floor(angle * (2.0 / math.pi) + 0.5)
    rest = ((angle - turns * 1.5703125) - turns * 4.837512969970703125e-4) - turns * 7.549789954891e-8
    square = rest * rest
    sine = rest + rest * square * (
        -1.6666654611e-1 + square * (8.3321608736e-3 + square * -1.9515295891e-4)
    )
    cosine = 1.0 - 0.5 * square + square * square * (
        4.166664568298827e-2 + square * (-1.388731625493765e-3 + square * 2.443315711809948e-5)
    )
    quadrant = turns.astype(jnp.int32) + jnp.where(rows >= WAVE, 1, 0)
    value = jnp.where((quadrant & 1) == 1, cosine, sine)
    value = jnp.where((quadrant & 2) == 2, -value, value)
    return value.astype(bf16).astype(f32)


def swap_lanes(value):
    return pltpu.roll(value, WAVE, 1)


def gelu_parts(value):
    t = 1.0 / (1.0 + (0.3275911 * math.sqrt(0.5)) * jnp.abs(value))
    bell = jnp.exp2(value * value * (-0.5 * math.log2(math.e)))
    half_tail = bell * t * (
        0.127414796 + t * (-0.142248368 + t * (0.7107068705 + t * (-0.7265760135 + t * 0.5307027145)))
    )
    return jnp.where(value >= 0, 1.0 - half_tail, half_tail), bell * (1.0 / math.sqrt(2.0 * math.pi))


def row_mean(value):
    return jnp.mean(value, axis=-1, keepdims=True)


ROWS = 256
BLOCK = 768
PIECE = 48
HALF = BLOCK // 2
SMALL = 512
STREAMS = 12
VECTORS = 6
LEVEL_FIRST = 7


def widths(width, ff):
    return 3 * width // 16, ff // 16, width // 16


class Route:
    def __init__(self):
        chip = lax.axis_index("fsdp")
        self.core = lax.axis_index("rep")
        self.level, self.me = chip // 4, chip % 4
        near_step, far_step = 1 + self.core, 2 - self.core
        near_move = near_step * (1 - 2 * ((self.me // near_step) % 2))
        far_move = far_step * (1 - 2 * ((self.me // far_step) % 2))
        self.near = self.me + near_move
        self.far = self.me + far_move
        self.across = self.me + near_move + far_move

    def chip(self, level, place):
        return level * 4 + place

    def levels(self):
        return [(self.level + k) % 4 for k in range(1, 4)]

    def peers(self):
        chips = [self.chip(level, self.me) for level in self.levels()]
        chips += [self.chip(self.level, self.near), self.chip(self.level, self.far)]
        return [(chip, self.core) for chip in chips] + [(self.chip(self.level, self.me), 1 - self.core)]


def remote(source, target, send, recv, chip, core):
    return pltpu.make_async_remote_copy(
        src_ref=source, dst_ref=target, send_sem=send, recv_sem=recv,
        device_id=(chip, core), device_id_type=pl.DeviceIdType.MESH,
    )


def half_columns(half, size):
    return pl.ds(pl.multiple_of(half * size, size), size)


class Streams:
    def __init__(self, held, stage, final, sems):
        self.held = held
        self.upper = held.at[: 8 * BLOCK].reshape(8, 4, 4, PIECE, BLOCK)
        self.lower = held.at[8 * BLOCK :].reshape(4, 4, 4, PIECE, BLOCK)
        self.stage = stage.reshape(STREAMS, 4, 4, PIECE, BLOCK)
        self.final = final
        self.gather_recv, self.gather_send, self.sum_recv, self.sum_send, self.final_sem = sems

    def on(self, stream, act):
        if isinstance(stream, int):
            act(self.upper.at[stream] if stream < 8 else self.lower.at[:, :, stream - 8])
        else:
            pl.when(stream < 8)(lambda: act(self.upper.at[stream]))
            pl.when(stream >= 8)(lambda: act(self.lower.at[:, :, stream - 8]))

    def half(self, half):
        return half_columns(half, HALF)

    def several(self, pieces):
        return self.held.at[: PIECE * pieces, :HALF]

    def landing(self, stream, kind):
        block = self.stage.at[(stream + 8) % STREAMS]
        if kind == 0:
            return block.at[:, :, :, :HALF]
        return block.at[(0, 0, 2, 3)[kind] : (0, 2, 3, 4)[kind], :, :, HALF:]

    def result(self, stream, half):
        return self.final.at[pl.ds(pl.multiple_of(stream * PIECE, 16), PIECE), self.half(half)]

    def results(self, last):
        return self.final.at[:PIECE, :HALF] if last else self.final.at[PIECE:, :HALF]


class Vectors:
    def __init__(self, held, stage, final, sems):
        self.held, self.flat, self.final = held, stage, final
        self.shards = held.reshape(4, 4, 8, SMALL)
        self.stage = stage.reshape(8, 4, 8, SMALL // 2)
        self.gather_recv, self.gather_send, self.sum_recv, self.sum_send, self.final_sem = sems

    def on(self, stream, act):
        act(self.shards)

    def half(self, half):
        return half_columns(half, SMALL // 2)

    def several(self, pieces):
        if pieces <= 16:
            return self.held.at[: 8 * pieces, : SMALL // 2]
        return self.flat.at[: 8 * pieces, :]

    def landing(self, stream, kind):
        return self.stage.at[(0, 4, 6, 7)[kind] : (4, 6, 7, 8)[kind]]

    def result(self, stream, half):
        return self.final.at[:, self.half(half)]

    def results(self, last):
        return self.final.at[:, : SMALL // 2]


def drain(view, sem):
    pltpu.make_async_copy(view, view, sem).wait()


class Exchange:
    def __init__(self, route, parts):
        self.route, self.parts = route, parts

    def send(self, source, target, send, recv, level, place, core):
        remote(source, target, send, recv, self.route.chip(level, place), core).start()


    def share(self, stream, view, place, kind):
        p, r = self.parts, self.route
        self.send(
            view, view, p.gather_send.at[stream, 0], p.gather_recv.at[stream, kind], r.level, place, r.core
        )

    def hand_over(self, stream, view):
        p, r = self.parts, self.route
        self.send(
            view, view, p.gather_send.at[stream, 1], p.gather_recv.at[stream, 3], r.level, r.me, 1 - r.core
        )

    def gather_own(self, stream):
        p, r = self.parts, self.route

        def act(shards):
            view = shards.at[r.level, r.me, :, p.half(r.core)]
            for level in r.levels():
                self.send(
                    view, view, p.gather_send.at[stream, 0], p.gather_recv.at[stream, 0], level, r.me, r.core
                )

        p.on(stream, act)

    def gather_column(self, stream):
        p, r = self.parts, self.route
        drain(p.several(3), p.gather_recv.at[stream, 0])

        def act(shards):
            view = shards.at[:, r.me, :, p.half(r.core)]
            self.share(stream, view, r.near, 1)
            self.share(stream, view, r.far, 2)
            for level in r.levels():
                self.hand_over(stream, shards.at[level, r.me, :, p.half(r.core)])

        p.on(stream, act)

    def gather_near(self, stream):
        p, r = self.parts, self.route
        drain(p.several(4), p.gather_recv.at[stream, 1])

        def act(shards):
            view = shards.at[:, r.near, :, p.half(r.core)]
            self.share(stream, view, r.far, 2)
            self.hand_over(stream, view)

        p.on(stream, act)

    def gather_far(self, stream):
        p, r = self.parts, self.route
        drain(p.several(8), p.gather_recv.at[stream, 2])

        def act(shards):
            for place in (r.far, r.across):
                self.hand_over(stream, shards.at[:, place, :, p.half(r.core)])

        p.on(stream, act)


    def level_own(self, stream):
        p, r = self.parts, self.route

        def act(shards):
            view = shards.at[r.level, r.me, :, p.half(r.core)]
            self.share(stream, view, r.near, 1)
            self.share(stream, view, r.far, 2)

        p.on(stream, act)

    def level_near(self, stream):
        p, r = self.parts, self.route
        drain(p.several(1), p.gather_recv.at[stream, 1])

        def act(shards):
            view = shards.at[r.level, r.near, :, p.half(r.core)]
            self.share(stream, view, r.far, 2)
            self.hand_over(stream, view)

        p.on(stream, act)

    def level_far(self, stream):
        p, r = self.parts, self.route
        drain(p.several(2), p.gather_recv.at[stream, 2])

        def act(shards):
            view = shards.at[r.level, :, :, p.half(r.core)]
            for level in r.levels():
                self.send(
                    view, view, p.gather_send.at[stream, 0], p.gather_recv.at[stream, 0], level, r.me, r.core
                )
            for place in (r.far, r.across):
                self.hand_over(stream, shards.at[r.level, place, :, p.half(r.core)])

        p.on(stream, act)

    def level_column(self, stream):
        p, r = self.parts, self.route
        drain(p.several(12), p.gather_recv.at[stream, 0])

        def act(shards):
            for level in r.levels():
                self.hand_over(stream, shards.at[level, :, :, p.half(r.core)])

        p.on(stream, act)

    def gathered(self, stream):
        p = self.parts
        drain(p.several(15), p.gather_recv.at[stream, 3])

    def gather_sent(self, stream):
        p = self.parts
        drain(p.several(15), p.gather_send.at[stream, 0])
        drain(p.several(15), p.gather_send.at[stream, 1])


    def pass_on(self, stream, view, landing, kind, level, place):
        p, r = self.parts, self.route
        self.send(view, landing, p.sum_send.at[stream], p.sum_recv.at[stream, kind], level, place, r.core)

    def sum_cores(self, stream):
        p, r = self.parts, self.route

        def act(shards):
            self.send(
                shards.at[:, :, :, p.half(1 - r.core)], p.landing(stream, 0),
                p.sum_send.at[stream], p.sum_recv.at[stream, 0], r.level, r.me, 1 - r.core,
            )

        p.on(stream, act)

    def sum_far(self, stream):
        p, r = self.parts, self.route
        drain(p.several(16), p.sum_recv.at[stream, 0])
        landed, target = p.landing(stream, 0), p.landing(stream, 1)

        def act(shards):
            def add(place):
                view = shards.at[:, place, :, p.half(r.core)]
                view[...] += landed[:, place]
                return view

            for index, place in enumerate((r.far, r.across)):
                self.pass_on(stream, add(place), target.at[index], 1, r.level, r.far)
            for place in (r.me, r.near):
                add(place)

        p.on(stream, act)

    def sum_near(self, stream):
        p, r = self.parts, self.route
        drain(p.several(8), p.sum_recv.at[stream, 1])
        landed, target = p.landing(stream, 1), p.landing(stream, 2)

        def act(shards):
            view = shards.at[:, r.near, :, p.half(r.core)]
            view[...] += landed[1]
            self.pass_on(stream, view, target.at[0], 2, r.level, r.near)
            view = shards.at[:, r.me, :, p.half(r.core)]
            view[...] += landed[0]

        p.on(stream, act)

    def sum_column(self, stream):
        p, r = self.parts, self.route
        drain(p.several(4), p.sum_recv.at[stream, 2])
        landed, target = p.landing(stream, 2), p.landing(stream, 3)

        def act(shards):
            view = shards.at[:, r.me, :, p.half(r.core)]
            view[...] += landed[0]
            for index, level in enumerate(r.levels()):
                self.pass_on(
                    stream, shards.at[level, r.me, :, p.half(r.core)], target.at[0, index], 3, level, r.me
                )

        p.on(stream, act)

    def sum_end(self, stream):
        p, r = self.parts, self.route
        drain(p.several(3), p.sum_recv.at[stream, 3])
        landed = p.landing(stream, 3)
        view = p.result(stream, r.core)

        def act(shards):
            total = shards[r.level, r.me, :, p.half(r.core)].astype(f32)
            for index in range(3):
                total += landed[0, index].astype(f32)
            view[...] = total

        p.on(stream, act)
        last = 1 if isinstance(stream, int) and stream == 0 else 0
        self.send(view, view, p.final_sem.at[last, 0], p.final_sem.at[last, 1], r.level, r.me, 1 - r.core)

    def summed(self, stream):
        p = self.parts
        drain(p.several(31), p.sum_send.at[stream])

    def results_in(self, last):
        p = self.parts
        for side in range(2):
            drain(p.results(last), p.final_sem.at[last, side])


def owner_tables(start, share, depth, order=None):
    col = lax.broadcasted_iota(jnp.int32, (1, BLOCK), 1) + start
    source = col if order is None else order(col)
    owner, entry = source // share, source % share
    pick = (entry == lax.broadcasted_iota(jnp.int32, (depth, BLOCK), 0)).astype(bf16)
    row = lax.broadcasted_iota(jnp.int32, (128, BLOCK), 0)
    return pick, owner == (row >> 3), row & 7


def quad_order(col):
    return (col % BLOCK) // QUAD * BLOCK + col // BLOCK * QUAD + col % QUAD


def layer_kernel(comm, *refs):
    refs = list(refs)

    def take(count):
        taken, refs[:] = refs[:count], refs[count:]
        return taken

    tok_in, cot_in, coords_in, segs_in = take(4)
    if comm:
        w_qkv_in, w_out_in, w_up_in, w_down_in = take(4)
        small_in = take(9)
    else:
        held_in, w_box_in, b_qkv_in, b_up_in, vectors_in = take(5)
    layer_out, g_tok_out, e_hbm = take(3)
    if comm:
        final_out, small_out = take(2)
    else:
        g_held, g_w_box_out, g_b_qkv_out, g_b_up_out, g_vectors_out = take(5)
    (held, stage, slope, q8t, k8t, v_row, ctx_t, wave_t, wave_r, e_buf, normed, total, flip, g_down, tok_t, g_ctx_t,
     inv_one, inv_total, w_box, w_box_t, b_qkv, b_up, vectors, g_w_box, g_b_qkv, g_b_up, g_vectors, e_sem, io_sem, coords, segs, w_pair, w_pair_t) = take(33)
    if comm:
        final, small, small_stage, g_small, small_final, mid_sem = take(6)
        small_held = take(9)
        block_sems, small_sems, small_final_sems = take(5), take(4), take(1)

    count, width = tok_t.shape[1], tok_t.shape[0]
    ff = slope.shape[0] // count * BLOCK
    slots, pairs = count // SLOT, HEADS // 2
    row_blocks = count // ROWS
    up_blocks = ff // BLOCK
    quads = pairs // 2
    ctx, low, cot, tok = [stage.at[part * count : (part + 1) * count] for part in range(4)]
    act = stage.at[STREAMS * BLOCK - up_blocks * count :]
    up_at, down_at = 4 * BLOCK, 8 * BLOCK

    def copy_in(source, target, index=0):
        return pltpu.make_async_copy(source, target, io_sem.at[index])

    tok_copy = copy_in(tok_in, tok, 0)
    cot_copy = copy_in(cot_in, cot, 1)
    coord_copy = copy_in(coords_in, coords, 2)
    seg_copy = copy_in(segs_in, segs, 3)

    if comm:
        route = Route()
        chip = route.chip(route.level, route.me)
        blocks = Exchange(route, Streams(held, stage, final, block_sems))
        extras = Exchange(route, Vectors(small, small_stage, small_final, [*small_sems, *small_final_sems]))
        sums = Exchange(route, Vectors(g_small, small_stage, small_final, [*small_sems, *small_final_sems]))
        barrier = pltpu.get_barrier_semaphore()
        for peer, core in route.peers():
            pl.semaphore_signal(barrier, inc=1, device_id=(peer, core), device_id_type=pl.DeviceIdType.MESH)
        moves = []
        for quad in range(quads):
            for part in range(3):
                moves.append((
                    w_qkv_in.at[:, part * width + quad * QUAD : part * width + (quad + 1) * QUAD],
                    total.at[quad * PIECE : (quad + 1) * PIECE, part * QUAD : (part + 1) * QUAD],
                ))
        moves.append((w_out_in, total.at[3 * PIECE : 4 * PIECE]))
        for block in range(up_blocks):
            moves.append((
                w_up_in.at[:, block * BLOCK : (block + 1) * BLOCK],
                total.at[(4 + block) * PIECE : (5 + block) * PIECE],
            ))
        moves.append((w_down_in, total.at[8 * PIECE : 12 * PIECE]))
        moves += list(zip(small_in, small_held))
        moves = [copy_in(source, target, 4 + index) for index, (source, target) in enumerate(moves)]
        first = 3 * quads
        for copy in moves[:first] + moves[first + 1 + up_blocks + 1 :] + moves[first : first + 1 + up_blocks + 1]:
            copy.start()
        for copy in (coord_copy, seg_copy, tok_copy, cot_copy):
            copy.start()

        def round_block(block):
            at = pl.ds(pl.multiple_of(block * BLOCK + PIECE * chip, 16), PIECE)
            held[at, :] = total[block * PIECE : (block + 1) * PIECE, :].astype(bf16)

        g_small[:8, :] = jnp.zeros((8, SMALL), f32)
        for copy in moves[:first]:
            copy.wait()
        for block in range(quads):
            round_block(block)
        for copy in moves[first + 1 + up_blocks + 1 :]:
            copy.wait()
        g_small[:8, :HD] = small_held[8][...].astype(bf16).astype(f32)
        for row in range(8):
            value = small_held[row][...].astype(bf16).astype(f32)
            g_small[row : row + 1, 128 : 128 + value.shape[1]] = value
        small[pl.ds(pl.multiple_of(chip * 8, 8), 8), :] = g_small[:8, :]
        pl.semaphore_wait(barrier, 6)
        extras.gather_own(0)
        for stream in range(quads):
            blocks.gather_own(stream)
        for copy in moves[first : first + 1 + up_blocks + 1]:
            copy.wait()
        for block in range(quads, STREAMS - up_blocks):
            round_block(block)
        at = pl.ds(pl.multiple_of(down_at + 4 * PIECE * chip, 16), 4 * PIECE)
        held[at, :] = total[8 * PIECE : 12 * PIECE, :].astype(bf16)
        blocks.level_own(LEVEL_FIRST)
        for stream in range(quads, STREAMS):
            if stream != LEVEL_FIRST:
                blocks.gather_own(stream)
    else:
        for copy in (coord_copy, seg_copy, tok_copy, cot_copy):
            copy.start()
        copy_in(held_in, held, 4).start()
        w_box[...] = w_box_in[...]
        b_qkv[...] = b_qkv_in[...]
        b_up[...] = b_up_in[...]
        vectors[...] = vectors_in[...]

    coord_copy.wait()
    seg_copy.wait()
    wave_t[...] = wave_rows(coords[...])
    wave_r[...] = jnp.transpose(wave_t[...])
    for slot in range(slots):
        seg_i = jnp.broadcast_to(segs[:, slot * SLOT : (slot + 1) * SLOT].astype(f32), (SLOT, SLOT))
        seg_j = jnp.transpose(seg_i)
        normed[slot * SLOT : (slot + 1) * SLOT, :SLOT] = jnp.where(seg_i == seg_j, 0.0, neg_large)
    g_w_box[...] = jnp.zeros_like(g_w_box)
    g_b_up[...] = jnp.zeros_like(g_b_up)
    g_vectors[...] = jnp.zeros_like(g_vectors)
    tok_copy.wait()

    if comm:
        extras.gather_column(0)
        blocks.gather_column(0)
        extras.gather_near(0)
        blocks.gather_near(0)
        blocks.gather_column(1)
        extras.gather_far(0)
        blocks.gather_far(0)
        blocks.gather_near(1)
        blocks.gather_column(2)
        blocks.level_near(LEVEL_FIRST)
        extras.gathered(0)
        table = small[...].astype(bf16)
        w_box[...] = table[:, :HD]
        share_qkv, share_up, share = widths(width, ff)
        for row, columns, share_of, depth, order, target in (
            (0, 3 * width, share_qkv, 256, quad_order, b_qkv),
            (1, ff, share_up, 256, None, b_up),
            (None, width, share, 128, None, vectors),
        ):
            @pl.loop(0, columns // BLOCK)
            def _(block):
                pick, owned, row_of = owner_tables(block * BLOCK, share_of, depth, order)
                spread = dot_nn(table[:, 128 : 128 + depth], pick)
                keep = owned if row is None else owned & (row_of == row)
                rows = jnp.sum(jnp.where(keep, spread, 0.0).reshape(16, 8, BLOCK), axis=0)
                target[:, aligned(block, BLOCK)] = rows if row is None else jnp.sum(rows, axis=0, keepdims=True)

    else:
        copy_in(held_in, held, 4).wait()
    w_box_t[...] = jnp.transpose(w_box[...].astype(f32)).astype(bf16)
    blank = jnp.zeros((2 * WAVE, HD), bf16)
    w_pair_t[: 2 * WAVE, :] = jnp.concatenate([w_box[...], blank], axis=1)
    w_pair_t[2 * WAVE :, :] = jnp.concatenate([blank, w_box[...]], axis=1)
    w_pair[...] = jnp.transpose(w_pair_t[...].astype(f32)).astype(bf16)

    def gather_tick(step):
        if not comm:
            return

        def stream_of(order):
            return order + order // LEVEL_FIRST

        for ahead, act_on in ((1, blocks.gather_near), (3, blocks.gather_column), (0, blocks.gather_far)):
            order = step + ahead
            if isinstance(order, int):
                if order < STREAMS - 1:
                    act_on(stream_of(order))
            else:
                pl.when(order < STREAMS - 1)(functools.partial(act_on, stream_of(order)))

    def need(stream):
        if comm:
            blocks.gathered(stream)

    b_out, gain_one, shift_one, b_down, gain_two, shift_two = [vectors[2 + i : 3 + i, :] for i in range(VECTORS)]
    lane = lax.broadcasted_iota(jnp.int32, (SLOT, PAIR), 1)
    scores = total.reshape(2, SLOT, width)

    def project(quad, slot):
        rows = tok[aligned(slot, SLOT), :]

        def columns(part):
            weight = held[aligned(quad, BLOCK), part * QUAD : (part + 1) * QUAD]
            shift = b_qkv[:, pl.ds(pl.multiple_of(quad * BLOCK + part * QUAD, QUAD), QUAD)]
            return (dot_nn(rows, weight) + shift).astype(bf16)

        q, k, v = columns(0), columns(1), columns(2)
        low[aligned(slot, SLOT), aligned(quad, QUAD)] = k
        flip[aligned(quad, QUAD), aligned(slot, SLOT)] = jnp.transpose(v.astype(f32)).astype(bf16)
        qt = jnp.transpose(q.astype(f32) * scale_factor).astype(bf16)
        kt = jnp.transpose(k.astype(f32) * scale_factor).astype(bf16)
        for part in range(2):
            here = slice(part * PAIR, (part + 1) * PAIR)
            q8t[slot, quad * 2 + part] = qt[here]
            k8t[slot, quad * 2 + part] = kt[here]
            v_row[slot, quad * 2 + part] = v[:, here]

    def e_copy(place, head, index, out):
        pair = (e_buf.at[place, head], e_hbm.at[index])
        return pltpu.make_async_copy(*(pair if out else pair[::-1]), e_sem.at[place, head])

    def attend(step):
        pair, slot = step // slots, step % slots
        cols = aligned(slot, SLOT)
        place = step % 2

        @pl.when(step >= 2)
        def _():
            for head in range(2):
                e_copy(place, head, 0, True).wait()

        sine_t, cosine_t = wave_t[:WAVE, cols], wave_t[WAVE:, cols]
        sc_t = (wave_t[:, cols] * scale_factor).astype(bf16)
        sc_r = wave_r[cols, :]
        cs_r = swap_lanes(sc_r)
        cc_r = jnp.where(lane < WAVE, cs_r, sc_r)
        ss_r = jnp.where(lane < WAVE, sc_r, -cs_r)
        cs_low = cs_r.astype(bf16)
        keys = low[cols, aligned(pair, PAIR)]
        queries = q8t[slot, pair]
        key_box = dot_nn(keys, w_pair[...])
        query_box = dot_nn(w_pair_t[...], queries)
        low_exps, inverse, heads_t = [], [], []
        for head in range(2):
            here = slice(head * 2 * WAVE, (head + 1) * 2 * WAVE)
            side = key_box[:, here]
            k_side = (side * cc_r + swap_lanes(side) * ss_r).astype(bf16)
            first, second = query_box[here][:WAVE], query_box[here][WAVE:]
            q_side = jnp.concatenate(
                [first * sine_t + second * cosine_t, second * sine_t - first * cosine_t], axis=0
            ).astype(bf16)
            q_t = queries[head * HD : (head + 1) * HD]
            zero = jnp.zeros_like(q_t)
            q_pair = [q_t, zero] if head == 0 else [zero, q_t]
            k_full = jnp.concatenate([keys, cs_low, k_side], axis=1)
            q_full = jnp.concatenate(q_pair + [q_side, sc_t], axis=0)
            scores[head, :, :SLOT] = dot_nn(k_full, q_full) + normed[cols, :SLOT]
        for head in range(2):
            masked = scores[head, :, :SLOT]
            exps = jnp.exp(masked - jnp.max(masked, axis=0, keepdims=True))
            inverse.append(1.0 / jnp.sum(exps, axis=0, keepdims=True))
            low_exps.append(exps.astype(bf16))
            e_buf[place, head] = low_exps[head]
            e_copy(place, head, step * 2 + head, True).start()
            inv_total[step * 2 + head] = inverse[head]
        for head in range(2):
            at = pl.ds(pl.multiple_of(pair * PAIR + head * HD, HD), HD)
            heads_t.append(dot_nn(flip[at, cols], low_exps[head]) * inverse[head])
        both = jnp.concatenate(heads_t, axis=0)
        ctx_t[aligned(pair, PAIR), cols] = both.astype(bf16)
        ctx[cols, aligned(pair, PAIR)] = jnp.transpose(both).astype(bf16)

    steps = slots * pairs
    quad_steps = 2 * slots

    @pl.loop(0, quads)
    def _(quad):
        need(quad)

        @pl.loop(0, slots)
        def _(slot):
            project(quad, slot)

        @pl.loop(0, quad_steps)
        def _(inner):
            step = quad * quad_steps + inner
            if comm:
                @pl.when(step == 1)
                def _():
                    blocks.gather_column(quads)
                    blocks.level_far(LEVEL_FIRST)

                pl.when((step % 2 == 0) & (step > 0))(functools.partial(gather_tick, step // 2))
            attend(step)

    for place in range(2):
        for head in range(2):
            e_copy(place, head, 0, True).wait()

    def column_sum(value):
        return jnp.sum(value, axis=0, keepdims=True)

    need(3)
    gather_tick(6)

    @pl.loop(0, row_blocks)
    def _(block):
        rows = aligned(block, ROWS)
        token_rows = tok[rows, :].astype(f32)
        tok_t[:, rows] = jnp.transpose(token_rows).astype(bf16)
        pre = token_rows + dot_nn(ctx[rows, :], held[3 * BLOCK : 4 * BLOCK, :]) + b_out
        center = pre - row_mean(pre)
        invdev = lax.rsqrt(row_mean(center * center) + eps_norm)
        unit = center * invdev
        inv_one[rows, :] = jnp.broadcast_to(invdev, (ROWS, 128))
        normed[rows, :] = unit
        hidden = unit * gain_one + shift_one
        low[rows, :] = hidden.astype(bf16)
        flip[:, rows] = jnp.transpose(hidden).astype(bf16)

    @pl.loop(0, up_blocks)
    def _(block):
        gather_tick(7 + block)
        if comm:
            pl.when(block == 2)(functools.partial(blocks.level_column, LEVEL_FIRST))
        need(4 + block)

        weight = held[pl.ds(pl.multiple_of(up_at + block * BLOCK, BLOCK), BLOCK), :]
        for row in range(row_blocks):
            rows = slice(row * ROWS, (row + 1) * ROWS)
            total[rows, :] = dot_nn(low[rows, :], weight) + b_up[:, aligned(block, BLOCK)]
        for row in range(row_blocks):
            at = pl.ds(pl.multiple_of(block * count + row * ROWS, ROWS), ROWS)
            up = total[row * ROWS : (row + 1) * ROWS, :]
            cdf, pdf = gelu_parts(up)
            act[at, :] = (up * cdf).astype(bf16)
            slope[at, :] = (cdf + up * pdf).astype(bf16)

    for block in range(up_blocks):
        need(8 + block)
    cot_copy.wait()

    @pl.loop(0, row_blocks)
    def _(block):
        rows = aligned(block, ROWS)
        pre = normed[rows, :] * gain_one + shift_one + b_down
        for part in range(up_blocks):
            at = pl.ds(pl.multiple_of(part * count + block * ROWS, ROWS), ROWS)
            pre += dot_nn(act[at, :], held[down_at + part * BLOCK : down_at + (part + 1) * BLOCK, :])
        center = pre - row_mean(pre)
        invdev = lax.rsqrt(row_mean(center * center) + eps_norm)
        unit = center * invdev
        grad = cot[rows, :].astype(f32)
        cot[rows, :] = (unit * gain_two + shift_two).astype(bf16)
        scaled = grad * gain_two
        g_pre = invdev * (scaled - row_mean(scaled) - unit * row_mean(scaled * unit))
        total[rows, :] = g_pre
        low_pre = g_pre.astype(bf16)
        g_down[rows, :] = low_pre
        g_vectors[5:6, :] += column_sum(low_pre.astype(f32))
        g_vectors[6:7, :] += column_sum(grad * unit)
        g_vectors[7:8, :] += column_sum(grad)

    out_copy = pltpu.make_async_copy(cot, layer_out, io_sem.at[0])
    out_copy.start()
    if comm:
        for stream in range(STREAMS):
            blocks.gather_sent(stream)
        extras.gather_sent(0)

    def last(step):
        turn = step // 4
        return STREAMS - 1 - step + (14 - 6 * turn) * turn - 4

    def sum_start(step):
        if comm:
            blocks.sum_cores(last(step))

    def sum_tick(step, stages=(0, 1, 2, 3)):
        if not comm:
            return
        acts = (blocks.sum_far, blocks.sum_near, blocks.sum_column, blocks.sum_end)
        for behind in stages:
            at = step - behind
            if isinstance(at, int):
                if 0 <= at < STREAMS:
                    acts[behind](last(at))
            else:
                pl.when((at >= 0) & (at < STREAMS))(functools.partial(acts[behind], last(at)))

    def meet(sem):
        if comm:
            for peer, core in route.peers():
                pl.semaphore_signal(sem, inc=1, device_id=(peer, core), device_id_type=pl.DeviceIdType.MESH)
            pl.semaphore_wait(sem, 6)

    out_copy.wait()
    if comm:
        meet(mid_sem.at[0])

    @pl.loop(0, up_blocks)
    def _(index):
        block = up_blocks - 1 - index
        down_rows = pl.ds(pl.multiple_of(down_at + block * BLOCK, BLOCK), BLOCK)
        up_rows = pl.ds(pl.multiple_of(up_at + block * BLOCK, BLOCK), BLOCK)
        for row in range(2):
            rows = slice(row * (count // 2), (row + 1) * (count // 2))
            at = pl.ds(pl.multiple_of(block * count + row * (count // 2), count // 2), count // 2)
            g_act = dot_nt(g_down[rows, :], held[down_rows, :])
            g_up = (g_act * slope[at, :].astype(f32)).astype(bf16)
            slope[at, :] = g_up
            g_b_up[:, aligned(block, BLOCK)] += column_sum(g_up.astype(f32))
            total[rows, :] += dot_nt(g_up, held[up_rows, :])
        sum_tick(index - 1, (0,))
        sum_tick(index - 1, (1, 2, 3))
        g_up = slope[aligned(block, count), :]
        for part in range(2):
            at = pl.ds(pl.multiple_of(up_at + block * BLOCK + part * HALF, HALF), HALF)
            held[at, :] = dot_nn(flip[part * HALF : (part + 1) * HALF, :], g_up).astype(bf16)
        sum_start(index)
        for part in range(2):
            at = pl.ds(pl.multiple_of(down_at + block * BLOCK + part * HALF, HALF), HALF)
            grads = dot_tn(act[aligned(block, count), part * HALF : (part + 1) * HALF], g_down[...])
            held[at, :] = grads.astype(bf16)

    if comm:
        meet(mid_sem.at[1])
    sum_tick(3)
    for step in range(up_blocks):
        sum_start(up_blocks + step)

    @pl.loop(0, row_blocks)
    def _(block):
        rows = aligned(block, ROWS)
        grad, unit = total[rows, :], normed[rows, :]
        scaled = grad * gain_one
        g_pre = inv_one[rows, :1] * (scaled - row_mean(scaled) - unit * row_mean(scaled * unit))
        total[rows, :] = g_pre
        low_pre = g_pre.astype(bf16)
        g_down[rows, :] = low_pre
        g_vectors[2:3, :] += column_sum(low_pre.astype(f32))
        g_vectors[3:4, :] += column_sum(grad * unit)
        g_vectors[4:5, :] += column_sum(grad)

    for part in range(2):
        rows = slice(part * (count // 2), (part + 1) * (count // 2))
        g_ctx_t[:, rows] = dot_nt(held[3 * BLOCK : 4 * BLOCK, :], g_down[rows, :]).astype(bf16)
    for part in range(2):
        at = slice(3 * BLOCK + part * HALF, 3 * BLOCK + (part + 1) * HALF)
        held[at, :] = dot_nn(ctx_t[part * HALF : (part + 1) * HALF, :], g_down[...]).astype(bf16)

    sum_start(8)
    sum_tick(4)

    def fold(block, row, share_of, source, order=None):
        pick, owned, row_of = owner_tables(block * BLOCK, share_of, 256, order)
        keep = owned if row is None else owned & (row_of == row)
        wide = 1 if row is not None else 8
        full = source[:, aligned(block, BLOCK)].reshape(1, wide, BLOCK)
        spread = jnp.broadcast_to(full, (16, 8, BLOCK)).reshape(128, BLOCK)
        spread = jnp.where(keep, spread, 0.0)
        upper = spread.astype(bf16)
        g_small[:, 128:384] += dot_nt(upper, pick) + dot_nt((spread - upper.astype(f32)).astype(bf16), pick)

    if comm:
        g_small[...] = jnp.zeros_like(g_small)
        share_qkv, share_up, share = widths(width, ff)

        @pl.loop(0, up_blocks)
        def _(block):
            fold(block, 1, share_up, g_b_up)

        fold(0, None, share, g_vectors)

    def e_step(order):
        quad = quads - 1 - order // quad_steps
        return quad * quad_steps + order % quad_steps

    def fetch(order):
        for head in range(2):
            e_copy(order % 2, head, e_step(order) * 2 + head, False).start()

    fetch(0)
    ones = jnp.ones((16, count), bf16)

    def attend_back(order):
        step = e_step(order)
        pair, slot = step // slots, step % slots
        cols = aligned(slot, SLOT)
        place = order % 2

        @pl.when(order + 1 < steps)
        def _():
            fetch(order + 1)

        for head in range(2):
            e_copy(place, head, 0, False).wait()
        sine_t, cosine_t = wave_t[:WAVE, cols], wave_t[WAVE:, cols]
        sc_t = (wave_t[:, cols] * scale_factor).astype(bf16)
        cs_t = (jnp.concatenate([cosine_t, sine_t], axis=0) * scale_factor).astype(bf16)
        values = v_row[slot, pair]
        g_lows, row_dots, g_probs, g_scores, g_qs, g_ks = [], [], [], [], [], []
        g_parts = [[], [], []]
        spans = [slice(head * HD, (head + 1) * HD) for head in range(2)]
        for head in range(2):
            at = pl.ds(pl.multiple_of(pair * PAIR + head * HD, HD), HD)
            g_rows = g_ctx_t[at, cols].astype(f32) * inv_total[step * 2 + head]
            row_dots.append(jnp.sum(g_rows * ctx_t[at, cols].astype(f32), axis=0, keepdims=True))
            g_lows.append(g_rows.astype(bf16))
            zero = jnp.zeros_like(g_lows[head])
            g_pair = jnp.concatenate([g_lows[head], zero] if head == 0 else [zero, g_lows[head]], axis=0)
            g_probs.append(dot_nn(values, g_pair))
        for head in range(2):
            g_scores.append((e_buf[place, head].astype(f32) * (g_probs[head] - row_dots[head])).astype(bf16))
        for head in range(2):
            g_qs.append(dot_nn(jnp.concatenate([k8t[slot, pair, spans[head], :], cs_t], axis=0), g_scores[head]))
        for head in range(2):
            g_ks.append(dot_nt(jnp.concatenate([q8t[slot, pair, spans[head], :], sc_t], axis=0), g_scores[head]))
        for head in range(2):
            g_parts[2].append(dot_nt(g_lows[head], e_buf[place, head]))
        for head in range(2):
            k_t, q_t = k8t[slot, pair, spans[head], :], q8t[slot, pair, spans[head], :]
            g_q, g_k = g_qs[head], g_ks[head]
            first, second = g_q[HD : HD + WAVE], g_q[HD + WAVE :]
            g_qbox = jnp.concatenate(
                [first * sine_t - second * cosine_t, first * cosine_t + second * sine_t], axis=0
            ).astype(bf16)
            first, second = g_k[HD : HD + WAVE], g_k[HD + WAVE :]
            g_kbox = jnp.concatenate(
                [first * cosine_t - second * sine_t, first * sine_t + second * cosine_t], axis=0
            ).astype(bf16)
            g_parts[0].append(g_q[:HD] + dot_nn(w_box_t[...], g_qbox))
            g_parts[1].append(g_k[:HD] + dot_nn(w_box_t[...], g_kbox))
            g_w_box[...] += dot_nt(g_qbox, q_t) + dot_nt(g_kbox, k_t)
        for part in range(3):
            at = pl.ds(pl.multiple_of(part * QUAD + pair % 2 * PAIR, PAIR), PAIR)
            flip[at, cols] = jnp.concatenate(g_parts[part], axis=0).astype(bf16)

    kept = [slope.at[(2 + turn) * count : (2 + turn) * count + BLOCK] for turn in range(2)]
    kept_last = g_down.at[:BLOCK]

    @pl.loop(0, quads)
    def _(turn):
        quad = quads - 1 - turn

        @pl.loop(0, quad_steps)
        def _(inner):
            order = turn * quad_steps + inner
            if comm:
                pl.when(order % 2 == 1)(functools.partial(sum_tick, 5 + order // 2, (0,)))
                pl.when((order % 2 == 0) & (order > 0))(functools.partial(sum_tick, 4 + order // 2, (1, 2, 3)))
            attend_back(order)

        if comm:
            pl.when(turn == quads - 1)(functools.partial(sum_tick, 10, (1, 2, 3)))

        @pl.when(turn < quads - 1)
        def _():
            at = pl.ds(pl.multiple_of((2 + turn) * count, count), BLOCK)
            slope[at, :] = held[aligned(quad, BLOCK), :]

        @pl.when(turn == quads - 1)
        def _():
            kept_last[...] = held[aligned(quad, BLOCK), :]

        for part in range(2):
            at = pl.ds(pl.multiple_of(quad * BLOCK + part * HALF, HALF), HALF)
            held[at, :] = dot_nt(tok_t[part * HALF : (part + 1) * HALF, :], flip[...]).astype(bf16)
        sum_start(9 + turn)
        g_b_qkv[:, aligned(quad, BLOCK)] = dot_nt(ones, flip[...])[:1]
        if comm:
            fold(quad, 0, share_qkv, g_b_qkv, quad_order)

        @pl.when(turn < quads - 1)
        def _():
            for block in range(row_blocks):
                at = pl.ds(pl.multiple_of(turn * count + block * ROWS, ROWS), ROWS)
                rows = slice(block * ROWS, (block + 1) * ROWS)
                slope[at, :] = jnp.transpose(flip[:, rows].astype(f32)).astype(bf16)

    g_w_box[...] = g_w_box[...] * (1.0 / scale_factor)
    tok_out = []

    def token_grad(block):
        rows = slice(block * ROWS, (block + 1) * ROWS)
        last_part = jnp.transpose(dot_nn(kept_last[...], flip[:, rows]))
        first_part = dot_nt(slope[rows, :], kept[0][...])
        rest = dot_nt(slope[count + rows.start : count + rows.stop, :], kept[1][...])
        total[rows, :] += last_part + first_part + rest
        tok_out.append(pltpu.make_async_copy(total.at[rows], g_tok_out.at[rows], io_sem.at[4 + block]))
        tok_out[-1].start()

    if comm:
        g_small[:, :HD] = g_w_box[...]
        sums.sum_cores(0)
        sum_tick(11, (1, 2, 3))
        sum_tick(11, (0,))
        sums.sum_far(0)
        sum_tick(12, (2, 3))
        token_grad(0)
        token_grad(1)
        sum_tick(12, (1,))
        sums.sum_near(0)
        token_grad(2)
        sum_tick(13, (3,))
        sum_tick(13, (2,))
        sums.sum_column(0)
        token_grad(3)
        blocks.results_in(0)
        moves = [copy_in(final.at[PIECE:], final_out.at[PIECE:], 2)]
        moves[0].start()
        sum_tick(14, (3,))
        sums.sum_end(0)
        for stream in range(STREAMS):
            blocks.summed(stream)
        sums.summed(0)
        blocks.results_in(1)
        moves.append(copy_in(final.at[:PIECE], final_out.at[:PIECE], 3))
        moves[1].start()
        sums.results_in(1)
        moves.append(copy_in(small_final, small_out, 8))
        moves[2].start()
        for copy in moves:
            copy.wait()
    else:
        for block in range(row_blocks):
            token_grad(block)
        g_w_box_out[...] = g_w_box[...]
        g_b_qkv_out[...] = g_b_qkv[...]
        g_b_up_out[...] = g_b_up[...]
        g_vectors_out[...] = g_vectors[...]
        out = copy_in(held, g_held, 2)
        out.start()
        out.wait()
    for copy in tok_out:
        copy.wait()


def shaped(shape, dtype):
    return jax.ShapeDtypeStruct(shape, dtype)


def in_vmem(count):
    return [pl.BlockSpec(memory_space=pltpu.VMEM)] * count


def in_hbm(count):
    return [pl.BlockSpec(memory_space=pl.ANY)] * count


def run_layer(comm, tokens, cotangent, coords, segs, big, little):
    count, width = tokens.shape
    ff = 4 * BLOCK
    slots, pairs = count // SLOT, HEADS // 2
    held_shape = (STREAMS * BLOCK, BLOCK)
    out_shape = [
        shaped((count, width), bf16),
        shaped((count, width), f32),
        shaped((slots * HEADS, SLOT, SLOT), bf16),
    ]
    out_specs = in_hbm(3)
    if comm:
        out_shape += [shaped((STREAMS * PIECE, BLOCK), f32), shaped((8, SMALL), f32)]
        out_specs += in_hbm(2)
    else:
        out_shape += [shaped(held_shape, bf16), shaped((2 * WAVE, HD), f32), shaped((1, 3 * width), f32)]
        out_shape += [shaped((1, ff), f32), shaped((8, width), f32)]
        out_specs += in_hbm(1) + in_vmem(4)
    vmem = pltpu.VMEM
    dma = pltpu.SemaphoreType.DMA
    scratch = [
        vmem(held_shape, bf16),
        vmem(held_shape, bf16),
        vmem((ff // BLOCK * count, BLOCK), bf16),
        vmem((slots, pairs, PAIR, SLOT), bf16),
        vmem((slots, pairs, PAIR, SLOT), bf16),
        vmem((slots, pairs, SLOT, PAIR), bf16),
        vmem((width, count), bf16),
        vmem((2 * WAVE, count), f32),
        vmem((count, 2 * WAVE), f32),
        vmem((2, 2, SLOT, SLOT), bf16),
        vmem((count, width), f32),
        vmem((count, width), f32),
        vmem((width, count), bf16),
        vmem((count, width), bf16),
        vmem((width, count), bf16),
        vmem((width, count), bf16),
        vmem((count, 128), f32),
        vmem((slots * HEADS, 1, SLOT), f32),
        vmem((2 * WAVE, HD), bf16),
        vmem((HD, 2 * WAVE), bf16),
        vmem((1, 3 * width), f32),
        vmem((1, ff), f32),
        vmem((8, width), f32),
        vmem((2 * WAVE, HD), f32),
        vmem((1, 3 * width), f32),
        vmem((1, ff), f32),
        vmem((8, width), f32),
        dma((2, 2)),
        dma((32,)),
        vmem(coords.shape, jnp.int32),
        vmem(segs.shape, jnp.int32),
        vmem((PAIR, 4 * WAVE), bf16),
        vmem((4 * WAVE, PAIR), bf16),
    ]
    if comm:
        scratch += [
            vmem((STREAMS * PIECE, BLOCK), f32),
            vmem((128, SMALL), f32),
            vmem((256, SMALL // 2), f32),
            vmem((128, SMALL), f32),
            vmem((8, SMALL), f32),
            pltpu.SemaphoreType.REGULAR((2,)),
            *[vmem(value.shape, f32) for value in little],
            dma((STREAMS, 4)), dma((STREAMS, 2)), dma((STREAMS, 4)), dma((STREAMS,)), dma((2, 2)),
            dma((1, 4)), dma((1, 2)), dma((1, 4)), dma((1,)),
            dma((2, 2)),
        ]
        extra = dict(collective_id=0, has_side_effects=True)
    else:
        extra = {}
    return pl.pallas_call(
        functools.partial(layer_kernel, comm),
        out_shape=out_shape,
        in_specs=in_hbm(4 + len(big)) + (in_hbm if comm else in_vmem)(len(little)),
        out_specs=out_specs,
        scratch_shapes=scratch,
        compiler_params=pltpu.CompilerParams(vmem_limit_bytes=vmem_limit, **extra),
        name="layer",
    )(tokens, cotangent, coords, segs, *big, *little)


def finish_kernel(*refs):
    layer_in, tok_in, blocks_in, small_in = refs[:4]
    layer_out, tok_out, p_qkv, p_out, p_up, p_down = refs[4:10]
    small_out = refs[10:19]
    layer, tok, blocks, small = refs[19:23]
    small_rows = refs[23:32]
    load_sem, store_sem = refs[32:]
    width = layer_in.shape[1]
    loads, stores = [], []
    parts = 4
    rows = layer_in.shape[0] // parts
    small_load = pltpu.make_async_copy(small_in, small, load_sem.at[0])
    loads.append((pltpu.make_async_copy(blocks_in, blocks, load_sem.at[1]), []))
    for quad in range(width // QUAD):
        for part in range(3):
            loads[0][1].append((
                blocks.at[quad * PIECE : (quad + 1) * PIECE, part * QUAD : (part + 1) * QUAD],
                p_qkv.at[:, part * width + quad * QUAD : part * width + (quad + 1) * QUAD],
            ))
    loads[0][1].append((blocks.at[3 * PIECE : 4 * PIECE], p_out))
    for block in range(4):
        loads[0][1].append((
            blocks.at[(4 + block) * PIECE : (5 + block) * PIECE], p_up.at[:, block * BLOCK : (block + 1) * BLOCK]
        ))
    loads[0][1].append((blocks.at[8 * PIECE : 12 * PIECE], p_down))
    for source, held, target in ((tok_in, tok, tok_out), (layer_in, layer, layer_out)):
        for part in range(parts):
            at = slice(part * rows, (part + 1) * rows)
            copy = pltpu.make_async_copy(source.at[at], held.at[at], load_sem.at[1 + len(loads)])
            loads.append((copy, [(held.at[at], target.at[at])]))
    small_load.start()
    for copy, _ in loads:
        copy.start()

    def store(source, target):
        stores.append(pltpu.make_async_copy(source, target, store_sem.at[len(stores)]))
        stores[-1].start()

    small_load.wait()
    for row in range(8):
        small_rows[row][...] = small[row : row + 1, 128 : 128 + small_rows[row].shape[1]]
    small_rows[8][...] = small[:, :HD]
    for source, target in zip(small_rows, small_out):
        store(source, target)
    for copy, moves in loads:
        copy.wait()
        for source, target in moves:
            store(source, target)
    for copy in stores:
        copy.wait()


def run_finish(layer_out, g_tok, blocks, small, big, little):
    shapes = [shaped(layer_out.shape, bf16), shaped(g_tok.shape, f32)]
    shapes += [shaped(w.shape, f32) for w in big + little]
    dma = pltpu.SemaphoreType.DMA
    return pl.pallas_call(
        finish_kernel,
        out_shape=shapes,
        in_specs=in_hbm(4),
        out_specs=in_hbm(len(shapes)),
        scratch_shapes=[
            pltpu.VMEM(layer_out.shape, bf16), pltpu.VMEM(g_tok.shape, f32), pltpu.VMEM(blocks.shape, f32),
            pltpu.VMEM(small.shape, f32), *[pltpu.VMEM(v.shape, f32) for v in little], dma((16,)), dma((40,)),
        ],
        compiler_params=pltpu.CompilerParams(vmem_limit_bytes=vmem_limit),
        name="finish",
    )(layer_out, g_tok, blocks, small)


def to_blocks(w_qkv, w_out, w_up, w_down):
    width = w_out.shape[1]
    qkv = w_qkv.reshape(width, 3, width // QUAD, QUAD).transpose(2, 0, 1, 3).reshape(-1, BLOCK)
    up = w_up.reshape(width, -1, BLOCK).transpose(1, 0, 2).reshape(-1, BLOCK)
    return jnp.concatenate([qkv, w_out, up, w_down], axis=0)


def from_blocks(held, width):
    qkv = held[: 3 * BLOCK].reshape(width // QUAD, width, 3, QUAD).transpose(1, 2, 0, 3).reshape(width, -1)
    up = held[4 * BLOCK : 8 * BLOCK].reshape(-1, width, BLOCK).transpose(1, 0, 2).reshape(width, -1)
    return qkv, held[3 * BLOCK : 4 * BLOCK], up, held[8 * BLOCK :]


def per_device(
    mesh_shape, tokens, cotangent, segments, box_coords, w_qkv, b_qkv, w_box, w_out, b_out, gain_one, shift_one,
    w_up, b_up, w_down, b_down, gain_two, shift_two,
):
    count, width = tokens.shape
    segs = segments.reshape(1, -1)
    vectors = [b_qkv, b_up, b_out, gain_one, shift_one, b_down, gain_two, shift_two]
    if mesh_shape == (16, 2):
        little = [v.reshape(1, -1) for v in vectors] + [w_box]
        big = [w_qkv, w_out, w_up, w_down]
        layer_out, g_tok, _, blocks, small = run_layer(True, tokens, cotangent, box_coords, segs, big, little)
        layer_out, g_tok, p_wq, p_wo, p_wu, p_wd, *rest = run_finish(layer_out, g_tok, blocks, small, big, little)
        p_bq, p_bu, p_bo, p_g1, p_s1, p_bd, p_g2, p_s2 = [v.reshape(-1) for v in rest[:8]]
        p_wb = rest[8]
    else:
        low = lambda value: value.astype(bf16)
        gather = lambda value: lax.all_gather(low(value), "fsdp", axis=0, tiled=True)
        held = to_blocks(gather(w_qkv), gather(w_out), gather(w_up), gather(w_down))
        wb, bq, bu, *six = [gather(v) for v in [w_box] + vectors]
        order = quad_order(jnp.arange(3 * width))
        rows = jnp.stack([jnp.zeros((width,), bf16)] * 2 + six).astype(f32)
        layer_out, g_tok, _, g_held, g_wb, g_bq, g_bu, g_six = run_layer(
            False, tokens, cotangent, box_coords, segs, [held],
            [wb, bq[order].astype(f32).reshape(1, -1), bu.astype(f32).reshape(1, -1), rows],
        )

        def scatter(grad):
            part = lax.psum_scatter(grad, "fsdp", scatter_dimension=0, tiled=True)
            return lax.psum(part, "rep").astype(f32)

        p_wq, p_wo, p_wu, p_wd = [scatter(g) for g in from_blocks(g_held, width)]
        g_bq = jnp.zeros((3 * width,), f32).at[order].set(g_bq[0])
        p_wb, p_bq, p_bu = scatter(g_wb), scatter(g_bq), scatter(g_bu[0])
        p_bo, p_g1, p_s1, p_bd, p_g2, p_s2 = [scatter(g_six[2 + i]) for i in range(VECTORS)]
    return (
        layer_out, g_tok, p_wq, p_bq, p_wb, p_wo, p_bo, p_g1, p_s1,
        p_wu, p_bu, p_wd, p_bd, p_g2, p_s2,
    )


def solution(mesh):
    tokens = P(("fsdp", "rep"), None)
    matrix, vector = P("fsdp", None), P("fsdp")
    kinds = [matrix, vector, matrix, matrix, vector, vector, vector, matrix, vector, matrix, vector, vector, vector]
    return jax.shard_map(
        functools.partial(per_device, (mesh.shape["fsdp"], mesh.shape["rep"])),
        mesh=mesh,
        in_specs=(tokens, tokens, P(("fsdp", "rep")), P(None, ("fsdp", "rep")), *kinds),
        out_specs=(tokens, tokens, *kinds),
        check_vma=False,
    )
```

```python
import functools
import math

import jax
import jax.numpy as jnp
from jax import lax
from jax.experimental import pallas as pl
from jax.experimental.pallas import tpu as pltpu
from jax.sharding import PartitionSpec as P

HEADS = 12
HD = 64
FREQ = 16
SLOT = 512
WAVE = 4 * FREQ
PAIR = 2 * HD
QUAD = 4 * HD

f32 = jnp.float32
bf16 = jnp.bfloat16
neg_large = -1e30
eps_norm = 1e-12
scale_factor = 1.0 / math.sqrt(HD)
vmem_limit = 67_000_000


def dot_nn(left, right):
    return lax.dot_general(left, right, (((1,), (0,)), ((), ())), preferred_element_type=f32)


def dot_nt(left, right):
    return lax.dot_general(left, right, (((1,), (1,)), ((), ())), preferred_element_type=f32)


def dot_tn(left, right):
    return lax.dot_general(left, right, (((0,), (0,)), ((), ())), preferred_element_type=f32)


def aligned(index, size):
    return pl.ds(pl.multiple_of(index * size, size), size)


def wave_rows(coords):
    count = coords.shape[1]
    spread = [jnp.broadcast_to(coords[c : c + 1, :].astype(f32), (FREQ, count)) for c in range(4)]
    scaled = jnp.concatenate(spread + spread, axis=0) * (100.0 / 1024.0)
    rows = lax.broadcasted_iota(jnp.int32, scaled.shape, 0)
    frequency = jnp.exp(-math.log(10000.0) * (rows & (FREQ - 1)).astype(f32) / FREQ)
    angle = scaled * frequency
    turns = jnp.floor(angle * (2.0 / math.pi) + 0.5)
    rest = ((angle - turns * 1.5703125) - turns * 4.837512969970703125e-4) - turns * 7.549789954891e-8
    square = rest * rest
    sine = rest + rest * square * (
        -1.6666654611e-1 + square * (8.3321608736e-3 + square * -1.9515295891e-4)
    )
    cosine = 1.0 - 0.5 * square + square * square * (
        4.166664568298827e-2 + square * (-1.388731625493765e-3 + square * 2.443315711809948e-5)
    )
    quadrant = turns.astype(jnp.int32) + jnp.where(rows >= WAVE, 1, 0)
    value = jnp.where((quadrant & 1) == 1, cosine, sine)
    value = jnp.where((quadrant & 2) == 2, -value, value)
    return value.astype(bf16).astype(f32)


def swap_lanes(value):
    return pltpu.roll(value, WAVE, 1)


def gelu_parts(value):
    t = 1.0 / (1.0 + (0.3275911 * math.sqrt(0.5)) * jnp.abs(value))
    bell = jnp.exp2(value * value * (-0.5 * math.log2(math.e)))
    half_tail = bell * t * (
        0.127414796 + t * (-0.142248368 + t * (0.7107068705 + t * (-0.7265760135 + t * 0.5307027145)))
    )
    return jnp.where(value >= 0, 1.0 - half_tail, half_tail), bell * (1.0 / math.sqrt(2.0 * math.pi))


def row_mean(value):
    return jnp.mean(value, axis=-1, keepdims=True)


ROWS = 256
BLOCK = 768
PIECE = 48
HALF = BLOCK // 2
SMALL = 512
STREAMS = 12
VECTORS = 6
LEVEL_FIRST = 11


def widths(width, ff):
    return 3 * width // 16, ff // 16, width // 16


class Route:
    def __init__(self):
        chip = lax.axis_index("fsdp")
        self.core = lax.axis_index("rep")
        self.level, self.me = chip // 4, chip % 4
        near_step, far_step = 1 + self.core, 2 - self.core
        near_move = near_step * (1 - 2 * ((self.me // near_step) % 2))
        far_move = far_step * (1 - 2 * ((self.me // far_step) % 2))
        self.near = self.me + near_move
        self.far = self.me + far_move
        self.across = self.me + near_move + far_move

    def chip(self, level, place):
        return level * 4 + place

    def levels(self):
        return [(self.level + k) % 4 for k in range(1, 4)]

    def peers(self):
        chips = [self.chip(level, self.me) for level in self.levels()]
        chips += [self.chip(self.level, self.near), self.chip(self.level, self.far)]
        return [(chip, self.core) for chip in chips] + [(self.chip(self.level, self.me), 1 - self.core)]


def remote(source, target, send, recv, chip, core):
    return pltpu.make_async_remote_copy(
        src_ref=source, dst_ref=target, send_sem=send, recv_sem=recv,
        device_id=(chip, core), device_id_type=pl.DeviceIdType.MESH,
    )


def half_columns(half, size):
    return pl.ds(pl.multiple_of(half * size, size), size)


class Streams:
    def __init__(self, held, stage, final, sems):
        self.held = held
        self.upper = held.at[: 8 * BLOCK].reshape(8, 4, 4, PIECE, BLOCK)
        self.lower = held.at[8 * BLOCK :].reshape(4, 4, 4, PIECE, BLOCK)
        self.stage = stage.reshape(STREAMS, 4, 4, PIECE, BLOCK)
        self.final = final
        self.gather_recv, self.gather_send, self.sum_recv, self.sum_send, self.final_sem = sems

    def on(self, stream, act):
        if isinstance(stream, int):
            act(self.upper.at[stream] if stream < 8 else self.lower.at[:, :, stream - 8])
        else:
            pl.when(stream < 8)(lambda: act(self.upper.at[stream]))
            pl.when(stream >= 8)(lambda: act(self.lower.at[:, :, stream - 8]))

    def half(self, half):
        return half_columns(half, HALF)

    def several(self, pieces):
        return self.held.at[: PIECE * pieces, :HALF]

    def landing(self, stream, kind):
        block = self.stage.at[(stream + 8) % STREAMS]
        if kind == 0:
            return block.at[:, :, :, :HALF]
        return block.at[(0, 0, 2, 3)[kind] : (0, 2, 3, 4)[kind], :, :, HALF:]

    def result(self, stream, half):
        return self.final.at[pl.ds(pl.multiple_of(stream * PIECE, 16), PIECE), self.half(half)]

    def results(self, last):
        return self.final.at[:PIECE, :HALF] if last else self.final.at[PIECE:, :HALF]


class Vectors:
    def __init__(self, held, stage, final, sems):
        self.held, self.flat, self.final = held, stage, final
        self.shards = held.reshape(4, 4, 8, SMALL)
        self.stage = stage.reshape(8, 4, 8, SMALL // 2)
        self.gather_recv, self.gather_send, self.sum_recv, self.sum_send, self.final_sem = sems

    def on(self, stream, act):
        act(self.shards)

    def half(self, half):
        return half_columns(half, SMALL // 2)

    def several(self, pieces):
        if pieces <= 16:
            return self.held.at[: 8 * pieces, : SMALL // 2]
        return self.flat.at[: 8 * pieces, :]

    def landing(self, stream, kind):
        return self.stage.at[(0, 4, 6, 7)[kind] : (4, 6, 7, 8)[kind]]

    def result(self, stream, half):
        return self.final.at[:, self.half(half)]

    def results(self, last):
        return self.final.at[:, : SMALL // 2]


def drain(view, sem):
    pltpu.make_async_copy(view, view, sem).wait()


class Exchange:
    def __init__(self, route, parts):
        self.route, self.parts = route, parts

    def send(self, source, target, send, recv, level, place, core):
        remote(source, target, send, recv, self.route.chip(level, place), core).start()


    def share(self, stream, view, place, kind):
        p, r = self.parts, self.route
        self.send(
            view, view, p.gather_send.at[stream, 0], p.gather_recv.at[stream, kind], r.level, place, r.core
        )

    def hand_over(self, stream, view):
        p, r = self.parts, self.route
        self.send(
            view, view, p.gather_send.at[stream, 1], p.gather_recv.at[stream, 3], r.level, r.me, 1 - r.core
        )

    def gather_own(self, stream):
        p, r = self.parts, self.route

        def act(shards):
            view = shards.at[r.level, r.me, :, p.half(r.core)]
            for level in r.levels():
                self.send(
                    view, view, p.gather_send.at[stream, 0], p.gather_recv.at[stream, 0], level, r.me, r.core
                )

        p.on(stream, act)

    def gather_column(self, stream):
        p, r = self.parts, self.route
        drain(p.several(3), p.gather_recv.at[stream, 0])

        def act(shards):
            view = shards.at[:, r.me, :, p.half(r.core)]
            self.share(stream, view, r.near, 1)
            self.share(stream, view, r.far, 2)
            for level in r.levels():
                self.hand_over(stream, shards.at[level, r.me, :, p.half(r.core)])

        p.on(stream, act)

    def gather_near(self, stream):
        p, r = self.parts, self.route
        drain(p.several(4), p.gather_recv.at[stream, 1])

        def act(shards):
            view = shards.at[:, r.near, :, p.half(r.core)]
            self.share(stream, view, r.far, 2)
            self.hand_over(stream, view)

        p.on(stream, act)

    def gather_far(self, stream):
        p, r = self.parts, self.route
        drain(p.several(8), p.gather_recv.at[stream, 2])

        def act(shards):
            for place in (r.far, r.across):
                self.hand_over(stream, shards.at[:, place, :, p.half(r.core)])

        p.on(stream, act)


    def level_own(self, stream):
        p, r = self.parts, self.route

        def act(shards):
            view = shards.at[r.level, r.me, :, p.half(r.core)]
            self.share(stream, view, r.near, 1)
            self.share(stream, view, r.far, 2)

        p.on(stream, act)

    def level_near(self, stream):
        p, r = self.parts, self.route
        drain(p.several(1), p.gather_recv.at[stream, 1])

        def act(shards):
            view = shards.at[r.level, r.near, :, p.half(r.core)]
            self.share(stream, view, r.far, 2)
            self.hand_over(stream, view)

        p.on(stream, act)

    def level_far(self, stream):
        p, r = self.parts, self.route
        drain(p.several(2), p.gather_recv.at[stream, 2])

        def act(shards):
            view = shards.at[r.level, :, :, p.half(r.core)]
            for level in r.levels():
                self.send(
                    view, view, p.gather_send.at[stream, 0], p.gather_recv.at[stream, 0], level, r.me, r.core
                )
            for place in (r.far, r.across):
                self.hand_over(stream, shards.at[r.level, place, :, p.half(r.core)])

        p.on(stream, act)

    def level_column(self, stream):
        p, r = self.parts, self.route
        drain(p.several(12), p.gather_recv.at[stream, 0])

        def act(shards):
            for level in r.levels():
                self.hand_over(stream, shards.at[level, :, :, p.half(r.core)])

        p.on(stream, act)

    def gathered(self, stream):
        p = self.parts
        drain(p.several(15), p.gather_recv.at[stream, 3])

    def gather_sent(self, stream):
        p = self.parts
        drain(p.several(15), p.gather_send.at[stream, 0])
        drain(p.several(15), p.gather_send.at[stream, 1])


    def pass_on(self, stream, view, landing, kind, level, place):
        p, r = self.parts, self.route
        self.send(view, landing, p.sum_send.at[stream], p.sum_recv.at[stream, kind], level, place, r.core)

    def sum_cores(self, stream):
        p, r = self.parts, self.route

        def act(shards):
            self.send(
                shards.at[:, :, :, p.half(1 - r.core)], p.landing(stream, 0),
                p.sum_send.at[stream], p.sum_recv.at[stream, 0], r.level, r.me, 1 - r.core,
            )

        p.on(stream, act)

    def sum_far(self, stream):
        p, r = self.parts, self.route
        drain(p.several(16), p.sum_recv.at[stream, 0])
        landed, target = p.landing(stream, 0), p.landing(stream, 1)

        def act(shards):
            def add(place):
                view = shards.at[:, place, :, p.half(r.core)]
                view[...] += landed[:, place]
                return view

            for index, place in enumerate((r.far, r.across)):
                self.pass_on(stream, add(place), target.at[index], 1, r.level, r.far)
            for place in (r.me, r.near):
                add(place)

        p.on(stream, act)

    def sum_near(self, stream):
        p, r = self.parts, self.route
        drain(p.several(8), p.sum_recv.at[stream, 1])
        landed, target = p.landing(stream, 1), p.landing(stream, 2)

        def act(shards):
            view = shards.at[:, r.near, :, p.half(r.core)]
            view[...] += landed[1]
            self.pass_on(stream, view, target.at[0], 2, r.level, r.near)
            view = shards.at[:, r.me, :, p.half(r.core)]
            view[...] += landed[0]

        p.on(stream, act)

    def sum_column(self, stream):
        p, r = self.parts, self.route
        drain(p.several(4), p.sum_recv.at[stream, 2])
        landed, target = p.landing(stream, 2), p.landing(stream, 3)

        def act(shards):
            view = shards.at[:, r.me, :, p.half(r.core)]
            view[...] += landed[0]
            for index, level in enumerate(r.levels()):
                self.pass_on(
                    stream, shards.at[level, r.me, :, p.half(r.core)], target.at[0, index], 3, level, r.me
                )

        p.on(stream, act)

    def sum_end(self, stream):
        p, r = self.parts, self.route
        drain(p.several(3), p.sum_recv.at[stream, 3])
        landed = p.landing(stream, 3)
        view = p.result(stream, r.core)

        def act(shards):
            total = shards[r.level, r.me, :, p.half(r.core)].astype(f32)
            for index in range(3):
                total += landed[0, index].astype(f32)
            view[...] = total

        p.on(stream, act)
        last = 1 if isinstance(stream, int) and stream == 0 else 0
        self.send(view, view, p.final_sem.at[last, 0], p.final_sem.at[last, 1], r.level, r.me, 1 - r.core)

    def summed(self, stream):
        p = self.parts
        drain(p.several(31), p.sum_send.at[stream])

    def results_in(self, last):
        p = self.parts
        for side in range(2):
            drain(p.results(last), p.final_sem.at[last, side])


def owner_tables(start, share, depth, order=None):
    col = lax.broadcasted_iota(jnp.int32, (1, BLOCK), 1) + start
    source = col if order is None else order(col)
    owner, entry = source // share, source % share
    pick = (entry == lax.broadcasted_iota(jnp.int32, (depth, BLOCK), 0)).astype(bf16)
    row = lax.broadcasted_iota(jnp.int32, (128, BLOCK), 0)
    return pick, owner == (row >> 3), row & 7


def quad_order(col):
    return (col % BLOCK) // QUAD * BLOCK + col // BLOCK * QUAD + col % QUAD


def layer_kernel(comm, *refs):
    refs = list(refs)

    def take(count):
        taken, refs[:] = refs[:count], refs[count:]
        return taken

    tok_in, cot_in, coords_in, segs_in = take(4)
    if comm:
        w_qkv_in, w_out_in, w_up_in, w_down_in = take(4)
        small_in = take(9)
    else:
        held_in, w_box_in, b_qkv_in, b_up_in, vectors_in = take(5)
    layer_out, g_tok_out, e_hbm = take(3)
    if comm:
        final_out, small_out = take(2)
    else:
        g_held, g_w_box_out, g_b_qkv_out, g_b_up_out, g_vectors_out = take(5)
    (held, stage, slope, q8t, k8t, v_row, ctx_t, wave_t, wave_r, e_buf, normed, total, flip, g_down, tok_t, g_ctx_t,
     inv_one, inv_total, w_box, w_box_t, b_qkv, b_up, vectors, g_w_box, g_b_qkv, g_b_up, g_vectors, e_sem, io_sem, coords, segs, w_pair, w_pair_t) = take(33)
    if comm:
        final, small, small_stage, g_small, small_final, mid_sem = take(6)
        small_held = take(9)
        block_sems, small_sems, small_final_sems = take(5), take(4), take(1)

    count, width = tok_t.shape[1], tok_t.shape[0]
    ff = slope.shape[0] // count * BLOCK
    slots, pairs = count // SLOT, HEADS // 2
    row_blocks = count // ROWS
    up_blocks = ff // BLOCK
    quads = pairs // 2
    ctx, low, cot, tok = [stage.at[part * count : (part + 1) * count] for part in range(4)]
    act = stage.at[STREAMS * BLOCK - up_blocks * count :]
    up_at, down_at = 4 * BLOCK, 8 * BLOCK

    def copy_in(source, target, index=0):
        return pltpu.make_async_copy(source, target, io_sem.at[index])

    tok_copy = copy_in(tok_in, tok, 0)
    cot_copy = copy_in(cot_in, cot, 1)
    coord_copy = copy_in(coords_in, coords, 2)
    seg_copy = copy_in(segs_in, segs, 3)

    if comm:
        route = Route()
        chip = route.chip(route.level, route.me)
        blocks = Exchange(route, Streams(held, stage, final, block_sems))
        extras = Exchange(route, Vectors(small, small_stage, small_final, [*small_sems, *small_final_sems]))
        sums = Exchange(route, Vectors(g_small, small_stage, small_final, [*small_sems, *small_final_sems]))
        barrier = pltpu.get_barrier_semaphore()
        for peer, core in route.peers():
            pl.semaphore_signal(barrier, inc=1, device_id=(peer, core), device_id_type=pl.DeviceIdType.MESH)
        moves = []
        for quad in range(quads):
            for part in range(3):
                moves.append((
                    w_qkv_in.at[:, part * width + quad * QUAD : part * width + (quad + 1) * QUAD],
                    total.at[quad * PIECE : (quad + 1) * PIECE, part * QUAD : (part + 1) * QUAD],
                ))
        moves.append((w_out_in, total.at[3 * PIECE : 4 * PIECE]))
        for block in range(up_blocks):
            moves.append((
                w_up_in.at[:, block * BLOCK : (block + 1) * BLOCK],
                total.at[(4 + block) * PIECE : (5 + block) * PIECE],
            ))
        moves.append((w_down_in, total.at[8 * PIECE : 12 * PIECE]))
        moves += list(zip(small_in, small_held))
        moves = [copy_in(source, target, 4 + index) for index, (source, target) in enumerate(moves)]
        first = 3 * quads
        for copy in moves[:first] + moves[first + 1 + up_blocks + 1 :] + moves[first : first + 1 + up_blocks + 1]:
            copy.start()
        for copy in (coord_copy, seg_copy, tok_copy, cot_copy):
            copy.start()

        def round_block(block):
            at = pl.ds(pl.multiple_of(block * BLOCK + PIECE * chip, 16), PIECE)
            held[at, :] = total[block * PIECE : (block + 1) * PIECE, :].astype(bf16)

        g_small[:8, :] = jnp.zeros((8, SMALL), f32)
        for copy in moves[:first]:
            copy.wait()
        for block in range(quads):
            round_block(block)
        for copy in moves[first + 1 + up_blocks + 1 :]:
            copy.wait()
        g_small[:8, :HD] = small_held[8][...].astype(bf16).astype(f32)
        for row in range(8):
            value = small_held[row][...].astype(bf16).astype(f32)
            g_small[row : row + 1, 128 : 128 + value.shape[1]] = value
        small[pl.ds(pl.multiple_of(chip * 8, 8), 8), :] = g_small[:8, :]
        pl.semaphore_wait(barrier, 6)
        extras.gather_own(0)
        for stream in range(quads):
            blocks.gather_own(stream)
        for copy in moves[first : first + 1 + up_blocks + 1]:
            copy.wait()
        for block in range(quads, STREAMS - up_blocks):
            round_block(block)
        at = pl.ds(pl.multiple_of(down_at + 4 * PIECE * chip, 16), 4 * PIECE)
        held[at, :] = total[8 * PIECE : 12 * PIECE, :].astype(bf16)
        blocks.level_own(LEVEL_FIRST)
        for stream in range(quads, STREAMS):
            if stream != LEVEL_FIRST:
                blocks.gather_own(stream)
    else:
        for copy in (coord_copy, seg_copy, tok_copy, cot_copy):
            copy.start()
        copy_in(held_in, held, 4).start()
        w_box[...] = w_box_in[...]
        b_qkv[...] = b_qkv_in[...]
        b_up[...] = b_up_in[...]
        vectors[...] = vectors_in[...]

    coord_copy.wait()
    seg_copy.wait()
    wave_t[...] = wave_rows(coords[...])
    wave_r[...] = jnp.transpose(wave_t[...])
    for slot in range(slots):
        seg_i = jnp.broadcast_to(segs[:, slot * SLOT : (slot + 1) * SLOT].astype(f32), (SLOT, SLOT))
        seg_j = jnp.transpose(seg_i)
        normed[slot * SLOT : (slot + 1) * SLOT, :SLOT] = jnp.where(seg_i == seg_j, 0.0, neg_large)
    g_w_box[...] = jnp.zeros_like(g_w_box)
    g_b_up[...] = jnp.zeros_like(g_b_up)
    g_vectors[...] = jnp.zeros_like(g_vectors)
    tok_copy.wait()

    if comm:
        extras.gather_column(0)
        blocks.gather_column(0)
        extras.gather_near(0)
        blocks.gather_near(0)
        blocks.gather_column(1)
        extras.gather_far(0)
        blocks.gather_far(0)
        blocks.gather_near(1)
        blocks.gather_column(2)
        blocks.level_near(LEVEL_FIRST)
        extras.gathered(0)
        table = small[...].astype(bf16)
        w_box[...] = table[:, :HD]
        share_qkv, share_up, share = widths(width, ff)
        for row, columns, share_of, depth, order, target in (
            (0, 3 * width, share_qkv, 256, quad_order, b_qkv),
            (1, ff, share_up, 256, None, b_up),
            (None, width, share, 128, None, vectors),
        ):
            @pl.loop(0, columns // BLOCK)
            def _(block):
                pick, owned, row_of = owner_tables(block * BLOCK, share_of, depth, order)
                spread = dot_nn(table[:, 128 : 128 + depth], pick)
                keep = owned if row is None else owned & (row_of == row)
                rows = jnp.sum(jnp.where(keep, spread, 0.0).reshape(16, 8, BLOCK), axis=0)
                target[:, aligned(block, BLOCK)] = rows if row is None else jnp.sum(rows, axis=0, keepdims=True)

    else:
        copy_in(held_in, held, 4).wait()
    w_box_t[...] = jnp.transpose(w_box[...].astype(f32)).astype(bf16)
    blank = jnp.zeros((2 * WAVE, HD), bf16)
    w_pair_t[: 2 * WAVE, :] = jnp.concatenate([w_box[...], blank], axis=1)
    w_pair_t[2 * WAVE :, :] = jnp.concatenate([blank, w_box[...]], axis=1)
    w_pair[...] = jnp.transpose(w_pair_t[...].astype(f32)).astype(bf16)

    def gather_tick(step):
        if not comm:
            return

        def stream_of(order):
            return order + order // LEVEL_FIRST

        for ahead, act_on in ((1, blocks.gather_near), (3, blocks.gather_column), (0, blocks.gather_far)):
            order = step + ahead
            if isinstance(order, int):
                if order < STREAMS - 1:
                    act_on(stream_of(order))
            else:
                pl.when(order < STREAMS - 1)(functools.partial(act_on, stream_of(order)))

    def need(stream):
        if comm:
            blocks.gathered(stream)

    b_out, gain_one, shift_one, b_down, gain_two, shift_two = [vectors[2 + i : 3 + i, :] for i in range(VECTORS)]
    lane = lax.broadcasted_iota(jnp.int32, (SLOT, PAIR), 1)
    scores = total.reshape(2, SLOT, width)

    def project(quad, slot):
        rows = tok[aligned(slot, SLOT), :]

        def columns(part):
            weight = held[aligned(quad, BLOCK), part * QUAD : (part + 1) * QUAD]
            shift = b_qkv[:, pl.ds(pl.multiple_of(quad * BLOCK + part * QUAD, QUAD), QUAD)]
            return (dot_nn(rows, weight) + shift).astype(bf16)

        q, k, v = columns(0), columns(1), columns(2)
        low[aligned(slot, SLOT), aligned(quad, QUAD)] = k
        flip[aligned(quad, QUAD), aligned(slot, SLOT)] = jnp.transpose(v.astype(f32)).astype(bf16)
        qt = jnp.transpose(q.astype(f32) * scale_factor).astype(bf16)
        kt = jnp.transpose(k.astype(f32) * scale_factor).astype(bf16)
        for part in range(2):
            here = slice(part * PAIR, (part + 1) * PAIR)
            q8t[slot, quad * 2 + part] = qt[here]
            k8t[slot, quad * 2 + part] = kt[here]
            v_row[slot, quad * 2 + part] = v[:, here]

    def e_copy(place, head, index, out):
        pair = (e_buf.at[place, head], e_hbm.at[index])
        return pltpu.make_async_copy(*(pair if out else pair[::-1]), e_sem.at[place, head])

    def attend(step):
        pair, slot = step // slots, step % slots
        cols = aligned(slot, SLOT)
        place = step % 2

        @pl.when(step >= 2)
        def _():
            for head in range(2):
                e_copy(place, head, 0, True).wait()

        sine_t, cosine_t = wave_t[:WAVE, cols], wave_t[WAVE:, cols]
        sc_t = (wave_t[:, cols] * scale_factor).astype(bf16)
        sc_r = wave_r[cols, :]
        cs_r = swap_lanes(sc_r)
        cc_r = jnp.where(lane < WAVE, cs_r, sc_r)
        ss_r = jnp.where(lane < WAVE, sc_r, -cs_r)
        cs_low = cs_r.astype(bf16)
        keys = low[cols, aligned(pair, PAIR)]
        queries = q8t[slot, pair]
        key_box = dot_nn(keys, w_pair[...])
        query_box = dot_nn(w_pair_t[...], queries)
        low_exps, inverse, heads_t = [], [], []
        for head in range(2):
            here = slice(head * 2 * WAVE, (head + 1) * 2 * WAVE)
            side = key_box[:, here]
            k_side = (side * cc_r + swap_lanes(side) * ss_r).astype(bf16)
            first, second = query_box[here][:WAVE], query_box[here][WAVE:]
            q_side = jnp.concatenate(
                [first * sine_t + second * cosine_t, second * sine_t - first * cosine_t], axis=0
            ).astype(bf16)
            q_t = queries[head * HD : (head + 1) * HD]
            zero = jnp.zeros_like(q_t)
            q_pair = [q_t, zero] if head == 0 else [zero, q_t]
            k_full = jnp.concatenate([keys, cs_low, k_side], axis=1)
            q_full = jnp.concatenate(q_pair + [q_side, sc_t], axis=0)
            scores[head, :, :SLOT] = dot_nn(k_full, q_full) + normed[cols, :SLOT]
        for head in range(2):
            masked = scores[head, :, :SLOT]
            exps = jnp.exp(masked - jnp.max(masked, axis=0, keepdims=True))
            inverse.append(1.0 / jnp.sum(exps, axis=0, keepdims=True))
            low_exps.append(exps.astype(bf16))
            e_buf[place, head] = low_exps[head]
            e_copy(place, head, step * 2 + head, True).start()
            inv_total[step * 2 + head] = inverse[head]
        for head in range(2):
            at = pl.ds(pl.multiple_of(pair * PAIR + head * HD, HD), HD)
            heads_t.append(dot_nn(flip[at, cols], low_exps[head]) * inverse[head])
        both = jnp.concatenate(heads_t, axis=0)
        ctx_t[aligned(pair, PAIR), cols] = both.astype(bf16)
        ctx[cols, aligned(pair, PAIR)] = jnp.transpose(both).astype(bf16)

    steps = slots * pairs
    quad_steps = 2 * slots

    @pl.loop(0, quads)
    def _(quad):
        need(quad)

        @pl.loop(0, slots)
        def _(slot):
            project(quad, slot)

        @pl.loop(0, quad_steps)
        def _(inner):
            step = quad * quad_steps + inner
            if comm:
                @pl.when(step == 1)
                def _():
                    blocks.gather_column(quads)
                    blocks.level_far(LEVEL_FIRST)

                pl.when((step % 2 == 0) & (step > 0))(functools.partial(gather_tick, step // 2))
            attend(step)

    for place in range(2):
        for head in range(2):
            e_copy(place, head, 0, True).wait()

    def column_sum(value):
        return jnp.sum(value, axis=0, keepdims=True)

    need(3)
    gather_tick(6)

    @pl.loop(0, row_blocks)
    def _(block):
        rows = aligned(block, ROWS)
        token_rows = tok[rows, :].astype(f32)
        tok_t[:, rows] = jnp.transpose(token_rows).astype(bf16)
        pre = token_rows + dot_nn(ctx[rows, :], held[3 * BLOCK : 4 * BLOCK, :]) + b_out
        center = pre - row_mean(pre)
        invdev = lax.rsqrt(row_mean(center * center) + eps_norm)
        unit = center * invdev
        inv_one[rows, :] = jnp.broadcast_to(invdev, (ROWS, 128))
        normed[rows, :] = unit
        hidden = unit * gain_one + shift_one
        low[rows, :] = hidden.astype(bf16)
        flip[:, rows] = jnp.transpose(hidden).astype(bf16)

    @pl.loop(0, up_blocks)
    def _(block):
        gather_tick(7 + block)
        if comm:
            pl.when(block == 2)(functools.partial(blocks.level_column, LEVEL_FIRST))
        need(4 + block)

        weight = held[pl.ds(pl.multiple_of(up_at + block * BLOCK, BLOCK), BLOCK), :]
        for row in range(row_blocks):
            rows = slice(row * ROWS, (row + 1) * ROWS)
            total[rows, :] = dot_nn(low[rows, :], weight) + b_up[:, aligned(block, BLOCK)]
        for row in range(row_blocks):
            at = pl.ds(pl.multiple_of(block * count + row * ROWS, ROWS), ROWS)
            up = total[row * ROWS : (row + 1) * ROWS, :]
            cdf, pdf = gelu_parts(up)
            act[at, :] = (up * cdf).astype(bf16)
            slope[at, :] = (cdf + up * pdf).astype(bf16)

    for block in range(up_blocks):
        need(8 + block)
    cot_copy.wait()

    @pl.loop(0, row_blocks)
    def _(block):
        rows = aligned(block, ROWS)
        pre = normed[rows, :] * gain_one + shift_one + b_down
        for part in range(up_blocks):
            at = pl.ds(pl.multiple_of(part * count + block * ROWS, ROWS), ROWS)
            pre += dot_nn(act[at, :], held[down_at + part * BLOCK : down_at + (part + 1) * BLOCK, :])
        center = pre - row_mean(pre)
        invdev = lax.rsqrt(row_mean(center * center) + eps_norm)
        unit = center * invdev
        grad = cot[rows, :].astype(f32)
        cot[rows, :] = (unit * gain_two + shift_two).astype(bf16)
        pltpu.make_async_copy(cot.at[rows], layer_out.at[rows], io_sem.at[0]).start()
        scaled = grad * gain_two
        g_pre = invdev * (scaled - row_mean(scaled) - unit * row_mean(scaled * unit))
        total[rows, :] = g_pre
        low_pre = g_pre.astype(bf16)
        g_down[rows, :] = low_pre
        g_vectors[5:6, :] += column_sum(low_pre.astype(f32))
        g_vectors[6:7, :] += column_sum(grad * unit)
        g_vectors[7:8, :] += column_sum(grad)

    out_copy = pltpu.make_async_copy(cot, layer_out, io_sem.at[0])
    if comm:
        for stream in range(STREAMS):
            blocks.gather_sent(stream)
        extras.gather_sent(0)

    def last(step):
        turn = step // 4
        return STREAMS - 1 - step + (14 - 6 * turn) * turn - 4

    def sum_start(step):
        if comm:
            blocks.sum_cores(last(step))

    def sum_tick(step, stages=(0, 1, 2, 3)):
        if not comm:
            return
        acts = (blocks.sum_far, blocks.sum_near, blocks.sum_column, blocks.sum_end)
        for behind in stages:
            at = step - behind
            if isinstance(at, int):
                if 0 <= at < STREAMS:
                    acts[behind](last(at))
            else:
                pl.when((at >= 0) & (at < STREAMS))(functools.partial(acts[behind], last(at)))

    def tell(sem):
        if comm:
            for peer, core in route.peers():
                pl.semaphore_signal(sem, inc=1, device_id=(peer, core), device_id_type=pl.DeviceIdType.MESH)

    def told(sem):
        if comm:
            pl.semaphore_wait(sem, 6)

    out_copy.wait()
    if comm:
        tell(mid_sem.at[0])

    @pl.loop(0, up_blocks)
    def _(index):
        block = up_blocks - 1 - index
        down_rows = pl.ds(pl.multiple_of(down_at + block * BLOCK, BLOCK), BLOCK)
        up_rows = pl.ds(pl.multiple_of(up_at + block * BLOCK, BLOCK), BLOCK)
        for row in range(2):
            rows = slice(row * (count // 2), (row + 1) * (count // 2))
            at = pl.ds(pl.multiple_of(block * count + row * (count // 2), count // 2), count // 2)
            g_act = dot_nt(g_down[rows, :], held[down_rows, :])
            g_up = (g_act * slope[at, :].astype(f32)).astype(bf16)
            slope[at, :] = g_up
            g_b_up[:, aligned(block, BLOCK)] += column_sum(g_up.astype(f32))
            total[rows, :] += dot_nt(g_up, held[up_rows, :])
        sum_tick(index - 1, (0,))
        sum_tick(index - 1, (1, 2, 3))
        g_up = slope[aligned(block, count), :]
        for part in range(2):
            at = pl.ds(pl.multiple_of(up_at + block * BLOCK + part * HALF, HALF), HALF)
            held[at, :] = dot_nn(flip[part * HALF : (part + 1) * HALF, :], g_up).astype(bf16)
        if comm:
            pl.when(index == 0)(lambda: told(mid_sem.at[0]))
        sum_start(index)
        for part in range(2):
            at = pl.ds(pl.multiple_of(down_at + block * BLOCK + part * HALF, HALF), HALF)
            grads = dot_tn(act[aligned(block, count), part * HALF : (part + 1) * HALF], g_down[...])
            held[at, :] = grads.astype(bf16)

    if comm:
        tell(mid_sem.at[1])
    sum_tick(3)
    if comm:
        told(mid_sem.at[1])
    for step in range(up_blocks):
        sum_start(up_blocks + step)
    for head in range(2):
        e_copy(0, head, (quads - 1) * quad_steps * 2 + head, False).start()

    @pl.loop(0, row_blocks)
    def _(block):
        rows = aligned(block, ROWS)
        grad, unit = total[rows, :], normed[rows, :]
        scaled = grad * gain_one
        g_pre = inv_one[rows, :1] * (scaled - row_mean(scaled) - unit * row_mean(scaled * unit))
        total[rows, :] = g_pre
        low_pre = g_pre.astype(bf16)
        g_down[rows, :] = low_pre
        g_vectors[2:3, :] += column_sum(low_pre.astype(f32))
        g_vectors[3:4, :] += column_sum(grad * unit)
        g_vectors[4:5, :] += column_sum(grad)

    for part in range(2):
        rows = slice(part * (count // 2), (part + 1) * (count // 2))
        g_ctx_t[:, rows] = dot_nt(held[3 * BLOCK : 4 * BLOCK, :], g_down[rows, :]).astype(bf16)
    for part in range(2):
        at = slice(3 * BLOCK + part * HALF, 3 * BLOCK + (part + 1) * HALF)
        held[at, :] = dot_nn(ctx_t[part * HALF : (part + 1) * HALF, :], g_down[...]).astype(bf16)

    sum_start(8)
    sum_tick(4)

    def fold(block, row, share_of, source, order=None):
        pick, owned, row_of = owner_tables(block * BLOCK, share_of, 256, order)
        keep = owned if row is None else owned & (row_of == row)
        wide = 1 if row is not None else 8
        full = source[:, aligned(block, BLOCK)].reshape(1, wide, BLOCK)
        spread = jnp.broadcast_to(full, (16, 8, BLOCK)).reshape(128, BLOCK)
        spread = jnp.where(keep, spread, 0.0)
        upper = spread.astype(bf16)
        g_small[:, 128:384] += dot_nt(upper, pick) + dot_nt((spread - upper.astype(f32)).astype(bf16), pick)

    if comm:
        g_small[...] = jnp.zeros_like(g_small)
        share_qkv, share_up, share = widths(width, ff)

        @pl.loop(0, up_blocks)
        def _(block):
            fold(block, 1, share_up, g_b_up)

        fold(0, None, share, g_vectors)

    def e_step(order):
        quad = quads - 1 - order // quad_steps
        return quad * quad_steps + order % quad_steps

    def fetch(order):
        for head in range(2):
            e_copy(order % 2, head, e_step(order) * 2 + head, False).start()

    ones = jnp.ones((16, count), bf16)

    def attend_back(order):
        step = e_step(order)
        pair, slot = step // slots, step % slots
        cols = aligned(slot, SLOT)
        place = order % 2

        @pl.when(order + 1 < steps)
        def _():
            fetch(order + 1)

        for head in range(2):
            e_copy(place, head, 0, False).wait()
        sine_t, cosine_t = wave_t[:WAVE, cols], wave_t[WAVE:, cols]
        sc_t = (wave_t[:, cols] * scale_factor).astype(bf16)
        cs_t = (jnp.concatenate([cosine_t, sine_t], axis=0) * scale_factor).astype(bf16)
        values = v_row[slot, pair]
        g_lows, row_dots, g_probs, g_scores, g_qs, g_ks = [], [], [], [], [], []
        g_parts = [[], [], []]
        spans = [slice(head * HD, (head + 1) * HD) for head in range(2)]
        for head in range(2):
            at = pl.ds(pl.multiple_of(pair * PAIR + head * HD, HD), HD)
            g_rows = g_ctx_t[at, cols].astype(f32) * inv_total[step * 2 + head]
            row_dots.append(jnp.sum(g_rows * ctx_t[at, cols].astype(f32), axis=0, keepdims=True))
            g_lows.append(g_rows.astype(bf16))
            zero = jnp.zeros_like(g_lows[head])
            g_pair = jnp.concatenate([g_lows[head], zero] if head == 0 else [zero, g_lows[head]], axis=0)
            g_probs.append(dot_nn(values, g_pair))
        for head in range(2):
            g_scores.append((e_buf[place, head].astype(f32) * (g_probs[head] - row_dots[head])).astype(bf16))
        for head in range(2):
            g_qs.append(dot_nn(jnp.concatenate([k8t[slot, pair, spans[head], :], cs_t], axis=0), g_scores[head]))
        for head in range(2):
            g_ks.append(dot_nt(jnp.concatenate([q8t[slot, pair, spans[head], :], sc_t], axis=0), g_scores[head]))
        for head in range(2):
            g_parts[2].append(dot_nt(g_lows[head], e_buf[place, head]))
        for head in range(2):
            k_t, q_t = k8t[slot, pair, spans[head], :], q8t[slot, pair, spans[head], :]
            g_q, g_k = g_qs[head], g_ks[head]
            first, second = g_q[HD : HD + WAVE], g_q[HD + WAVE :]
            g_qbox = jnp.concatenate(
                [first * sine_t - second * cosine_t, first * cosine_t + second * sine_t], axis=0
            ).astype(bf16)
            first, second = g_k[HD : HD + WAVE], g_k[HD + WAVE :]
            g_kbox = jnp.concatenate(
                [first * cosine_t - second * sine_t, first * sine_t + second * cosine_t], axis=0
            ).astype(bf16)
            g_parts[0].append(g_q[:HD] + dot_nn(w_box_t[...], g_qbox))
            g_parts[1].append(g_k[:HD] + dot_nn(w_box_t[...], g_kbox))
            g_w_box[...] += dot_nt(g_qbox, q_t) + dot_nt(g_kbox, k_t)
        for part in range(3):
            at = pl.ds(pl.multiple_of(part * QUAD + pair % 2 * PAIR, PAIR), PAIR)
            flip[at, cols] = jnp.concatenate(g_parts[part], axis=0).astype(bf16)

    kept = [slope.at[(2 + turn) * count : (2 + turn) * count + BLOCK] for turn in range(2)]
    kept_last = g_down.at[:BLOCK]

    @pl.loop(0, quads)
    def _(turn):
        quad = quads - 1 - turn

        @pl.loop(0, quad_steps)
        def _(inner):
            order = turn * quad_steps + inner
            if comm:
                pl.when(order % 2 == 1)(functools.partial(sum_tick, 5 + order // 2, (0,)))
                pl.when((order % 2 == 0) & (order > 0))(functools.partial(sum_tick, 4 + order // 2, (1, 2, 3)))
            attend_back(order)

        if comm:
            pl.when(turn == quads - 1)(functools.partial(sum_tick, 10, (1, 2, 3)))

        @pl.when(turn < quads - 1)
        def _():
            at = pl.ds(pl.multiple_of((2 + turn) * count, count), BLOCK)
            slope[at, :] = held[aligned(quad, BLOCK), :]

        @pl.when(turn == quads - 1)
        def _():
            kept_last[...] = held[aligned(quad, BLOCK), :]

        for part in range(2):
            at = pl.ds(pl.multiple_of(quad * BLOCK + part * HALF, HALF), HALF)
            held[at, :] = dot_nt(tok_t[part * HALF : (part + 1) * HALF, :], flip[...]).astype(bf16)
        sum_start(9 + turn)
        g_b_qkv[:, aligned(quad, BLOCK)] = dot_nt(ones, flip[...])[:1]
        if comm:
            fold(quad, 0, share_qkv, g_b_qkv, quad_order)

        @pl.when(turn < quads - 1)
        def _():
            for block in range(row_blocks):
                at = pl.ds(pl.multiple_of(turn * count + block * ROWS, ROWS), ROWS)
                rows = slice(block * ROWS, (block + 1) * ROWS)
                slope[at, :] = jnp.transpose(flip[:, rows].astype(f32)).astype(bf16)

    g_w_box[...] = g_w_box[...] * (1.0 / scale_factor)
    tok_out = []

    def token_grad(block):
        rows = slice(block * ROWS, (block + 1) * ROWS)
        last_part = jnp.transpose(dot_nn(kept_last[...], flip[:, rows]))
        first_part = dot_nt(slope[rows, :], kept[0][...])
        rest = dot_nt(slope[count + rows.start : count + rows.stop, :], kept[1][...])
        total[rows, :] += last_part + first_part + rest
        tok_out.append(pltpu.make_async_copy(total.at[rows], g_tok_out.at[rows], io_sem.at[4 + block]))
        tok_out[-1].start()

    if comm:
        g_small[:, :HD] = g_w_box[...]
        sums.sum_cores(0)
        sum_tick(11, (1, 2, 3))
        sum_tick(11, (0,))
        sums.sum_far(0)
        sum_tick(12, (2, 3))
        token_grad(0)
        token_grad(1)
        sum_tick(12, (1,))
        sums.sum_near(0)
        token_grad(2)
        sum_tick(13, (3,))
        sum_tick(13, (2,))
        sums.sum_column(0)
        token_grad(3)
        blocks.results_in(0)
        moves = [copy_in(final.at[PIECE:], final_out.at[PIECE:], 2)]
        moves[0].start()
        sum_tick(14, (3,))
        sums.sum_end(0)
        for stream in range(STREAMS):
            blocks.summed(stream)
        sums.summed(0)
        blocks.results_in(1)
        moves.append(copy_in(final.at[:PIECE], final_out.at[:PIECE], 3))
        moves[1].start()
        sums.results_in(1)
        moves.append(copy_in(small_final, small_out, 8))
        moves[2].start()
        for copy in moves:
            copy.wait()
    else:
        for block in range(row_blocks):
            token_grad(block)
        g_w_box_out[...] = g_w_box[...]
        g_b_qkv_out[...] = g_b_qkv[...]
        g_b_up_out[...] = g_b_up[...]
        g_vectors_out[...] = g_vectors[...]
        out = copy_in(held, g_held, 2)
        out.start()
        out.wait()
    for copy in tok_out:
        copy.wait()


def shaped(shape, dtype):
    return jax.ShapeDtypeStruct(shape, dtype)


def in_vmem(count):
    return [pl.BlockSpec(memory_space=pltpu.VMEM)] * count


def in_hbm(count):
    return [pl.BlockSpec(memory_space=pl.ANY)] * count


def run_layer(comm, tokens, cotangent, coords, segs, big, little):
    count, width = tokens.shape
    ff = 4 * BLOCK
    slots, pairs = count // SLOT, HEADS // 2
    held_shape = (STREAMS * BLOCK, BLOCK)
    out_shape = [
        shaped((count, width), bf16),
        shaped((count, width), f32),
        shaped((slots * HEADS, SLOT, SLOT), bf16),
    ]
    out_specs = in_hbm(3)
    if comm:
        out_shape += [shaped((STREAMS * PIECE, BLOCK), f32), shaped((8, SMALL), f32)]
        out_specs += in_hbm(2)
    else:
        out_shape += [shaped(held_shape, bf16), shaped((2 * WAVE, HD), f32), shaped((1, 3 * width), f32)]
        out_shape += [shaped((1, ff), f32), shaped((8, width), f32)]
        out_specs += in_hbm(1) + in_vmem(4)
    vmem = pltpu.VMEM
    dma = pltpu.SemaphoreType.DMA
    scratch = [
        vmem(held_shape, bf16),
        vmem(held_shape, bf16),
        vmem((ff // BLOCK * count, BLOCK), bf16),
        vmem((slots, pairs, PAIR, SLOT), bf16),
        vmem((slots, pairs, PAIR, SLOT), bf16),
        vmem((slots, pairs, SLOT, PAIR), bf16),
        vmem((width, count), bf16),
        vmem((2 * WAVE, count), f32),
        vmem((count, 2 * WAVE), f32),
        vmem((2, 2, SLOT, SLOT), bf16),
        vmem((count, width), f32),
        vmem((count, width), f32),
        vmem((width, count), bf16),
        vmem((count, width), bf16),
        vmem((width, count), bf16),
        vmem((width, count), bf16),
        vmem((count, 128), f32),
        vmem((slots * HEADS, 1, SLOT), f32),
        vmem((2 * WAVE, HD), bf16),
        vmem((HD, 2 * WAVE), bf16),
        vmem((1, 3 * width), f32),
        vmem((1, ff), f32),
        vmem((8, width), f32),
        vmem((2 * WAVE, HD), f32),
        vmem((1, 3 * width), f32),
        vmem((1, ff), f32),
        vmem((8, width), f32),
        dma((2, 2)),
        dma((32,)),
        vmem(coords.shape, jnp.int32),
        vmem(segs.shape, jnp.int32),
        vmem((PAIR, 4 * WAVE), bf16),
        vmem((4 * WAVE, PAIR), bf16),
    ]
    if comm:
        scratch += [
            vmem((STREAMS * PIECE, BLOCK), f32),
            vmem((128, SMALL), f32),
            vmem((256, SMALL // 2), f32),
            vmem((128, SMALL), f32),
            vmem((8, SMALL), f32),
            pltpu.SemaphoreType.REGULAR((2,)),
            *[vmem(value.shape, f32) for value in little],
            dma((STREAMS, 4)), dma((STREAMS, 2)), dma((STREAMS, 4)), dma((STREAMS,)), dma((2, 2)),
            dma((1, 4)), dma((1, 2)), dma((1, 4)), dma((1,)),
            dma((2, 2)),
        ]
        extra = dict(collective_id=0, has_side_effects=True)
    else:
        extra = {}
    return pl.pallas_call(
        functools.partial(layer_kernel, comm),
        out_shape=out_shape,
        in_specs=in_hbm(4 + len(big)) + (in_hbm if comm else in_vmem)(len(little)),
        out_specs=out_specs,
        scratch_shapes=scratch,
        compiler_params=pltpu.CompilerParams(vmem_limit_bytes=vmem_limit, **extra),
        name="layer",
    )(tokens, cotangent, coords, segs, *big, *little)


def finish_kernel(*refs):
    layer_in, tok_in, blocks_in, small_in = refs[:4]
    layer_out, tok_out, p_qkv, p_out, p_up, p_down = refs[4:10]
    small_out = refs[10:19]
    layer, tok, blocks, small = refs[19:23]
    small_rows = refs[23:32]
    load_sem, store_sem = refs[32:]
    width = layer_in.shape[1]
    loads, stores = [], []
    parts = 4
    rows = layer_in.shape[0] // parts
    small_load = pltpu.make_async_copy(small_in, small, load_sem.at[0])
    loads.append((pltpu.make_async_copy(blocks_in, blocks, load_sem.at[1]), []))
    for quad in range(width // QUAD):
        for part in range(3):
            loads[0][1].append((
                blocks.at[quad * PIECE : (quad + 1) * PIECE, part * QUAD : (part + 1) * QUAD],
                p_qkv.at[:, part * width + quad * QUAD : part * width + (quad + 1) * QUAD],
            ))
    loads[0][1].append((blocks.at[3 * PIECE : 4 * PIECE], p_out))
    for block in range(4):
        loads[0][1].append((
            blocks.at[(4 + block) * PIECE : (5 + block) * PIECE], p_up.at[:, block * BLOCK : (block + 1) * BLOCK]
        ))
    loads[0][1].append((blocks.at[8 * PIECE : 12 * PIECE], p_down))
    for source, held, target in ((tok_in, tok, tok_out), (layer_in, layer, layer_out)):
        for part in range(parts):
            at = slice(part * rows, (part + 1) * rows)
            copy = pltpu.make_async_copy(source.at[at], held.at[at], load_sem.at[1 + len(loads)])
            loads.append((copy, [(held.at[at], target.at[at])]))
    small_load.start()
    for copy, _ in loads:
        copy.start()

    def store(source, target):
        stores.append(pltpu.make_async_copy(source, target, store_sem.at[len(stores)]))
        stores[-1].start()

    small_load.wait()
    for row in range(8):
        small_rows[row][...] = small[row : row + 1, 128 : 128 + small_rows[row].shape[1]]
    small_rows[8][...] = small[:, :HD]
    for source, target in zip(small_rows, small_out):
        store(source, target)
    for copy, moves in loads:
        copy.wait()
        for source, target in moves:
            store(source, target)
    for copy in stores:
        copy.wait()


def run_finish(layer_out, g_tok, blocks, small, big, little):
    shapes = [shaped(layer_out.shape, bf16), shaped(g_tok.shape, f32)]
    shapes += [shaped(w.shape, f32) for w in big + little]
    dma = pltpu.SemaphoreType.DMA
    return pl.pallas_call(
        finish_kernel,
        out_shape=shapes,
        in_specs=in_hbm(4),
        out_specs=in_hbm(len(shapes)),
        scratch_shapes=[
            pltpu.VMEM(layer_out.shape, bf16), pltpu.VMEM(g_tok.shape, f32), pltpu.VMEM(blocks.shape, f32),
            pltpu.VMEM(small.shape, f32), *[pltpu.VMEM(v.shape, f32) for v in little], dma((16,)), dma((40,)),
        ],
        compiler_params=pltpu.CompilerParams(vmem_limit_bytes=vmem_limit),
        name="finish",
    )(layer_out, g_tok, blocks, small)


def to_blocks(w_qkv, w_out, w_up, w_down):
    width = w_out.shape[1]
    qkv = w_qkv.reshape(width, 3, width // QUAD, QUAD).transpose(2, 0, 1, 3).reshape(-1, BLOCK)
    up = w_up.reshape(width, -1, BLOCK).transpose(1, 0, 2).reshape(-1, BLOCK)
    return jnp.concatenate([qkv, w_out, up, w_down], axis=0)


def from_blocks(held, width):
    qkv = held[: 3 * BLOCK].reshape(width // QUAD, width, 3, QUAD).transpose(1, 2, 0, 3).reshape(width, -1)
    up = held[4 * BLOCK : 8 * BLOCK].reshape(-1, width, BLOCK).transpose(1, 0, 2).reshape(width, -1)
    return qkv, held[3 * BLOCK : 4 * BLOCK], up, held[8 * BLOCK :]


def per_device(
    mesh_shape, tokens, cotangent, segments, box_coords, w_qkv, b_qkv, w_box, w_out, b_out, gain_one, shift_one,
    w_up, b_up, w_down, b_down, gain_two, shift_two,
):
    count, width = tokens.shape
    segs = segments.reshape(1, -1)
    vectors = [b_qkv, b_up, b_out, gain_one, shift_one, b_down, gain_two, shift_two]
    if mesh_shape == (16, 2):
        little = [v.reshape(1, -1) for v in vectors] + [w_box]
        big = [w_qkv, w_out, w_up, w_down]
        layer_out, g_tok, _, blocks, small = run_layer(True, tokens, cotangent, box_coords, segs, big, little)
        layer_out, g_tok, p_wq, p_wo, p_wu, p_wd, *rest = run_finish(layer_out, g_tok, blocks, small, big, little)
        p_bq, p_bu, p_bo, p_g1, p_s1, p_bd, p_g2, p_s2 = [v.reshape(-1) for v in rest[:8]]
        p_wb = rest[8]
    else:
        low = lambda value: value.astype(bf16)
        gather = lambda value: lax.all_gather(low(value), "fsdp", axis=0, tiled=True)
        held = to_blocks(gather(w_qkv), gather(w_out), gather(w_up), gather(w_down))
        wb, bq, bu, *six = [gather(v) for v in [w_box] + vectors]
        order = quad_order(jnp.arange(3 * width))
        rows = jnp.stack([jnp.zeros((width,), bf16)] * 2 + six).astype(f32)
        layer_out, g_tok, _, g_held, g_wb, g_bq, g_bu, g_six = run_layer(
            False, tokens, cotangent, box_coords, segs, [held],
            [wb, bq[order].astype(f32).reshape(1, -1), bu.astype(f32).reshape(1, -1), rows],
        )

        def scatter(grad):
            part = lax.psum_scatter(grad, "fsdp", scatter_dimension=0, tiled=True)
            return lax.psum(part, "rep").astype(f32)

        p_wq, p_wo, p_wu, p_wd = [scatter(g) for g in from_blocks(g_held, width)]
        g_bq = jnp.zeros((3 * width,), f32).at[order].set(g_bq[0])
        p_wb, p_bq, p_bu = scatter(g_wb), scatter(g_bq), scatter(g_bu[0])
        p_bo, p_g1, p_s1, p_bd, p_g2, p_s2 = [scatter(g_six[2 + i]) for i in range(VECTORS)]
    return (
        layer_out, g_tok, p_wq, p_bq, p_wb, p_wo, p_bo, p_g1, p_s1,
        p_wu, p_bu, p_wd, p_bd, p_g2, p_s2,
    )


def solution(mesh):
    tokens = P(("fsdp", "rep"), None)
    matrix, vector = P("fsdp", None), P("fsdp")
    kinds = [matrix, vector, matrix, matrix, vector, vector, vector, matrix, vector, matrix, vector, vector, vector]
    return jax.shard_map(
        functools.partial(per_device, (mesh.shape["fsdp"], mesh.shape["rep"])),
        mesh=mesh,
        in_specs=(tokens, tokens, P(("fsdp", "rep")), P(None, ("fsdp", "rep")), *kinds),
        out_specs=(tokens, tokens, *kinds),
        check_vma=False,
    )
```

```python
import functools
import math

import jax
import jax.numpy as jnp
from jax import lax
from jax.experimental import pallas as pl
from jax.experimental.pallas import tpu as pltpu
from jax.sharding import PartitionSpec as P

HEADS = 12
HD = 64
FREQ = 16
SLOT = 512
WAVE = 4 * FREQ
PAIR = 2 * HD
QUAD = 4 * HD

f32 = jnp.float32
bf16 = jnp.bfloat16
neg_large = -1e30
eps_norm = 1e-12
scale_factor = 1.0 / math.sqrt(HD)
vmem_limit = 67_000_000


def dot_nn(left, right):
    return lax.dot_general(left, right, (((1,), (0,)), ((), ())), preferred_element_type=f32)


def dot_nt(left, right):
    return lax.dot_general(left, right, (((1,), (1,)), ((), ())), preferred_element_type=f32)


def dot_tn(left, right):
    return lax.dot_general(left, right, (((0,), (0,)), ((), ())), preferred_element_type=f32)


def aligned(index, size):
    return pl.ds(pl.multiple_of(index * size, size), size)


def wave_rows(coords):
    count = coords.shape[1]
    spread = [jnp.broadcast_to(coords[c : c + 1, :].astype(f32), (FREQ, count)) for c in range(4)]
    scaled = jnp.concatenate(spread + spread, axis=0) * (100.0 / 1024.0)
    rows = lax.broadcasted_iota(jnp.int32, scaled.shape, 0)
    frequency = jnp.exp(-math.log(10000.0) * (rows & (FREQ - 1)).astype(f32) / FREQ)
    angle = scaled * frequency
    turns = jnp.floor(angle * (2.0 / math.pi) + 0.5)
    rest = ((angle - turns * 1.5703125) - turns * 4.837512969970703125e-4) - turns * 7.549789954891e-8
    square = rest * rest
    sine = rest + rest * square * (
        -1.6666654611e-1 + square * (8.3321608736e-3 + square * -1.9515295891e-4)
    )
    cosine = 1.0 - 0.5 * square + square * square * (
        4.166664568298827e-2 + square * (-1.388731625493765e-3 + square * 2.443315711809948e-5)
    )
    quadrant = turns.astype(jnp.int32) + jnp.where(rows >= WAVE, 1, 0)
    value = jnp.where((quadrant & 1) == 1, cosine, sine)
    value = jnp.where((quadrant & 2) == 2, -value, value)
    return value.astype(bf16).astype(f32)


def swap_lanes(value):
    return pltpu.roll(value, WAVE, 1)


def gelu_parts(value):
    t = 1.0 / (1.0 + (0.3275911 * math.sqrt(0.5)) * jnp.abs(value))
    bell = jnp.exp2(value * value * (-0.5 * math.log2(math.e)))
    half_tail = bell * t * (
        0.127414796 + t * (-0.142248368 + t * (0.7107068705 + t * (-0.7265760135 + t * 0.5307027145)))
    )
    return jnp.where(value >= 0, 1.0 - half_tail, half_tail), bell * (1.0 / math.sqrt(2.0 * math.pi))


def row_mean(value):
    return jnp.mean(value, axis=-1, keepdims=True)


ROWS = 256
BLOCK = 768
PIECE = 48
HALF = BLOCK // 2
SMALL = 512
STREAMS = 12
VECTORS = 6
LEVEL_FIRST = 11


def widths(width, ff):
    return 3 * width // 16, ff // 16, width // 16


class Route:
    def __init__(self):
        chip = lax.axis_index("fsdp")
        self.core = lax.axis_index("rep")
        self.level, self.me = chip // 4, chip % 4
        near_step, far_step = 1 + self.core, 2 - self.core
        near_move = near_step * (1 - 2 * ((self.me // near_step) % 2))
        far_move = far_step * (1 - 2 * ((self.me // far_step) % 2))
        self.near = self.me + near_move
        self.far = self.me + far_move
        self.across = self.me + near_move + far_move

    def chip(self, level, place):
        return level * 4 + place

    def levels(self):
        return [(self.level + k) % 4 for k in range(1, 4)]

    def peers(self):
        chips = [self.chip(level, self.me) for level in self.levels()]
        chips += [self.chip(self.level, self.near), self.chip(self.level, self.far)]
        return [(chip, self.core) for chip in chips] + [(self.chip(self.level, self.me), 1 - self.core)]


def remote(source, target, send, recv, chip, core):
    return pltpu.make_async_remote_copy(
        src_ref=source, dst_ref=target, send_sem=send, recv_sem=recv,
        device_id=(chip, core), device_id_type=pl.DeviceIdType.MESH,
    )


def half_columns(half, size):
    return pl.ds(pl.multiple_of(half * size, size), size)


class Streams:
    def __init__(self, held, stage, final, sems):
        self.held = held
        self.upper = held.at[: 8 * BLOCK].reshape(8, 4, 4, PIECE, BLOCK)
        self.lower = held.at[8 * BLOCK :].reshape(4, 4, 4, PIECE, BLOCK)
        self.stage = stage.reshape(STREAMS, 4, 4, PIECE, BLOCK)
        self.final = final
        self.gather_recv, self.gather_send, self.sum_recv, self.sum_send, self.final_sem = sems

    def on(self, stream, act):
        if isinstance(stream, int):
            act(self.upper.at[stream] if stream < 8 else self.lower.at[:, :, stream - 8])
        else:
            pl.when(stream < 8)(lambda: act(self.upper.at[stream]))
            pl.when(stream >= 8)(lambda: act(self.lower.at[:, :, stream - 8]))

    def half(self, half):
        return half_columns(half, HALF)

    def several(self, pieces):
        return self.held.at[: PIECE * pieces, :HALF]

    def landing(self, stream, kind):
        block = self.stage.at[(stream + 8) % STREAMS]
        if kind == 0:
            return block.at[:, :, :, :HALF]
        return block.at[(0, 0, 2, 3)[kind] : (0, 2, 3, 4)[kind], :, :, HALF:]

    def result(self, stream, half):
        return self.final.at[pl.ds(pl.multiple_of(stream * PIECE, 16), PIECE), self.half(half)]

    def results(self, last):
        return self.final.at[:PIECE, :HALF] if last else self.final.at[PIECE:, :HALF]


class Vectors:
    def __init__(self, held, stage, final, sems):
        self.held, self.flat, self.final = held, stage, final
        self.shards = held.reshape(4, 4, 8, SMALL)
        self.stage = stage.reshape(8, 4, 8, SMALL // 2)
        self.gather_recv, self.gather_send, self.sum_recv, self.sum_send, self.final_sem = sems

    def on(self, stream, act):
        act(self.shards)

    def half(self, half):
        return half_columns(half, SMALL // 2)

    def several(self, pieces):
        if pieces <= 16:
            return self.held.at[: 8 * pieces, : SMALL // 2]
        return self.flat.at[: 8 * pieces, :]

    def landing(self, stream, kind):
        return self.stage.at[(0, 4, 6, 7)[kind] : (4, 6, 7, 8)[kind]]

    def result(self, stream, half):
        return self.final.at[:, self.half(half)]

    def results(self, last):
        return self.final.at[:, : SMALL // 2]


def drain(view, sem):
    pltpu.make_async_copy(view, view, sem).wait()


class Exchange:
    def __init__(self, route, parts):
        self.route, self.parts = route, parts

    def send(self, source, target, send, recv, level, place, core):
        remote(source, target, send, recv, self.route.chip(level, place), core).start()


    def share(self, stream, view, place, kind):
        p, r = self.parts, self.route
        self.send(
            view, view, p.gather_send.at[stream, 0], p.gather_recv.at[stream, kind], r.level, place, r.core
        )

    def hand_over(self, stream, view):
        p, r = self.parts, self.route
        self.send(
            view, view, p.gather_send.at[stream, 1], p.gather_recv.at[stream, 3], r.level, r.me, 1 - r.core
        )

    def gather_own(self, stream):
        p, r = self.parts, self.route

        def act(shards):
            view = shards.at[r.level, r.me, :, p.half(r.core)]
            for level in r.levels():
                self.send(
                    view, view, p.gather_send.at[stream, 0], p.gather_recv.at[stream, 0], level, r.me, r.core
                )

        p.on(stream, act)

    def gather_column(self, stream):
        p, r = self.parts, self.route
        drain(p.several(3), p.gather_recv.at[stream, 0])

        def act(shards):
            view = shards.at[:, r.me, :, p.half(r.core)]
            self.share(stream, view, r.near, 1)
            self.share(stream, view, r.far, 2)
            for level in r.levels():
                self.hand_over(stream, shards.at[level, r.me, :, p.half(r.core)])

        p.on(stream, act)

    def gather_near(self, stream):
        p, r = self.parts, self.route
        drain(p.several(4), p.gather_recv.at[stream, 1])

        def act(shards):
            view = shards.at[:, r.near, :, p.half(r.core)]
            self.share(stream, view, r.far, 2)
            self.hand_over(stream, view)

        p.on(stream, act)

    def gather_far(self, stream):
        p, r = self.parts, self.route
        drain(p.several(8), p.gather_recv.at[stream, 2])

        def act(shards):
            for place in (r.far, r.across):
                self.hand_over(stream, shards.at[:, place, :, p.half(r.core)])

        p.on(stream, act)


    def level_own(self, stream):
        p, r = self.parts, self.route

        def act(shards):
            view = shards.at[r.level, r.me, :, p.half(r.core)]
            self.share(stream, view, r.near, 1)
            self.share(stream, view, r.far, 2)

        p.on(stream, act)

    def level_near(self, stream):
        p, r = self.parts, self.route
        drain(p.several(1), p.gather_recv.at[stream, 1])

        def act(shards):
            view = shards.at[r.level, r.near, :, p.half(r.core)]
            self.share(stream, view, r.far, 2)
            self.hand_over(stream, view)

        p.on(stream, act)

    def level_far(self, stream):
        p, r = self.parts, self.route
        drain(p.several(2), p.gather_recv.at[stream, 2])

        def act(shards):
            view = shards.at[r.level, :, :, p.half(r.core)]
            for level in r.levels():
                self.send(
                    view, view, p.gather_send.at[stream, 0], p.gather_recv.at[stream, 0], level, r.me, r.core
                )
            for place in (r.far, r.across):
                self.hand_over(stream, shards.at[r.level, place, :, p.half(r.core)])

        p.on(stream, act)

    def level_column(self, stream):
        p, r = self.parts, self.route
        drain(p.several(12), p.gather_recv.at[stream, 0])

        def act(shards):
            for level in r.levels():
                self.hand_over(stream, shards.at[level, :, :, p.half(r.core)])

        p.on(stream, act)

    def gathered(self, stream):
        p = self.parts
        drain(p.several(15), p.gather_recv.at[stream, 3])

    def gather_sent(self, stream):
        p = self.parts
        drain(p.several(15), p.gather_send.at[stream, 0])
        drain(p.several(15), p.gather_send.at[stream, 1])


    def pass_on(self, stream, view, landing, kind, level, place):
        p, r = self.parts, self.route
        self.send(view, landing, p.sum_send.at[stream], p.sum_recv.at[stream, kind], level, place, r.core)

    def sum_cores(self, stream):
        p, r = self.parts, self.route

        def act(shards):
            self.send(
                shards.at[:, :, :, p.half(1 - r.core)], p.landing(stream, 0),
                p.sum_send.at[stream], p.sum_recv.at[stream, 0], r.level, r.me, 1 - r.core,
            )

        p.on(stream, act)

    def sum_far(self, stream):
        p, r = self.parts, self.route
        drain(p.several(16), p.sum_recv.at[stream, 0])
        landed, target = p.landing(stream, 0), p.landing(stream, 1)

        def act(shards):
            def add(place):
                view = shards.at[:, place, :, p.half(r.core)]
                view[...] += landed[:, place]
                return view

            for index, place in enumerate((r.far, r.across)):
                self.pass_on(stream, add(place), target.at[index], 1, r.level, r.far)
            for place in (r.me, r.near):
                add(place)

        p.on(stream, act)

    def sum_near(self, stream):
        p, r = self.parts, self.route
        drain(p.several(8), p.sum_recv.at[stream, 1])
        landed, target = p.landing(stream, 1), p.landing(stream, 2)

        def act(shards):
            view = shards.at[:, r.near, :, p.half(r.core)]
            view[...] += landed[1]
            self.pass_on(stream, view, target.at[0], 2, r.level, r.near)
            view = shards.at[:, r.me, :, p.half(r.core)]
            view[...] += landed[0]

        p.on(stream, act)

    def sum_column(self, stream):
        p, r = self.parts, self.route
        drain(p.several(4), p.sum_recv.at[stream, 2])
        landed, target = p.landing(stream, 2), p.landing(stream, 3)

        def act(shards):
            view = shards.at[:, r.me, :, p.half(r.core)]
            view[...] += landed[0]
            for index, level in enumerate(r.levels()):
                self.pass_on(
                    stream, shards.at[level, r.me, :, p.half(r.core)], target.at[0, index], 3, level, r.me
                )

        p.on(stream, act)

    def sum_end(self, stream):
        p, r = self.parts, self.route
        drain(p.several(3), p.sum_recv.at[stream, 3])
        landed = p.landing(stream, 3)
        view = p.result(stream, r.core)

        def act(shards):
            total = shards[r.level, r.me, :, p.half(r.core)].astype(f32)
            for index in range(3):
                total += landed[0, index].astype(f32)
            view[...] = total

        p.on(stream, act)
        last = 1 if isinstance(stream, int) and stream == 0 else 0
        self.send(view, view, p.final_sem.at[last, 0], p.final_sem.at[last, 1], r.level, r.me, 1 - r.core)

    def summed(self, stream):
        p = self.parts
        drain(p.several(31), p.sum_send.at[stream])

    def results_in(self, last):
        p = self.parts
        for side in range(2):
            drain(p.results(last), p.final_sem.at[last, side])


def owner_tables(start, share, depth, order=None):
    col = lax.broadcasted_iota(jnp.int32, (1, BLOCK), 1) + start
    source = col if order is None else order(col)
    owner, entry = source // share, source % share
    pick = (entry == lax.broadcasted_iota(jnp.int32, (depth, BLOCK), 0)).astype(bf16)
    row = lax.broadcasted_iota(jnp.int32, (128, BLOCK), 0)
    return pick, owner == (row >> 3), row & 7


def quad_order(col):
    return (col % BLOCK) // QUAD * BLOCK + col // BLOCK * QUAD + col % QUAD


def layer_kernel(comm, *refs):
    refs = list(refs)

    def take(count):
        taken, refs[:] = refs[:count], refs[count:]
        return taken

    tok_in, cot_in, coords_in, segs_in = take(4)
    if comm:
        w_qkv_in, w_out_in, w_up_in, w_down_in = take(4)
        small_in = take(9)
    else:
        held_in, w_box_in, b_qkv_in, b_up_in, vectors_in = take(5)
    layer_out, g_tok_out, e_hbm = take(3)
    if comm:
        final_out, small_out = take(2)
    else:
        g_held, g_w_box_out, g_b_qkv_out, g_b_up_out, g_vectors_out = take(5)
    (held, stage, slope, q8t, k8t, v_row, ctx_t, wave_t, wave_r, e_buf, normed, total, flip, g_down, tok_t, g_ctx_t,
     inv_one, inv_total, w_box, w_box_t, b_qkv, b_up, vectors, g_w_box, g_b_qkv, g_b_up, g_vectors, e_sem, io_sem, coords, segs, w_pair, w_pair_t) = take(33)
    if comm:
        final, small, small_stage, g_small, small_final, mid_sem = take(6)
        small_held = take(9)
        block_sems, small_sems, small_final_sems = take(5), take(4), take(1)

    count, width = tok_t.shape[1], tok_t.shape[0]
    ff = slope.shape[0] // count * BLOCK
    slots, pairs = count // SLOT, HEADS // 2
    row_blocks = count // ROWS
    up_blocks = ff // BLOCK
    quads = pairs // 2
    ctx, low, cot, tok = [stage.at[part * count : (part + 1) * count] for part in range(4)]
    act = stage.at[STREAMS * BLOCK - up_blocks * count :]
    up_at, down_at = 4 * BLOCK, 8 * BLOCK

    def copy_in(source, target, index=0):
        return pltpu.make_async_copy(source, target, io_sem.at[index])

    tok_copy = copy_in(tok_in, tok, 0)
    cot_copy = copy_in(cot_in, cot, 1)
    coord_copy = copy_in(coords_in, coords, 2)
    seg_copy = copy_in(segs_in, segs, 3)

    if comm:
        route = Route()
        chip = route.chip(route.level, route.me)
        blocks = Exchange(route, Streams(held, stage, final, block_sems))
        extras = Exchange(route, Vectors(small, small_stage, small_final, [*small_sems, *small_final_sems]))
        sums = Exchange(route, Vectors(g_small, small_stage, small_final, [*small_sems, *small_final_sems]))
        barrier = pltpu.get_barrier_semaphore()
        for peer, core in route.peers():
            pl.semaphore_signal(barrier, inc=1, device_id=(peer, core), device_id_type=pl.DeviceIdType.MESH)
        moves = []
        for quad in range(quads):
            for part in range(3):
                moves.append((
                    w_qkv_in.at[:, part * width + quad * QUAD : part * width + (quad + 1) * QUAD],
                    total.at[quad * PIECE : (quad + 1) * PIECE, part * QUAD : (part + 1) * QUAD],
                ))
        moves.append((w_out_in, total.at[3 * PIECE : 4 * PIECE]))
        for block in range(up_blocks):
            moves.append((
                w_up_in.at[:, block * BLOCK : (block + 1) * BLOCK],
                total.at[(4 + block) * PIECE : (5 + block) * PIECE],
            ))
        moves.append((w_down_in, total.at[8 * PIECE : 12 * PIECE]))
        moves += list(zip(small_in, small_held))
        moves = [copy_in(source, target, 4 + index) for index, (source, target) in enumerate(moves)]
        first = 3 * quads
        for copy in moves[:first] + moves[first + 1 + up_blocks + 1 :] + moves[first : first + 1 + up_blocks + 1]:
            copy.start()
        for copy in (coord_copy, seg_copy, tok_copy, cot_copy):
            copy.start()

        def round_block(block):
            at = pl.ds(pl.multiple_of(block * BLOCK + PIECE * chip, 16), PIECE)
            held[at, :] = total[block * PIECE : (block + 1) * PIECE, :].astype(bf16)

        g_small[:8, :] = jnp.zeros((8, SMALL), f32)
        for copy in moves[:first]:
            copy.wait()
        for block in range(quads):
            round_block(block)
        for copy in moves[first + 1 + up_blocks + 1 :]:
            copy.wait()
        g_small[:8, :HD] = small_held[8][...].astype(bf16).astype(f32)
        for row in range(8):
            value = small_held[row][...].astype(bf16).astype(f32)
            g_small[row : row + 1, 128 : 128 + value.shape[1]] = value
        small[pl.ds(pl.multiple_of(chip * 8, 8), 8), :] = g_small[:8, :]
        pl.semaphore_wait(barrier, 6)
        extras.gather_own(0)
        for stream in range(quads):
            blocks.gather_own(stream)
        for copy in moves[first : first + 1 + up_blocks + 1]:
            copy.wait()
        for block in range(quads, STREAMS - up_blocks):
            round_block(block)
        at = pl.ds(pl.multiple_of(down_at + 4 * PIECE * chip, 16), 4 * PIECE)
        held[at, :] = total[8 * PIECE : 12 * PIECE, :].astype(bf16)
        blocks.level_own(LEVEL_FIRST)
        for stream in range(quads, STREAMS):
            if stream != LEVEL_FIRST:
                blocks.gather_own(stream)
    else:
        for copy in (coord_copy, seg_copy, tok_copy, cot_copy):
            copy.start()
        copy_in(held_in, held, 4).start()
        w_box[...] = w_box_in[...]
        b_qkv[...] = b_qkv_in[...]
        b_up[...] = b_up_in[...]
        vectors[...] = vectors_in[...]

    coord_copy.wait()
    seg_copy.wait()
    wave_t[...] = wave_rows(coords[...])
    wave_r[...] = jnp.transpose(wave_t[...])
    for slot in range(slots):
        seg_i = jnp.broadcast_to(segs[:, slot * SLOT : (slot + 1) * SLOT].astype(f32), (SLOT, SLOT))
        seg_j = jnp.transpose(seg_i)
        normed[slot * SLOT : (slot + 1) * SLOT, :SLOT] = jnp.where(seg_i == seg_j, 0.0, neg_large)
    g_w_box[...] = jnp.zeros_like(g_w_box)
    g_b_up[...] = jnp.zeros_like(g_b_up)
    g_vectors[...] = jnp.zeros_like(g_vectors)
    tok_copy.wait()

    if comm:
        extras.gather_column(0)
        blocks.gather_column(0)
        extras.gather_near(0)
        blocks.gather_near(0)
        blocks.gather_column(1)
        extras.gather_far(0)
        blocks.gather_far(0)
        blocks.gather_near(1)
        blocks.gather_column(2)
        blocks.level_near(LEVEL_FIRST)
        extras.gathered(0)
        table = small[...].astype(bf16)
        w_box[...] = table[:, :HD]
        share_qkv, share_up, share = widths(width, ff)
        for row, columns, share_of, depth, order, target in (
            (0, 3 * width, share_qkv, 256, quad_order, b_qkv),
            (1, ff, share_up, 256, None, b_up),
            (None, width, share, 128, None, vectors),
        ):
            @pl.loop(0, columns // BLOCK)
            def _(block):
                pick, owned, row_of = owner_tables(block * BLOCK, share_of, depth, order)
                spread = dot_nn(table[:, 128 : 128 + depth], pick)
                keep = owned if row is None else owned & (row_of == row)
                rows = jnp.sum(jnp.where(keep, spread, 0.0).reshape(16, 8, BLOCK), axis=0)
                target[:, aligned(block, BLOCK)] = rows if row is None else jnp.sum(rows, axis=0, keepdims=True)

    else:
        copy_in(held_in, held, 4).wait()
    w_box_t[...] = jnp.transpose(w_box[...].astype(f32)).astype(bf16)
    blank = jnp.zeros((2 * WAVE, HD), bf16)
    w_pair_t[: 2 * WAVE, :] = jnp.concatenate([w_box[...], blank], axis=1)
    w_pair_t[2 * WAVE :, :] = jnp.concatenate([blank, w_box[...]], axis=1)
    w_pair[...] = jnp.transpose(w_pair_t[...].astype(f32)).astype(bf16)

    def gather_tick(step):
        if not comm:
            return

        def stream_of(order):
            return order + order // LEVEL_FIRST

        for ahead, act_on in ((1, blocks.gather_near), (3, blocks.gather_column), (0, blocks.gather_far)):
            order = step + ahead
            if isinstance(order, int):
                if order < STREAMS - 1:
                    act_on(stream_of(order))
            else:
                pl.when(order < STREAMS - 1)(functools.partial(act_on, stream_of(order)))

    def need(stream):
        if comm:
            blocks.gathered(stream)

    b_out, gain_one, shift_one, b_down, gain_two, shift_two = [vectors[2 + i : 3 + i, :] for i in range(VECTORS)]
    lane = lax.broadcasted_iota(jnp.int32, (SLOT, PAIR), 1)
    scores = total.reshape(2, SLOT, width)

    def project(quad, slot):
        rows = tok[aligned(slot, SLOT), :]

        def columns(part):
            weight = held[aligned(quad, BLOCK), part * QUAD : (part + 1) * QUAD]
            shift = b_qkv[:, pl.ds(pl.multiple_of(quad * BLOCK + part * QUAD, QUAD), QUAD)]
            return (dot_nn(rows, weight) + shift).astype(bf16)

        q, k, v = columns(0), columns(1), columns(2)
        low[aligned(slot, SLOT), aligned(quad, QUAD)] = k
        flip[aligned(quad, QUAD), aligned(slot, SLOT)] = jnp.transpose(v.astype(f32)).astype(bf16)
        qt = jnp.transpose(q.astype(f32) * scale_factor).astype(bf16)
        kt = jnp.transpose(k.astype(f32) * scale_factor).astype(bf16)
        for part in range(2):
            here = slice(part * PAIR, (part + 1) * PAIR)
            q8t[slot, quad * 2 + part] = qt[here]
            k8t[slot, quad * 2 + part] = kt[here]
            v_row[slot, quad * 2 + part] = v[:, here]

    def e_copy(place, head, index, out):
        pair = (e_buf.at[place, head], e_hbm.at[index])
        return pltpu.make_async_copy(*(pair if out else pair[::-1]), e_sem.at[place, head])

    def attend(step):
        pair, slot = step // slots, step % slots
        cols = aligned(slot, SLOT)
        place = step % 2

        @pl.when(step >= 2)
        def _():
            for head in range(2):
                e_copy(place, head, 0, True).wait()

        sine_t, cosine_t = wave_t[:WAVE, cols], wave_t[WAVE:, cols]
        sc_t = (wave_t[:, cols] * scale_factor).astype(bf16)
        sc_r = wave_r[cols, :]
        cs_r = swap_lanes(sc_r)
        cc_r = jnp.where(lane < WAVE, cs_r, sc_r)
        ss_r = jnp.where(lane < WAVE, sc_r, -cs_r)
        cs_low = cs_r.astype(bf16)
        keys = low[cols, aligned(pair, PAIR)]
        queries = q8t[slot, pair]
        key_box = dot_nn(keys, w_pair[...])
        query_box = dot_nn(w_pair_t[...], queries)
        low_exps, inverse, heads_t = [], [], []
        for head in range(2):
            here = slice(head * 2 * WAVE, (head + 1) * 2 * WAVE)
            side = key_box[:, here]
            k_side = (side * cc_r + swap_lanes(side) * ss_r).astype(bf16)
            first, second = query_box[here][:WAVE], query_box[here][WAVE:]
            q_side = jnp.concatenate(
                [first * sine_t + second * cosine_t, second * sine_t - first * cosine_t], axis=0
            ).astype(bf16)
            q_t = queries[head * HD : (head + 1) * HD]
            zero = jnp.zeros_like(q_t)
            q_pair = [q_t, zero] if head == 0 else [zero, q_t]
            k_full = jnp.concatenate([keys, cs_low, k_side], axis=1)
            q_full = jnp.concatenate(q_pair + [q_side, sc_t], axis=0)
            scores[head, :, :SLOT] = dot_nn(k_full, q_full) + normed[cols, :SLOT]
        for head in range(2):
            masked = scores[head, :, :SLOT]
            exps = jnp.exp(masked - jnp.max(masked, axis=0, keepdims=True))
            inverse.append(1.0 / jnp.sum(exps, axis=0, keepdims=True))
            low_exps.append(exps.astype(bf16))
            e_buf[place, head] = low_exps[head]
            e_copy(place, head, step * 2 + head, True).start()
            inv_total[step * 2 + head] = inverse[head]
        for head in range(2):
            at = pl.ds(pl.multiple_of(pair * PAIR + head * HD, HD), HD)
            heads_t.append(dot_nn(flip[at, cols], low_exps[head]) * inverse[head])
        both = jnp.concatenate(heads_t, axis=0)
        ctx_t[aligned(pair, PAIR), cols] = both.astype(bf16)
        ctx[cols, aligned(pair, PAIR)] = jnp.transpose(both).astype(bf16)

    steps = slots * pairs
    quad_steps = 2 * slots

    @pl.loop(0, quads)
    def _(quad):
        need(quad)

        @pl.loop(0, slots)
        def _(slot):
            project(quad, slot)

        @pl.loop(0, quad_steps)
        def _(inner):
            step = quad * quad_steps + inner
            if comm:
                @pl.when(step == 1)
                def _():
                    blocks.gather_column(quads)
                    blocks.level_far(LEVEL_FIRST)

                pl.when((step % 2 == 0) & (step > 0))(functools.partial(gather_tick, step // 2))
            attend(step)

    for place in range(2):
        for head in range(2):
            e_copy(place, head, 0, True).wait()

    def column_sum(value):
        return jnp.sum(value, axis=0, keepdims=True)

    gather_tick(6)
    need(3)

    @pl.loop(0, row_blocks)
    def _(block):
        rows = aligned(block, ROWS)
        token_rows = tok[rows, :].astype(f32)
        tok_t[:, rows] = jnp.transpose(token_rows).astype(bf16)
        pre = token_rows + dot_nn(ctx[rows, :], held[3 * BLOCK : 4 * BLOCK, :]) + b_out
        center = pre - row_mean(pre)
        invdev = lax.rsqrt(row_mean(center * center) + eps_norm)
        unit = center * invdev
        inv_one[rows, :] = jnp.broadcast_to(invdev, (ROWS, 128))
        normed[rows, :] = unit
        hidden = unit * gain_one + shift_one
        low[rows, :] = hidden.astype(bf16)
        flip[:, rows] = jnp.transpose(hidden).astype(bf16)

    @pl.loop(0, up_blocks)
    def _(block):
        gather_tick(7 + block)
        if comm:
            pl.when(block == 2)(functools.partial(blocks.level_column, LEVEL_FIRST))
        need(4 + block)

        weight = held[pl.ds(pl.multiple_of(up_at + block * BLOCK, BLOCK), BLOCK), :]
        for row in range(row_blocks):
            rows = slice(row * ROWS, (row + 1) * ROWS)
            total[rows, :] = dot_nn(low[rows, :], weight) + b_up[:, aligned(block, BLOCK)]
        for row in range(row_blocks):
            at = pl.ds(pl.multiple_of(block * count + row * ROWS, ROWS), ROWS)
            up = total[row * ROWS : (row + 1) * ROWS, :]
            cdf, pdf = gelu_parts(up)
            act[at, :] = (up * cdf).astype(bf16)
            slope[at, :] = (cdf + up * pdf).astype(bf16)

    for block in range(up_blocks):
        need(8 + block)
    cot_copy.wait()

    @pl.loop(0, row_blocks)
    def _(block):
        rows = aligned(block, ROWS)
        pre = normed[rows, :] * gain_one + shift_one + b_down
        for part in range(up_blocks):
            at = pl.ds(pl.multiple_of(part * count + block * ROWS, ROWS), ROWS)
            pre += dot_nn(act[at, :], held[down_at + part * BLOCK : down_at + (part + 1) * BLOCK, :])
        center = pre - row_mean(pre)
        invdev = lax.rsqrt(row_mean(center * center) + eps_norm)
        unit = center * invdev
        grad = cot[rows, :].astype(f32)
        cot[rows, :] = (unit * gain_two + shift_two).astype(bf16)
        pltpu.make_async_copy(cot.at[rows], layer_out.at[rows], io_sem.at[0]).start()
        scaled = grad * gain_two
        g_pre = invdev * (scaled - row_mean(scaled) - unit * row_mean(scaled * unit))
        total[rows, :] = g_pre
        low_pre = g_pre.astype(bf16)
        g_down[rows, :] = low_pre
        g_vectors[5:6, :] += column_sum(low_pre.astype(f32))
        g_vectors[6:7, :] += column_sum(grad * unit)
        g_vectors[7:8, :] += column_sum(grad)

    out_copy = pltpu.make_async_copy(cot, layer_out, io_sem.at[0])
    if comm:
        for stream in range(STREAMS):
            blocks.gather_sent(stream)
        extras.gather_sent(0)

    def last(step):
        turn = step // 4
        return STREAMS - 1 - step + (14 - 6 * turn) * turn - 4

    def sum_start(step):
        if comm:
            blocks.sum_cores(last(step))

    def sum_tick(step, stages=(0, 1, 2, 3)):
        if not comm:
            return
        acts = (blocks.sum_far, blocks.sum_near, blocks.sum_column, blocks.sum_end)
        for behind in stages:
            at = step - behind
            if isinstance(at, int):
                if 0 <= at < STREAMS:
                    acts[behind](last(at))
            else:
                pl.when((at >= 0) & (at < STREAMS))(functools.partial(acts[behind], last(at)))

    def tell(sem):
        if comm:
            for peer, core in route.peers():
                pl.semaphore_signal(sem, inc=1, device_id=(peer, core), device_id_type=pl.DeviceIdType.MESH)

    def told(sem):
        if comm:
            pl.semaphore_wait(sem, 6)

    out_copy.wait()
    if comm:
        tell(mid_sem.at[0])

    @pl.loop(0, up_blocks)
    def _(index):
        block = up_blocks - 1 - index
        down_rows = pl.ds(pl.multiple_of(down_at + block * BLOCK, BLOCK), BLOCK)
        up_rows = pl.ds(pl.multiple_of(up_at + block * BLOCK, BLOCK), BLOCK)
        for row in range(2):
            rows = slice(row * (count // 2), (row + 1) * (count // 2))
            at = pl.ds(pl.multiple_of(block * count + row * (count // 2), count // 2), count // 2)
            g_act = dot_nt(g_down[rows, :], held[down_rows, :])
            g_up = (g_act * slope[at, :].astype(f32)).astype(bf16)
            slope[at, :] = g_up
            g_b_up[:, aligned(block, BLOCK)] += column_sum(g_up.astype(f32))
            total[rows, :] += dot_nt(g_up, held[up_rows, :])
        sum_tick(index - 1, (0,))
        sum_tick(index - 1, (1, 2, 3))
        g_up = slope[aligned(block, count), :]
        for part in range(2):
            at = pl.ds(pl.multiple_of(up_at + block * BLOCK + part * HALF, HALF), HALF)
            held[at, :] = dot_nn(flip[part * HALF : (part + 1) * HALF, :], g_up).astype(bf16)
        if comm:
            pl.when(index == 0)(lambda: told(mid_sem.at[0]))
        sum_start(index)
        for part in range(2):
            at = pl.ds(pl.multiple_of(down_at + block * BLOCK + part * HALF, HALF), HALF)
            grads = dot_tn(act[aligned(block, count), part * HALF : (part + 1) * HALF], g_down[...])
            held[at, :] = grads.astype(bf16)

    if comm:
        tell(mid_sem.at[1])
    sum_tick(3)
    if comm:
        told(mid_sem.at[1])
    for step in range(up_blocks):
        sum_start(up_blocks + step)
    for head in range(2):
        e_copy(0, head, (quads - 1) * quad_steps * 2 + head, False).start()

    @pl.loop(0, row_blocks)
    def _(block):
        rows = aligned(block, ROWS)
        grad, unit = total[rows, :], normed[rows, :]
        scaled = grad * gain_one
        g_pre = inv_one[rows, :1] * (scaled - row_mean(scaled) - unit * row_mean(scaled * unit))
        total[rows, :] = g_pre
        low_pre = g_pre.astype(bf16)
        g_down[rows, :] = low_pre
        g_vectors[2:3, :] += column_sum(low_pre.astype(f32))
        g_vectors[3:4, :] += column_sum(grad * unit)
        g_vectors[4:5, :] += column_sum(grad)

    for part in range(2):
        rows = slice(part * (count // 2), (part + 1) * (count // 2))
        g_ctx_t[:, rows] = dot_nt(held[3 * BLOCK : 4 * BLOCK, :], g_down[rows, :]).astype(bf16)
    for part in range(2):
        at = slice(3 * BLOCK + part * HALF, 3 * BLOCK + (part + 1) * HALF)
        held[at, :] = dot_nn(ctx_t[part * HALF : (part + 1) * HALF, :], g_down[...]).astype(bf16)

    sum_start(8)
    sum_tick(4)

    def fold(block, row, share_of, source, order=None):
        pick, owned, row_of = owner_tables(block * BLOCK, share_of, 256, order)
        keep = owned if row is None else owned & (row_of == row)
        wide = 1 if row is not None else 8
        full = source[:, aligned(block, BLOCK)].reshape(1, wide, BLOCK)
        spread = jnp.broadcast_to(full, (16, 8, BLOCK)).reshape(128, BLOCK)
        spread = jnp.where(keep, spread, 0.0)
        upper = spread.astype(bf16)
        g_small[:, 128:384] += dot_nt(upper, pick) + dot_nt((spread - upper.astype(f32)).astype(bf16), pick)

    if comm:
        g_small[...] = jnp.zeros_like(g_small)
        share_qkv, share_up, share = widths(width, ff)

        @pl.loop(0, up_blocks)
        def _(block):
            fold(block, 1, share_up, g_b_up)

        fold(0, None, share, g_vectors)

    def e_step(order):
        quad = quads - 1 - order // quad_steps
        return quad * quad_steps + order % quad_steps

    def fetch(order):
        for head in range(2):
            e_copy(order % 2, head, e_step(order) * 2 + head, False).start()

    ones = jnp.ones((16, count), bf16)

    def attend_back(order):
        step = e_step(order)
        pair, slot = step // slots, step % slots
        cols = aligned(slot, SLOT)
        place = order % 2

        @pl.when(order + 1 < steps)
        def _():
            fetch(order + 1)

        for head in range(2):
            e_copy(place, head, 0, False).wait()
        sine_t, cosine_t = wave_t[:WAVE, cols], wave_t[WAVE:, cols]
        sc_t = (wave_t[:, cols] * scale_factor).astype(bf16)
        cs_t = (jnp.concatenate([cosine_t, sine_t], axis=0) * scale_factor).astype(bf16)
        values = v_row[slot, pair]
        g_lows, row_dots, g_probs, g_scores, g_qs, g_ks = [], [], [], [], [], []
        g_parts = [[], [], []]
        spans = [slice(head * HD, (head + 1) * HD) for head in range(2)]
        for head in range(2):
            at = pl.ds(pl.multiple_of(pair * PAIR + head * HD, HD), HD)
            g_rows = g_ctx_t[at, cols].astype(f32) * inv_total[step * 2 + head]
            row_dots.append(jnp.sum(g_rows * ctx_t[at, cols].astype(f32), axis=0, keepdims=True))
            g_lows.append(g_rows.astype(bf16))
            zero = jnp.zeros_like(g_lows[head])
            g_pair = jnp.concatenate([g_lows[head], zero] if head == 0 else [zero, g_lows[head]], axis=0)
            g_probs.append(dot_nn(values, g_pair))
        for head in range(2):
            g_scores.append((e_buf[place, head].astype(f32) * (g_probs[head] - row_dots[head])).astype(bf16))
        for head in range(2):
            g_qs.append(dot_nn(jnp.concatenate([k8t[slot, pair, spans[head], :], cs_t], axis=0), g_scores[head]))
        for head in range(2):
            g_ks.append(dot_nt(jnp.concatenate([q8t[slot, pair, spans[head], :], sc_t], axis=0), g_scores[head]))
        for head in range(2):
            g_parts[2].append(dot_nt(g_lows[head], e_buf[place, head]))
        for head in range(2):
            k_t, q_t = k8t[slot, pair, spans[head], :], q8t[slot, pair, spans[head], :]
            g_q, g_k = g_qs[head], g_ks[head]
            first, second = g_q[HD : HD + WAVE], g_q[HD + WAVE :]
            g_qbox = jnp.concatenate(
                [first * sine_t - second * cosine_t, first * cosine_t + second * sine_t], axis=0
            ).astype(bf16)
            first, second = g_k[HD : HD + WAVE], g_k[HD + WAVE :]
            g_kbox = jnp.concatenate(
                [first * cosine_t - second * sine_t, first * sine_t + second * cosine_t], axis=0
            ).astype(bf16)
            g_parts[0].append(g_q[:HD] + dot_nn(w_box_t[...], g_qbox))
            g_parts[1].append(g_k[:HD] + dot_nn(w_box_t[...], g_kbox))
            g_w_box[...] += dot_nt(g_qbox, q_t) + dot_nt(g_kbox, k_t)
        for part in range(3):
            at = pl.ds(pl.multiple_of(part * QUAD + pair % 2 * PAIR, PAIR), PAIR)
            flip[at, cols] = jnp.concatenate(g_parts[part], axis=0).astype(bf16)

    kept = [slope.at[(2 + turn) * count : (2 + turn) * count + BLOCK] for turn in range(2)]
    kept_last = g_down.at[:BLOCK]

    @pl.loop(0, quads)
    def _(turn):
        quad = quads - 1 - turn

        @pl.loop(0, quad_steps)
        def _(inner):
            order = turn * quad_steps + inner
            if comm:
                pl.when(order % 2 == 1)(functools.partial(sum_tick, 5 + order // 2, (0,)))
                pl.when((order % 2 == 0) & (order > 0))(functools.partial(sum_tick, 4 + order // 2, (1, 2, 3)))
            attend_back(order)

        if comm:
            pl.when(turn == quads - 1)(functools.partial(sum_tick, 10, (1, 2, 3)))

        @pl.when(turn < quads - 1)
        def _():
            at = pl.ds(pl.multiple_of((2 + turn) * count, count), BLOCK)
            slope[at, :] = held[aligned(quad, BLOCK), :]

        @pl.when(turn == quads - 1)
        def _():
            kept_last[...] = held[aligned(quad, BLOCK), :]

        for part in range(2):
            at = pl.ds(pl.multiple_of(quad * BLOCK + part * HALF, HALF), HALF)
            held[at, :] = dot_nt(tok_t[part * HALF : (part + 1) * HALF, :], flip[...]).astype(bf16)
        sum_start(9 + turn)
        g_b_qkv[:, aligned(quad, BLOCK)] = dot_nt(ones, flip[...])[:1]
        if comm:
            fold(quad, 0, share_qkv, g_b_qkv, quad_order)

        @pl.when(turn < quads - 1)
        def _():
            for block in range(row_blocks):
                at = pl.ds(pl.multiple_of(turn * count + block * ROWS, ROWS), ROWS)
                rows = slice(block * ROWS, (block + 1) * ROWS)
                slope[at, :] = jnp.transpose(flip[:, rows].astype(f32)).astype(bf16)

    g_w_box[...] = g_w_box[...] * (1.0 / scale_factor)
    tok_out = []

    def token_grad(block):
        rows = slice(block * ROWS, (block + 1) * ROWS)
        last_part = jnp.transpose(dot_nn(kept_last[...], flip[:, rows]))
        first_part = dot_nt(slope[rows, :], kept[0][...])
        rest = dot_nt(slope[count + rows.start : count + rows.stop, :], kept[1][...])
        total[rows, :] += last_part + first_part + rest
        tok_out.append(pltpu.make_async_copy(total.at[rows], g_tok_out.at[rows], io_sem.at[4 + block]))
        tok_out[-1].start()

    if comm:
        g_small[:, :HD] = g_w_box[...]
        sums.sum_cores(0)
        sum_tick(11, (1, 2, 3))
        sum_tick(11, (0,))
        sums.sum_far(0)
        sum_tick(12, (2, 3))
        token_grad(0)
        token_grad(1)
        sum_tick(12, (1,))
        sums.sum_near(0)
        token_grad(2)
        sum_tick(13, (3,))
        sum_tick(13, (2,))
        sums.sum_column(0)
        token_grad(3)
        blocks.results_in(0)
        moves = [copy_in(final.at[PIECE:], final_out.at[PIECE:], 2)]
        moves[0].start()
        sum_tick(14, (3,))
        sums.sum_end(0)
        for stream in range(STREAMS):
            blocks.summed(stream)
        sums.summed(0)
        blocks.results_in(1)
        moves.append(copy_in(final.at[:PIECE], final_out.at[:PIECE], 3))
        moves[1].start()
        sums.results_in(1)
        moves.append(copy_in(small_final, small_out, 8))
        moves[2].start()
        for copy in moves:
            copy.wait()
    else:
        for block in range(row_blocks):
            token_grad(block)
        g_w_box_out[...] = g_w_box[...]
        g_b_qkv_out[...] = g_b_qkv[...]
        g_b_up_out[...] = g_b_up[...]
        g_vectors_out[...] = g_vectors[...]
        out = copy_in(held, g_held, 2)
        out.start()
        out.wait()
    for copy in tok_out:
        copy.wait()


def shaped(shape, dtype):
    return jax.ShapeDtypeStruct(shape, dtype)


def in_vmem(count):
    return [pl.BlockSpec(memory_space=pltpu.VMEM)] * count


def in_hbm(count):
    return [pl.BlockSpec(memory_space=pl.ANY)] * count


def run_layer(comm, tokens, cotangent, coords, segs, big, little):
    count, width = tokens.shape
    ff = 4 * BLOCK
    slots, pairs = count // SLOT, HEADS // 2
    held_shape = (STREAMS * BLOCK, BLOCK)
    out_shape = [
        shaped((count, width), bf16),
        shaped((count, width), f32),
        shaped((slots * HEADS, SLOT, SLOT), bf16),
    ]
    out_specs = in_hbm(3)
    if comm:
        out_shape += [shaped((STREAMS * PIECE, BLOCK), f32), shaped((8, SMALL), f32)]
        out_specs += in_hbm(2)
    else:
        out_shape += [shaped(held_shape, bf16), shaped((2 * WAVE, HD), f32), shaped((1, 3 * width), f32)]
        out_shape += [shaped((1, ff), f32), shaped((8, width), f32)]
        out_specs += in_hbm(1) + in_vmem(4)
    vmem = pltpu.VMEM
    dma = pltpu.SemaphoreType.DMA
    scratch = [
        vmem(held_shape, bf16),
        vmem(held_shape, bf16),
        vmem((ff // BLOCK * count, BLOCK), bf16),
        vmem((slots, pairs, PAIR, SLOT), bf16),
        vmem((slots, pairs, PAIR, SLOT), bf16),
        vmem((slots, pairs, SLOT, PAIR), bf16),
        vmem((width, count), bf16),
        vmem((2 * WAVE, count), f32),
        vmem((count, 2 * WAVE), f32),
        vmem((2, 2, SLOT, SLOT), bf16),
        vmem((count, width), f32),
        vmem((count, width), f32),
        vmem((width, count), bf16),
        vmem((count, width), bf16),
        vmem((width, count), bf16),
        vmem((width, count), bf16),
        vmem((count, 128), f32),
        vmem((slots * HEADS, 1, SLOT), f32),
        vmem((2 * WAVE, HD), bf16),
        vmem((HD, 2 * WAVE), bf16),
        vmem((1, 3 * width), f32),
        vmem((1, ff), f32),
        vmem((8, width), f32),
        vmem((2 * WAVE, HD), f32),
        vmem((1, 3 * width), f32),
        vmem((1, ff), f32),
        vmem((8, width), f32),
        dma((2, 2)),
        dma((32,)),
        vmem(coords.shape, jnp.int32),
        vmem(segs.shape, jnp.int32),
        vmem((PAIR, 4 * WAVE), bf16),
        vmem((4 * WAVE, PAIR), bf16),
    ]
    if comm:
        scratch += [
            vmem((STREAMS * PIECE, BLOCK), f32),
            vmem((128, SMALL), f32),
            vmem((256, SMALL // 2), f32),
            vmem((128, SMALL), f32),
            vmem((8, SMALL), f32),
            pltpu.SemaphoreType.REGULAR((2,)),
            *[vmem(value.shape, f32) for value in little],
            dma((STREAMS, 4)), dma((STREAMS, 2)), dma((STREAMS, 4)), dma((STREAMS,)), dma((2, 2)),
            dma((1, 4)), dma((1, 2)), dma((1, 4)), dma((1,)),
            dma((2, 2)),
        ]
        extra = dict(collective_id=0, has_side_effects=True)
    else:
        extra = {}
    return pl.pallas_call(
        functools.partial(layer_kernel, comm),
        out_shape=out_shape,
        in_specs=in_hbm(4 + len(big)) + (in_hbm if comm else in_vmem)(len(little)),
        out_specs=out_specs,
        scratch_shapes=scratch,
        compiler_params=pltpu.CompilerParams(vmem_limit_bytes=vmem_limit, **extra),
        name="layer",
    )(tokens, cotangent, coords, segs, *big, *little)


def finish_kernel(*refs):
    layer_in, tok_in, blocks_in, small_in = refs[:4]
    layer_out, tok_out, p_qkv, p_out, p_up, p_down = refs[4:10]
    small_out = refs[10:19]
    layer, tok, blocks, small = refs[19:23]
    small_rows = refs[23:32]
    load_sem, store_sem = refs[32:]
    width = layer_in.shape[1]
    loads, stores = [], []
    parts = 4
    rows = layer_in.shape[0] // parts
    small_load = pltpu.make_async_copy(small_in, small, load_sem.at[0])
    loads.append((pltpu.make_async_copy(blocks_in, blocks, load_sem.at[1]), []))
    for quad in range(width // QUAD):
        for part in range(3):
            loads[0][1].append((
                blocks.at[quad * PIECE : (quad + 1) * PIECE, part * QUAD : (part + 1) * QUAD],
                p_qkv.at[:, part * width + quad * QUAD : part * width + (quad + 1) * QUAD],
            ))
    loads[0][1].append((blocks.at[3 * PIECE : 4 * PIECE], p_out))
    for block in range(4):
        loads[0][1].append((
            blocks.at[(4 + block) * PIECE : (5 + block) * PIECE], p_up.at[:, block * BLOCK : (block + 1) * BLOCK]
        ))
    loads[0][1].append((blocks.at[8 * PIECE : 12 * PIECE], p_down))
    for source, held, target in ((tok_in, tok, tok_out), (layer_in, layer, layer_out)):
        for part in range(parts):
            at = slice(part * rows, (part + 1) * rows)
            copy = pltpu.make_async_copy(source.at[at], held.at[at], load_sem.at[1 + len(loads)])
            loads.append((copy, [(held.at[at], target.at[at])]))
    small_load.start()
    for copy, _ in loads:
        copy.start()

    def store(source, target):
        stores.append(pltpu.make_async_copy(source, target, store_sem.at[len(stores)]))
        stores[-1].start()

    small_load.wait()
    for row in range(8):
        small_rows[row][...] = small[row : row + 1, 128 : 128 + small_rows[row].shape[1]]
    small_rows[8][...] = small[:, :HD]
    for source, target in zip(small_rows, small_out):
        store(source, target)
    for copy, moves in loads:
        copy.wait()
        for source, target in moves:
            store(source, target)
    for copy in stores:
        copy.wait()


def run_finish(layer_out, g_tok, blocks, small, big, little):
    shapes = [shaped(layer_out.shape, bf16), shaped(g_tok.shape, f32)]
    shapes += [shaped(w.shape, f32) for w in big + little]
    dma = pltpu.SemaphoreType.DMA
    return pl.pallas_call(
        finish_kernel,
        out_shape=shapes,
        in_specs=in_hbm(4),
        out_specs=in_hbm(len(shapes)),
        scratch_shapes=[
            pltpu.VMEM(layer_out.shape, bf16), pltpu.VMEM(g_tok.shape, f32), pltpu.VMEM(blocks.shape, f32),
            pltpu.VMEM(small.shape, f32), *[pltpu.VMEM(v.shape, f32) for v in little], dma((16,)), dma((40,)),
        ],
        compiler_params=pltpu.CompilerParams(vmem_limit_bytes=vmem_limit),
        name="finish",
    )(layer_out, g_tok, blocks, small)


def to_blocks(w_qkv, w_out, w_up, w_down):
    width = w_out.shape[1]
    qkv = w_qkv.reshape(width, 3, width // QUAD, QUAD).transpose(2, 0, 1, 3).reshape(-1, BLOCK)
    up = w_up.reshape(width, -1, BLOCK).transpose(1, 0, 2).reshape(-1, BLOCK)
    return jnp.concatenate([qkv, w_out, up, w_down], axis=0)


def from_blocks(held, width):
    qkv = held[: 3 * BLOCK].reshape(width // QUAD, width, 3, QUAD).transpose(1, 2, 0, 3).reshape(width, -1)
    up = held[4 * BLOCK : 8 * BLOCK].reshape(-1, width, BLOCK).transpose(1, 0, 2).reshape(width, -1)
    return qkv, held[3 * BLOCK : 4 * BLOCK], up, held[8 * BLOCK :]


def per_device(
    mesh_shape, tokens, cotangent, segments, box_coords, w_qkv, b_qkv, w_box, w_out, b_out, gain_one, shift_one,
    w_up, b_up, w_down, b_down, gain_two, shift_two,
):
    count, width = tokens.shape
    segs = segments.reshape(1, -1)
    vectors = [b_qkv, b_up, b_out, gain_one, shift_one, b_down, gain_two, shift_two]
    if mesh_shape == (16, 2):
        little = [v.reshape(1, -1) for v in vectors] + [w_box]
        big = [w_qkv, w_out, w_up, w_down]
        layer_out, g_tok, _, blocks, small = run_layer(True, tokens, cotangent, box_coords, segs, big, little)
        layer_out, g_tok, p_wq, p_wo, p_wu, p_wd, *rest = run_finish(layer_out, g_tok, blocks, small, big, little)
        p_bq, p_bu, p_bo, p_g1, p_s1, p_bd, p_g2, p_s2 = [v.reshape(-1) for v in rest[:8]]
        p_wb = rest[8]
    else:
        low = lambda value: value.astype(bf16)
        gather = lambda value: lax.all_gather(low(value), "fsdp", axis=0, tiled=True)
        held = to_blocks(gather(w_qkv), gather(w_out), gather(w_up), gather(w_down))
        wb, bq, bu, *six = [gather(v) for v in [w_box] + vectors]
        order = quad_order(jnp.arange(3 * width))
        rows = jnp.stack([jnp.zeros((width,), bf16)] * 2 + six).astype(f32)
        layer_out, g_tok, _, g_held, g_wb, g_bq, g_bu, g_six = run_layer(
            False, tokens, cotangent, box_coords, segs, [held],
            [wb, bq[order].astype(f32).reshape(1, -1), bu.astype(f32).reshape(1, -1), rows],
        )

        def scatter(grad):
            part = lax.psum_scatter(grad, "fsdp", scatter_dimension=0, tiled=True)
            return lax.psum(part, "rep").astype(f32)

        p_wq, p_wo, p_wu, p_wd = [scatter(g) for g in from_blocks(g_held, width)]
        g_bq = jnp.zeros((3 * width,), f32).at[order].set(g_bq[0])
        p_wb, p_bq, p_bu = scatter(g_wb), scatter(g_bq), scatter(g_bu[0])
        p_bo, p_g1, p_s1, p_bd, p_g2, p_s2 = [scatter(g_six[2 + i]) for i in range(VECTORS)]
    return (
        layer_out, g_tok, p_wq, p_bq, p_wb, p_wo, p_bo, p_g1, p_s1,
        p_wu, p_bu, p_wd, p_bd, p_g2, p_s2,
    )


def solution(mesh):
    tokens = P(("fsdp", "rep"), None)
    matrix, vector = P("fsdp", None), P("fsdp")
    kinds = [matrix, vector, matrix, matrix, vector, vector, vector, matrix, vector, matrix, vector, vector, vector]
    return jax.shard_map(
        functools.partial(per_device, (mesh.shape["fsdp"], mesh.shape["rep"])),
        mesh=mesh,
        in_specs=(tokens, tokens, P(("fsdp", "rep")), P(None, ("fsdp", "rep")), *kinds),
        out_specs=(tokens, tokens, *kinds),
        check_vma=False,
    )
```
